32 devices in a mesh: dp: 16 (over z, x, core), mp: 2 (over y).
Axes of the slice: x: 2, y: 2, z: 4, core: 2. Of those that a mesh axis runs over, the one named last changes fastest.
Arguments:
- hidden: bfloat16 [49152, 768], P('dp'), may hold values from -6 to 6
- doc_lengths: int32 [48, 8], P('dp'), may hold values from 1 to 512, 1024 in all within a row
- query_weight: bfloat16 [768, 384], P('dp', 'mp'), may hold values from -0.21875 to 0.21875
- key_weight: bfloat16 [768, 384], P('dp', 'mp'), may hold values from -0.21875 to 0.21875
- value_weight: bfloat16 [768, 384], P('dp', 'mp'), may hold values from -0.21875 to 0.21875
- query_bias: float32 [384], P('mp'), may hold values from -3 to 3
- value_bias: float32 [384], P('mp'), may hold values from -2 to 2
- depth_weight: bfloat16 [9, 768], P(None, 'dp'), may hold values from -2 to 2
- point_weight: bfloat16 [768, 384], P('dp', 'mp'), may hold values from -0.21875 to 0.21875
- point_bias: float32 [384], P('mp'), may hold values from -2 to 2
- kernel_weight: bfloat16 [384, 54], P('mp'), may hold values from -0.3125 to 0.3125
- kernel_bias: float32 [54], replicated, may hold values from -3 to 3
- conv_weight: bfloat16 [768, 384], P('dp', 'mp'), may hold values from -0.21875 to 0.21875
- conv_bias: float32 [384], P('mp'), may hold values from -2 to 2
- out_weight: bfloat16 [2, 384, 768], P(None, 'mp', 'dp'), may hold values from -0.625 to 0.625
- out_bias: float32 [768], replicated, may hold values from -2 to 2
- norm1_gain: float32 [768], replicated, may hold values from 0.5 to 1.5
- norm1_bias: float32 [768], replicated, may hold values from -2 to 2
- ffn_in_weight: bfloat16 [2, 384, 1536], P('mp', None, 'dp'), may hold values from -0.3125 to 0.3125
- ffn_in_bias: float32 [2, 1536], P('mp'), may hold values from -3 to 3
- ffn_out_weight: bfloat16 [2, 1536, 384], P('mp', 'dp'), may hold values from -0.15625 to 0.15625
- ffn_out_bias: float32 [768], P('mp'), may hold values from -2 to 2
- norm2_gain: float32 [768], P('mp'), may hold values from 0.5 to 1.5
- norm2_bias: float32 [768], P('mp'), may hold values from -2 to 2
- out_grad: bfloat16 [49152, 768], P('dp', 'mp'), may hold values from -6 to 6
Outputs:
- output: bfloat16 [49152, 768], P('dp', 'mp')
- input_grad: float32 [49152, 768], P('dp', 'mp')
- query_weight_grad: float32 [768, 384], P('dp', 'mp')
- key_weight_grad: float32 [768, 384], P('dp', 'mp')
- value_weight_grad: float32 [768, 384], P('dp', 'mp')
- query_bias_grad: float32 [384], P('mp')
- value_bias_grad: float32 [384], P('mp')
- depth_weight_grad: float32 [9, 768], P(None, 'dp')
- point_weight_grad: float32 [768, 384], P('dp', 'mp')
- point_bias_grad: float32 [384], P('mp')
- kernel_weight_grad: float32 [384, 54], P('mp')
- kernel_bias_grad: float32 [54], replicated
- conv_weight_grad: float32 [768, 384], P('dp', 'mp')
- conv_bias_grad: float32 [384], P('mp')
- out_weight_grad: float32 [2, 384, 768], P(None, 'mp', 'dp')
- out_bias_grad: float32 [768], replicated
- norm1_gain_grad: float32 [768], replicated
- norm1_bias_grad: float32 [768], replicated
- ffn_in_weight_grad: float32 [2, 384, 1536], P('mp', None, 'dp')
- ffn_in_bias_grad: float32 [2, 1536], P('mp')
- ffn_out_weight_grad: float32 [2, 1536, 384], P('mp', 'dp')
- ffn_out_bias_grad: float32 [768], P('mp')
- norm2_gain_grad: float32 [768], P('mp')
- norm2_bias_grad: float32 [768], P('mp')
The draws below stay inside these ranges and needn't reach their ends.
Inputs may be any that keep to these rules, and one draw needn't show every extreme that they name: `doc_lengths`: row s lists, in order, the lengths of the 8 documents packed into sequence s; every row sums to 1024 and its longest document has exactly 512 tokens.
All inputs are finite; a program needn't handle non-finite values.
Results may differ from the reference program's by a relative error of at most 0.014.
Values may be sent and summed in bfloat16 or wider, within the bound.
A program may use at most 320 MiB of HBM per device.

```python
import math
import jax
import jax.numpy as jnp
import numpy as np
from jax import lax

D = 768
HEADS = 6
HEAD_DIM = 64
KERNEL = 9
GROUPS = 2
SEQ_LEN = 1024
DOCS = 8
MOST_DOC = 512
A = 384
GIN = 384
GH = 1536
SEQS = 48
TOKENS = 49152


def block_scale(own_key, shape, pieces, least, largest):
    loudness, own = 1.0, jax.random.fold_in(own_key, 6)
    for axis_at, shards_of in pieces:
        steps = jnp.exp(jax.random.uniform(jax.random.fold_in(own, axis_at), (shards_of,), jnp.float32, least / len(pieces), largest / len(pieces)))
        loudness = loudness * jnp.repeat(steps, shape[axis_at] // shards_of).reshape([-1 if axis == axis_at else 1 for axis in range(len(shape))])
    return loudness


def split_up(amount, total, most, lean):
    weights = [(1 << 20) // math.isqrt(standing ** lean) + 1 for standing in range(2, amount + 1)]
    rest, counts = total - most - (amount - 1), [1] * (amount - 1)
    while rest > 0:
        candidates = [i for i in range(amount - 1) if counts[i] < most]
        mass, budget = sum([weights[i] for i in candidates]), rest
        for i in candidates:
            extra = min(most - counts[i], max(1, budget * weights[i] // mass), rest)
            counts[i] = counts[i] + extra
            rest = rest - extra
    return np.array([most] + counts)


def uneven(own_key, amount, total, most, skew):
    if amount == 2:
        one = jax.random.randint(own_key, (), max(1, total - most), min(most, total - 1) + 1)
        return jnp.stack([one, total - one])
    sizes = jnp.asarray(split_up(amount, total, most, skew), jnp.int32)
    pairs = (amount - 1) // 2
    donor, receiver = sizes[1:1 + 2 * pairs:2], sizes[2:2 + 2 * pairs:2]
    room = jnp.minimum(donor - 1, most - receiver)
    passed = jax.random.randint(jax.random.fold_in(own_key, 1), (pairs,), 0, 1 << 20) % (room + 1)
    sizes = sizes.at[1:1 + 2 * pairs:2].set(donor - passed).at[2:2 + 2 * pairs:2].set(receiver + passed)
    return sizes[jax.random.permutation(jax.random.fold_in(own_key, 2), amount)]


def gaussian(stream_key, shape, width, most, split=(), kind=jnp.bfloat16):
    factor_of = block_scale(stream_key, shape, split, -0.22, 0.18) if split else 1.0
    values = jax.random.normal(stream_key, shape, jnp.float32) * width * factor_of
    return jnp.minimum(jnp.maximum(values, -most), most).astype(kind)


def setup_inputs(seed: int = 0) -> dict:
    key_list = jax.random.split(jax.random.key(seed), 26)
    hidden = gaussian(key_list[0], (TOKENS, D), 1.0, 6.0, ((0, 16),))
    doc_lengths = jax.vmap(lambda own: uneven(own, DOCS, SEQ_LEN, MOST_DOC, 2))(jax.random.split(key_list[1], SEQS)).reshape((SEQS, DOCS)).astype(jnp.int32)
    query_weight = gaussian(key_list[2], (D, A), D ** -0.5, 0.21875, ((0, 16), (1, 2)))
    key_weight = gaussian(key_list[3], (D, A), D ** -0.5, 0.21875, ((0, 16), (1, 2)))
    value_weight = gaussian(key_list[4], (D, A), D ** -0.5, 0.21875, ((0, 16), (1, 2)))
    query_bias = gaussian(key_list[5], (A,), 0.5, 3.0, ((0, 2),), jnp.float32)
    value_bias = gaussian(key_list[6], (A,), 0.3, 2.0, ((0, 2),), jnp.float32)
    depth_weight = gaussian(key_list[7], (KERNEL, D), KERNEL ** -0.5, 2.0, ((1, 16),))
    point_weight = gaussian(key_list[8], (D, A), D ** -0.5, 0.21875, ((0, 16), (1, 2)))
    point_bias = gaussian(key_list[9], (A,), 0.3, 2.0, ((0, 2),), jnp.float32)
    kernel_weight = gaussian(key_list[10], (A, HEADS * KERNEL), A ** -0.5, 0.3125, ((0, 2),))
    kernel_bias = gaussian(key_list[11], (HEADS * KERNEL,), 0.5, 3.0, (), jnp.float32)
    conv_weight = gaussian(key_list[12], (D, A), D ** -0.5, 0.21875, ((0, 16), (1, 2)))
    conv_bias = gaussian(key_list[13], (A,), 0.3, 2.0, ((0, 2),), jnp.float32)
    out_weight = gaussian(key_list[14], (2, A, D), (D // 8) ** -0.5, 0.625, ((1, 2), (2, 16)))
    out_bias = gaussian(key_list[15], (D,), 0.3, 2.0, (), jnp.float32)
    norm1_gain = jnp.clip(1.0 + 0.1 * jax.random.normal(key_list[16], (D,), jnp.float32), 0.5, 1.5)
    norm1_bias = gaussian(key_list[17], (D,), 0.3, 2.0, (), jnp.float32)
    ffn_in_weight = gaussian(key_list[18], (GROUPS, GIN, GH), GIN ** -0.5, 0.3125, ((0, 2), (2, 16)))
    ffn_in_bias = gaussian(key_list[19], (GROUPS, GH), 0.5, 3.0, ((0, 2),), jnp.float32)
    ffn_out_weight = gaussian(key_list[20], (GROUPS, GH, GIN), GH ** -0.5, 0.15625, ((0, 2), (1, 16)))
    ffn_out_bias = gaussian(key_list[21], (D,), 0.3, 2.0, ((0, 2),), jnp.float32)
    norm2_gain = jnp.clip(1.0 + 0.1 * jax.random.normal(key_list[22], (D,), jnp.float32), 0.5, 1.5)
    norm2_bias = gaussian(key_list[23], (D,), 0.3, 2.0, ((0, 2),), jnp.float32)
    out_grad = gaussian(key_list[24], (TOKENS, D), 1.0, 6.0, ((0, 16), (1, 2)))
    return dict(hidden=hidden, doc_lengths=doc_lengths, query_weight=query_weight, key_weight=key_weight, value_weight=value_weight, query_bias=query_bias, value_bias=value_bias, depth_weight=depth_weight, point_weight=point_weight, point_bias=point_bias, kernel_weight=kernel_weight, kernel_bias=kernel_bias, conv_weight=conv_weight, conv_bias=conv_bias, out_weight=out_weight, out_bias=out_bias, norm1_gain=norm1_gain, norm1_bias=norm1_bias, ffn_in_weight=ffn_in_weight, ffn_in_bias=ffn_in_bias, ffn_out_weight=ffn_out_weight, ffn_out_bias=ffn_out_bias, norm2_gain=norm2_gain, norm2_bias=norm2_bias, out_grad=out_grad)


@jax.custom_vjp
def low(v):
    return lax.optimization_barrier(v.astype(jnp.bfloat16)).astype(jnp.float32)

@jax.custom_vjp
def low_back(v):
    return v

def low_keep(v):
    return (low(v), None)

def low_pass(kept, grad):
    return (grad,)

def back_keep(v):
    return (v, None)

def back_low(kept, grad):
    return (low(grad),)
low.defvjp(low_keep, low_pass)
low_back.defvjp(back_keep, back_low)
EPSILON = 1e-06
MASK_FILL = -1e+30
INV_ROOT2 = 0.7071067811865476

def both_ways(tensor):
    return low_back(low(tensor))

def matmul(left, right):
    return jnp.dot(left, right, precision=lax.Precision.HIGHEST)

def shifted(tensor, offset, half_width):
    filler = jnp.zeros((half_width,) + tensor.shape[1:], tensor.dtype)
    padded = jnp.concatenate([filler, tensor, filler], axis=0)
    return padded[half_width + offset:half_width + offset + tensor.shape[0]]

def same_segment(segment, offset, half_width):
    filler = jnp.full((half_width,), -1, dtype=jnp.int32)
    padded = jnp.concatenate([filler, segment, filler])
    return padded[half_width + offset:half_width + offset + segment.shape[0]] == segment

def segment_ids(lengths_row, seq_rows):
    doc_ends = jnp.cumsum(lengths_row).astype(jnp.int32)
    positions = jnp.arange(seq_rows, dtype=jnp.int32)
    return lax.optimization_barrier(jnp.sum((positions[:, None] >= doc_ends[None, :]).astype(jnp.int32), axis=1))

def gelu(tensor):
    return 0.5 * tensor * (1.0 + lax.erf(tensor * INV_ROOT2))

def layer_norm(tensor, gain_vec, shift_vec):
    mean_row = lax.optimization_barrier(jnp.mean(tensor, axis=-1, keepdims=True))
    centered_input = tensor - mean_row
    spread_row = lax.optimization_barrier(jnp.mean(centered_input * centered_input, axis=-1, keepdims=True))
    return centered_input * lax.rsqrt(spread_row + EPSILON) * gain_vec + shift_vec

def layer(rows_in, segment, params):
    w_query, w_key, w_value, b_query, b_value, w_depth, w_point, b_point, w_kernel, b_kernel, w_conv, b_conv, w_out, b_out, first_norm_gain, first_norm_bias, w_inner, b_inner, w_outer, b_outer, second_norm_gain, second_norm_bias = params
    seq_rows = rows_in.shape[0]
    half_width = KERNEL // 2
    scale_factor = HEAD_DIM ** (-0.5)
    queries = both_ways(matmul(rows_in, w_query) + b_query)
    keys_all = both_ways(matmul(rows_in, w_key))
    values_all = both_ways(matmul(rows_in, w_value) + b_value)
    tap_masks = [same_segment(segment, tap_index - half_width, half_width).astype(jnp.float32)[:, None] for tap_index in range(KERNEL)]
    depthwise = jnp.zeros_like(rows_in)
    for tap_index in range(KERNEL):
        moved_rows = shifted(rows_in, tap_index - half_width, half_width)
        depthwise = depthwise + w_depth[tap_index] * moved_rows * tap_masks[tap_index]
    depthwise = low(depthwise)
    key_conv = low_back(matmul(depthwise, w_point) + b_point)
    conv_attn = both_ways(key_conv * queries)
    logits = low_back(matmul(conv_attn, w_kernel) + b_kernel)
    kernel_probs = jax.nn.softmax(logits.reshape(seq_rows, HEADS, KERNEL), axis=-1)
    conv_values = low_back(matmul(rows_in, w_conv) + b_conv).reshape(seq_rows, HEADS, HEAD_DIM)
    conv_context = jnp.zeros_like(conv_values)
    for tap_index in range(KERNEL):
        weights_now = kernel_probs[:, :, tap_index] * tap_masks[tap_index]
        conv_context = conv_context + weights_now[:, :, None] * shifted(conv_values, tap_index - half_width, half_width)
    conv_context = both_ways(conv_context.reshape(seq_rows, HEADS * HEAD_DIM))
    query_heads = queries.reshape(seq_rows, HEADS, HEAD_DIM)
    key_heads = keys_all.reshape(seq_rows, HEADS, HEAD_DIM)
    value_heads = values_all.reshape(seq_rows, HEADS, HEAD_DIM)
    scores = low_back(jnp.einsum('qhd,khd->hqk', query_heads, key_heads, precision=lax.Precision.HIGHEST) * scale_factor)
    allowed = segment[:, None] == segment[None, :]
    scores = jnp.where(allowed[None], scores, MASK_FILL)
    probs = low(jax.nn.softmax(scores, axis=-1))
    context = jnp.einsum('hqk,khd->qhd', probs, value_heads, precision=lax.Precision.HIGHEST)
    context = both_ways(context.reshape(seq_rows, HEADS * HEAD_DIM))
    branch = low_back(matmul(context, w_out[0]) + matmul(conv_context, w_out[1]) + b_out)
    normalized_rows = layer_norm(rows_in + branch, first_norm_gain, first_norm_bias)
    grouped = low(normalized_rows).reshape(seq_rows, GROUPS, D // GROUPS)
    inner_pre = low_back(jnp.einsum('lgi,gih->lgh', grouped, w_inner, precision=lax.Precision.HIGHEST) + b_inner)
    activated = low(gelu(inner_pre))
    outer = jnp.einsum('lgh,ghi->lgi', activated, w_outer, precision=lax.Precision.HIGHEST).reshape(seq_rows, D)
    outer = low_back(outer + b_outer)
    return layer_norm(normalized_rows + outer, second_norm_gain, second_norm_bias)

def reference(hidden, doc_lengths, query_weight, key_weight, value_weight, query_bias, value_bias, depth_weight, point_weight, point_bias, kernel_weight, kernel_bias, conv_weight, conv_bias, out_weight, out_bias, norm1_gain, norm1_bias, ffn_in_weight, ffn_in_bias, ffn_out_weight, ffn_out_bias, norm2_gain, norm2_bias, out_grad):
    weights = (query_weight, key_weight, value_weight, query_bias, value_bias, depth_weight, point_weight, point_bias, kernel_weight, kernel_bias, conv_weight, conv_bias, out_weight, out_bias, norm1_gain, norm1_bias, ffn_in_weight, ffn_in_bias, ffn_out_weight, ffn_out_bias, norm2_gain, norm2_bias)
    params = tuple((item.astype(jnp.float32) for item in weights))
    seq_hidden = hidden.reshape(SEQS, SEQ_LEN, D)
    seq_cotangent = out_grad.reshape(SEQS, SEQ_LEN, D)

    def one_sequence(running, inputs):
        rows_in, lengths_row, cotangent = inputs
        segment = segment_ids(lengths_row, SEQ_LEN)

        def apply_layer(rows_arg, *param_args):
            return layer(rows_arg, segment, param_args)
        layer_output, pullback = jax.vjp(apply_layer, rows_in.astype(jnp.float32), *params)
        gradients = pullback(cotangent.astype(jnp.float32))
        running = tuple((earlier + gradient for earlier, gradient in zip(running, gradients[1:])))
        return (running, (layer_output.astype(jnp.bfloat16), gradients[0]))
    zeros_init = tuple((jnp.zeros_like(item) for item in params))
    totals, (outputs, input_grads) = lax.scan(one_sequence, zeros_init, (seq_hidden, doc_lengths, seq_cotangent))
    return (outputs.reshape(TOKENS, D), input_grads.reshape(TOKENS, D), totals[0], totals[1], totals[2], totals[3], totals[4], totals[5], totals[6], totals[7], totals[8], totals[9], totals[10], totals[11], totals[12], totals[13], totals[14], totals[15], totals[16], totals[17], totals[18], totals[19], totals[20], totals[21])
```

```python
import functools
import jax
import jax.numpy as jnp
from jax import lax
from jax.experimental import pallas as pl
from jax.experimental.pallas import tpu as pltpu

from jax.sharding import PartitionSpec as P

MESH = pl.DeviceIdType.MESH


def at(dp, mp):
    return (dp, mp)


def places(count):
    dp = lax.axis_index("dp")
    core = lax.rem(dp, 2)
    side = lax.rem(lax.div(dp, 2), 2)
    deep = lax.div(dp, 4)
    return lax.axis_index("mp"), core, side, deep, count // 4


def index_of(deep, side, core):
    return (deep * 2 + side) * 2 + core


def greet(count):
    mp, core, side, deep, parts = places(count)
    barrier = pltpu.get_barrier_semaphore()
    peers = [index_of(lax.rem(deep + k, parts), side, core) for k in range(1, parts)]
    peers += [index_of(deep, 1 - side, core), index_of(deep, side, 1 - core)]
    for peer in peers:
        pl.semaphore_signal(barrier, inc=1, device_id=at(peer, mp), device_id_type=MESH)
    pl.semaphore_wait(barrier, len(peers))


def gather_kernel(count, own_ref, out_ref, own_sem, send_sem, recv_sem):
    mp, core, side, deep, parts = places(count)
    me = index_of(deep, side, core)
    greet(count)
    local = pltpu.make_async_copy(own_ref.at[0], out_ref.at[me], own_sem)
    local.start()
    started = []

    def push(source, block, target):
        copy = pltpu.make_async_remote_copy(
            src_ref=source,
            dst_ref=out_ref.at[block],
            send_sem=send_sem.at[len(started)],
            recv_sem=recv_sem.at[block],
            device_id=at(target, mp),
            device_id_type=MESH,
        )
        copy.start()
        started.append(copy)

    def arrive(block):
        pltpu.make_async_copy(own_ref.at[0], out_ref.at[block], recv_sem.at[block]).wait()

    beside = index_of(deep, 1 - side, core)
    twin = index_of(deep, side, 1 - core)
    for k in range(1, parts):
        push(own_ref.at[0], me, index_of(lax.rem(deep + k, parts), side, core))
    push(own_ref.at[0], me, beside)
    push(own_ref.at[0], me, twin)
    arrive(beside)
    push(out_ref.at[beside], beside, twin)
    for k in range(1, parts):
        block = index_of(lax.rem(deep + parts - k, parts), side, core)
        arrive(block)
        push(out_ref.at[block], block, beside)
        push(out_ref.at[block], block, twin)
    for k in range(1, parts):
        block = index_of(lax.rem(deep + parts - k, parts), 1 - side, core)
        arrive(block)
        push(out_ref.at[block], block, twin)
    for k in range(parts):
        for other in range(2):
            arrive(index_of(lax.rem(deep + parts - k, parts), other, 1 - core))
    for copy in started:
        copy.wait_send()
    local.wait()


def gather(own, count, ident):
    parts = count // 4
    sends = (parts - 1) * 4 + 3
    shape = (count,) + own.shape[1:]
    return pl.pallas_call(
        functools.partial(gather_kernel, count),
        out_shape=jax.ShapeDtypeStruct(shape, own.dtype),
        in_specs=[pl.BlockSpec(memory_space=pl.ANY)],
        out_specs=pl.BlockSpec(memory_space=pl.ANY),
        scratch_shapes=[
            pltpu.SemaphoreType.DMA,
            pltpu.SemaphoreType.DMA((sends,)),
            pltpu.SemaphoreType.DMA((count,)),
        ],
        compiler_params=pltpu.CompilerParams(collective_id=ident, has_side_effects=True),
        name="weight_gather",
    )(own)


def scatter_kernel(
    count, in_ref, small_ref, out_ref, total_ref,
    twin_in, side_in, deep_in, twin_sum, side_sum,
    small_in, small_out, send_sem, recv_sem, small_send, small_recv,
):
    mp, core, side, deep, parts = places(count)
    me = index_of(deep, side, core)
    barrier = pltpu.get_barrier_semaphore()
    pl.semaphore_signal(barrier, inc=1, device_id=at(me, 1 - mp), device_id_type=MESH)
    peers = [index_of(lax.rem(deep + k, parts), side, core) for k in range(1, parts)]
    peers += [index_of(deep, 1 - side, core), index_of(deep, side, 1 - core)]
    for peer in peers:
        pl.semaphore_signal(barrier, inc=1, device_id=at(peer, mp), device_id_type=MESH)
    pl.semaphore_wait(barrier, len(peers) + 1)
    beside = index_of(deep, 1 - side, core)
    twin = index_of(deep, side, 1 - core)
    started = []
    rows = in_ref.shape[1]
    step = rows // 4 if rows % 64 == 0 else rows

    def push(source, target_ref, slot, target, sends=send_sem, recvs=recv_sem, plane=mp):
        copy = pltpu.make_async_remote_copy(
            src_ref=source,
            dst_ref=target_ref,
            send_sem=sends.at[slot],
            recv_sem=recvs.at[slot],
            device_id=at(target, plane),
            device_id_type=MESH,
        )
        copy.start()
        started.append(copy)
        return copy

    def add(target, first, second):
        @pl.loop(0, rows // step)
        def _(i):
            part = pl.ds(pl.multiple_of(i * step, step), step)
            total = first[part, :].astype(jnp.float32) + second[part, :].astype(jnp.float32)
            target[part, :] = total.astype(target.dtype)

    small_hop = push(small_ref, small_in.at[0], 0, me, small_send, small_recv, 1 - mp)
    order = [(k, other) for k in list(range(1, parts)) + [0] for other in (1, 0)]
    hop = {}
    for slot, (k, other) in enumerate(order):
        z = lax.rem(deep + k, parts)
        s = 1 - side if other else side
        hop[(k, other)] = push(
            in_ref.at[index_of(z, s, 1 - core)], twin_in.at[slot], slot, twin
        )
    small_hop.wait_recv()
    shared = small_ref.shape[0] - SHARED_ROWS
    small_out[0, pl.ds(0, shared), :] = small_ref[pl.ds(0, shared), :]
    small_out[0, pl.ds(shared, SHARED_ROWS), :] = (
        small_ref[pl.ds(shared, SHARED_ROWS), :] + small_in[0, pl.ds(shared, SHARED_ROWS), :]
    )
    small_hop = push(small_out.at[0], small_in.at[1], 1, twin, small_send, small_recv)
    base = len(order)
    hop2 = {}
    for slot, (k, other) in enumerate(order):
        z = lax.rem(deep + k, parts)
        s = 1 - side if other else side
        hop[(k, other)].wait_recv()
        add(twin_sum.at[slot], in_ref.at[index_of(z, s, core)], twin_in.at[slot])
        if other:
            place = slot // 2
            hop2[k] = push(twin_sum.at[slot], side_in.at[place], base + place, beside)
        if slot == 1:
            small_hop.wait_recv()
            small_out[1] = small_out[0] + small_in[1]
            small_hop = push(small_out.at[1], small_in.at[2], 2, beside, small_send, small_recv)
    base2 = base + parts
    hop3 = []
    small_hops = []
    for place, k in enumerate(list(range(1, parts)) + [0]):
        hop2[k].wait_recv()
        add(side_sum.at[place], twin_sum.at[2 * place + 1], side_in.at[place])
        if k:
            z = lax.rem(deep + k, parts)
            hop3.append(
                push(side_sum.at[place], deep_in.at[place], base2 + place, index_of(z, side, core))
            )
        if place == 0:
            small_hop.wait_recv()
            small_out[2] = small_out[1] + small_in[2]
            for j in range(1, parts):
                z = lax.rem(deep + j, parts)
                small_hops.append(
                    push(small_out.at[2], small_in.at[2 + j], 2 + j, index_of(z, side, core), small_send, small_recv)
                )
    for copy in small_hops:
        copy.wait_recv()
    total = small_out[2]
    for j in range(1, parts):
        total = total + small_in[2 + j]
    total_ref[...] = total
    for copy in hop3:
        copy.wait_recv()

    @pl.loop(0, rows // step)
    def _(i):
        part = pl.ds(pl.multiple_of(i * step, step), step)
        total = side_sum[parts - 1, part, :].astype(jnp.float32)
        for place in range(parts - 1):
            total = total + deep_in[place, part, :].astype(jnp.float32)
        out_ref[part, :] = total

    for copy in started:
        copy.wait_send()


def scatter(blocks, small, count, ident):
    parts = count // 4
    _, rows, columns = blocks.shape
    sends = 4 * parts - 1
    kind = blocks.dtype
    return pl.pallas_call(
        functools.partial(scatter_kernel, count),
        out_shape=(
            jax.ShapeDtypeStruct((rows, columns), jnp.float32),
            jax.ShapeDtypeStruct(small.shape, jnp.float32),
        ),
        in_specs=[pl.BlockSpec(memory_space=pltpu.VMEM)] * 2,
        out_specs=(pl.BlockSpec(memory_space=pltpu.VMEM),) * 2,
        scratch_shapes=[
            pltpu.VMEM((2 * parts, rows, columns), kind),
            pltpu.VMEM((parts, rows, columns), kind),
            pltpu.VMEM((max(parts - 1, 1), rows, columns), kind),
            pltpu.VMEM((2 * parts, rows, columns), kind),
            pltpu.VMEM((parts, rows, columns), kind),
            pltpu.VMEM((parts + 2,) + small.shape, jnp.float32),
            pltpu.VMEM((3,) + small.shape, jnp.float32),
            pltpu.SemaphoreType.DMA((sends,)),
            pltpu.SemaphoreType.DMA((sends,)),
            pltpu.SemaphoreType.DMA((parts + 2,)),
            pltpu.SemaphoreType.DMA((parts + 2,)),
        ],
        compiler_params=pltpu.CompilerParams(
            collective_id=ident, has_side_effects=True, vmem_limit_bytes=60 << 20
        ),
        name="gradient_scatter",
    )(blocks, small)

HEAD_DIM = 64
KERNEL = 9
HALF = KERNEL // 2
EPSILON = 1e-06
MASK_FILL = -1e30
INV_ROOT2 = 0.7071067811865476
INV_ROOT_TWO_PI = 0.3989422804014327
SHARED_ROWS = 24
SWAP = [(0, 1), (1, 0)]
BF16 = jnp.bfloat16
F32 = jnp.float32


class Group:
    def __init__(self, **parts):
        self.__dict__.update(parts)


def total_of(groups):
    return Group(**{k: sum(vars(g)[k] for g in groups) for k in vars(groups[0])})


def nn(left, right):
    return jnp.dot(left, right, preferred_element_type=F32)


def tn(left, right):
    return lax.dot_general(left, right, (((0,), (0,)), ((), ())), preferred_element_type=F32)


def nt(left, right):
    return lax.dot_general(left, right, (((1,), (1,)), ((), ())), preferred_element_type=F32)


def swap(value):
    return lax.ppermute(value, "mp", SWAP)


def shifted(tensor, offset, half_width):
    filler = jnp.zeros((half_width,) + tensor.shape[1:], tensor.dtype)
    padded = jnp.concatenate([filler, tensor, filler], axis=0)
    return padded[half_width + offset : half_width + offset + tensor.shape[0]]


def same_segment(segment, offset, half_width):
    filler = jnp.full((half_width,), -1, dtype=jnp.int32)
    padded = jnp.concatenate([filler, segment, filler])
    return padded[half_width + offset : half_width + offset + segment.shape[0]] == segment


def segment_ids(lengths_row, seq_rows):
    doc_ends = jnp.cumsum(lengths_row)
    positions = jnp.arange(seq_rows, dtype=jnp.int32)
    return jnp.sum((positions[:, None] >= doc_ends[None, :]).astype(jnp.int32), axis=1)


def tap_mask_list(segment):
    return [
        same_segment(segment, tap - HALF, HALF).astype(F32)[:, None] for tap in range(KERNEL)
    ]


def gelu(tensor):
    return 0.5 * tensor * (1.0 + lax.erf(tensor * INV_ROOT2))


def gelu_slope(tensor):
    normal_cdf = 0.5 * (1.0 + lax.erf(tensor * INV_ROOT2))
    return normal_cdf + tensor * jnp.exp(-0.5 * tensor * tensor) * INV_ROOT_TWO_PI


def halves(value, me):
    width = value.shape[1] // 2
    return (
        lax.dynamic_slice_in_dim(value, me * width, width, 1),
        lax.dynamic_slice_in_dim(value, (1 - me) * width, width, 1),
    )


def joined(own, other, me):
    return jnp.where(me == 0, jnp.concatenate([own, other], 1), jnp.concatenate([other, own], 1))


def part_a(rows_in, segment, w, p, me):
    seq_rows = rows_in.shape[0]
    width = w.query.shape[1]
    heads = width // HEAD_DIM
    queries = (nn(rows_in, w.query) + p.query_bias).astype(BF16)
    keys = nn(rows_in, w.key).astype(BF16)
    values = (nn(rows_in, w.value) + p.value_bias).astype(BF16)
    masks = tap_mask_list(segment)
    depthwise = jnp.zeros(rows_in.shape, F32)
    for tap in range(KERNEL):
        moved = shifted(rows_in, tap - HALF, HALF).astype(F32)
        depthwise = depthwise + w.depth[tap].astype(F32) * moved * masks[tap]
    depthwise = depthwise.astype(BF16)
    key_conv = nn(depthwise, w.point) + p.point_bias
    conv_attn = (key_conv * queries.astype(F32)).astype(BF16)
    own, other = halves(nn(conv_attn, p.kernel_weight), me)
    logits = own + swap(other) + halves(p.kernel_bias[None], me)[0]
    kernel_probs = jax.nn.softmax(logits.reshape(seq_rows, heads, KERNEL), axis=-1)
    conv_values = (nn(rows_in, w.conv) + p.conv_bias).reshape(seq_rows, heads, HEAD_DIM)
    conv_context = jnp.zeros((seq_rows, heads, HEAD_DIM), F32)
    for tap in range(KERNEL):
        now = kernel_probs[:, :, tap] * masks[tap]
        conv_context = conv_context + now[:, :, None] * shifted(conv_values, tap - HALF, HALF)
    conv_context = conv_context.reshape(seq_rows, width).astype(BF16)
    query_heads = queries.reshape(seq_rows, heads, HEAD_DIM)
    key_heads = keys.reshape(seq_rows, heads, HEAD_DIM)
    value_heads = values.reshape(seq_rows, heads, HEAD_DIM)
    scores = jnp.einsum("qhd,khd->hqk", query_heads, key_heads, preferred_element_type=F32) * 0.125
    scores = jnp.where((segment[:, None] == segment[None, :])[None], scores, MASK_FILL)
    top = jnp.max(scores, axis=-1, keepdims=True)
    exponent = jnp.exp(scores - top)
    total = jnp.sum(exponent, axis=-1, keepdims=True)
    probs_low = (exponent / total).astype(BF16)
    context = jnp.einsum("hqk,khd->qhd", probs_low, value_heads, preferred_element_type=F32)
    context = context.reshape(seq_rows, width).astype(BF16)
    log_total = top[:, :, 0] + jnp.log(total[:, :, 0])
    return (queries, keys, values, depthwise, key_conv, conv_attn, kernel_probs, conv_values, conv_context, context, log_total)


def moments(sum_own, square_own, sum_other, square_other, width):
    mean = (sum_own + sum_other) / (2 * width)
    apart = (sum_own - sum_other) / width
    spread = (square_own + square_other + apart * apart * (width / 2)) / (2 * width)
    return mean, lax.rsqrt(spread + EPSILON)


def transposed_stats(columns):
    rows = columns[0].shape[0]
    lane = lax.broadcasted_iota(jnp.int32, (rows, 128), 1)
    packed = jnp.zeros((rows, 128), F32)
    for place, column in enumerate(columns):
        packed = jnp.where(lane == place, column, packed)
    return jnp.transpose(packed)[:8]


def stat_columns(message, amount):
    rows = message.shape[1]
    wide = jnp.concatenate([message, jnp.zeros((120, rows), F32)], 0)
    tall = jnp.transpose(wide)
    return [tall[:, k : k + 1] for k in range(amount)]


def row_sums(value):
    rows, columns = value.shape
    return jnp.sum(value.reshape(rows // 8, 8, columns), axis=0)


SLOTS = 4
FFN_STEP = 256


def middle_kernel(
    blocks,
    context_ref, conv_ref, hidden_ref, grad_ref, grad_late_ref, out0_ref, out1_ref, inner_ref, outer_ref, vec_ref,
    output_ref, residual_ref, branch_ref, big_inner_ref, big_outer_ref, small_ref,
    state, scale_ring, act_ring, slope_ring, low_ring, summed_ring, normed_ring, stat_ring,
    acc_inner, acc_outer, acc_small, acc_bias,
    branch_out, branch_in, stat1_out, stat1_in, stat2_out, stat2_in, stat3_out, stat3_in, back_out, back_in,
    send_sem, recv_sem,
):
    i = pl.program_id(0)
    me = lax.axis_index("mp")
    dp = lax.axis_index("dp")
    width = summed_ring.shape[2]
    hidden_units = inner_ref.shape[0]
    inverse = 1.0 / (2 * width)

    def message(kind, source, target, slot):
        return pltpu.make_async_remote_copy(
            src_ref=source.at[slot],
            dst_ref=target.at[slot],
            send_sem=send_sem.at[kind, slot],
            recv_sem=recv_sem.at[kind, slot],
            device_id=(dp, 1 - me),
            device_id_type=MESH,
        )

    kinds = [
        (branch_out, branch_in), (stat1_out, stat1_in), (stat2_out, stat2_in), (stat3_out, stat3_in), (back_out, back_in),
    ]

    def fresh(kind, b, slot):
        @pl.when(b >= SLOTS)
        def _():
            message(kind, *kinds[kind], slot).wait_send()

    def vec(row):
        return vec_ref[row : row + 1, :width]

    @pl.when(i == 0)
    def _():
        barrier = pltpu.get_barrier_semaphore()
        pl.semaphore_signal(barrier, inc=1, device_id=(dp, 1 - me), device_id_type=MESH)
        pl.semaphore_wait(barrier, 1)
        acc_inner[...] = jnp.zeros_like(acc_inner)
        acc_outer[...] = jnp.zeros_like(acc_outer)
        acc_small[...] = jnp.zeros_like(acc_small)
        acc_bias[...] = jnp.zeros_like(acc_bias)

    @pl.when(i < blocks)
    def _():
        b = i
        slot = lax.rem(b, SLOTS)
        fresh(0, b, slot)
        theirs = pl.ds(pl.multiple_of((1 - me) * width, width), width)
        ours = pl.ds(pl.multiple_of(me * width, width), width)
        other = nt(context_ref[...], out0_ref[theirs, :]) + nt(conv_ref[...], out1_ref[theirs, :])
        branch_out[slot] = other.astype(BF16)
        message(0, *kinds[0], slot).start()
        own = nt(context_ref[...], out0_ref[ours, :]) + nt(conv_ref[...], out1_ref[ours, :])
        state[lax.rem(b, 8)] = hidden_ref[:, ours].astype(F32) + (own + vec(0))

    @pl.when(jnp.logical_and(i >= 1, i < blocks + 1))
    def _():
        b = i - 1
        slot = lax.rem(b, SLOTS)
        message(0, *kinds[0], slot).wait_recv()
        fresh(1, b, slot)
        residual = state[lax.rem(b, 8)] + branch_in[slot].astype(F32)
        state[lax.rem(b, 8)] = residual
        total = jnp.sum(residual, axis=1, keepdims=True)
        apart = residual - total * (1.0 / width)
        stat1_out[slot] = transposed_stats([total, jnp.sum(apart * apart, axis=1, keepdims=True)])
        message(1, *kinds[1], slot).start()

    @pl.when(jnp.logical_and(i >= 2, i < blocks + 2))
    def _():
        b = i - 2
        slot = lax.rem(b, SLOTS)
        two = lax.rem(b, 2)
        message(1, *kinds[1], slot).wait_recv()
        fresh(2, b, slot)
        total, square = stat_columns(stat1_out[slot], 2)
        total_o, square_o = stat_columns(stat1_in[slot], 2)
        mean, scale = moments(total, square, total_o, square_o, width)
        standard = (state[lax.rem(b, 8)] - mean) * scale
        state[lax.rem(b, 8)] = standard
        scale_ring[lax.rem(b, 4)] = jnp.broadcast_to(scale, scale_ring.shape[1:])
        normed = standard * vec(1) + vec(2)
        low = normed.astype(BF16)
        low_ring[two] = low
        summed = normed + vec(3)
        for start in range(0, hidden_units, FFN_STEP):
            part = pl.ds(start, FFN_STEP)
            inner = nt(low, inner_ref[part, :]) + vec_ref[7:8, start : start + FFN_STEP]
            cdf = 0.5 * (1.0 + lax.erf(inner * INV_ROOT2))
            act = (inner * cdf).astype(BF16)
            act_ring[two, :, part] = act
            slope_ring[two, :, part] = cdf + inner * jnp.exp(-0.5 * inner * inner) * INV_ROOT_TWO_PI
            summed = summed + nn(act, outer_ref[part, :])
        summed_ring[two] = summed
        scaled = grad_ref[...].astype(F32) * vec(4)
        total = jnp.sum(summed, axis=1, keepdims=True)
        apart = summed - total * (1.0 / width)
        stat2_out[slot] = transposed_stats(
            [
                total,
                jnp.sum(apart * apart, axis=1, keepdims=True),
                jnp.sum(scaled, axis=1, keepdims=True),
                jnp.sum(scaled * apart, axis=1, keepdims=True),
            ]
        )
        message(2, *kinds[2], slot).start()

    @pl.when(jnp.logical_and(i >= 3, i < blocks + 3))
    def _():
        b = i - 3
        slot = lax.rem(b, SLOTS)
        two = lax.rem(b, 2)
        message(2, *kinds[2], slot).wait_recv()
        fresh(3, b, slot)
        total, square, grads, cross = stat_columns(stat2_out[slot], 4)
        total_o, square_o, grads_o, cross_o = stat_columns(stat2_in[slot], 4)
        mean, scale = moments(total, square, total_o, square_o, width)
        mean_grad = (grads + grads_o) * inverse
        product = cross + cross_o + (total * (1.0 / width) - mean) * grads + (total_o * (1.0 / width) - mean) * grads_o
        mean_product = product * scale * inverse
        standard = (summed_ring[two] - mean) * scale
        output_ref[...] = (standard * vec(4) + vec(5)).astype(BF16)
        gradient = grad_late_ref[...].astype(F32)
        grad_summed = scale * (gradient * vec(4) - mean_grad - standard * mean_product)
        low = grad_summed.astype(BF16)
        acc_small[0] += row_sums(low.astype(F32))
        acc_small[1] += row_sums(gradient * standard)
        acc_small[2] += row_sums(gradient)
        normed_low = low_ring[two]
        grad_normed = grad_summed
        for start in range(0, hidden_units, FFN_STEP):
            part = pl.ds(start, FFN_STEP)
            grad_inner = nt(low, outer_ref[part, :]) * slope_ring[two, :, part]
            inner_low = grad_inner.astype(BF16)
            acc_bias[:, part] += row_sums(inner_low.astype(F32))
            grad_normed = grad_normed + nn(inner_low, inner_ref[part, :])
            acc_outer[part, :] += tn(act_ring[two, :, part], low)
            acc_inner[part, :] += tn(inner_low, normed_low)
        normed_ring[two] = grad_normed
        standard1 = state[lax.rem(b, 8)]
        scaled = grad_normed * vec(1)
        acc_small[3] += row_sums(grad_normed * standard1)
        acc_small[4] += row_sums(grad_normed)
        sums = transposed_stats(
            [jnp.sum(scaled, axis=1, keepdims=True), jnp.sum(scaled * standard1, axis=1, keepdims=True)]
        )
        stat3_out[slot] = sums
        message(3, *kinds[3], slot).start()

    @pl.when(jnp.logical_and(i >= 4, i < blocks + 4))
    def _():
        b = i - 4
        slot = lax.rem(b, SLOTS)
        message(3, *kinds[3], slot).wait_recv()
        fresh(4, b, slot)
        first, second = stat_columns(stat3_out[slot] + stat3_in[slot], 2)
        standard = state[lax.rem(b, 8)]
        scaled = normed_ring[lax.rem(b, 2)] * vec(1)
        residual = scale_ring[lax.rem(b, 4)][:, :1] * (scaled - first * inverse - standard * (second * inverse))
        residual_ref[...] = residual
        low = residual.astype(BF16)
        acc_small[5] += row_sums(low.astype(F32))
        back_out[slot] = low
        message(4, *kinds[4], slot).start()

    @pl.when(i >= 5)
    def _():
        b = i - 5
        slot = lax.rem(b, SLOTS)
        message(4, *kinds[4], slot).wait_recv()
        theirs = pl.ds(pl.multiple_of((1 - me) * width, width), width)
        ours = pl.ds(pl.multiple_of(me * width, width), width)
        branch_ref[:, ours] = back_out[slot]
        branch_ref[:, theirs] = back_in[slot]

    @pl.when(i == blocks + 4)
    def _():
        for kind in range(5):
            for slot in range(SLOTS):
                message(kind, *kinds[kind], slot).wait_send()
        big_inner_ref[...] = acc_inner[...].astype(BF16)
        big_outer_ref[...] = acc_outer[...].astype(BF16)
        small_ref[...] = jnp.zeros_like(small_ref)
        for row in range(6):
            small_ref[row : row + 1, :width] = jnp.sum(acc_small[row], axis=0, keepdims=True)
        small_ref[6:7, :] = jnp.sum(acc_bias[...], axis=0, keepdims=True)


def middle(context, conv_context, hidden, out_grad, w, p, me, ident):
    tokens, model = hidden.shape
    width = model // 2
    local = context.shape[1]
    units = w.inner.shape[0]
    rows = 256
    blocks = tokens // rows

    def mine(value):
        return lax.dynamic_slice_in_dim(value, me * width, width, 0)

    vectors = [
        mine(p.out_bias), mine(p.norm1_gain), mine(p.norm1_bias), p.ffn_out_bias, p.norm2_gain, p.norm2_bias,
    ]
    table = jnp.stack([jnp.pad(v, (0, units - width)) for v in vectors] + [jnp.zeros((units,), F32), p.ffn_in_bias])

    def block(columns, lag):
        return pl.BlockSpec((rows, columns), lambda i: (jnp.clip(i - lag, 0, blocks - 1), 0))

    whole = pl.BlockSpec(memory_space=pltpu.VMEM)
    stat = pltpu.VMEM((SLOTS, 8, rows), F32)
    half = pltpu.VMEM((SLOTS, rows, width), BF16)
    return pl.pallas_call(
        functools.partial(middle_kernel, blocks),
        grid=(blocks + 5,),
        out_shape=(
            jax.ShapeDtypeStruct((tokens, width), BF16),
            jax.ShapeDtypeStruct((tokens, width), F32),
            jax.ShapeDtypeStruct((tokens, model), BF16),
            jax.ShapeDtypeStruct((units, width), BF16),
            jax.ShapeDtypeStruct((units, width), BF16),
            jax.ShapeDtypeStruct((8, units), F32),
        ),
        in_specs=[
            block(local, 0), block(local, 0), block(model, 0), block(width, 2), block(width, 3),
            whole, whole, whole, whole, whole,
        ],
        out_specs=(block(width, 3), block(width, 4), block(model, 5), whole, whole, whole),
        scratch_shapes=[
            pltpu.VMEM((8, rows, width), F32),
            pltpu.VMEM((4, rows, 128), F32),
            pltpu.VMEM((2, rows, units), BF16),
            pltpu.VMEM((2, rows, units), F32),
            pltpu.VMEM((2, rows, width), BF16),
            pltpu.VMEM((2, rows, width), F32),
            pltpu.VMEM((2, rows, width), F32),
            pltpu.VMEM((8, 128), F32),
            pltpu.VMEM((units, width), F32),
            pltpu.VMEM((units, width), F32),
            pltpu.VMEM((6, 8, width), F32),
            pltpu.VMEM((8, units), F32),
            half, half, stat, stat, stat, stat, stat, stat, half, half,
            pltpu.SemaphoreType.DMA((5, SLOTS)),
            pltpu.SemaphoreType.DMA((5, SLOTS)),
        ],
        compiler_params=pltpu.CompilerParams(
            collective_id=ident, has_side_effects=True, vmem_limit_bytes=60 << 20
        ),
        name="middle",
    )(context, conv_context, hidden, out_grad, out_grad, w.out0, w.out1, w.inner, w.outer, table)


def part_c(rows_in, segment, grad_branch, grad_residual, kept, w, p, me):
    (queries, keys, values, depthwise, key_conv, conv_attn, kernel_probs, conv_values, conv_context, context, log_total) = kept
    seq_rows = rows_in.shape[0]
    width = queries.shape[1]
    heads = width // HEAD_DIM
    masks = tap_mask_list(segment)
    big = Group(out0=tn(grad_branch, context), out1=tn(grad_branch, conv_context))
    small = Group()
    grad_context = nn(grad_branch, w.out0).astype(BF16).reshape(seq_rows, heads, HEAD_DIM)
    grad_conv = nn(grad_branch, w.out1).astype(BF16).reshape(seq_rows, heads, HEAD_DIM)
    tap_grads = []
    grad_conv_values = jnp.zeros((seq_rows, heads, HEAD_DIM), F32)
    for tap in range(KERNEL):
        tap_grads.append(
            masks[tap] * jnp.sum(grad_conv * shifted(conv_values, tap - HALF, HALF), axis=2)
        )
        now = kernel_probs[:, :, tap] * masks[tap]
        grad_conv_values = grad_conv_values + shifted(now[:, :, None] * grad_conv, HALF - tap, HALF)
    grad_taps = jnp.stack(tap_grads, axis=2)
    grad_logits = kernel_probs * (grad_taps - jnp.sum(kernel_probs * grad_taps, axis=2, keepdims=True))
    logits_own = grad_logits.reshape(seq_rows, heads * KERNEL).astype(BF16)
    logits_low = joined(logits_own, swap(logits_own), me)
    small.kernel_bias = jnp.sum(logits_low, axis=0, dtype=F32)
    small.kernel_weight = tn(conv_attn, logits_low)
    attn_wide = nt(logits_low, p.kernel_weight).astype(BF16).astype(F32)
    key_low = (attn_wide * queries.astype(F32)).astype(BF16)
    small.point_bias = jnp.sum(key_low, axis=0, dtype=F32)
    big.point = tn(depthwise, key_low)
    grad_depthwise = nt(key_low, w.point)
    depth_rows = []
    grad_rows = jnp.zeros(rows_in.shape, F32)
    for tap in range(KERNEL):
        masked = grad_depthwise * masks[tap]
        moved = shifted(rows_in, tap - HALF, HALF).astype(F32)
        depth_rows.append(jnp.sum(masked * moved, axis=0))
        grad_rows = grad_rows + shifted(masked * w.depth[tap].astype(F32), HALF - tap, HALF)
    small.depth = jnp.stack(depth_rows, axis=0)
    conv_low = grad_conv_values.reshape(seq_rows, width).astype(BF16)
    small.conv_bias = jnp.sum(conv_low, axis=0, dtype=F32)
    big.conv = tn(rows_in, conv_low)
    grad_rows = grad_rows + nt(conv_low, w.conv)
    query_heads = queries.reshape(seq_rows, heads, HEAD_DIM)
    key_heads = keys.reshape(seq_rows, heads, HEAD_DIM)
    value_heads = values.reshape(seq_rows, heads, HEAD_DIM)
    scores = jnp.einsum("qhd,khd->hqk", query_heads, key_heads, preferred_element_type=F32) * 0.125
    scores = jnp.where((segment[:, None] == segment[None, :])[None], scores, MASK_FILL)
    probs = jnp.exp(scores - log_total[:, :, None])
    probs_low = probs.astype(BF16)
    grad_probs = jnp.einsum("qhd,khd->hqk", grad_context, value_heads, preferred_element_type=F32)
    scores_low = (probs * (grad_probs - jnp.sum(probs * grad_probs, axis=2, keepdims=True))).astype(BF16)
    grad_queries = jnp.einsum("hqk,khd->qhd", scores_low, key_heads, preferred_element_type=F32) * 0.125
    grad_queries = (grad_queries.reshape(seq_rows, width) + attn_wide * key_conv).astype(BF16)
    grad_keys = jnp.einsum("hqk,qhd->khd", scores_low, query_heads, preferred_element_type=F32) * 0.125
    grad_keys = grad_keys.reshape(seq_rows, width).astype(BF16)
    grad_values = jnp.einsum("hqk,qhd->khd", probs_low, grad_context, preferred_element_type=F32)
    grad_values = grad_values.reshape(seq_rows, width).astype(BF16)
    small.query_bias = jnp.sum(grad_queries, axis=0, dtype=F32)
    small.value_bias = jnp.sum(grad_values, axis=0, dtype=F32)
    big.query = tn(rows_in, grad_queries)
    big.key = tn(rows_in, grad_keys)
    big.value = tn(rows_in, grad_values)
    grad_rows = grad_rows + nt(grad_queries, w.query) + nt(grad_keys, w.key) + nt(grad_values, w.value)
    own, other = halves(grad_rows, me)
    grad_input = own + grad_residual + swap(other.astype(BF16)).astype(F32)
    return grad_input, big, small


def padded(value, multiple):
    rows = value.shape[-2]
    extra = -rows % multiple
    return jnp.pad(value, [(0, 0)] * (value.ndim - 2) + [(0, extra), (0, 0)])


def on_device(
    count,
    hidden, doc_lengths, query_weight, key_weight, value_weight, query_bias, value_bias,
    depth_weight, point_weight, point_bias, kernel_weight, kernel_bias, conv_weight, conv_bias,
    out_weight, out_bias, norm1_gain, norm1_bias, ffn_in_weight, ffn_in_bias, ffn_out_weight,
    ffn_out_bias, norm2_gain, norm2_bias, out_grad,
):
    me = lax.axis_index("mp")
    share, width = query_weight.shape
    model = hidden.shape[1]
    group = ffn_out_bias.shape[0]
    share_ffn = ffn_out_weight.shape[1]
    depth_wide = jnp.pad(depth_weight.T, ((0, 0), (0, width - KERNEL)))
    first = jnp.concatenate(
        [
            jnp.concatenate([query_weight, key_weight], 1),
            jnp.concatenate([value_weight, conv_weight], 1),
            jnp.concatenate([point_weight, depth_wide], 1),
        ],
        0,
    )
    out_cut = jnp.concatenate([out_weight[0].T, out_weight[1].T], 1)
    second = jnp.concatenate([out_cut, ffn_in_weight[0].T, ffn_out_weight[0]], 0)
    first_all = gather(padded(first, 16)[None], count, 1)
    second_all = gather(padded(second, 16)[None], count, 2)

    def cut(source, start, size, low, high):
        return source[:, start : start + size, low:high].reshape(count * size, high - low)

    w = Group(
        query=cut(first_all, 0, share, 0, width),
        key=cut(first_all, 0, share, width, 2 * width),
        value=cut(first_all, share, share, 0, width),
        conv=cut(first_all, share, share, width, 2 * width),
        point=cut(first_all, 2 * share, share, 0, width),
        depth=cut(first_all, 2 * share, share, width, width + KERNEL).T,
        out0=cut(second_all, 0, share, 0, width),
        out1=cut(second_all, 0, share, width, 2 * width),
        inner=cut(second_all, share, share_ffn, 0, group),
        outer=cut(second_all, share + share_ffn, share_ffn, 0, group),
    )
    p = Group(
        query_bias=query_bias, value_bias=value_bias, point_bias=point_bias, kernel_weight=kernel_weight,
        kernel_bias=kernel_bias, conv_bias=conv_bias, out_bias=out_bias, norm1_gain=norm1_gain,
        norm1_bias=norm1_bias, ffn_in_bias=ffn_in_bias[0], ffn_out_bias=ffn_out_bias,
        norm2_gain=norm2_gain, norm2_bias=norm2_bias,
    )
    seqs = doc_lengths.shape[0]
    seq_rows = hidden.shape[0] // seqs
    spans = [slice(s * seq_rows, (s + 1) * seq_rows) for s in range(seqs)]
    segments = [segment_ids(doc_lengths[s], seq_rows) for s in range(seqs)]
    kept = [part_a(hidden[spans[s]], segments[s], w, p, me) for s in range(seqs)]
    output, grad_residual, grad_branch, big_inner, big_outer, sums_mid = middle(
        jnp.concatenate([k[9] for k in kept], 0),
        jnp.concatenate([k[8] for k in kept], 0),
        hidden, out_grad, w, p, me, 4,
    )
    last = [
        part_c(hidden[spans[s]], segments[s], grad_branch[spans[s]], grad_residual[spans[s]], kept[s], w, p, me)
        for s in range(seqs)
    ]
    grad_input = jnp.concatenate([t[0] for t in last], 0)
    big = total_of([t[1] for t in last])
    small = total_of([t[2] for t in last])

    def widened(value):
        empty = jnp.zeros_like(value)
        return jnp.where(me == 0, jnp.concatenate([value, empty]), jnp.concatenate([empty, value]))


    def blocks(value):
        return value.reshape(count, value.shape[0] // count, value.shape[1])

    pieces = jnp.concatenate(
        [
            blocks(jnp.concatenate([big.query, big.key], 1)),
            blocks(jnp.concatenate([big.value, big.conv], 1)),
            blocks(jnp.concatenate([big.point, jnp.zeros_like(big.point)], 1)),
            blocks(jnp.concatenate([big.out0, big.out1], 1)),
        ],
        1,
    ).astype(BF16)
    pieces = jnp.concatenate([pieces, blocks(big_inner), blocks(big_outer)], 1)
    own_parts = [
        small.query_bias, small.value_bias, small.point_bias, small.kernel_weight, small.kernel_bias,
        small.conv_bias, sums_mid[6], sums_mid[0, :group], sums_mid[1, :group], sums_mid[2, :group],
    ]
    columns = group

    def table(parts, rows):
        flat = jnp.concatenate([part.reshape(-1) for part in parts])
        return jnp.pad(flat, (0, rows * columns - flat.shape[0])).reshape(rows, columns)

    own_size = sum(part.size for part in own_parts)
    own_rows = -(-own_size // columns)
    own_rows += -own_rows % 8
    shared_parts = [small.depth] + [widened(sums_mid[k, :group]) for k in (3, 4, 5)]
    smalls = jnp.concatenate([table(own_parts, own_rows), table(shared_parts, SHARED_ROWS)], 0)
    sums, totals = scatter(padded(pieces, 16), smalls, count, 3)

    def untable(value, parts):
        flat, result, start = value.reshape(-1), [], 0
        for part in parts:
            result.append(flat[start : start + part.size].reshape(part.shape))
            start += part.size
        return result

    query_b, value_b, point_b, kernel_w, kernel_b, conv_b, in_b, outer_b, gain2, bias2 = untable(
        totals[:own_rows], own_parts
    )
    depth_g, gain1, bias1, out_b = untable(totals[own_rows:], shared_parts)
    place = lax.axis_index("dp")
    depth_own = lax.dynamic_slice_in_dim(depth_g, place * share, share, 1)
    at_rows = lambda k: sums[k * share : (k + 1) * share]
    qk, vc, po, oo = at_rows(0), at_rows(1), at_rows(2), at_rows(3)
    inner_own = sums[4 * share : 4 * share + share_ffn]
    outer_own = sums[4 * share + share_ffn : 4 * share + 2 * share_ffn]
    return (
        output,
        grad_input,
        qk[:, :width],
        qk[:, width:],
        vc[:, :width],
        query_b,
        value_b,
        depth_own,
        po[:, :width],
        point_b,
        kernel_w,
        kernel_b,
        vc[:, width:],
        conv_b,
        jnp.stack([oo[:, :width].T, oo[:, width:].T]),
        out_b,
        gain1,
        bias1,
        inner_own.T[None],
        in_b[None],
        outer_own[None],
        outer_b,
        gain2,
        bias2,
    )


def solution(mesh):
    in_specs = (
        P("dp", None),
        P("dp", None),
        P("dp", "mp"),
        P("dp", "mp"),
        P("dp", "mp"),
        P("mp"),
        P("mp"),
        P(None, "dp"),
        P("dp", "mp"),
        P("mp"),
        P("mp", None),
        P(),
        P("dp", "mp"),
        P("mp"),
        P(None, "mp", "dp"),
        P(),
        P(),
        P(),
        P("mp", None, "dp"),
        P("mp", None),
        P("mp", "dp", None),
        P("mp"),
        P("mp"),
        P("mp"),
        P("dp", "mp"),
    )
    out_specs = (
        P("dp", "mp"),
        P("dp", "mp"),
        P("dp", "mp"),
        P("dp", "mp"),
        P("dp", "mp"),
        P("mp"),
        P("mp"),
        P(None, "dp"),
        P("dp", "mp"),
        P("mp"),
        P("mp", None),
        P(),
        P("dp", "mp"),
        P("mp"),
        P(None, "mp", "dp"),
        P(),
        P(),
        P(),
        P("mp", None, "dp"),
        P("mp", None),
        P("mp", "dp", None),
        P("mp"),
        P("mp"),
        P("mp"),
    )
    return jax.shard_map(
        functools.partial(on_device, mesh.shape["dp"]), mesh=mesh, in_specs=in_specs, out_specs=out_specs, check_vma=False
    )
```

```python
import functools
import jax
import jax.numpy as jnp
from jax import lax
from jax.experimental import pallas as pl
from jax.experimental.pallas import tpu as pltpu

from jax.sharding import PartitionSpec as P

MESH = pl.DeviceIdType.MESH


def at(dp, mp):
    return (dp, mp)


def places(count):
    dp = lax.axis_index("dp")
    core = lax.rem(dp, 2)
    side = lax.rem(lax.div(dp, 2), 2)
    deep = lax.div(dp, 4)
    return lax.axis_index("mp"), core, side, deep, count // 4


def index_of(deep, side, core):
    return (deep * 2 + side) * 2 + core


def greet(count):
    mp, core, side, deep, parts = places(count)
    barrier = pltpu.get_barrier_semaphore()
    peers = [index_of(lax.rem(deep + k, parts), side, core) for k in range(1, parts)]
    peers += [index_of(deep, 1 - side, core), index_of(deep, side, 1 - core)]
    for peer in peers:
        pl.semaphore_signal(barrier, inc=1, device_id=at(peer, mp), device_id_type=MESH)
    pl.semaphore_wait(barrier, len(peers))


def gather_kernel(count, own_ref, out_ref, own_sem, send_sem, recv_sem):
    mp, core, side, deep, parts = places(count)
    me = index_of(deep, side, core)
    greet(count)
    local = pltpu.make_async_copy(own_ref.at[0], out_ref.at[me], own_sem)
    local.start()
    started = []

    def push(source, block, target):
        copy = pltpu.make_async_remote_copy(
            src_ref=source,
            dst_ref=out_ref.at[block],
            send_sem=send_sem.at[len(started)],
            recv_sem=recv_sem.at[block],
            device_id=at(target, mp),
            device_id_type=MESH,
        )
        copy.start()
        started.append(copy)

    def arrive(block):
        pltpu.make_async_copy(own_ref.at[0], out_ref.at[block], recv_sem.at[block]).wait()

    beside = index_of(deep, 1 - side, core)
    twin = index_of(deep, side, 1 - core)
    for k in range(1, parts):
        push(own_ref.at[0], me, index_of(lax.rem(deep + k, parts), side, core))
    push(own_ref.at[0], me, beside)
    push(own_ref.at[0], me, twin)
    arrive(beside)
    push(out_ref.at[beside], beside, twin)
    for k in range(1, parts):
        block = index_of(lax.rem(deep + parts - k, parts), side, core)
        arrive(block)
        push(out_ref.at[block], block, beside)
        push(out_ref.at[block], block, twin)
    for k in range(1, parts):
        block = index_of(lax.rem(deep + parts - k, parts), 1 - side, core)
        arrive(block)
        push(out_ref.at[block], block, twin)
    for k in range(parts):
        for other in range(2):
            arrive(index_of(lax.rem(deep + parts - k, parts), other, 1 - core))
    for copy in started:
        copy.wait_send()
    local.wait()


def gather(own, count, ident):
    parts = count // 4
    sends = (parts - 1) * 4 + 3
    shape = (count,) + own.shape[1:]
    return pl.pallas_call(
        functools.partial(gather_kernel, count),
        out_shape=jax.ShapeDtypeStruct(shape, own.dtype),
        in_specs=[pl.BlockSpec(memory_space=pl.ANY)],
        out_specs=pl.BlockSpec(memory_space=pl.ANY),
        scratch_shapes=[
            pltpu.SemaphoreType.DMA,
            pltpu.SemaphoreType.DMA((sends,)),
            pltpu.SemaphoreType.DMA((count,)),
        ],
        compiler_params=pltpu.CompilerParams(collective_id=ident, has_side_effects=True),
        name="weight_gather",
    )(own)


def scatter_kernel(
    count, in_ref, small_ref, out_ref, total_ref,
    twin_in, side_in, deep_in, twin_sum, side_sum,
    small_in, small_out, send_sem, recv_sem, small_send, small_recv,
):
    mp, core, side, deep, parts = places(count)
    me = index_of(deep, side, core)
    barrier = pltpu.get_barrier_semaphore()
    pl.semaphore_signal(barrier, inc=1, device_id=at(me, 1 - mp), device_id_type=MESH)
    peers = [index_of(lax.rem(deep + k, parts), side, core) for k in range(1, parts)]
    peers += [index_of(deep, 1 - side, core), index_of(deep, side, 1 - core)]
    for peer in peers:
        pl.semaphore_signal(barrier, inc=1, device_id=at(peer, mp), device_id_type=MESH)
    pl.semaphore_wait(barrier, len(peers) + 1)
    beside = index_of(deep, 1 - side, core)
    twin = index_of(deep, side, 1 - core)
    started = []
    rows = in_ref.shape[1]
    step = rows // 4 if rows % 64 == 0 else rows

    def push(source, target_ref, slot, target, sends=send_sem, recvs=recv_sem, plane=mp):
        copy = pltpu.make_async_remote_copy(
            src_ref=source,
            dst_ref=target_ref,
            send_sem=sends.at[slot],
            recv_sem=recvs.at[slot],
            device_id=at(target, plane),
            device_id_type=MESH,
        )
        copy.start()
        started.append(copy)
        return copy

    def add(target, first, second):
        @pl.loop(0, rows // step)
        def _(i):
            part = pl.ds(pl.multiple_of(i * step, step), step)
            total = first[part, :].astype(jnp.float32) + second[part, :].astype(jnp.float32)
            target[part, :] = total.astype(target.dtype)

    small_hop = push(small_ref, small_in.at[0], 0, me, small_send, small_recv, 1 - mp)
    order = [(k, other) for k in list(range(1, parts)) + [0] for other in (1, 0)]
    hop = {}
    for slot, (k, other) in enumerate(order):
        z = lax.rem(deep + k, parts)
        s = 1 - side if other else side
        hop[(k, other)] = push(
            in_ref.at[index_of(z, s, 1 - core)], twin_in.at[slot], slot, twin
        )
    small_hop.wait_recv()
    shared = small_ref.shape[0] - SHARED_ROWS
    small_out[0, pl.ds(0, shared), :] = small_ref[pl.ds(0, shared), :]
    small_out[0, pl.ds(shared, SHARED_ROWS), :] = (
        small_ref[pl.ds(shared, SHARED_ROWS), :] + small_in[0, pl.ds(shared, SHARED_ROWS), :]
    )
    small_hop = push(small_out.at[0], small_in.at[1], 1, twin, small_send, small_recv)
    base = len(order)
    hop2 = {}
    for slot, (k, other) in enumerate(order):
        z = lax.rem(deep + k, parts)
        s = 1 - side if other else side
        hop[(k, other)].wait_recv()
        add(twin_sum.at[slot], in_ref.at[index_of(z, s, core)], twin_in.at[slot])
        if other:
            place = slot // 2
            hop2[k] = push(twin_sum.at[slot], side_in.at[place], base + place, beside)
        if slot == 1:
            small_hop.wait_recv()
            small_out[1] = small_out[0] + small_in[1]
            small_hop = push(small_out.at[1], small_in.at[2], 2, beside, small_send, small_recv)
    base2 = base + parts
    hop3 = []
    small_hops = []
    for place, k in enumerate(list(range(1, parts)) + [0]):
        hop2[k].wait_recv()
        add(side_sum.at[place], twin_sum.at[2 * place + 1], side_in.at[place])
        if k:
            z = lax.rem(deep + k, parts)
            hop3.append(
                push(side_sum.at[place], deep_in.at[place], base2 + place, index_of(z, side, core))
            )
        if place == 0:
            small_hop.wait_recv()
            small_out[2] = small_out[1] + small_in[2]
            for j in range(1, parts):
                z = lax.rem(deep + j, parts)
                small_hops.append(
                    push(small_out.at[2], small_in.at[2 + j], 2 + j, index_of(z, side, core), small_send, small_recv)
                )
    for copy in small_hops:
        copy.wait_recv()
    total = small_out[2]
    for j in range(1, parts):
        total = total + small_in[2 + j]
    total_ref[...] = total
    for copy in hop3:
        copy.wait_recv()

    @pl.loop(0, rows // step)
    def _(i):
        part = pl.ds(pl.multiple_of(i * step, step), step)
        total = side_sum[parts - 1, part, :].astype(jnp.float32)
        for place in range(parts - 1):
            total = total + deep_in[place, part, :].astype(jnp.float32)
        out_ref[part, :] = total

    for copy in started:
        copy.wait_send()


def scatter(blocks, small, count, ident):
    parts = count // 4
    _, rows, columns = blocks.shape
    sends = 4 * parts - 1
    kind = blocks.dtype
    return pl.pallas_call(
        functools.partial(scatter_kernel, count),
        out_shape=(
            jax.ShapeDtypeStruct((rows, columns), jnp.float32),
            jax.ShapeDtypeStruct(small.shape, jnp.float32),
        ),
        in_specs=[pl.BlockSpec(memory_space=pltpu.VMEM)] * 2,
        out_specs=(pl.BlockSpec(memory_space=pltpu.VMEM),) * 2,
        scratch_shapes=[
            pltpu.VMEM((2 * parts, rows, columns), kind),
            pltpu.VMEM((parts, rows, columns), kind),
            pltpu.VMEM((max(parts - 1, 1), rows, columns), kind),
            pltpu.VMEM((2 * parts, rows, columns), kind),
            pltpu.VMEM((parts, rows, columns), kind),
            pltpu.VMEM((parts + 2,) + small.shape, jnp.float32),
            pltpu.VMEM((3,) + small.shape, jnp.float32),
            pltpu.SemaphoreType.DMA((sends,)),
            pltpu.SemaphoreType.DMA((sends,)),
            pltpu.SemaphoreType.DMA((parts + 2,)),
            pltpu.SemaphoreType.DMA((parts + 2,)),
        ],
        compiler_params=pltpu.CompilerParams(
            collective_id=ident, has_side_effects=True, vmem_limit_bytes=60 << 20
        ),
        name="gradient_scatter",
    )(blocks, small)

HEAD_DIM = 64
KERNEL = 9
HALF = KERNEL // 2
EPSILON = 1e-06
MASK_FILL = -1e30
INV_ROOT2 = 0.7071067811865476
INV_ROOT_TWO_PI = 0.3989422804014327
SHARED_ROWS = 24
SWAP = [(0, 1), (1, 0)]
BF16 = jnp.bfloat16
F32 = jnp.float32


class Group:
    def __init__(self, **parts):
        self.__dict__.update(parts)


def nn(left, right):
    return jnp.dot(left, right, preferred_element_type=F32)


def tn(left, right):
    return lax.dot_general(left, right, (((0,), (0,)), ((), ())), preferred_element_type=F32)


def nt(left, right):
    return lax.dot_general(left, right, (((1,), (1,)), ((), ())), preferred_element_type=F32)


def swap(value):
    return lax.ppermute(value, "mp", SWAP)


def shifted(tensor, offset, half_width):
    filler = jnp.zeros((half_width,) + tensor.shape[1:], tensor.dtype)
    padded = jnp.concatenate([filler, tensor, filler], axis=0)
    return padded[half_width + offset : half_width + offset + tensor.shape[0]]


def same_segment(segment, offset, half_width):
    filler = jnp.full((half_width,), -1, dtype=jnp.int32)
    padded = jnp.concatenate([filler, segment, filler])
    return padded[half_width + offset : half_width + offset + segment.shape[0]] == segment


def segment_ids(lengths_row, seq_rows):
    doc_ends = jnp.cumsum(lengths_row)
    positions = jnp.arange(seq_rows, dtype=jnp.int32)
    return jnp.sum((positions[:, None] >= doc_ends[None, :]).astype(jnp.int32), axis=1)


def tap_mask_list(segment):
    return [
        same_segment(segment, tap - HALF, HALF).astype(F32)[:, None] for tap in range(KERNEL)
    ]


def gelu(tensor):
    return 0.5 * tensor * (1.0 + lax.erf(tensor * INV_ROOT2))


def gelu_slope(tensor):
    normal_cdf = 0.5 * (1.0 + lax.erf(tensor * INV_ROOT2))
    return normal_cdf + tensor * jnp.exp(-0.5 * tensor * tensor) * INV_ROOT_TWO_PI


def halves(value, me):
    width = value.shape[1] // 2
    return (
        lax.dynamic_slice_in_dim(value, me * width, width, 1),
        lax.dynamic_slice_in_dim(value, (1 - me) * width, width, 1),
    )


def joined(own, other, me):
    return jnp.where(me == 0, jnp.concatenate([own, other], 1), jnp.concatenate([other, own], 1))


def moments(sum_own, square_own, sum_other, square_other, width):
    mean = (sum_own + sum_other) / (2 * width)
    apart = (sum_own - sum_other) / width
    spread = (square_own + square_other + apart * apart * (width / 2)) / (2 * width)
    return mean, lax.rsqrt(spread + EPSILON)


TAP_ROWS = 16
WIDE = 256
LANES = 128
EDGE = 8


def spread_marks(marks_ref, columns_ref, masks_ref):
    rows = marks_ref.shape[2]
    columns_ref[...] = jnp.transpose(
        jnp.concatenate([marks_ref[0], jnp.zeros((LANES - TAP_ROWS, rows), F32)], 0)
    )
    for tap in range(KERNEL):
        masks_ref[tap] = jnp.broadcast_to(columns_ref[:, tap : tap + 1], (rows, LANES))


def head_lanes(head):
    lane = lax.broadcasted_iota(jnp.int32, (1, WIDE), 1)
    return jnp.logical_and(lane >= head * HEAD_DIM, lane < (head + 1) * HEAD_DIM)


def only(value, head):
    return jnp.where(head_lanes(head), value.astype(F32), 0.0)


def high_low(weights, heads):
    high = weights.astype(BF16).astype(F32)
    low = weights - high
    rest = jnp.zeros((LANES - 2 * heads * TAP_ROWS, weights.shape[1]), F32)
    return jnp.transpose(jnp.concatenate([high, low, rest], 0)).astype(BF16)


def front_kernel(
    seqs, count,
    hidden_ref, marks_ref, query_ref, key_ref, value_ref, conv_ref, point_ref, taps_ref, vec_ref, depth_ref, bias_ref,
    expand_ref, second_ref,
    q_ref, k_ref, v_ref, cv_ref, dl_ref, kc_ref, ca_ref, probs_ref, cc_ref, ctx_ref, lse_ref, second_all_ref,
    rows_pad, conv_pad, masks, columns, weights, tops, tap_out, tap_in,
    send_sem, recv_sem, own_sem, gather_send, gather_recv,
):
    s = pl.program_id(0)
    mp, core, side, deep, parts = places(count)
    me = index_of(deep, side, core)
    rows, model = hidden_ref.shape
    chunks = model // LANES
    heads = probs_ref.shape[1] // TAP_ROWS
    tap_rows = heads * TAP_ROWS
    beside = index_of(deep, 1 - side, core)
    twin = index_of(deep, side, 1 - core)

    def push(source, block, target, slot):
        return pltpu.make_async_remote_copy(
            src_ref=source,
            dst_ref=second_all_ref.at[block],
            send_sem=gather_send.at[slot],
            recv_sem=gather_recv.at[block],
            device_id=at(target, mp),
            device_id_type=MESH,
        )

    def arrive(block):
        pltpu.make_async_copy(second_ref.at[0], second_all_ref.at[block], gather_recv.at[block]).wait()

    own_copy = pltpu.make_async_copy(second_ref.at[0], second_all_ref.at[me], own_sem)
    first_hops = [
        push(second_ref.at[0], me, index_of(lax.rem(deep + k, parts), side, core), k - 1) for k in range(1, parts)
    ]
    first_hops += [push(second_ref.at[0], me, beside, parts - 1), push(second_ref.at[0], me, twin, parts)]
    second_hops = [(beside, twin, parts + 1)]
    for k in range(1, parts):
        block = index_of(lax.rem(deep + parts - k, parts), side, core)
        second_hops += [(block, beside, parts + 2 * k), (block, twin, parts + 2 * k + 1)]
    third_hops = [
        (index_of(lax.rem(deep + parts - k, parts), 1 - side, core), twin, 3 * parts + k - 1) for k in range(1, parts)
    ]

    @pl.when(s == 0)
    def _():
        barrier = pltpu.get_barrier_semaphore()
        pl.semaphore_signal(barrier, inc=1, device_id=at(me, 1 - mp), device_id_type=MESH)
        peers = [index_of(lax.rem(deep + k, parts), side, core) for k in range(1, parts)] + [beside, twin]
        for peer in peers:
            pl.semaphore_signal(barrier, inc=1, device_id=at(peer, mp), device_id_type=MESH)
        pl.semaphore_wait(barrier, len(peers) + 1)
        own_copy.start()
        for copy in first_hops:
            copy.start()
        rows_pad[:, :EDGE, :] = jnp.zeros((chunks, EDGE, LANES), F32)
        rows_pad[:, pl.ds(EDGE + rows, EDGE), :] = jnp.zeros((chunks, EDGE, LANES), F32)
        conv_pad[:, :EDGE, :] = jnp.zeros((2, EDGE, LANES), F32)
        conv_pad[:, pl.ds(EDGE + rows, EDGE), :] = jnp.zeros((2, EDGE, LANES), F32)

    spread_marks(marks_ref, columns, masks)
    hidden = hidden_ref[...]
    for c in range(chunks):
        rows_pad[c, pl.ds(EDGE, rows), :] = hidden[:, c * LANES : (c + 1) * LANES].astype(F32)

    step = 32

    def depth_step(i, carry):
        base = pl.multiple_of(i * step, step)
        total = [jnp.zeros((step, LANES), F32)] * chunks
        for tap in range(KERNEL):
            mask = masks[tap, pl.ds(base, step), :]
            for c in range(chunks):
                moved = rows_pad[c, pl.ds(base + EDGE + tap - HALF, step), :]
                total[c] = total[c] + (moved * mask) * depth_ref[tap : tap + 1, c * LANES : (c + 1) * LANES]
        for c in range(chunks):
            dl_ref[pl.ds(base, step), c * LANES : (c + 1) * LANES] = total[c].astype(BF16)
        return carry

    lax.fori_loop(0, rows // step, depth_step, 0)
    queries = (nn(hidden, query_ref[...]) + vec_ref[0:1, :]).astype(BF16)
    q_ref[...] = queries
    key_conv = nn(dl_ref[...], point_ref[...]) + vec_ref[2:3, :]
    kc_ref[...] = key_conv
    conv_attn = (key_conv * queries.astype(F32)).astype(BF16)
    ca_ref[...] = conv_attn
    tap_terms = nt(taps_ref[...], conv_attn)
    slot = lax.rem(s, 2)
    tap_out[slot] = tap_terms[tap_rows : 2 * tap_rows]
    swap_taps = pltpu.make_async_remote_copy(
        src_ref=tap_out.at[slot],
        dst_ref=tap_in.at[slot],
        send_sem=send_sem.at[slot],
        recv_sem=recv_sem.at[slot],
        device_id=at(me, 1 - mp),
        device_id_type=MESH,
    )
    swap_taps.start()
    own_terms = tap_terms[:tap_rows]
    k_ref[...] = nn(hidden, key_ref[...]).astype(BF16)
    v_ref[...] = (nn(hidden, value_ref[...]) + vec_ref[1:2, :]).astype(BF16)
    conv_values = nn(hidden, conv_ref[...]) + vec_ref[3:4, :]
    cv_ref[...] = conv_values
    for c in range(2):
        conv_pad[c, pl.ds(EDGE, rows), :] = conv_values[:, c * LANES : (c + 1) * LANES]

    block = 256
    seg_row = marks_ref[0, KERNEL : KERNEL + 1, :]
    lane = lax.broadcasted_iota(jnp.int32, (block, LANES), 1)

    def attention_step(i, carry):
        part = pl.ds(pl.multiple_of(i * block, block), block)
        allowed = columns[part, KERNEL : KERNEL + 1] == seg_row
        query = q_ref[part, :]
        total = jnp.zeros((block, WIDE), F32)
        packed = jnp.zeros((block, LANES), F32)
        for head in range(heads):
            mine = (only(query, head) * (HEAD_DIM**-0.5)).astype(BF16)
            scores = jnp.where(allowed, nt(mine, k_ref[...]), MASK_FILL)
            top = jnp.max(scores, axis=1, keepdims=True)
            exponent = jnp.exp(scores - top)
            amount = jnp.sum(exponent, axis=1, keepdims=True)
            probs = (exponent * (1.0 / amount)).astype(BF16)
            total = total + nn(probs, only(v_ref[...], head).astype(BF16))
            packed = jnp.where(lane == head, top + jnp.log(amount), packed)
        ctx_ref[part, :] = total.astype(BF16)
        tops[part, :] = packed
        return carry

    lax.fori_loop(0, rows // block, attention_step, 0)
    lse_ref[0] = jnp.transpose(tops[...])[:8]

    swap_taps.wait()
    logits = (own_terms + tap_in[slot] + bias_ref[:, :1]).reshape(heads, TAP_ROWS, rows)
    tap = lax.broadcasted_iota(jnp.int32, (heads, TAP_ROWS, rows), 1)
    logits = jnp.where(tap < KERNEL, logits, MASK_FILL)
    exponent = jnp.exp(logits - jnp.max(logits, axis=1, keepdims=True))
    probs = exponent / jnp.sum(exponent, axis=1, keepdims=True)
    probs_ref[0] = probs.reshape(tap_rows, rows)
    tap_mask = jnp.where(tap[0] < KERNEL, marks_ref[0], 0.0)
    weights[...] = high_low((probs * tap_mask[None]).reshape(tap_rows, rows), heads)
    conv_block = 128

    def conv_step(i, carry):
        base = pl.multiple_of(i * conv_block, conv_block)
        part = pl.ds(base, conv_block)
        scale = nn(weights[part, :], expand_ref[...])
        for c in range(2):
            total = jnp.zeros((conv_block, LANES), F32)
            for tap in range(KERNEL):
                low = tap * WIDE + c * LANES
                moved = conv_pad[c, pl.ds(base + EDGE + tap - HALF, conv_block), :]
                total = total + scale[:, low : low + LANES] * moved
            cc_ref[part, c * LANES : (c + 1) * LANES] = total.astype(BF16)
        return carry

    lax.fori_loop(0, rows // conv_block, conv_step, 0)

    @pl.when(s == 0)
    def _():
        for block, target, place in second_hops:
            if target is twin and place == parts + 1:
                arrive(block)
            elif target is beside:
                arrive(block)
            push(second_all_ref.at[block], block, target, place).start()

    @pl.when(s == min(1, seqs - 1))
    def _():
        for block, target, place in third_hops:
            arrive(block)
            push(second_all_ref.at[block], block, target, place).start()

    @pl.when(s == seqs - 1)
    def _():
        for k in range(parts):
            for other in range(2):
                arrive(index_of(lax.rem(deep + parts - k, parts), other, 1 - core))
        for copy in first_hops:
            copy.wait_send()
        for block, target, place in second_hops + third_hops:
            push(second_all_ref.at[block], block, target, place).wait_send()
        own_copy.wait()


def whole():
    return pl.BlockSpec(memory_space=pltpu.VMEM)


def by_seq(rows, columns):
    return pl.BlockSpec((rows, columns), lambda s: (s, 0))


def by_seq_row(rows, columns):
    return pl.BlockSpec((1, rows, columns), lambda s: (s, 0, 0))


def front(hidden, marks, w, vectors, depth, bias, expand, taps, second, count, ident):
    seqs, _, rows = marks.shape
    tokens, model = hidden.shape
    tap_rows = bias.shape[0]
    parts = count // 4

    def wide(kind):
        return jax.ShapeDtypeStruct((tokens, WIDE), kind)

    return pl.pallas_call(
        functools.partial(front_kernel, seqs, count),
        grid=(seqs,),
        out_shape=(
            wide(BF16), wide(BF16), wide(BF16), wide(F32),
            jax.ShapeDtypeStruct((tokens, model), BF16),
            wide(F32), wide(BF16),
            jax.ShapeDtypeStruct((seqs, tap_rows, rows), F32),
            wide(BF16), wide(BF16),
            jax.ShapeDtypeStruct((seqs, 8, rows), F32),
            jax.ShapeDtypeStruct((count,) + second.shape[1:], BF16),
        ),
        in_specs=[by_seq(rows, model), by_seq_row(TAP_ROWS, rows)] + [whole()] * 10 + [pl.BlockSpec(memory_space=pl.ANY)],
        out_specs=(
            by_seq(rows, WIDE), by_seq(rows, WIDE), by_seq(rows, WIDE), by_seq(rows, WIDE), by_seq(rows, model),
            by_seq(rows, WIDE), by_seq(rows, WIDE), by_seq_row(tap_rows, rows), by_seq(rows, WIDE), by_seq(rows, WIDE),
            by_seq_row(8, rows), pl.BlockSpec(memory_space=pl.ANY),
        ),
        scratch_shapes=[
            pltpu.VMEM((model // LANES, rows + 2 * EDGE, LANES), F32),
            pltpu.VMEM((2, rows + 2 * EDGE, LANES), F32),
            pltpu.VMEM((KERNEL, rows, LANES), F32),
            pltpu.VMEM((rows, LANES), F32),
            pltpu.VMEM((rows, LANES), BF16),
            pltpu.VMEM((rows, LANES), F32),
            pltpu.VMEM((2, tap_rows, rows), F32),
            pltpu.VMEM((2, tap_rows, rows), F32),
            pltpu.SemaphoreType.DMA((2,)),
            pltpu.SemaphoreType.DMA((2,)),
            pltpu.SemaphoreType.DMA,
            pltpu.SemaphoreType.DMA((4 * parts - 1,)),
            pltpu.SemaphoreType.DMA((count,)),
        ],
        compiler_params=pltpu.CompilerParams(
            collective_id=ident, has_side_effects=True, vmem_limit_bytes=60 << 20
        ),
        name="front",
    )(
        hidden, marks, w.query, w.key, w.value, w.conv, w.point, taps, vectors, depth, bias, expand, second,
    )


def transposed_stats(columns):
    rows = columns[0].shape[0]
    lane = lax.broadcasted_iota(jnp.int32, (rows, 128), 1)
    packed = jnp.zeros((rows, 128), F32)
    for place, column in enumerate(columns):
        packed = jnp.where(lane == place, column, packed)
    return jnp.transpose(packed)[:8]


def stat_columns(message, amount):
    rows = message.shape[1]
    wide = jnp.concatenate([message, jnp.zeros((120, rows), F32)], 0)
    tall = jnp.transpose(wide)
    return [tall[:, k : k + 1] for k in range(amount)]


def row_sums(value):
    rows, columns = value.shape
    return jnp.sum(value.reshape(rows // 8, 8, columns), axis=0)


SLOTS = 4
FFN_STEP = 256


def middle_kernel(
    blocks,
    context_ref, conv_ref, context_late_ref, conv_late_ref, hidden_ref, grad_ref, grad_late_ref, out0_ref, out1_ref, inner_ref, outer_ref, vec_ref,
    output_ref, residual_ref, grad_context_ref, grad_conv_ref, big_inner_ref, big_outer_ref, big_out_ref, small_ref,
    branch_ref, acc_out0, acc_out1, state, scale_ring, act_ring, slope_ring, low_ring, summed_ring, normed_ring, stat_ring,
    acc_inner, acc_outer, acc_small, acc_bias,
    branch_out, branch_in, stat1_out, stat1_in, stat2_out, stat2_in, stat3_out, stat3_in, back_out, back_in,
    send_sem, recv_sem,
):
    i = pl.program_id(0)
    me = lax.axis_index("mp")
    dp = lax.axis_index("dp")
    width = summed_ring.shape[2]
    hidden_units = inner_ref.shape[0]
    inverse = 1.0 / (2 * width)

    def message(kind, source, target, slot):
        return pltpu.make_async_remote_copy(
            src_ref=source.at[slot],
            dst_ref=target.at[slot],
            send_sem=send_sem.at[kind, slot],
            recv_sem=recv_sem.at[kind, slot],
            device_id=(dp, 1 - me),
            device_id_type=MESH,
        )

    kinds = [
        (branch_out, branch_in), (stat1_out, stat1_in), (stat2_out, stat2_in), (stat3_out, stat3_in), (back_out, back_in),
    ]

    def fresh(kind, b, slot):
        @pl.when(b >= SLOTS)
        def _():
            message(kind, *kinds[kind], slot).wait_send()

    def vec(row):
        return vec_ref[row : row + 1, :width]

    @pl.when(i == 0)
    def _():
        barrier = pltpu.get_barrier_semaphore()
        pl.semaphore_signal(barrier, inc=1, device_id=(dp, 1 - me), device_id_type=MESH)
        pl.semaphore_wait(barrier, 1)
        acc_inner[...] = jnp.zeros_like(acc_inner)
        acc_outer[...] = jnp.zeros_like(acc_outer)
        acc_out0[...] = jnp.zeros_like(acc_out0)
        acc_out1[...] = jnp.zeros_like(acc_out1)
        acc_small[...] = jnp.zeros_like(acc_small)
        acc_bias[...] = jnp.zeros_like(acc_bias)

    @pl.when(i < blocks)
    def _():
        b = i
        slot = lax.rem(b, SLOTS)
        fresh(0, b, slot)
        theirs = pl.ds(pl.multiple_of((1 - me) * width, width), width)
        ours = pl.ds(pl.multiple_of(me * width, width), width)
        other = nt(context_ref[...], out0_ref[theirs, :]) + nt(conv_ref[...], out1_ref[theirs, :])
        branch_out[slot] = other.astype(BF16)
        message(0, *kinds[0], slot).start()
        own = nt(context_ref[...], out0_ref[ours, :]) + nt(conv_ref[...], out1_ref[ours, :])
        state[lax.rem(b, 8)] = hidden_ref[:, ours].astype(F32) + (own + vec(0))

    @pl.when(jnp.logical_and(i >= 1, i < blocks + 1))
    def _():
        b = i - 1
        slot = lax.rem(b, SLOTS)
        message(0, *kinds[0], slot).wait_recv()
        fresh(1, b, slot)
        residual = state[lax.rem(b, 8)] + branch_in[slot].astype(F32)
        state[lax.rem(b, 8)] = residual
        total = jnp.sum(residual, axis=1, keepdims=True)
        apart = residual - total * (1.0 / width)
        stat1_out[slot] = transposed_stats([total, jnp.sum(apart * apart, axis=1, keepdims=True)])
        message(1, *kinds[1], slot).start()

    @pl.when(jnp.logical_and(i >= 2, i < blocks + 2))
    def _():
        b = i - 2
        slot = lax.rem(b, SLOTS)
        two = lax.rem(b, 2)
        message(1, *kinds[1], slot).wait_recv()
        fresh(2, b, slot)
        total, square = stat_columns(stat1_out[slot], 2)
        total_o, square_o = stat_columns(stat1_in[slot], 2)
        mean, scale = moments(total, square, total_o, square_o, width)
        standard = (state[lax.rem(b, 8)] - mean) * scale
        state[lax.rem(b, 8)] = standard
        scale_ring[lax.rem(b, 4)] = jnp.broadcast_to(scale, scale_ring.shape[1:])
        normed = standard * vec(1) + vec(2)
        low = normed.astype(BF16)
        low_ring[two] = low
        summed = normed + vec(3)
        for start in range(0, hidden_units, FFN_STEP):
            part = pl.ds(start, FFN_STEP)
            inner = nt(low, inner_ref[part, :]) + vec_ref[7:8, start : start + FFN_STEP]
            cdf = 0.5 * (1.0 + lax.erf(inner * INV_ROOT2))
            act = (inner * cdf).astype(BF16)
            act_ring[two, :, part] = act
            slope_ring[two, :, part] = cdf + inner * jnp.exp(-0.5 * inner * inner) * INV_ROOT_TWO_PI
            summed = summed + nn(act, outer_ref[part, :])
        summed_ring[two] = summed
        scaled = grad_ref[...].astype(F32) * vec(4)
        total = jnp.sum(summed, axis=1, keepdims=True)
        apart = summed - total * (1.0 / width)
        stat2_out[slot] = transposed_stats(
            [
                total,
                jnp.sum(apart * apart, axis=1, keepdims=True),
                jnp.sum(scaled, axis=1, keepdims=True),
                jnp.sum(scaled * apart, axis=1, keepdims=True),
            ]
        )
        message(2, *kinds[2], slot).start()

    @pl.when(jnp.logical_and(i >= 3, i < blocks + 3))
    def _():
        b = i - 3
        slot = lax.rem(b, SLOTS)
        two = lax.rem(b, 2)
        message(2, *kinds[2], slot).wait_recv()
        fresh(3, b, slot)
        total, square, grads, cross = stat_columns(stat2_out[slot], 4)
        total_o, square_o, grads_o, cross_o = stat_columns(stat2_in[slot], 4)
        mean, scale = moments(total, square, total_o, square_o, width)
        mean_grad = (grads + grads_o) * inverse
        product = cross + cross_o + (total * (1.0 / width) - mean) * grads + (total_o * (1.0 / width) - mean) * grads_o
        mean_product = product * scale * inverse
        standard = (summed_ring[two] - mean) * scale
        output_ref[...] = (standard * vec(4) + vec(5)).astype(BF16)
        gradient = grad_late_ref[...].astype(F32)
        grad_summed = scale * (gradient * vec(4) - mean_grad - standard * mean_product)
        low = grad_summed.astype(BF16)
        acc_small[0] += row_sums(low.astype(F32))
        acc_small[1] += row_sums(gradient * standard)
        acc_small[2] += row_sums(gradient)
        normed_low = low_ring[two]
        grad_normed = grad_summed
        for start in range(0, hidden_units, FFN_STEP):
            part = pl.ds(start, FFN_STEP)
            grad_inner = nt(low, outer_ref[part, :]) * slope_ring[two, :, part]
            inner_low = grad_inner.astype(BF16)
            acc_bias[:, part] += row_sums(inner_low.astype(F32))
            grad_normed = grad_normed + nn(inner_low, inner_ref[part, :])
            acc_outer[part, :] += tn(act_ring[two, :, part], low)
            acc_inner[part, :] += tn(inner_low, normed_low)
        normed_ring[two] = grad_normed
        standard1 = state[lax.rem(b, 8)]
        scaled = grad_normed * vec(1)
        acc_small[3] += row_sums(grad_normed * standard1)
        acc_small[4] += row_sums(grad_normed)
        sums = transposed_stats(
            [jnp.sum(scaled, axis=1, keepdims=True), jnp.sum(scaled * standard1, axis=1, keepdims=True)]
        )
        stat3_out[slot] = sums
        message(3, *kinds[3], slot).start()

    @pl.when(jnp.logical_and(i >= 4, i < blocks + 4))
    def _():
        b = i - 4
        slot = lax.rem(b, SLOTS)
        message(3, *kinds[3], slot).wait_recv()
        fresh(4, b, slot)
        first, second = stat_columns(stat3_out[slot] + stat3_in[slot], 2)
        standard = state[lax.rem(b, 8)]
        scaled = normed_ring[lax.rem(b, 2)] * vec(1)
        residual = scale_ring[lax.rem(b, 4)][:, :1] * (scaled - first * inverse - standard * (second * inverse))
        residual_ref[...] = residual
        low = residual.astype(BF16)
        acc_small[5] += row_sums(low.astype(F32))
        back_out[slot] = low
        message(4, *kinds[4], slot).start()

    @pl.when(i >= 5)
    def _():
        b = i - 5
        slot = lax.rem(b, SLOTS)
        message(4, *kinds[4], slot).wait_recv()
        theirs = pl.ds(pl.multiple_of((1 - me) * width, width), width)
        ours = pl.ds(pl.multiple_of(me * width, width), width)
        branch_ref[:, ours] = back_out[slot]
        branch_ref[:, theirs] = back_in[slot]
        branch = branch_ref[...]
        grad_context_ref[...] = nn(branch, out0_ref[...]).astype(BF16)
        grad_conv_ref[...] = nn(branch, out1_ref[...]).astype(BF16)
        acc_out0[...] += tn(branch, context_late_ref[...])
        acc_out1[...] += tn(branch, conv_late_ref[...])

    @pl.when(i == blocks + 4)
    def _():
        for kind in range(5):
            for slot in range(SLOTS):
                message(kind, *kinds[kind], slot).wait_send()
        big_inner_ref[...] = acc_inner[...].astype(BF16)
        big_outer_ref[...] = acc_outer[...].astype(BF16)
        big_out_ref[...] = jnp.concatenate([acc_out0[:, : width // 2], acc_out1[:, : width // 2]], 1).astype(BF16)
        small_ref[...] = jnp.zeros_like(small_ref)
        for row in range(6):
            small_ref[row : row + 1, :width] = jnp.sum(acc_small[row], axis=0, keepdims=True)
        small_ref[6:7, :] = jnp.sum(acc_bias[...], axis=0, keepdims=True)


def middle(context, conv_context, hidden, out_grad, w, p, me, ident):
    tokens, model = hidden.shape
    width = model // 2
    local = context.shape[1]
    units = w.inner.shape[0]
    rows = 256
    blocks = tokens // rows

    def mine(value):
        return lax.dynamic_slice_in_dim(value, me * width, width, 0)

    vectors = [
        mine(p.out_bias), mine(p.norm1_gain), mine(p.norm1_bias), p.ffn_out_bias, p.norm2_gain, p.norm2_bias,
    ]
    table = jnp.stack([jnp.pad(v, (0, units - width)) for v in vectors] + [jnp.zeros((units,), F32), p.ffn_in_bias])

    def block(columns, lag):
        return pl.BlockSpec((rows, columns), lambda i: (jnp.clip(i - lag, 0, blocks - 1), 0))

    whole = pl.BlockSpec(memory_space=pltpu.VMEM)
    stat = pltpu.VMEM((SLOTS, 8, rows), F32)
    half = pltpu.VMEM((SLOTS, rows, width), BF16)
    return pl.pallas_call(
        functools.partial(middle_kernel, blocks),
        grid=(blocks + 5,),
        out_shape=(
            jax.ShapeDtypeStruct((tokens, width), BF16),
            jax.ShapeDtypeStruct((tokens, width), F32),
            jax.ShapeDtypeStruct((tokens, local), BF16),
            jax.ShapeDtypeStruct((tokens, local), BF16),
            jax.ShapeDtypeStruct((units, width), BF16),
            jax.ShapeDtypeStruct((units, width), BF16),
            jax.ShapeDtypeStruct((model, width), BF16),
            jax.ShapeDtypeStruct((8, units), F32),
        ),
        in_specs=[
            block(local, 0), block(local, 0), block(local, 5), block(local, 5), block(model, 0), block(width, 2),
            block(width, 3),
            whole, whole, whole, whole, whole,
        ],
        out_specs=(block(width, 3), block(width, 4), block(local, 5), block(local, 5), whole, whole, whole, whole),
        scratch_shapes=[
            pltpu.VMEM((rows, model), BF16),
            pltpu.VMEM((model, local), F32),
            pltpu.VMEM((model, local), F32),
            pltpu.VMEM((8, rows, width), F32),
            pltpu.VMEM((4, rows, 128), F32),
            pltpu.VMEM((2, rows, units), BF16),
            pltpu.VMEM((2, rows, units), F32),
            pltpu.VMEM((2, rows, width), BF16),
            pltpu.VMEM((2, rows, width), F32),
            pltpu.VMEM((2, rows, width), F32),
            pltpu.VMEM((8, 128), F32),
            pltpu.VMEM((units, width), F32),
            pltpu.VMEM((units, width), F32),
            pltpu.VMEM((6, 8, width), F32),
            pltpu.VMEM((8, units), F32),
            half, half, stat, stat, stat, stat, stat, stat, half, half,
            pltpu.SemaphoreType.DMA((5, SLOTS)),
            pltpu.SemaphoreType.DMA((5, SLOTS)),
        ],
        compiler_params=pltpu.CompilerParams(
            collective_id=ident, has_side_effects=True, vmem_limit_bytes=60 << 20
        ),
        name="middle",
    )(context, conv_context, context, conv_context, hidden, out_grad, out_grad, w.out0, w.out1, w.inner, w.outer, table)


def back_kernel(
    seqs,
    hidden_ref, grad_context, grad_conv_ref, residual_ref, marks_ref, q_ref, k_ref, v_ref, cv_ref, dl_ref, kc_ref, ca_ref, probs_ref,
    lse_ref,
    inputs_ref, point_ref, taps_ref, depth_ref, expand_ref, gather_ref,
    own_ref, other_ref, big_qk_ref, big_vc_ref, big_point_ref, bias_ref, tap_grad_ref, tap_bias_ref, depth_grad_ref,
    depth_pad, conv_pad, grad_pad, masks, columns, weights, shifted_weights, tap_terms, products,
    grads, grad_q, grad_k, grad_v, rows_total, tap_all,
    acc_in, acc_point, acc_bias, acc_tap, acc_tap_bias, acc_depth,
    tap_out, tap_in, send_sem, recv_sem,
):
    s = pl.program_id(0)
    mp = lax.axis_index("mp")
    dp = lax.axis_index("dp")
    rows, model = hidden_ref.shape
    chunks = model // LANES
    heads = probs_ref.shape[1] // TAP_ROWS
    tap_rows = heads * TAP_ROWS
    half = chunks // 2
    slot = lax.rem(s, 2)

    @pl.when(s == 0)
    def _():
        barrier = pltpu.get_barrier_semaphore()
        pl.semaphore_signal(barrier, inc=1, device_id=(dp, 1 - mp), device_id_type=MESH)
        pl.semaphore_wait(barrier, 1)
        for pad in (depth_pad, conv_pad, grad_pad):
            for start in (0, EDGE + rows):
                pad[:, pl.ds(start, EDGE), :] = jnp.zeros((pad.shape[0], EDGE, LANES), F32)
        for acc in (acc_in, acc_point, acc_bias, acc_tap, acc_tap_bias, acc_depth):
            acc[...] = jnp.zeros_like(acc)

    spread_marks(marks_ref, columns, masks)
    block = 256

    for c in range(2):
        lanes = slice(c * LANES, (c + 1) * LANES)
        grad_pad[c, pl.ds(EDGE, rows), :] = grad_conv_ref[:, lanes].astype(F32)
        conv_pad[c, pl.ds(EDGE, rows), :] = cv_ref[:, lanes]

    probs = probs_ref[0].reshape(heads, TAP_ROWS, rows)
    tap = lax.broadcasted_iota(jnp.int32, (heads, TAP_ROWS, rows), 1)
    tap_mask = jnp.where(tap < KERNEL, jnp.broadcast_to(marks_ref[...], (heads, TAP_ROWS, rows)), 0.0)
    masked = (probs * tap_mask).reshape(tap_rows, rows)
    flat_tap = tap.reshape(tap_rows, rows)
    moved = jnp.zeros_like(masked)
    for j in range(KERNEL):
        turn = (j - HALF) % rows
        turned = pltpu.roll(masked, turn, 1) if turn else masked
        moved = jnp.where(flat_tap == j, turned, moved)
    shifted_weights[...] = high_low(moved, heads)
    conv_block = 128

    def conv_step(i, carry):
        base = pl.multiple_of(i * conv_block, conv_block)
        part = pl.ds(base, conv_block)
        scale = nn(shifted_weights[part, :], expand_ref[...])
        for c in range(2):
            here = grad_pad[c, pl.ds(base + EDGE, conv_block), :]
            total = jnp.zeros((conv_block, LANES), F32)
            for j in range(KERNEL):
                low = j * WIDE + c * LANES
                products[:, low : low + LANES] = (
                    here * conv_pad[c, pl.ds(base + EDGE + j - HALF, conv_block), :]
                ).astype(BF16)
                total = total + scale[:, low : low + LANES] * grad_pad[
                    c, pl.ds(base + EDGE + HALF - j, conv_block), :
                ]
            grads[part, 3 * WIDE + c * LANES : 3 * WIDE + (c + 1) * LANES] = total.astype(BF16)
        tap_terms[part, :] = nn(products[...], gather_ref[...])
        return carry

    lax.fori_loop(0, rows // conv_block, conv_step, 0)
    grad_taps = jnp.transpose(tap_terms[...])[:tap_rows].reshape(heads, TAP_ROWS, rows) * tap_mask
    grad_logits = probs * (grad_taps - jnp.sum(probs * grad_taps, axis=1, keepdims=True))
    grad_logits = grad_logits.reshape(tap_rows, rows).astype(BF16)
    tap_out[slot] = grad_logits
    swap_taps = pltpu.make_async_remote_copy(
        src_ref=tap_out.at[slot],
        dst_ref=tap_in.at[slot],
        send_sem=send_sem.at[slot],
        recv_sem=recv_sem.at[slot],
        device_id=(dp, 1 - mp),
        device_id_type=MESH,
    )
    swap_taps.start()

    grad_k[...] = jnp.zeros_like(grad_k)
    grad_v[...] = jnp.zeros_like(grad_v)

    def attention_step(i, carry):
        part = pl.ds(pl.multiple_of(i * block, block), block)
        allowed = columns[:, KERNEL : KERNEL + 1] == marks_ref[0, KERNEL : KERNEL + 1, part]
        query = q_ref[part, :]
        context = grad_context[part, :]
        total = jnp.zeros((block, WIDE), F32)
        for head in range(heads):
            mine = (only(query, head) * (HEAD_DIM**-0.5)).astype(BF16)
            grad_mine = only(context, head).astype(BF16)
            scores = jnp.where(allowed, nt(k_ref[...], mine), MASK_FILL)
            probs = jnp.exp(scores - lse_ref[0, head : head + 1, part])
            grad_v[...] += nn(probs.astype(BF16), grad_mine)
            grad_probs = nt(v_ref[...], grad_mine)
            mixed = probs * grad_probs
            grad_scores = (mixed - probs * jnp.sum(mixed, axis=0, keepdims=True)).astype(BF16)
            grad_k[...] += nn(grad_scores, mine)
            total = total + tn(grad_scores, only(k_ref[...], head).astype(BF16))
        grad_q[part, :] = total
        return carry

    lax.fori_loop(0, rows // block, attention_step, 0)

    swap_taps.wait()
    tap_all[...] = jnp.zeros_like(tap_all)
    tap_all[:tap_rows, :] = tap_out[slot].astype(F32)
    tap_all[tap_rows : 2 * tap_rows, :] = tap_in[slot].astype(F32)
    every = tap_all[...]
    acc_tap[...] += nn(every.astype(BF16), ca_ref[...])
    acc_tap_bias[...] += sum(every[:, c * LANES : (c + 1) * LANES] for c in range(rows // LANES))
    weights[...] = jnp.transpose(every).astype(BF16)

    def key_step(i, carry):
        base = pl.multiple_of(i * block, block)
        part = pl.ds(base, block)
        grad_attn = nn(weights[part, :], taps_ref[...]).astype(BF16).astype(F32)
        query = q_ref[part, :].astype(F32)
        key_low = (grad_attn * query).astype(BF16)
        grads[part, 4 * WIDE : 5 * WIDE] = key_low
        grad_query = grad_q[part, :] * (HEAD_DIM**-0.5) + grad_attn * kc_ref[part, :]
        grads[part, :WIDE] = grad_query.astype(BF16)
        grads[part, WIDE : 2 * WIDE] = grad_k[part, :].astype(BF16)
        grads[part, 2 * WIDE : 3 * WIDE] = grad_v[part, :].astype(BF16)
        acc_bias[...] += row_sums(grads[part, :].astype(F32))
        grad_depth = nt(key_low, point_ref[...])
        total = nt(grads[part, : 4 * WIDE], inputs_ref[...])
        for c in range(chunks):
            lanes = slice(c * LANES, (c + 1) * LANES)
            depth_pad[c, pl.ds(base + EDGE, block), :] = grad_depth[:, lanes]
            rows_total[c, part, :] = total[:, lanes]
        return carry

    lax.fori_loop(0, rows // block, key_step, 0)
    acc_point[...] += tn(dl_ref[...], grads[:, 4 * WIDE : 5 * WIDE])
    acc_in[...] += tn(hidden_ref[...], grads[:, : 4 * WIDE])
    step = 64

    for c in range(chunks):
        lanes = slice(c * LANES, (c + 1) * LANES)

        def depth_step(i, carry, c=c, lanes=lanes):
            base = pl.multiple_of(i * step, step)
            part = pl.ds(base, step)
            here = hidden_ref[part, lanes].astype(F32)
            total = rows_total[c, part, :]
            sums = []
            for j in range(KERNEL):
                mirror = KERNEL - 1 - j
                near = depth_pad[c, pl.ds(base + EDGE + j - HALF, step), :] * masks[j, part, :]
                total = total + near * depth_ref[mirror : mirror + 1, lanes]
                sums.append(carry[j] + jnp.sum((near * here).reshape(step // 8, 8, LANES), axis=0))
            rows_total[c, part, :] = total
            return tuple(sums)

        sums = lax.fori_loop(0, rows // step, depth_step, tuple(jnp.zeros((8, LANES), F32) for _ in range(KERNEL)))
        for j in range(KERNEL):
            acc_depth[KERNEL - 1 - j, :, lanes] += sums[j]
    for c in range(half):
        lanes = slice(c * LANES, (c + 1) * LANES)
        own_ref[:, lanes] = rows_total[mp * half + c] + residual_ref[:, lanes]
        other_ref[:, lanes] = rows_total[(1 - mp) * half + c].astype(BF16)

    @pl.when(s == seqs - 1)
    def _():
        width = heads * HEAD_DIM

        def pair(first, second):
            return jnp.concatenate([first[:, :width], second[:, :width]], 1).astype(BF16)

        big_qk_ref[...] = pair(acc_in[:, :WIDE], acc_in[:, WIDE : 2 * WIDE])
        big_vc_ref[...] = pair(acc_in[:, 2 * WIDE : 3 * WIDE], acc_in[:, 3 * WIDE :])
        big_point_ref[...] = pair(acc_point[...], jnp.zeros_like(acc_point))
        bias_ref[...] = jnp.sum(acc_bias[...], axis=0, keepdims=True) + jnp.zeros_like(bias_ref)
        tap_grad_ref[...] = acc_tap[...]
        tap_bias_ref[...] = jnp.sum(acc_tap_bias[...], axis=1, keepdims=True) + jnp.zeros_like(tap_bias_ref)
        for j in range(KERNEL):
            depth_grad_ref[j : j + 1, :] = jnp.sum(acc_depth[j], axis=0, keepdims=True)
        depth_grad_ref[KERNEL:, :] = jnp.zeros((TAP_ROWS - KERNEL, model), F32)


def back(hidden, grad_context, grad_conv, residual, marks, kept, w, taps, depth, expand, ident):
    q, k, v, cv, dl, kc, ca, probs, lse = kept
    seqs, _, rows = marks.shape
    tokens, model = hidden.shape
    width = model // 2
    tap_rows = probs.shape[1]

    def seq(columns):
        return by_seq(rows, columns)

    def shape(columns, kind, count=tokens):
        return jax.ShapeDtypeStruct((count, columns), kind)

    padded_rows = rows + 2 * EDGE
    vmem = pltpu.VMEM
    return pl.pallas_call(
        functools.partial(back_kernel, seqs),
        grid=(seqs,),
        out_shape=(
            shape(width, F32), shape(width, BF16),
            shape(width, BF16, model), shape(width, BF16, model), shape(width, BF16, model),
            shape(5 * WIDE, F32, 8), shape(WIDE, F32, LANES), shape(LANES, F32, LANES), shape(model, F32, TAP_ROWS),
        ),
        in_specs=[
            seq(model), seq(WIDE), seq(WIDE), seq(width), by_seq_row(TAP_ROWS, rows), seq(WIDE), seq(WIDE), seq(WIDE), seq(WIDE),
            seq(model), seq(WIDE), seq(WIDE), by_seq_row(tap_rows, rows), by_seq_row(8, rows),
        ] + [whole()] * 6,
        out_specs=(seq(width), seq(width)) + (whole(),) * 7,
        scratch_shapes=[
            vmem((model // LANES, padded_rows, LANES), F32),
            vmem((2, padded_rows, LANES), F32),
            vmem((2, padded_rows, LANES), F32),
            vmem((KERNEL, rows, LANES), F32),
            vmem((rows, LANES), F32),
            vmem((rows, LANES), BF16),
            vmem((rows, LANES), BF16),
            vmem((rows, LANES), F32),
            vmem((128, KERNEL * WIDE), BF16),
            vmem((rows, 5 * WIDE), BF16),
            vmem((rows, WIDE), F32),
            vmem((rows, WIDE), F32),
            vmem((rows, WIDE), F32),
            vmem((model // LANES, rows, LANES), F32),
            vmem((LANES, rows), F32),
            vmem((model, 4 * WIDE), F32),
            vmem((model, WIDE), F32),
            vmem((8, 5 * WIDE), F32),
            vmem((LANES, WIDE), F32),
            vmem((LANES, LANES), F32),
            vmem((TAP_ROWS, 8, model), F32),
            vmem((2, tap_rows, rows), BF16),
            vmem((2, tap_rows, rows), BF16),
            pltpu.SemaphoreType.DMA((2,)),
            pltpu.SemaphoreType.DMA((2,)),
        ],
        compiler_params=pltpu.CompilerParams(
            collective_id=ident, has_side_effects=True, vmem_limit_bytes=62 << 20
        ),
        name="back",
    )(
        hidden, grad_context, grad_conv, residual, marks, q, k, v, cv, dl, kc, ca, probs, lse,
        jnp.concatenate([w.query, w.key, w.value, w.conv], 1), w.point, taps, depth, expand,
        jnp.pad(expand[:tap_rows], ((0, LANES - tap_rows), (0, 0))).T,
    )


def marks_of(segment):
    masks = [same_segment(segment, tap - HALF, HALF) for tap in range(KERNEL)]
    blank = jnp.zeros_like(segment)
    return jnp.stack([m.astype(F32) for m in masks] + [segment.astype(F32)] + [blank.astype(F32)] * (TAP_ROWS - KERNEL - 1))


def expansion(heads):
    row = lax.broadcasted_iota(jnp.int32, (LANES, KERNEL * WIDE), 0)
    column = lax.broadcasted_iota(jnp.int32, (LANES, KERNEL * WIDE), 1)
    tap, lane = column // WIDE, column % WIDE
    wanted = (lane // HEAD_DIM) * TAP_ROWS + tap
    inside = jnp.logical_and(lane < heads * HEAD_DIM, row < 2 * heads * TAP_ROWS)
    return jnp.logical_and(inside, row % (heads * TAP_ROWS) == wanted).astype(BF16)


def padded(value, multiple):
    rows = value.shape[-2]
    extra = -rows % multiple
    return jnp.pad(value, [(0, 0)] * (value.ndim - 2) + [(0, extra), (0, 0)])


def on_device(
    count,
    hidden, doc_lengths, query_weight, key_weight, value_weight, query_bias, value_bias,
    depth_weight, point_weight, point_bias, kernel_weight, kernel_bias, conv_weight, conv_bias,
    out_weight, out_bias, norm1_gain, norm1_bias, ffn_in_weight, ffn_in_bias, ffn_out_weight,
    ffn_out_bias, norm2_gain, norm2_bias, out_grad,
):
    me = lax.axis_index("mp")
    share, width = query_weight.shape
    model = hidden.shape[1]
    group = ffn_out_bias.shape[0]
    share_ffn = ffn_out_weight.shape[1]
    depth_wide = jnp.pad(depth_weight.T, ((0, 0), (0, width - KERNEL)))
    first = jnp.concatenate(
        [
            jnp.concatenate([query_weight, key_weight], 1),
            jnp.concatenate([value_weight, conv_weight], 1),
            jnp.concatenate([point_weight, depth_wide], 1),
        ],
        0,
    )
    out_cut = jnp.concatenate([out_weight[0].T, out_weight[1].T], 1)
    second = jnp.concatenate([out_cut, ffn_in_weight[0].T, ffn_out_weight[0]], 0)
    first_all = gather(padded(first, 16)[None], count, 1)

    def cut(source, start, size, low, high):
        return source[:, start : start + size, low:high].reshape(count * size, high - low)

    def cut_wide(source, start, low):
        return jnp.pad(cut(source, start, share, low, low + width), ((0, 0), (0, WIDE - width)))

    w = Group(
        query=cut_wide(first_all, 0, 0),
        key=cut_wide(first_all, 0, width),
        value=cut_wide(first_all, share, 0),
        conv=cut_wide(first_all, share, width),
        point=cut_wide(first_all, 2 * share, 0),
        depth=cut(first_all, 2 * share, share, width, width + TAP_ROWS).T,
    )
    p = Group(
        query_bias=query_bias, value_bias=value_bias, point_bias=point_bias, kernel_weight=kernel_weight,
        kernel_bias=kernel_bias, conv_bias=conv_bias, out_bias=out_bias, norm1_gain=norm1_gain,
        norm1_bias=norm1_bias, ffn_in_bias=ffn_in_bias[0], ffn_out_bias=ffn_out_bias,
        norm2_gain=norm2_gain, norm2_bias=norm2_bias,
    )
    seqs = doc_lengths.shape[0]
    seq_rows = hidden.shape[0] // seqs
    spans = [slice(s * seq_rows, (s + 1) * seq_rows) for s in range(seqs)]
    segments = [segment_ids(doc_lengths[q], seq_rows) for q in range(seqs)]
    marks = jnp.stack([marks_of(segment) for segment in segments])
    heads = width // HEAD_DIM
    vectors = jnp.stack(
        [jnp.pad(b, (0, WIDE - width)) for b in (query_bias, value_bias, point_bias, conv_bias)] * 2
    )
    order = kernel_weight.T.reshape(2, heads, KERNEL, width)
    order = jnp.where(me == 0, order, order[::-1])
    taps = jnp.pad(order, ((0, 0), (0, 0), (0, TAP_ROWS - KERNEL), (0, WIDE - width))).reshape(-1, WIDE)
    taps = jnp.pad(taps, ((0, LANES - taps.shape[0]), (0, 0)))
    bias = lax.dynamic_slice_in_dim(kernel_bias.reshape(2, heads, KERNEL), me, 1, 0)[0]
    bias = jnp.pad(bias, ((0, 0), (0, TAP_ROWS - KERNEL))).reshape(-1, 1)
    bias = jnp.broadcast_to(bias, (bias.shape[0], LANES))
    expand = expansion(heads)
    q, k, v, cv, dl, kc, ca, probs, cc, ctx, lse, second_all = front(
        hidden, marks, w, vectors, w.depth.astype(F32), bias, expand, taps, padded(second, 16)[None], count, 2
    )
    w.out0 = cut_wide(second_all, 0, 0)
    w.out1 = cut_wide(second_all, 0, width)
    w.inner = cut(second_all, share, share_ffn, 0, group)
    w.outer = cut(second_all, share + share_ffn, share_ffn, 0, group)
    output, grad_residual, grad_context, grad_conv, big_inner, big_outer, big_out, sums_mid = middle(
        ctx, cc, hidden, out_grad, w, p, me, 4
    )
    depth = w.depth.astype(F32)
    part_own, part_other, big_qk, big_vc, big_point, bias_sums, tap_grads, tap_bias, depth_grads = back(
        hidden, grad_context, grad_conv, grad_residual, marks, (q, k, v, cv, dl, kc, ca, probs, lse),
        w, taps, depth, expand, 5,
    )
    grad_input = part_own + swap(part_other).astype(F32)

    def both(value):
        value = value[: 2 * heads * TAP_ROWS].reshape(2, heads, TAP_ROWS, -1)[:, :, :KERNEL]
        return jnp.where(me == 0, value, value[::-1]).reshape(2 * heads * KERNEL, -1)

    kernel_weight_grad = both(tap_grads)[:, :width].T
    kernel_bias_grad = both(tap_bias)[:, 0]

    def bias_of(place):
        return bias_sums[0, place * WIDE : place * WIDE + width]

    def widened(value):
        empty = jnp.zeros_like(value)
        return jnp.where(me == 0, jnp.concatenate([value, empty]), jnp.concatenate([empty, value]))


    def blocks(value):
        return value.reshape(count, value.shape[0] // count, value.shape[1])

    pieces = [blocks(value) for value in (big_qk, big_vc, big_point, big_out, big_inner, big_outer)]
    pieces = jnp.concatenate(pieces, 1)
    own_parts = [
        bias_of(0), bias_of(2), bias_of(4), kernel_weight_grad, kernel_bias_grad,
        bias_of(3), sums_mid[6], sums_mid[0, :group], sums_mid[1, :group], sums_mid[2, :group],
    ]
    columns = group

    def table(parts, rows):
        flat = jnp.concatenate([part.reshape(-1) for part in parts])
        return jnp.pad(flat, (0, rows * columns - flat.shape[0])).reshape(rows, columns)

    own_size = sum(part.size for part in own_parts)
    own_rows = -(-own_size // columns)
    own_rows += -own_rows % 8
    shared_parts = [depth_grads[:KERNEL]] + [widened(sums_mid[k, :group]) for k in (3, 4, 5)]
    smalls = jnp.concatenate([table(own_parts, own_rows), table(shared_parts, SHARED_ROWS)], 0)
    sums, totals = scatter(padded(pieces, 16), smalls, count, 3)

    def untable(value, parts):
        flat, result, start = value.reshape(-1), [], 0
        for part in parts:
            result.append(flat[start : start + part.size].reshape(part.shape))
            start += part.size
        return result

    query_b, value_b, point_b, kernel_w, kernel_b, conv_b, in_b, outer_b, gain2, bias2 = untable(
        totals[:own_rows], own_parts
    )
    depth_g, gain1, bias1, out_b = untable(totals[own_rows:], shared_parts)
    place = lax.axis_index("dp")
    depth_own = lax.dynamic_slice_in_dim(depth_g, place * share, share, 1)
    at_rows = lambda k: sums[k * share : (k + 1) * share]
    qk, vc, po, oo = at_rows(0), at_rows(1), at_rows(2), at_rows(3)
    inner_own = sums[4 * share : 4 * share + share_ffn]
    outer_own = sums[4 * share + share_ffn : 4 * share + 2 * share_ffn]
    return (
        output,
        grad_input,
        qk[:, :width],
        qk[:, width:],
        vc[:, :width],
        query_b,
        value_b,
        depth_own,
        po[:, :width],
        point_b,
        kernel_w,
        kernel_b,
        vc[:, width:],
        conv_b,
        jnp.stack([oo[:, :width].T, oo[:, width:].T]),
        out_b,
        gain1,
        bias1,
        inner_own.T[None],
        in_b[None],
        outer_own[None],
        outer_b,
        gain2,
        bias2,
    )


def solution(mesh):
    in_specs = (
        P("dp", None),
        P("dp", None),
        P("dp", "mp"),
        P("dp", "mp"),
        P("dp", "mp"),
        P("mp"),
        P("mp"),
        P(None, "dp"),
        P("dp", "mp"),
        P("mp"),
        P("mp", None),
        P(),
        P("dp", "mp"),
        P("mp"),
        P(None, "mp", "dp"),
        P(),
        P(),
        P(),
        P("mp", None, "dp"),
        P("mp", None),
        P("mp", "dp", None),
        P("mp"),
        P("mp"),
        P("mp"),
        P("dp", "mp"),
    )
    out_specs = (
        P("dp", "mp"),
        P("dp", "mp"),
        P("dp", "mp"),
        P("dp", "mp"),
        P("dp", "mp"),
        P("mp"),
        P("mp"),
        P(None, "dp"),
        P("dp", "mp"),
        P("mp"),
        P("mp", None),
        P(),
        P("dp", "mp"),
        P("mp"),
        P(None, "mp", "dp"),
        P(),
        P(),
        P(),
        P("mp", None, "dp"),
        P("mp", None),
        P("mp", "dp", None),
        P("mp"),
        P("mp"),
        P("mp"),
    )
    return jax.shard_map(
        functools.partial(on_device, mesh.shape["dp"]), mesh=mesh, in_specs=in_specs, out_specs=out_specs, check_vma=False
    )
```

```python
import functools
import jax
import jax.numpy as jnp
from jax import lax
from jax.experimental import pallas as pl
from jax.experimental.pallas import tpu as pltpu

from jax.sharding import PartitionSpec as P

MESH = pl.DeviceIdType.MESH
BF16 = jnp.bfloat16
F32 = jnp.float32


def at(dp, mp):
    return (dp, mp)


def places(count):
    dp = lax.axis_index("dp")
    core = lax.rem(dp, 2)
    side = lax.rem(lax.div(dp, 2), 2)
    deep = lax.div(dp, 4)
    return lax.axis_index("mp"), core, side, deep, count // 4


def index_of(deep, side, core):
    return (deep * 2 + side) * 2 + core


def greet(count):
    mp, core, side, deep, parts = places(count)
    barrier = pltpu.get_barrier_semaphore()
    peers = [index_of(lax.rem(deep + k, parts), side, core) for k in range(1, parts)]
    peers += [index_of(deep, 1 - side, core), index_of(deep, side, 1 - core)]
    for peer in peers:
        pl.semaphore_signal(barrier, inc=1, device_id=at(peer, mp), device_id_type=MESH)
    pl.semaphore_wait(barrier, len(peers))


def gather_kernel(count, own_ref, out_ref, own_sem, send_sem, recv_sem):
    mp, core, side, deep, parts = places(count)
    me = index_of(deep, side, core)
    greet(count)
    local = pltpu.make_async_copy(own_ref.at[0], out_ref.at[me], own_sem)
    local.start()
    started = []

    def push(source, block, target):
        copy = pltpu.make_async_remote_copy(
            src_ref=source,
            dst_ref=out_ref.at[block],
            send_sem=send_sem.at[len(started)],
            recv_sem=recv_sem.at[block],
            device_id=at(target, mp),
            device_id_type=MESH,
        )
        copy.start()
        started.append(copy)

    def arrive(block):
        pltpu.make_async_copy(own_ref.at[0], out_ref.at[block], recv_sem.at[block]).wait()

    beside = index_of(deep, 1 - side, core)
    twin = index_of(deep, side, 1 - core)
    for k in range(1, parts):
        push(own_ref.at[0], me, index_of(lax.rem(deep + k, parts), side, core))
    push(own_ref.at[0], me, beside)
    push(own_ref.at[0], me, twin)
    arrive(beside)
    push(out_ref.at[beside], beside, twin)
    for k in range(1, parts):
        block = index_of(lax.rem(deep + parts - k, parts), side, core)
        arrive(block)
        push(out_ref.at[block], block, beside)
        push(out_ref.at[block], block, twin)
    for k in range(1, parts):
        block = index_of(lax.rem(deep + parts - k, parts), 1 - side, core)
        arrive(block)
        push(out_ref.at[block], block, twin)
    for k in range(parts):
        for other in range(2):
            arrive(index_of(lax.rem(deep + parts - k, parts), other, 1 - core))
    for copy in started:
        copy.wait_send()
    local.wait()


def gather(own, count, ident):
    parts = count // 4
    sends = (parts - 1) * 4 + 3
    shape = (count,) + own.shape[1:]
    return pl.pallas_call(
        functools.partial(gather_kernel, count),
        out_shape=jax.ShapeDtypeStruct(shape, own.dtype),
        in_specs=[pl.BlockSpec(memory_space=pl.ANY)],
        out_specs=pl.BlockSpec(memory_space=pl.ANY),
        scratch_shapes=[
            pltpu.SemaphoreType.DMA,
            pltpu.SemaphoreType.DMA((sends,)),
            pltpu.SemaphoreType.DMA((count,)),
        ],
        compiler_params=pltpu.CompilerParams(collective_id=ident, has_side_effects=True),
        name="weight_gather",
    )(own)


class Hops:
    def __init__(self, count, in_ref, twin_in, side_in, deep_in, send_sem, recv_sem):
        self.mp, self.core, self.side, self.deep, self.parts = places(count)
        self.in_ref, self.twin_in, self.side_in, self.deep_in = in_ref, twin_in, side_in, deep_in
        self.send_sem, self.recv_sem = send_sem, recv_sem
        self.beside = index_of(self.deep, 1 - self.side, self.core)
        self.twin = index_of(self.deep, self.side, 1 - self.core)
        self.order = [(k, other) for k in list(range(1, self.parts)) + [0] for other in (1, 0)]
        self.rows = in_ref.shape[1]
        self.step = 48 if self.rows % 48 == 0 else 16

    def depth(self, k):
        return lax.rem(self.deep + k, self.parts)

    def copy(self, source, target_ref, slot, target):
        return pltpu.make_async_remote_copy(
            src_ref=source,
            dst_ref=target_ref,
            send_sem=self.send_sem.at[slot],
            recv_sem=self.recv_sem.at[slot],
            device_id=at(target, self.mp),
            device_id_type=MESH,
        )

    def block(self, slot, core):
        k, other = self.order[slot]
        return index_of(self.depth(k), 1 - self.side if other else self.side, core)

    def first(self, slot):
        return self.copy(self.in_ref.at[self.block(slot, 1 - self.core)], self.twin_in.at[slot], slot, self.twin)

    def second(self, place):
        return self.copy(
            self.twin_in.at[2 * place], self.side_in.at[place], 2 * self.parts + place, self.beside
        )

    def third(self, place):
        k = self.order[2 * place][0]
        target = index_of(self.depth(k), self.side, self.core)
        return self.copy(self.side_in.at[place], self.deep_in.at[place], 3 * self.parts + place, target)

    def add(self, target, term):
        @pl.loop(0, self.rows // self.step)
        def _(i):
            part = pl.ds(pl.multiple_of(i * self.step, 16), self.step)
            total = target[part, :].astype(F32) + term[part, :].astype(F32)
            target[part, :] = total.astype(target.dtype)

    def start_first(self):
        for slot in range(2 * self.parts):
            self.first(slot).start()

    def start_second(self):
        for slot in range(2 * self.parts):
            self.first(slot).wait_recv()
            self.add(self.twin_in.at[slot], self.in_ref.at[self.block(slot, self.core)])
            if self.order[slot][1]:
                self.second(slot // 2).start()

    def start_third(self):
        for place in range(self.parts):
            self.second(place).wait_recv()
            self.add(self.side_in.at[place], self.twin_in.at[2 * place + 1])
            if place < self.parts - 1:
                self.third(place).start()

    def finish(self, out_ref):
        for place in range(self.parts - 1):
            self.third(place).wait_recv()

        @pl.loop(0, self.rows // self.step)
        def _(i):
            part = pl.ds(pl.multiple_of(i * self.step, 16), self.step)
            total = self.side_in[self.parts - 1, part, :].astype(F32)
            for place in range(self.parts - 1):
                total = total + self.deep_in[place, part, :].astype(F32)
            out_ref[part, :] = total

        for slot in range(2 * self.parts):
            self.first(slot).wait_send()
        for place in range(self.parts):
            self.second(place).wait_send()
        for place in range(self.parts - 1):
            self.third(place).wait_send()


def hop_scratch(count, rows, columns):
    parts = count // 4
    return [
        pltpu.VMEM((2 * parts, rows, columns), BF16),
        pltpu.VMEM((parts, rows, columns), BF16),
        pltpu.VMEM((max(parts - 1, 1), rows, columns), BF16),
        pltpu.SemaphoreType.DMA((4 * parts - 1,)),
        pltpu.SemaphoreType.DMA((4 * parts - 1,)),
    ]


def greet_all(count):
    mp, core, side, deep, parts = places(count)
    me = index_of(deep, side, core)
    barrier = pltpu.get_barrier_semaphore()
    pl.semaphore_signal(barrier, inc=1, device_id=at(me, 1 - mp), device_id_type=MESH)
    peers = [index_of(lax.rem(deep + k, parts), side, core) for k in range(1, parts)]
    peers += [index_of(deep, 1 - side, core), index_of(deep, side, 1 - core)]
    for peer in peers:
        pl.semaphore_signal(barrier, inc=1, device_id=at(peer, mp), device_id_type=MESH)
    pl.semaphore_wait(barrier, len(peers) + 1)


PIECES = 4


def tail_kernel(
    count, start,
    in_ref, table_ref, own_ref, other_ref, rest_ref,
    out_ref, total_ref, grad_ref,
    twin_in, side_in, deep_in, send_sem, recv_sem,
    table_in, table_out, table_send, table_recv, piece_in, piece_sum, piece_send, piece_recv, store_sem,
):
    mp, core, side, deep, parts = places(count)
    me = index_of(deep, side, core)
    greet_all(count)
    beside = index_of(deep, 1 - side, core)
    twin = index_of(deep, side, 1 - core)
    hops = Hops(count, in_ref, twin_in, side_in, deep_in, send_sem, recv_sem)
    rows = own_ref.shape[0] // PIECES

    def table_hop(source, slot, target, plane):
        return pltpu.make_async_remote_copy(
            src_ref=source,
            dst_ref=table_in.at[slot],
            send_sem=table_send.at[slot],
            recv_sem=table_recv.at[slot],
            device_id=at(target, plane),
            device_id_type=MESH,
        )

    def piece(i):
        part = pl.ds(i * rows, rows)
        return pltpu.make_async_remote_copy(
            src_ref=other_ref.at[part],
            dst_ref=piece_in.at[part],
            send_sem=piece_send.at[i],
            recv_sem=piece_recv.at[i],
            device_id=at(me, 1 - mp),
            device_id_type=MESH,
        )

    def store(i):
        return pltpu.make_async_copy(
            piece_sum.at[pl.ds(i * rows, rows)], grad_ref.at[pl.ds(start + i * rows, rows)], store_sem.at[i]
        )

    first = table_hop(table_ref, 0, me, 1 - mp)
    first.start()
    hops.start_first()
    for i in range(PIECES):
        piece(i).start()
    first.wait_recv()
    shared = pl.ds(TABLE_OWN, TABLE_ROWS - TABLE_OWN)
    table_out[0, :TABLE_OWN, :] = table_ref[:TABLE_OWN, :]
    table_out[0, shared, :] = table_ref[shared, :] + table_in[0, shared, :]
    second = table_hop(table_out.at[0], 1, twin, mp)
    second.start()
    hops.start_second()
    second.wait_recv()
    table_out[1] = table_out[0] + table_in[1]
    third = table_hop(table_out.at[1], 2, beside, mp)
    third.start()
    hops.start_third()
    third.wait_recv()
    table_out[2] = table_out[1] + table_in[2]
    fourth = [
        table_hop(table_out.at[2], 2 + j, index_of(lax.rem(deep + j, parts), side, core), mp) for j in range(1, parts)
    ]
    for copy in fourth:
        copy.start()
    for i in range(PIECES):
        piece(i).wait_recv()
        part = pl.ds(i * rows, rows)
        piece_sum[part, :] = own_ref[part, :] + piece_in[part, :].astype(F32)
        store(i).start()
    hops.finish(out_ref)
    for copy in fourth:
        copy.wait_recv()
    total = table_out[2]
    for j in range(1, parts):
        total = total + table_in[2 + j]
    total_ref[...] = total
    for copy in [first, second, third] + fourth:
        copy.wait_send()
    for i in range(PIECES):
        piece(i).wait_send()
        store(i).wait()


def tail(blocks, table, own, other, grad_rows, count, ident):
    parts = count // 4
    _, rows, columns = blocks.shape
    start = grad_rows.shape[0] - own.shape[0]
    vmem = pl.BlockSpec(memory_space=pltpu.VMEM)
    place = pl.BlockSpec(memory_space=pl.ANY)
    return pl.pallas_call(
        functools.partial(tail_kernel, count, start),
        out_shape=(
            jax.ShapeDtypeStruct((rows, columns), F32),
            jax.ShapeDtypeStruct(table.shape, F32),
            jax.ShapeDtypeStruct(grad_rows.shape, F32),
        ),
        in_specs=[vmem, vmem, vmem, vmem, place],
        out_specs=(vmem, vmem, place),
        input_output_aliases={4: 2},
        scratch_shapes=hop_scratch(count, rows, columns)
        + [
            pltpu.VMEM((parts + 2,) + table.shape, F32),
            pltpu.VMEM((3,) + table.shape, F32),
            pltpu.SemaphoreType.DMA((parts + 2,)),
            pltpu.SemaphoreType.DMA((parts + 2,)),
            pltpu.VMEM(other.shape, BF16),
            pltpu.VMEM(own.shape, F32),
            pltpu.SemaphoreType.DMA((PIECES,)),
            pltpu.SemaphoreType.DMA((PIECES,)),
            pltpu.SemaphoreType.DMA((PIECES,)),
        ],
        compiler_params=pltpu.CompilerParams(
            collective_id=ident, has_side_effects=True, vmem_limit_bytes=60 << 20
        ),
        name="tail",
    )(blocks, table, own, other, grad_rows)


def wide_row(table, row, count):
    return jnp.concatenate([table[row + k : row + k + 1, :] for k in range(count)], 1)


def turned(tile, value):
    rows, columns = value.shape
    tile[...] = jnp.zeros_like(tile)
    tile[:rows, :columns] = value
    return jnp.transpose(tile[...])[:columns, :rows]


def final_kernel(
    count, first_ref, second_ref, table_ref,
    q_ref, k_ref, v_ref, qb_ref, vb_ref, depth_ref, p_ref, pb_ref, kw_ref, kb_ref, c_ref, cb_ref, out_ref, ob_ref,
    gain1_ref, bias1_ref, inner_ref, inb_ref, outer_ref, outb_ref, gain2_ref, bias2_ref,
    tile_out, tile_inner, tile_taps, spread,
):
    share, width = q_ref.shape
    share_ffn, group = outer_ref.shape
    q_ref[...] = second_ref[:share, :width]
    k_ref[...] = second_ref[:share, width : 2 * width]
    v_ref[...] = second_ref[share : 2 * share, :width]
    c_ref[...] = second_ref[share : 2 * share, width : 2 * width]
    p_ref[...] = second_ref[2 * share : 3 * share, :width]
    out_ref[0] = turned(tile_out, first_ref[:share, :width])
    out_ref[1] = turned(tile_out, first_ref[:share, width : 2 * width])
    inner_ref[...] = turned(tile_inner, first_ref[share : share + share_ffn, :])
    outer_ref[...] = first_ref[share + share_ffn : share + 2 * share_ffn, :]
    taps = kb_ref.shape[1]
    rows = jnp.transpose(jnp.concatenate([table_ref[:64, :], jnp.zeros((64, WIDE), F32)], 0))
    kw_ref[...] = rows[:width, :taps]
    kb_ref[...] = rows[width : width + 1, :taps]
    qb_ref[...] = table_ref[54:55, :width]
    vb_ref[...] = table_ref[55:56, :width]
    pb_ref[...] = table_ref[56:57, :width]
    cb_ref[...] = table_ref[57:58, :width]
    outb_ref[...] = wide_row(table_ref, 58, 2)[:, :group]
    gain2_ref[...] = wide_row(table_ref, 60, 2)[:, :group]
    bias2_ref[...] = wide_row(table_ref, 62, 2)[:, :group]
    inb_ref[...] = wide_row(table_ref, 64, 6)
    gain1_ref[...] = wide_row(table_ref, 99, 3)
    bias1_ref[...] = wide_row(table_ref, 102, 3)
    ob_ref[...] = wide_row(table_ref, 105, 3)
    spread[...] = jnp.zeros_like(spread)
    for k in range(3):
        spread[:KERNEL, k * WIDE : (k + 1) * WIDE] = table_ref[72 + KERNEL * k : 72 + KERNEL * (k + 1), :]
    model = spread.shape[1]
    dp = lax.axis_index("dp")
    moved = pltpu.roll(spread[...], lax.rem(model - dp * share, model), 1)
    depth_ref[...] = moved[:KERNEL, :share]


def final(first, second, table, share, share_ffn, width, group, taps, count):
    def shape(*sizes):
        return jax.ShapeDtypeStruct(sizes, F32)

    model = 2 * group
    return pl.pallas_call(
        functools.partial(final_kernel, count),
        out_shape=(
            shape(share, width), shape(share, width), shape(share, width), shape(1, width), shape(1, width),
            shape(KERNEL, share), shape(share, width), shape(1, width), shape(width, taps), shape(1, taps),
            shape(share, width), shape(1, width), shape(2, width, share), shape(1, model), shape(1, model),
            shape(1, model), shape(group, share_ffn), shape(1, 4 * group), shape(share_ffn, group), shape(1, group),
            shape(1, group), shape(1, group),
        ),
        in_specs=[whole()] * 3,
        out_specs=(whole(),) * 22,
        scratch_shapes=[
            pltpu.VMEM((WIDE, WIDE), F32),
            pltpu.VMEM((512, 512), F32),
            pltpu.VMEM((LANES, WIDE), F32),
            pltpu.VMEM((TAP_ROWS, model), F32),
        ],
        name="final",
    )(first, second, table)


HEAD_DIM = 64
KERNEL = 9
HALF = KERNEL // 2
EPSILON = 1e-06
MASK_FILL = -1e30
INV_ROOT2 = 0.7071067811865476
INV_ROOT_TWO_PI = 0.3989422804014327
CUTS = 16
TABLE_OWN = 72
TABLE_ROWS = 112
SWAP = [(0, 1), (1, 0)]


class Group:
    def __init__(self, **parts):
        self.__dict__.update(parts)


def nn(left, right):
    return jnp.dot(left, right, preferred_element_type=F32)


def tn(left, right):
    return lax.dot_general(left, right, (((0,), (0,)), ((), ())), preferred_element_type=F32)


def nt(left, right):
    return lax.dot_general(left, right, (((1,), (1,)), ((), ())), preferred_element_type=F32)


def swap(value):
    return lax.ppermute(value, "mp", SWAP)


def shifted(tensor, offset, half_width):
    filler = jnp.zeros((half_width,) + tensor.shape[1:], tensor.dtype)
    padded = jnp.concatenate([filler, tensor, filler], axis=0)
    return padded[half_width + offset : half_width + offset + tensor.shape[0]]


def same_segment(segment, offset, half_width):
    filler = jnp.full((half_width,), -1, dtype=jnp.int32)
    padded = jnp.concatenate([filler, segment, filler])
    return padded[half_width + offset : half_width + offset + segment.shape[0]] == segment


def segment_ids(lengths_row, seq_rows):
    doc_ends = jnp.cumsum(lengths_row)
    positions = jnp.arange(seq_rows, dtype=jnp.int32)
    return jnp.sum((positions[:, None] >= doc_ends[None, :]).astype(jnp.int32), axis=1)


def tap_mask_list(segment):
    return [
        same_segment(segment, tap - HALF, HALF).astype(F32)[:, None] for tap in range(KERNEL)
    ]


def gelu(tensor):
    return 0.5 * tensor * (1.0 + lax.erf(tensor * INV_ROOT2))


def gelu_slope(tensor):
    normal_cdf = 0.5 * (1.0 + lax.erf(tensor * INV_ROOT2))
    return normal_cdf + tensor * jnp.exp(-0.5 * tensor * tensor) * INV_ROOT_TWO_PI


def halves(value, me):
    width = value.shape[1] // 2
    return (
        lax.dynamic_slice_in_dim(value, me * width, width, 1),
        lax.dynamic_slice_in_dim(value, (1 - me) * width, width, 1),
    )


def joined(own, other, me):
    return jnp.where(me == 0, jnp.concatenate([own, other], 1), jnp.concatenate([other, own], 1))


def moments(sum_own, square_own, sum_other, square_other, width):
    mean = (sum_own + sum_other) / (2 * width)
    apart = (sum_own - sum_other) / width
    spread = (square_own + square_other + apart * apart * (width / 2)) / (2 * width)
    return mean, lax.rsqrt(spread + EPSILON)


TAP_ROWS = 16
WIDE = 256
LANES = 128
EDGE = 8


def spread_marks(marks_ref, columns_ref):
    rows = marks_ref.shape[2]
    columns_ref[...] = jnp.transpose(
        jnp.concatenate([marks_ref[0], jnp.zeros((LANES - TAP_ROWS, rows), F32)], 0)
    )


def head_lanes(head):
    lane = lax.broadcasted_iota(jnp.int32, (1, WIDE), 1)
    return jnp.logical_and(lane >= head * HEAD_DIM, lane < (head + 1) * HEAD_DIM)


def only(value, head):
    return jnp.where(head_lanes(head), value.astype(F32), 0.0)


def high_low(weights, heads):
    high = weights.astype(BF16).astype(F32)
    low = weights - high
    rest = jnp.zeros((LANES - 2 * heads * TAP_ROWS, weights.shape[1]), F32)
    return jnp.transpose(jnp.concatenate([high, low, rest], 0)).astype(BF16)


def front_kernel(
    seqs, count,
    hidden_ref, marks_ref, query_ref, key_ref, value_ref, conv_ref, point_ref, taps_ref, vec_ref, depth_ref, bias_ref,
    expand_ref, second_ref,
    q_ref, k_ref, v_ref, cv_ref, dl_ref, kc_ref, ca_ref, probs_ref, cc_ref, ctx_ref, lse_ref, second_all_ref,
    rows_pad, conv_pad, columns, weights, tops, tap_out, tap_in,
    send_sem, recv_sem, own_sem, gather_send, gather_recv,
):
    s = pl.program_id(0)
    mp, core, side, deep, parts = places(count)
    me = index_of(deep, side, core)
    rows, model = hidden_ref.shape
    chunks = model // LANES
    heads = probs_ref.shape[1] // TAP_ROWS
    tap_rows = heads * TAP_ROWS
    beside = index_of(deep, 1 - side, core)
    twin = index_of(deep, side, 1 - core)

    def push(source, block, target, slot):
        return pltpu.make_async_remote_copy(
            src_ref=source,
            dst_ref=second_all_ref.at[block],
            send_sem=gather_send.at[slot],
            recv_sem=gather_recv.at[block],
            device_id=at(target, mp),
            device_id_type=MESH,
        )

    def arrive(block):
        pltpu.make_async_copy(second_ref.at[0], second_all_ref.at[block], gather_recv.at[block]).wait()

    own_copy = pltpu.make_async_copy(second_ref.at[0], second_all_ref.at[me], own_sem)
    first_hops = [
        push(second_ref.at[0], me, index_of(lax.rem(deep + k, parts), side, core), k - 1) for k in range(1, parts)
    ]
    first_hops += [push(second_ref.at[0], me, beside, parts - 1), push(second_ref.at[0], me, twin, parts)]
    second_hops = [(beside, twin, parts + 1)]
    for k in range(1, parts):
        block = index_of(lax.rem(deep + parts - k, parts), side, core)
        second_hops += [(block, beside, parts + 2 * k), (block, twin, parts + 2 * k + 1)]
    third_hops = [
        (index_of(lax.rem(deep + parts - k, parts), 1 - side, core), twin, 3 * parts + k - 1) for k in range(1, parts)
    ]

    @pl.when(s == 0)
    def _():
        barrier = pltpu.get_barrier_semaphore()
        pl.semaphore_signal(barrier, inc=1, device_id=at(me, 1 - mp), device_id_type=MESH)
        peers = [index_of(lax.rem(deep + k, parts), side, core) for k in range(1, parts)] + [beside, twin]
        for peer in peers:
            pl.semaphore_signal(barrier, inc=1, device_id=at(peer, mp), device_id_type=MESH)
        pl.semaphore_wait(barrier, len(peers) + 1)
        own_copy.start()
        for copy in first_hops:
            copy.start()
        rows_pad[:, :EDGE, :] = jnp.zeros((chunks, EDGE, LANES), F32)
        rows_pad[:, pl.ds(EDGE + rows, EDGE), :] = jnp.zeros((chunks, EDGE, LANES), F32)
        conv_pad[:, :EDGE, :] = jnp.zeros((2, EDGE, LANES), F32)
        conv_pad[:, pl.ds(EDGE + rows, EDGE), :] = jnp.zeros((2, EDGE, LANES), F32)

    spread_marks(marks_ref, columns)
    hidden = hidden_ref[...]
    for c in range(chunks):
        rows_pad[c, pl.ds(EDGE, rows), :] = hidden[:, c * LANES : (c + 1) * LANES].astype(F32)

    step = 32

    def depth_step(i, carry):
        base = pl.multiple_of(i * step, step)
        total = [jnp.zeros((step, LANES), F32)] * chunks
        for tap in range(KERNEL):
            mask = jnp.broadcast_to(columns[pl.ds(base, step), tap : tap + 1], (step, LANES))
            for c in range(chunks):
                moved = rows_pad[c, pl.ds(base + EDGE + tap - HALF, step), :]
                total[c] = total[c] + (moved * mask) * depth_ref[tap : tap + 1, c * LANES : (c + 1) * LANES]
        for c in range(chunks):
            dl_ref[pl.ds(base, step), c * LANES : (c + 1) * LANES] = total[c].astype(BF16)
        return carry

    lax.fori_loop(0, rows // step, depth_step, 0)
    queries = (nn(hidden, query_ref[...]) + vec_ref[0:1, :]).astype(BF16)
    q_ref[...] = queries
    key_conv = nn(dl_ref[...], point_ref[...]) + vec_ref[2:3, :]
    kc_ref[...] = key_conv
    conv_attn = (key_conv * queries.astype(F32)).astype(BF16)
    ca_ref[...] = conv_attn
    tap_terms = nt(taps_ref[...], conv_attn)
    slot = lax.rem(s, 2)
    tap_out[slot] = tap_terms[tap_rows : 2 * tap_rows]
    swap_taps = pltpu.make_async_remote_copy(
        src_ref=tap_out.at[slot],
        dst_ref=tap_in.at[slot],
        send_sem=send_sem.at[slot],
        recv_sem=recv_sem.at[slot],
        device_id=at(me, 1 - mp),
        device_id_type=MESH,
    )
    swap_taps.start()
    own_terms = tap_terms[:tap_rows]
    k_ref[...] = nn(hidden, key_ref[...]).astype(BF16)
    v_ref[...] = (nn(hidden, value_ref[...]) + vec_ref[1:2, :]).astype(BF16)
    conv_values = nn(hidden, conv_ref[...]) + vec_ref[3:4, :]
    cv_ref[...] = conv_values
    for c in range(2):
        conv_pad[c, pl.ds(EDGE, rows), :] = conv_values[:, c * LANES : (c + 1) * LANES]

    block = 256
    seg_row = marks_ref[0, KERNEL : KERNEL + 1, :]
    lane = lax.broadcasted_iota(jnp.int32, (block, LANES), 1)

    def attention_step(i, carry):
        part = pl.ds(pl.multiple_of(i * block, block), block)
        allowed = columns[part, KERNEL : KERNEL + 1] == seg_row
        query = q_ref[part, :]
        total = jnp.zeros((block, WIDE), F32)
        packed = jnp.zeros((block, LANES), F32)
        for head in range(heads):
            mine = (only(query, head) * (HEAD_DIM**-0.5)).astype(BF16)
            scores = jnp.where(allowed, nt(mine, k_ref[...]), MASK_FILL)
            top = jnp.max(scores, axis=1, keepdims=True)
            exponent = jnp.exp(scores - top)
            amount = jnp.sum(exponent, axis=1, keepdims=True)
            probs = (exponent * (1.0 / amount)).astype(BF16)
            total = total + nn(probs, only(v_ref[...], head).astype(BF16))
            packed = jnp.where(lane == head, top + jnp.log(amount), packed)
        ctx_ref[part, :] = total.astype(BF16)
        tops[part, :] = packed
        return carry

    lax.fori_loop(0, rows // block, attention_step, 0)
    lse_ref[0] = jnp.transpose(tops[...])[:8]

    swap_taps.wait()
    logits = (own_terms + tap_in[slot] + bias_ref[:, :1]).reshape(heads, TAP_ROWS, rows)
    tap = lax.broadcasted_iota(jnp.int32, (heads, TAP_ROWS, rows), 1)
    logits = jnp.where(tap < KERNEL, logits, MASK_FILL)
    exponent = jnp.exp(logits - jnp.max(logits, axis=1, keepdims=True))
    probs = exponent / jnp.sum(exponent, axis=1, keepdims=True)
    probs_ref[0] = probs.reshape(tap_rows, rows)
    tap_mask = jnp.where(tap[0] < KERNEL, marks_ref[0], 0.0)
    weights[...] = high_low((probs * tap_mask[None]).reshape(tap_rows, rows), heads)
    conv_block = 128

    def conv_step(i, carry):
        base = pl.multiple_of(i * conv_block, conv_block)
        part = pl.ds(base, conv_block)
        scale = nn(weights[part, :], expand_ref[...])
        for c in range(2):
            total = jnp.zeros((conv_block, LANES), F32)
            for tap in range(KERNEL):
                low = tap * WIDE + c * LANES
                moved = conv_pad[c, pl.ds(base + EDGE + tap - HALF, conv_block), :]
                total = total + scale[:, low : low + LANES] * moved
            cc_ref[part, c * LANES : (c + 1) * LANES] = total.astype(BF16)
        return carry

    lax.fori_loop(0, rows // conv_block, conv_step, 0)

    @pl.when(s == 0)
    def _():
        for block, target, place in second_hops:
            if target is twin and place == parts + 1:
                arrive(block)
            elif target is beside:
                arrive(block)
            push(second_all_ref.at[block], block, target, place).start()

    @pl.when(s == min(1, seqs - 1))
    def _():
        for block, target, place in third_hops:
            arrive(block)
            push(second_all_ref.at[block], block, target, place).start()

    @pl.when(s == seqs - 1)
    def _():
        for k in range(parts):
            for other in range(2):
                arrive(index_of(lax.rem(deep + parts - k, parts), other, 1 - core))
        for copy in first_hops:
            copy.wait_send()
        for block, target, place in second_hops + third_hops:
            push(second_all_ref.at[block], block, target, place).wait_send()
        own_copy.wait()


def whole():
    return pl.BlockSpec(memory_space=pltpu.VMEM)


def by_seq(rows, columns):
    return pl.BlockSpec((rows, columns), lambda s: (s, 0))


def by_seq_row(rows, columns):
    return pl.BlockSpec((1, rows, columns), lambda s: (s, 0, 0))


def front(hidden, marks, w, vectors, depth, bias, expand, taps, second, count, ident):
    seqs, _, rows = marks.shape
    tokens, model = hidden.shape
    tap_rows = bias.shape[0]
    parts = count // 4

    def wide(kind):
        return jax.ShapeDtypeStruct((tokens, WIDE), kind)

    return pl.pallas_call(
        functools.partial(front_kernel, seqs, count),
        grid=(seqs,),
        out_shape=(
            wide(BF16), wide(BF16), wide(BF16), wide(F32),
            jax.ShapeDtypeStruct((tokens, model), BF16),
            wide(F32), wide(BF16),
            jax.ShapeDtypeStruct((seqs, tap_rows, rows), F32),
            wide(BF16), wide(BF16),
            jax.ShapeDtypeStruct((seqs, 8, rows), F32),
            jax.ShapeDtypeStruct((count,) + second.shape[1:], BF16),
        ),
        in_specs=[by_seq(rows, model), by_seq_row(TAP_ROWS, rows)] + [whole()] * 10 + [pl.BlockSpec(memory_space=pl.ANY)],
        out_specs=(
            by_seq(rows, WIDE), by_seq(rows, WIDE), by_seq(rows, WIDE), by_seq(rows, WIDE), by_seq(rows, model),
            by_seq(rows, WIDE), by_seq(rows, WIDE), by_seq_row(tap_rows, rows), by_seq(rows, WIDE), by_seq(rows, WIDE),
            by_seq_row(8, rows), pl.BlockSpec(memory_space=pl.ANY),
        ),
        scratch_shapes=[
            pltpu.VMEM((model // LANES, rows + 2 * EDGE, LANES), F32),
            pltpu.VMEM((2, rows + 2 * EDGE, LANES), F32),
            pltpu.VMEM((rows, LANES), F32),
            pltpu.VMEM((rows, LANES), BF16),
            pltpu.VMEM((rows, LANES), F32),
            pltpu.VMEM((2, tap_rows, rows), F32),
            pltpu.VMEM((2, tap_rows, rows), F32),
            pltpu.SemaphoreType.DMA((2,)),
            pltpu.SemaphoreType.DMA((2,)),
            pltpu.SemaphoreType.DMA,
            pltpu.SemaphoreType.DMA((4 * parts - 1,)),
            pltpu.SemaphoreType.DMA((count,)),
        ],
        compiler_params=pltpu.CompilerParams(
            collective_id=ident, has_side_effects=True, vmem_limit_bytes=60 << 20
        ),
        name="front",
    )(
        hidden, marks, w.query, w.key, w.value, w.conv, w.point, taps, vectors, depth, bias, expand, second,
    )


def transposed_stats(columns):
    rows = columns[0].shape[0]
    lane = lax.broadcasted_iota(jnp.int32, (rows, 128), 1)
    packed = jnp.zeros((rows, 128), F32)
    for place, column in enumerate(columns):
        packed = jnp.where(lane == place, column, packed)
    return jnp.transpose(packed)[:8]


def stat_columns(message, amount):
    rows = message.shape[1]
    wide = jnp.concatenate([message, jnp.zeros((120, rows), F32)], 0)
    tall = jnp.transpose(wide)
    return [tall[:, k : k + 1] for k in range(amount)]


def row_sums(value):
    rows, columns = value.shape
    return jnp.sum(value.reshape(rows // 8, 8, columns), axis=0)


SLOTS = 4
FFN_STEP = 256


def middle_kernel(
    blocks,
    context_ref, conv_ref, context_late_ref, conv_late_ref, hidden_ref, grad_ref, grad_late_ref, out0_ref, out1_ref, inner_ref, outer_ref, vec_ref,
    output_ref, residual_ref, grad_context_ref, grad_conv_ref, pack_ref, small_ref,
    branch_ref, acc_out0, acc_out1, state, scale_ring, act_ring, slope_ring, low_ring, summed_ring, normed_ring, stat_ring,
    acc_inner, acc_outer, acc_small, acc_bias,
    branch_out, branch_in, stat1_out, stat1_in, stat2_out, stat2_in, stat3_out, stat3_in, back_out, back_in,
    send_sem, recv_sem,
):
    i = pl.program_id(0)
    me = lax.axis_index("mp")
    dp = lax.axis_index("dp")
    width = summed_ring.shape[2]
    hidden_units = inner_ref.shape[0]
    inverse = 1.0 / (2 * width)

    def message(kind, source, target, slot):
        return pltpu.make_async_remote_copy(
            src_ref=source.at[slot],
            dst_ref=target.at[slot],
            send_sem=send_sem.at[kind, slot],
            recv_sem=recv_sem.at[kind, slot],
            device_id=(dp, 1 - me),
            device_id_type=MESH,
        )

    kinds = [
        (branch_out, branch_in), (stat1_out, stat1_in), (stat2_out, stat2_in), (stat3_out, stat3_in), (back_out, back_in),
    ]

    def fresh(kind, b, slot):
        @pl.when(b >= SLOTS)
        def _():
            message(kind, *kinds[kind], slot).wait_send()

    def vec(row):
        return vec_ref[row : row + 1, :width]

    @pl.when(i == 0)
    def _():
        barrier = pltpu.get_barrier_semaphore()
        pl.semaphore_signal(barrier, inc=1, device_id=(dp, 1 - me), device_id_type=MESH)
        pl.semaphore_wait(barrier, 1)
        acc_inner[...] = jnp.zeros_like(acc_inner)
        acc_outer[...] = jnp.zeros_like(acc_outer)
        acc_out0[...] = jnp.zeros_like(acc_out0)
        acc_out1[...] = jnp.zeros_like(acc_out1)
        acc_small[...] = jnp.zeros_like(acc_small)
        acc_bias[...] = jnp.zeros_like(acc_bias)

    @pl.when(i < blocks)
    def _():
        b = i
        slot = lax.rem(b, SLOTS)
        fresh(0, b, slot)
        theirs = pl.ds(pl.multiple_of((1 - me) * width, width), width)
        ours = pl.ds(pl.multiple_of(me * width, width), width)
        other = nt(context_ref[...], out0_ref[theirs, :]) + nt(conv_ref[...], out1_ref[theirs, :])
        branch_out[slot] = other.astype(BF16)
        message(0, *kinds[0], slot).start()
        own = nt(context_ref[...], out0_ref[ours, :]) + nt(conv_ref[...], out1_ref[ours, :])
        state[lax.rem(b, 8)] = hidden_ref[:, ours].astype(F32) + (own + vec(0))

    @pl.when(jnp.logical_and(i >= 1, i < blocks + 1))
    def _():
        b = i - 1
        slot = lax.rem(b, SLOTS)
        message(0, *kinds[0], slot).wait_recv()
        fresh(1, b, slot)
        residual = state[lax.rem(b, 8)] + branch_in[slot].astype(F32)
        state[lax.rem(b, 8)] = residual
        total = jnp.sum(residual, axis=1, keepdims=True)
        apart = residual - total * (1.0 / width)
        stat1_out[slot] = transposed_stats([total, jnp.sum(apart * apart, axis=1, keepdims=True)])
        message(1, *kinds[1], slot).start()

    @pl.when(jnp.logical_and(i >= 2, i < blocks + 2))
    def _():
        b = i - 2
        slot = lax.rem(b, SLOTS)
        two = lax.rem(b, 2)
        message(1, *kinds[1], slot).wait_recv()
        fresh(2, b, slot)
        total, square = stat_columns(stat1_out[slot], 2)
        total_o, square_o = stat_columns(stat1_in[slot], 2)
        mean, scale = moments(total, square, total_o, square_o, width)
        standard = (state[lax.rem(b, 8)] - mean) * scale
        state[lax.rem(b, 8)] = standard
        scale_ring[lax.rem(b, 4)] = jnp.broadcast_to(scale, scale_ring.shape[1:])
        normed = standard * vec(1) + vec(2)
        low = normed.astype(BF16)
        low_ring[two] = low
        summed = normed + vec(3)
        for start in range(0, hidden_units, FFN_STEP):
            part = pl.ds(start, FFN_STEP)
            inner = nt(low, inner_ref[part, :]) + vec_ref[7:8, start : start + FFN_STEP]
            cdf = 0.5 * (1.0 + lax.erf(inner * INV_ROOT2))
            act = (inner * cdf).astype(BF16)
            act_ring[two, :, part] = act
            slope_ring[two, :, part] = cdf + inner * jnp.exp(-0.5 * inner * inner) * INV_ROOT_TWO_PI
            summed = summed + nn(act, outer_ref[part, :])
        summed_ring[two] = summed
        scaled = grad_ref[...].astype(F32) * vec(4)
        total = jnp.sum(summed, axis=1, keepdims=True)
        apart = summed - total * (1.0 / width)
        stat2_out[slot] = transposed_stats(
            [
                total,
                jnp.sum(apart * apart, axis=1, keepdims=True),
                jnp.sum(scaled, axis=1, keepdims=True),
                jnp.sum(scaled * apart, axis=1, keepdims=True),
            ]
        )
        message(2, *kinds[2], slot).start()

    @pl.when(jnp.logical_and(i >= 3, i < blocks + 3))
    def _():
        b = i - 3
        slot = lax.rem(b, SLOTS)
        two = lax.rem(b, 2)
        message(2, *kinds[2], slot).wait_recv()
        fresh(3, b, slot)
        total, square, grads, cross = stat_columns(stat2_out[slot], 4)
        total_o, square_o, grads_o, cross_o = stat_columns(stat2_in[slot], 4)
        mean, scale = moments(total, square, total_o, square_o, width)
        mean_grad = (grads + grads_o) * inverse
        product = cross + cross_o + (total * (1.0 / width) - mean) * grads + (total_o * (1.0 / width) - mean) * grads_o
        mean_product = product * scale * inverse
        standard = (summed_ring[two] - mean) * scale
        output_ref[...] = (standard * vec(4) + vec(5)).astype(BF16)
        gradient = grad_late_ref[...].astype(F32)
        grad_summed = scale * (gradient * vec(4) - mean_grad - standard * mean_product)
        low = grad_summed.astype(BF16)
        acc_small[0] += row_sums(low.astype(F32))
        acc_small[1] += row_sums(gradient * standard)
        acc_small[2] += row_sums(gradient)
        normed_low = low_ring[two]
        grad_normed = grad_summed
        for start in range(0, hidden_units, FFN_STEP):
            part = pl.ds(start, FFN_STEP)
            grad_inner = nt(low, outer_ref[part, :]) * slope_ring[two, :, part]
            inner_low = grad_inner.astype(BF16)
            acc_bias[:, part] += row_sums(inner_low.astype(F32))
            grad_normed = grad_normed + nn(inner_low, inner_ref[part, :])
            acc_outer[part, :] += tn(act_ring[two, :, part], low)
            acc_inner[part, :] += tn(inner_low, normed_low)
        normed_ring[two] = grad_normed
        standard1 = state[lax.rem(b, 8)]
        scaled = grad_normed * vec(1)
        acc_small[3] += row_sums(grad_normed * standard1)
        acc_small[4] += row_sums(grad_normed)
        sums = transposed_stats(
            [jnp.sum(scaled, axis=1, keepdims=True), jnp.sum(scaled * standard1, axis=1, keepdims=True)]
        )
        stat3_out[slot] = sums
        message(3, *kinds[3], slot).start()

    @pl.when(jnp.logical_and(i >= 4, i < blocks + 4))
    def _():
        b = i - 4
        slot = lax.rem(b, SLOTS)
        message(3, *kinds[3], slot).wait_recv()
        fresh(4, b, slot)
        first, second = stat_columns(stat3_out[slot] + stat3_in[slot], 2)
        standard = state[lax.rem(b, 8)]
        scaled = normed_ring[lax.rem(b, 2)] * vec(1)
        residual = scale_ring[lax.rem(b, 4)][:, :1] * (scaled - first * inverse - standard * (second * inverse))
        residual_ref[...] = residual
        low = residual.astype(BF16)
        acc_small[5] += row_sums(low.astype(F32))
        back_out[slot] = low
        message(4, *kinds[4], slot).start()

    @pl.when(i >= 5)
    def _():
        b = i - 5
        slot = lax.rem(b, SLOTS)
        message(4, *kinds[4], slot).wait_recv()
        theirs = pl.ds(pl.multiple_of((1 - me) * width, width), width)
        ours = pl.ds(pl.multiple_of(me * width, width), width)
        branch_ref[:, ours] = back_out[slot]
        branch_ref[:, theirs] = back_in[slot]
        branch = branch_ref[...]
        grad_context_ref[...] = nn(branch, out0_ref[...]).astype(BF16)
        grad_conv_ref[...] = nn(branch, out1_ref[...]).astype(BF16)
        acc_out0[...] += tn(branch, context_late_ref[...])
        acc_out1[...] += tn(branch, conv_late_ref[...])

    @pl.when(i == blocks + 4)
    def _():
        for kind in range(5):
            for slot in range(SLOTS):
                message(kind, *kinds[kind], slot).wait_send()
        cut, cut_ffn = 2 * width // CUTS, hidden_units // CUTS
        for k in range(CUTS):
            part, part_ffn = pl.ds(k * cut, cut), pl.ds(k * cut_ffn, cut_ffn)
            both = jnp.concatenate([acc_out0[part, : width // 2], acc_out1[part, : width // 2]], 1)
            pack_ref[k, pl.ds(0, cut), :] = both.astype(BF16)
            pack_ref[k, pl.ds(cut, cut_ffn), :] = acc_inner[part_ffn, :].astype(BF16)
            pack_ref[k, pl.ds(cut + cut_ffn, cut_ffn), :] = acc_outer[part_ffn, :].astype(BF16)
        small_ref[...] = jnp.zeros_like(small_ref)
        for row in range(6):
            small_ref[row : row + 1, :width] = jnp.sum(acc_small[row], axis=0, keepdims=True)
        small_ref[6:7, :] = jnp.sum(acc_bias[...], axis=0, keepdims=True)


def middle(context, conv_context, hidden, out_grad, w, p, me, ident):
    tokens, model = hidden.shape
    width = model // 2
    local = context.shape[1]
    units = w.inner.shape[0]
    rows = 256
    blocks = tokens // rows

    def mine(value):
        return lax.dynamic_slice_in_dim(value, me * width, width, 0)

    vectors = [
        mine(p.out_bias), mine(p.norm1_gain), mine(p.norm1_bias), p.ffn_out_bias, p.norm2_gain, p.norm2_bias,
    ]
    table = jnp.stack([jnp.pad(v, (0, units - width)) for v in vectors] + [jnp.zeros((units,), F32), p.ffn_in_bias])

    def block(columns, lag):
        return pl.BlockSpec((rows, columns), lambda i: (jnp.clip(i - lag, 0, blocks - 1), 0))

    whole = pl.BlockSpec(memory_space=pltpu.VMEM)
    stat = pltpu.VMEM((SLOTS, 8, rows), F32)
    half = pltpu.VMEM((SLOTS, rows, width), BF16)
    return pl.pallas_call(
        functools.partial(middle_kernel, blocks),
        grid=(blocks + 5,),
        out_shape=(
            jax.ShapeDtypeStruct((tokens, width), BF16),
            jax.ShapeDtypeStruct((tokens, width), F32),
            jax.ShapeDtypeStruct((tokens, local), BF16),
            jax.ShapeDtypeStruct((tokens, local), BF16),
            jax.ShapeDtypeStruct((CUTS, (model + 2 * units) // CUTS, width), BF16),
            jax.ShapeDtypeStruct((8, units), F32),
        ),
        in_specs=[
            block(local, 0), block(local, 0), block(local, 5), block(local, 5), block(model, 0), block(width, 2),
            block(width, 3),
            whole, whole, whole, whole, whole,
        ],
        out_specs=(block(width, 3), block(width, 4), block(local, 5), block(local, 5), whole, whole),
        scratch_shapes=[
            pltpu.VMEM((rows, model), BF16),
            pltpu.VMEM((model, local), F32),
            pltpu.VMEM((model, local), F32),
            pltpu.VMEM((8, rows, width), F32),
            pltpu.VMEM((4, rows, 128), F32),
            pltpu.VMEM((2, rows, units), BF16),
            pltpu.VMEM((2, rows, units), F32),
            pltpu.VMEM((2, rows, width), BF16),
            pltpu.VMEM((2, rows, width), F32),
            pltpu.VMEM((2, rows, width), F32),
            pltpu.VMEM((8, 128), F32),
            pltpu.VMEM((units, width), F32),
            pltpu.VMEM((units, width), F32),
            pltpu.VMEM((6, 8, width), F32),
            pltpu.VMEM((8, units), F32),
            half, half, stat, stat, stat, stat, stat, stat, half, half,
            pltpu.SemaphoreType.DMA((5, SLOTS)),
            pltpu.SemaphoreType.DMA((5, SLOTS)),
        ],
        compiler_params=pltpu.CompilerParams(
            collective_id=ident, has_side_effects=True, vmem_limit_bytes=60 << 20
        ),
        name="middle",
    )(context, conv_context, context, conv_context, hidden, out_grad, out_grad, w.out0, w.out1, w.inner, w.outer, table)


def back_kernel(
    seqs, count,
    grad_context, grad_conv_ref, marks_ref, q_ref, k_ref, v_ref, cv_ref, ca_ref, probs_ref, lse_ref,
    hidden_any, residual_any, dl_any, kc_any,
    inputs_ref, point_ref, taps_ref, depth_ref, expand_ref, small_ref, pack_in_ref,
    grad_ref, own_ref, other_ref, pack_ref, table_ref, reduced_ref,
    hidden_ref, residual_ref, dl_ref, kc_ref, load_sem,
    other_out, other_in, other_send, other_recv,
    twin_in, side_in, deep_in, hop_send, hop_recv,
    depth_pad, conv_pad, grad_pad, columns, weights, shifted_weights, tap_terms, products,
    grads, grad_q, grad_k, grad_v, rows_total, tap_all,
    acc_in, acc_point, acc_bias, acc_tap, acc_tap_bias, acc_depth,
    tap_out, tap_in, send_sem, recv_sem,
):
    s = pl.program_id(0)
    mp = lax.axis_index("mp")
    dp = lax.axis_index("dp")
    rows, model = hidden_ref.shape
    chunks = model // LANES
    heads = probs_ref.shape[1] // TAP_ROWS
    tap_rows = heads * TAP_ROWS
    half = chunks // 2
    slot = lax.rem(s, 2)
    hops = Hops(count, pack_in_ref, twin_in, side_in, deep_in, hop_send, hop_recv)
    here_rows = pl.ds(pl.multiple_of(s * rows, rows), rows)
    loads = [
        pltpu.make_async_copy(source.at[here_rows], target, load_sem.at[k])
        for k, (source, target) in enumerate(
            [(hidden_any, hidden_ref), (residual_any, residual_ref), (dl_any, dl_ref), (kc_any, kc_ref)]
        )
    ]
    for load in loads:
        load.start()

    def swap_rows(which):
        return pltpu.make_async_remote_copy(
            src_ref=other_out.at[which],
            dst_ref=other_in.at[which],
            send_sem=other_send.at[which],
            recv_sem=other_recv.at[which],
            device_id=(dp, 1 - mp),
            device_id_type=MESH,
        )

    @pl.when(s == 0)
    def _():
        greet_all(count)
        hops.start_first()
        for pad in (depth_pad, conv_pad, grad_pad):
            for start in (0, EDGE + rows):
                pad[:, pl.ds(start, EDGE), :] = jnp.zeros((pad.shape[0], EDGE, LANES), F32)
        for acc in (acc_in, acc_point, acc_bias, acc_tap, acc_tap_bias, acc_depth):
            acc[...] = jnp.zeros_like(acc)

    spread_marks(marks_ref, columns)
    block = 256

    for c in range(2):
        lanes = slice(c * LANES, (c + 1) * LANES)
        grad_pad[c, pl.ds(EDGE, rows), :] = grad_conv_ref[:, lanes].astype(F32)
        conv_pad[c, pl.ds(EDGE, rows), :] = cv_ref[:, lanes]

    probs = probs_ref[0].reshape(heads, TAP_ROWS, rows)
    tap = lax.broadcasted_iota(jnp.int32, (heads, TAP_ROWS, rows), 1)
    tap_mask = jnp.where(tap < KERNEL, jnp.broadcast_to(marks_ref[...], (heads, TAP_ROWS, rows)), 0.0)
    masked = (probs * tap_mask).reshape(tap_rows, rows)
    flat_tap = tap.reshape(tap_rows, rows)
    moved = jnp.zeros_like(masked)
    for j in range(KERNEL):
        turn = (j - HALF) % rows
        turned = pltpu.roll(masked, turn, 1) if turn else masked
        moved = jnp.where(flat_tap == j, turned, moved)
    shifted_weights[...] = high_low(moved, heads)
    conv_block = 128

    def conv_step(i, carry):
        base = pl.multiple_of(i * conv_block, conv_block)
        part = pl.ds(base, conv_block)
        scale = nn(shifted_weights[part, :], expand_ref[...])
        for c in range(2):
            here = grad_pad[c, pl.ds(base + EDGE, conv_block), :]
            total = jnp.zeros((conv_block, LANES), F32)
            for j in range(KERNEL):
                low = j * WIDE + c * LANES
                products[:, low : low + LANES] = (
                    here * conv_pad[c, pl.ds(base + EDGE + j - HALF, conv_block), :]
                ).astype(BF16)
                total = total + scale[:, low : low + LANES] * grad_pad[
                    c, pl.ds(base + EDGE + HALF - j, conv_block), :
                ]
            grads[part, 3 * WIDE + c * LANES : 3 * WIDE + (c + 1) * LANES] = total.astype(BF16)
        tap_terms[part, :] = nt(products[...], expand_ref[...])
        return carry

    lax.fori_loop(0, rows // conv_block, conv_step, 0)
    grad_taps = jnp.transpose(tap_terms[...])[:tap_rows].reshape(heads, TAP_ROWS, rows) * tap_mask
    grad_logits = probs * (grad_taps - jnp.sum(probs * grad_taps, axis=1, keepdims=True))
    grad_logits = grad_logits.reshape(tap_rows, rows).astype(BF16)
    tap_out[slot] = grad_logits
    swap_taps = pltpu.make_async_remote_copy(
        src_ref=tap_out.at[slot],
        dst_ref=tap_in.at[slot],
        send_sem=send_sem.at[slot],
        recv_sem=recv_sem.at[slot],
        device_id=(dp, 1 - mp),
        device_id_type=MESH,
    )
    swap_taps.start()

    grad_k[...] = jnp.zeros_like(grad_k)
    grad_v[...] = jnp.zeros_like(grad_v)

    def attention_step(i, carry):
        part = pl.ds(pl.multiple_of(i * block, block), block)
        allowed = columns[:, KERNEL : KERNEL + 1] == marks_ref[0, KERNEL : KERNEL + 1, part]
        query = q_ref[part, :]
        context = grad_context[part, :]
        total = jnp.zeros((block, WIDE), F32)
        for head in range(heads):
            mine = (only(query, head) * (HEAD_DIM**-0.5)).astype(BF16)
            grad_mine = only(context, head).astype(BF16)
            scores = jnp.where(allowed, nt(k_ref[...], mine), MASK_FILL)
            probs = jnp.exp(scores - lse_ref[0, head : head + 1, part])
            grad_v[...] += nn(probs.astype(BF16), grad_mine)
            grad_probs = nt(v_ref[...], grad_mine)
            mixed = probs * grad_probs
            grad_scores = (mixed - probs * jnp.sum(mixed, axis=0, keepdims=True)).astype(BF16)
            grad_k[...] += nn(grad_scores, mine)
            total = total + tn(grad_scores, only(k_ref[...], head).astype(BF16))
        grad_q[part, :] = total
        return carry

    lax.fori_loop(0, rows // block, attention_step, 0)

    for load in loads:
        load.wait()
    swap_taps.wait()
    tap_all[...] = jnp.zeros_like(tap_all)
    tap_all[:tap_rows, :] = tap_out[slot].astype(F32)
    tap_all[tap_rows : 2 * tap_rows, :] = tap_in[slot].astype(F32)
    every = tap_all[...]
    acc_tap[...] += nn(every.astype(BF16), ca_ref[...])
    acc_tap_bias[...] += sum(every[:, c * LANES : (c + 1) * LANES] for c in range(rows // LANES))
    weights[...] = jnp.transpose(every).astype(BF16)

    def key_step(i, carry):
        base = pl.multiple_of(i * block, block)
        part = pl.ds(base, block)
        grad_attn = nn(weights[part, :], taps_ref[...]).astype(BF16).astype(F32)
        query = q_ref[part, :].astype(F32)
        key_low = (grad_attn * query).astype(BF16)
        grads[part, 4 * WIDE : 5 * WIDE] = key_low
        grad_query = grad_q[part, :] * (HEAD_DIM**-0.5) + grad_attn * kc_ref[part, :]
        grads[part, :WIDE] = grad_query.astype(BF16)
        grads[part, WIDE : 2 * WIDE] = grad_k[part, :].astype(BF16)
        grads[part, 2 * WIDE : 3 * WIDE] = grad_v[part, :].astype(BF16)
        acc_bias[...] += row_sums(grads[part, :].astype(F32))
        grad_depth = nt(key_low, point_ref[...])
        total = nt(grads[part, : 4 * WIDE], inputs_ref[...])
        for c in range(chunks):
            lanes = slice(c * LANES, (c + 1) * LANES)
            depth_pad[c, pl.ds(base + EDGE, block), :] = grad_depth[:, lanes]
            rows_total[c, part, :] = total[:, lanes]
        return carry

    lax.fori_loop(0, rows // block, key_step, 0)
    acc_point[...] += tn(dl_ref[...], grads[:, 4 * WIDE : 5 * WIDE])
    acc_in[...] += tn(hidden_ref[...], grads[:, : 4 * WIDE])
    step = 32

    def depth_step(i, carry):
        base = pl.multiple_of(i * step, step)
        part = pl.ds(base, step)
        total = [rows_total[c, part, :] for c in range(chunks)]
        for j in range(KERNEL):
            mirror = KERNEL - 1 - j
            mask = jnp.broadcast_to(columns[part, j : j + 1], (step, LANES))
            for c in range(chunks):
                lanes = slice(c * LANES, (c + 1) * LANES)
                near = depth_pad[c, pl.ds(base + EDGE + j - HALF, step), :] * mask
                total[c] = total[c] + near * depth_ref[mirror : mirror + 1, lanes]
                acc_depth[mirror, :, lanes] += row_sums(near * hidden_ref[part, lanes].astype(F32))
        for c in range(chunks):
            rows_total[c, part, :] = total[c]
        return carry

    lax.fori_loop(0, rows // step, depth_step, 0)

    @pl.when(s >= 1)
    def _():
        which = s - 1
        swap_rows(which).wait_recv()
        grad_ref[...] = own_ref[...] + other_in[which].astype(F32)

    for c in range(half):
        lanes = slice(c * LANES, (c + 1) * LANES)
        own_ref[:, lanes] = rows_total[mp * half + c] + residual_ref[:, lanes]

    @pl.when(s < seqs - 1)
    def _():
        for c in range(half):
            lanes = slice(c * LANES, (c + 1) * LANES)
            other_out[s, :, lanes] = rows_total[(1 - mp) * half + c].astype(BF16)
        swap_rows(s).start()

    @pl.when(s == 0)
    def _():
        hops.start_second()

    @pl.when(s == min(1, seqs - 1))
    def _():
        hops.start_third()

    @pl.when(s == seqs - 1)
    def _():
        for c in range(half):
            lanes = slice(c * LANES, (c + 1) * LANES)
            other_ref[:, lanes] = rows_total[(1 - mp) * half + c].astype(BF16)
        hops.finish(reduced_ref)
        for which in range(seqs - 1):
            swap_rows(which).wait_send()
        width = heads * HEAD_DIM
        group = model // 2
        cut = model // CUTS
        empty = jnp.zeros((cut, width), F32)
        for k in range(CUTS):
            part = pl.ds(k * cut, cut)
            for place in range(2):
                first = acc_in[part, 2 * place * WIDE : 2 * place * WIDE + width]
                second = acc_in[part, (2 * place + 1) * WIDE : (2 * place + 1) * WIDE + width]
                pack_ref[k, pl.ds(place * cut, cut), :] = jnp.concatenate([first, second], 1).astype(BF16)
            pack_ref[k, pl.ds(2 * cut, cut), :] = jnp.concatenate([acc_point[part, :width], empty], 1).astype(BF16)
        table_ref[...] = jnp.zeros_like(table_ref)
        lane = lax.broadcasted_iota(jnp.int32, (LANES, WIDE), 1)
        taps = jnp.where(lane == width, jnp.sum(acc_tap_bias[...], axis=1, keepdims=True), acc_tap[...])
        own_taps = [taps[h * TAP_ROWS : h * TAP_ROWS + KERNEL] for h in range(heads)]
        other_taps = [taps[tap_rows + h * TAP_ROWS : tap_rows + h * TAP_ROWS + KERNEL] for h in range(heads)]
        for h in range(heads):
            table_ref[KERNEL * h : KERNEL * (h + 1), :] = jnp.where(mp == 0, own_taps[h], other_taps[h])
            later = KERNEL * (heads + h)
            table_ref[later : later + KERNEL, :] = jnp.where(mp == 0, other_taps[h], own_taps[h])
        for row, place in ((54, 0), (55, 2), (56, 4), (57, 3)):
            table_ref[row : row + 1, :] = jnp.sum(acc_bias[:, place * WIDE : (place + 1) * WIDE], axis=0, keepdims=True)

        def lay(row, value):
            for k in range(-(-value.shape[1] // WIDE)):
                piece = value[:, k * WIDE : (k + 1) * WIDE]
                table_ref[row + k : row + k + 1, : piece.shape[1]] = piece

        for row, source in ((58, 0), (60, 1), (62, 2)):
            lay(row, small_ref[source : source + 1, :group])
        lay(64, small_ref[6:7, :])
        for row, source in ((99, 3), (102, 4), (105, 5)):
            value = small_ref[source : source + 1, :group]
            blank = jnp.zeros_like(value)
            lay(row, jnp.where(mp == 0, jnp.concatenate([value, blank], 1), jnp.concatenate([blank, value], 1)))
        for j in range(KERNEL):
            total = jnp.sum(acc_depth[j], axis=0, keepdims=True)
            for k in range(model // WIDE):
                row = TABLE_OWN + KERNEL * k + j
                table_ref[row : row + 1, :] = total[:, k * WIDE : (k + 1) * WIDE]


def back(hidden, grad_context, grad_conv, residual, marks, kept, w, taps, depth, expand, small, pack, count, ident):
    q, k, v, cv, dl, kc, ca, probs, lse = kept
    seqs, _, rows = marks.shape
    tokens, model = hidden.shape
    width = model // 2
    tap_rows = probs.shape[1]
    wide = by_seq(rows, WIDE)
    place = pl.BlockSpec(memory_space=pl.ANY)
    padded_rows = rows + 2 * EDGE
    vmem = pltpu.VMEM
    swaps = max(seqs - 1, 1)
    return pl.pallas_call(
        functools.partial(back_kernel, seqs, count),
        grid=(seqs,),
        out_shape=(
            jax.ShapeDtypeStruct((tokens, width), F32),
            jax.ShapeDtypeStruct((rows, width), F32),
            jax.ShapeDtypeStruct((rows, width), BF16),
            jax.ShapeDtypeStruct((CUTS, 3 * model // CUTS, width), BF16),
            jax.ShapeDtypeStruct((TABLE_ROWS, WIDE), F32),
            jax.ShapeDtypeStruct(pack.shape[1:], F32),
        ),
        in_specs=[wide, wide, by_seq_row(TAP_ROWS, rows), wide, wide, wide, wide, wide]
        + [by_seq_row(tap_rows, rows), by_seq_row(8, rows)]
        + [place] * 4
        + [whole()] * 7,
        out_specs=(pl.BlockSpec((rows, width), lambda s: (jnp.maximum(s - 1, 0), 0)),) + (whole(),) * 5,
        scratch_shapes=[
            vmem((rows, model), BF16),
            vmem((rows, width), F32),
            vmem((rows, model), BF16),
            vmem((rows, WIDE), F32),
            pltpu.SemaphoreType.DMA((4,)),
            vmem((swaps, rows, width), BF16),
            vmem((swaps, rows, width), BF16),
            pltpu.SemaphoreType.DMA((swaps,)),
            pltpu.SemaphoreType.DMA((swaps,)),
        ]
        + hop_scratch(count, pack.shape[1], pack.shape[2])
        + [
            vmem((model // LANES, padded_rows, LANES), F32),
            vmem((2, padded_rows, LANES), F32),
            vmem((2, padded_rows, LANES), F32),
            vmem((rows, LANES), F32),
            vmem((rows, LANES), BF16),
            vmem((rows, LANES), BF16),
            vmem((rows, LANES), F32),
            vmem((128, KERNEL * WIDE), BF16),
            vmem((rows, 5 * WIDE), BF16),
            vmem((rows, WIDE), F32),
            vmem((rows, WIDE), F32),
            vmem((rows, WIDE), F32),
            vmem((model // LANES, rows, LANES), F32),
            vmem((LANES, rows), F32),
            vmem((model, 4 * WIDE), F32),
            vmem((model, WIDE), F32),
            vmem((8, 5 * WIDE), F32),
            vmem((LANES, WIDE), F32),
            vmem((LANES, LANES), F32),
            vmem((TAP_ROWS, 8, model), F32),
            vmem((2, tap_rows, rows), BF16),
            vmem((2, tap_rows, rows), BF16),
            pltpu.SemaphoreType.DMA((2,)),
            pltpu.SemaphoreType.DMA((2,)),
        ],
        compiler_params=pltpu.CompilerParams(
            collective_id=ident, has_side_effects=True, vmem_limit_bytes=63 << 20
        ),
        name="back",
    )(
        grad_context, grad_conv, marks, q, k, v, cv, ca, probs, lse, hidden, residual, dl, kc,
        jnp.concatenate([w.query, w.key, w.value, w.conv], 1), w.point, taps, depth, expand, small, pack,
    )


def marks_of(segment):
    masks = [same_segment(segment, tap - HALF, HALF) for tap in range(KERNEL)]
    blank = jnp.zeros_like(segment)
    return jnp.stack([m.astype(F32) for m in masks] + [segment.astype(F32)] + [blank.astype(F32)] * (TAP_ROWS - KERNEL - 1))


def expansion(heads):
    row = lax.broadcasted_iota(jnp.int32, (LANES, KERNEL * WIDE), 0)
    column = lax.broadcasted_iota(jnp.int32, (LANES, KERNEL * WIDE), 1)
    tap, lane = column // WIDE, column % WIDE
    wanted = (lane // HEAD_DIM) * TAP_ROWS + tap
    inside = jnp.logical_and(lane < heads * HEAD_DIM, row < 2 * heads * TAP_ROWS)
    return jnp.logical_and(inside, row % (heads * TAP_ROWS) == wanted).astype(BF16)


def padded(value, multiple):
    rows = value.shape[-2]
    extra = -rows % multiple
    return jnp.pad(value, [(0, 0)] * (value.ndim - 2) + [(0, extra), (0, 0)])


def recut(pack, sizes, count):
    if count == CUTS:
        return pack
    unit, parts, start = pack.shape[1] // sum(sizes), [], 0
    for size in sizes:
        rows = pack[:, start : start + size * unit].reshape(-1, pack.shape[2])
        parts.append(rows.reshape(count, -1, pack.shape[2]))
        start += size * unit
    return padded(jnp.concatenate(parts, 1), 16)


def final_plain(first, second, table, share, share_ffn, width, group, taps):
    model = 2 * group
    depth = jnp.concatenate([table[72 + KERNEL * k : 72 + KERNEL * (k + 1)] for k in range(model // WIDE)], 1)
    row = lambda at_row, size: table[at_row : at_row + 6].reshape(1, -1)[:, :size]
    out = first[:share]
    return (
        second[:share, :width], second[:share, width:], second[share : 2 * share, :width],
        row(54, width), row(55, width),
        lax.dynamic_slice_in_dim(depth, lax.axis_index("dp") * share, share, 1),
        second[2 * share : 3 * share, :width], row(56, width),
        table[:taps, :width].T, table[None, :taps, width], second[share : 2 * share, width:], row(57, width),
        jnp.stack([out[:, :width].T, out[:, width:].T]), row(105, model), row(99, model), row(102, model),
        first[share : share + share_ffn].T, row(64, 4 * group), first[share + share_ffn : share + 2 * share_ffn],
        row(58, group), row(60, group), row(62, group),
    )


def on_device(
    count,
    hidden, doc_lengths, query_weight, key_weight, value_weight, query_bias, value_bias,
    depth_weight, point_weight, point_bias, kernel_weight, kernel_bias, conv_weight, conv_bias,
    out_weight, out_bias, norm1_gain, norm1_bias, ffn_in_weight, ffn_in_bias, ffn_out_weight,
    ffn_out_bias, norm2_gain, norm2_bias, out_grad,
):
    me = lax.axis_index("mp")
    share, width = query_weight.shape
    model = hidden.shape[1]
    group = ffn_out_bias.shape[0]
    share_ffn = ffn_out_weight.shape[1]
    depth_wide = jnp.pad(depth_weight.T, ((0, 0), (0, width - KERNEL)))
    first = jnp.concatenate(
        [
            jnp.concatenate([query_weight, key_weight], 1),
            jnp.concatenate([value_weight, conv_weight], 1),
            jnp.concatenate([point_weight, depth_wide], 1),
        ],
        0,
    )
    out_cut = jnp.concatenate([out_weight[0].T, out_weight[1].T], 1)
    second = jnp.concatenate([out_cut, ffn_in_weight[0].T, ffn_out_weight[0]], 0)
    first_all = gather(padded(first, 16)[None], count, 1)

    def cut(source, start, size, low, high):
        return source[:, start : start + size, low:high].reshape(count * size, high - low)

    def cut_wide(source, start, low):
        return jnp.pad(cut(source, start, share, low, low + width), ((0, 0), (0, WIDE - width)))

    w = Group(
        query=cut_wide(first_all, 0, 0),
        key=cut_wide(first_all, 0, width),
        value=cut_wide(first_all, share, 0),
        conv=cut_wide(first_all, share, width),
        point=cut_wide(first_all, 2 * share, 0),
        depth=cut(first_all, 2 * share, share, width, width + TAP_ROWS).T,
    )
    p = Group(
        query_bias=query_bias, value_bias=value_bias, point_bias=point_bias, kernel_weight=kernel_weight,
        kernel_bias=kernel_bias, conv_bias=conv_bias, out_bias=out_bias, norm1_gain=norm1_gain,
        norm1_bias=norm1_bias, ffn_in_bias=ffn_in_bias[0], ffn_out_bias=ffn_out_bias,
        norm2_gain=norm2_gain, norm2_bias=norm2_bias,
    )
    seqs = doc_lengths.shape[0]
    seq_rows = hidden.shape[0] // seqs
    spans = [slice(s * seq_rows, (s + 1) * seq_rows) for s in range(seqs)]
    segments = [segment_ids(doc_lengths[q], seq_rows) for q in range(seqs)]
    marks = jnp.stack([marks_of(segment) for segment in segments])
    heads = width // HEAD_DIM
    vectors = jnp.stack(
        [jnp.pad(b, (0, WIDE - width)) for b in (query_bias, value_bias, point_bias, conv_bias)] * 2
    )
    order = kernel_weight.T.reshape(2, heads, KERNEL, width)
    order = jnp.where(me == 0, order, order[::-1])
    taps = jnp.pad(order, ((0, 0), (0, 0), (0, TAP_ROWS - KERNEL), (0, WIDE - width))).reshape(-1, WIDE)
    taps = jnp.pad(taps, ((0, LANES - taps.shape[0]), (0, 0)))
    bias = lax.dynamic_slice_in_dim(kernel_bias.reshape(2, heads, KERNEL), me, 1, 0)[0]
    bias = jnp.pad(bias, ((0, 0), (0, TAP_ROWS - KERNEL))).reshape(-1, 1)
    bias = jnp.broadcast_to(bias, (bias.shape[0], LANES))
    expand = expansion(heads)
    q, k, v, cv, dl, kc, ca, probs, cc, ctx, lse, second_all = front(
        hidden, marks, w, vectors, w.depth.astype(F32), bias, expand, taps, padded(second, 16)[None], count, 2
    )
    w.out0 = cut_wide(second_all, 0, 0)
    w.out1 = cut_wide(second_all, 0, width)
    w.inner = cut(second_all, share, share_ffn, 0, group)
    w.outer = cut(second_all, share + share_ffn, share_ffn, 0, group)
    output, grad_residual, grad_context, grad_conv, pack_mid, sums_mid = middle(
        ctx, cc, hidden, out_grad, w, p, me, 4
    )
    grad_input, own_last, other_last, pack_back, table, first_sum = back(
        hidden, grad_context, grad_conv, grad_residual, marks, (q, k, v, cv, dl, kc, ca, probs, lse),
        w, taps, w.depth.astype(F32), expand, sums_mid, recut(pack_mid, (1, 2, 2), count), count, 5,
    )
    second_sum, totals, grad_input = tail(
        recut(pack_back, (1, 1, 1), count), table, own_last, other_last, grad_input, count, 3
    )
    small_cuts = (share, share_ffn, width, group, 2 * heads * KERNEL)
    if share % TAP_ROWS == 0:
        results = final(first_sum, second_sum, totals, *small_cuts, count)
    else:
        results = final_plain(first_sum, second_sum, totals, *small_cuts)
    q_g, k_g, v_g, q_b, v_b, depth_g, p_g, p_b, kw_g, kb_g, c_g, c_b, out_g, out_b, gain1, bias1 = results[:16]
    inner_g, inner_b, outer_g, outer_b, gain2, bias2 = results[16:]
    return (
        output, grad_input, q_g, k_g, v_g, q_b[0], v_b[0], depth_g, p_g, p_b[0], kw_g, kb_g[0], c_g, c_b[0], out_g,
        out_b[0], gain1[0], bias1[0], inner_g[None], inner_b, outer_g[None], outer_b[0], gain2[0], bias2[0],
    )


def solution(mesh):
    in_specs = (
        P("dp", None),
        P("dp", None),
        P("dp", "mp"),
        P("dp", "mp"),
        P("dp", "mp"),
        P("mp"),
        P("mp"),
        P(None, "dp"),
        P("dp", "mp"),
        P("mp"),
        P("mp", None),
        P(),
        P("dp", "mp"),
        P("mp"),
        P(None, "mp", "dp"),
        P(),
        P(),
        P(),
        P("mp", None, "dp"),
        P("mp", None),
        P("mp", "dp", None),
        P("mp"),
        P("mp"),
        P("mp"),
        P("dp", "mp"),
    )
    out_specs = (
        P("dp", "mp"),
        P("dp", "mp"),
        P("dp", "mp"),
        P("dp", "mp"),
        P("dp", "mp"),
        P("mp"),
        P("mp"),
        P(None, "dp"),
        P("dp", "mp"),
        P("mp"),
        P("mp", None),
        P(),
        P("dp", "mp"),
        P("mp"),
        P(None, "mp", "dp"),
        P(),
        P(),
        P(),
        P("mp", None, "dp"),
        P("mp", None),
        P("mp", "dp", None),
        P("mp"),
        P("mp"),
        P("mp"),
    )
    return jax.shard_map(
        functools.partial(on_device, mesh.shape["dp"]), mesh=mesh, in_specs=in_specs, out_specs=out_specs, check_vma=False
    )
```

```python
import functools
import jax
import jax.numpy as jnp
from jax import lax
from jax.experimental import pallas as pl
from jax.experimental.pallas import tpu as pltpu

from jax.sharding import PartitionSpec as P

MESH = pl.DeviceIdType.MESH
BF16 = jnp.bfloat16
F32 = jnp.float32
HEAD_DIM = 64
KERNEL = 9
HALF = KERNEL // 2
CUTS = 16
TABLE_OWN = 72
TABLE_ROWS = 112
TAP_ROWS = 16
WIDE = 256
LANES = 128
EDGE = 8
MOST_DOC = 512


def at(dp, mp):
    return (dp, mp)


def places(count):
    dp = lax.axis_index("dp")
    core = lax.rem(dp, 2)
    side = lax.rem(lax.div(dp, 2), 2)
    deep = lax.div(dp, 4)
    return lax.axis_index("mp"), core, side, deep, count // 4


def index_of(deep, side, core):
    return (deep * 2 + side) * 2 + core


def greet(count):
    mp, core, side, deep, parts = places(count)
    barrier = pltpu.get_barrier_semaphore()
    peers = [index_of(lax.rem(deep + k, parts), side, core) for k in range(1, parts)]
    peers += [index_of(deep, 1 - side, core), index_of(deep, side, 1 - core)]
    for peer in peers:
        pl.semaphore_signal(barrier, inc=1, device_id=at(peer, mp), device_id_type=MESH)
    pl.semaphore_wait(barrier, len(peers))


def turned(tile, value):
    rows, columns = value.shape
    tile[...] = jnp.zeros_like(tile)
    tile[:rows, :columns] = value.astype(F32)
    return jnp.transpose(tile[...])[:columns, :rows]


def beside_each(first, second):
    return jnp.concatenate([first.astype(F32), second.astype(F32)], 1).astype(BF16)


def gather_body(count, own_ref, out_ref, own_sem, send_sem, recv_sem):
    mp, core, side, deep, parts = places(count)
    me = index_of(deep, side, core)
    local = pltpu.make_async_copy(own_ref.at[0], out_ref.at[me], own_sem)
    local.start()
    started = []

    def push(source, block, target):
        copy = pltpu.make_async_remote_copy(
            src_ref=source,
            dst_ref=out_ref.at[block],
            send_sem=send_sem.at[len(started)],
            recv_sem=recv_sem.at[block],
            device_id=at(target, mp),
            device_id_type=MESH,
        )
        copy.start()
        started.append(copy)

    def arrive(block):
        pltpu.make_async_copy(own_ref.at[0], out_ref.at[block], recv_sem.at[block]).wait()

    beside = index_of(deep, 1 - side, core)
    twin = index_of(deep, side, 1 - core)
    for k in range(1, parts):
        push(own_ref.at[0], me, index_of(lax.rem(deep + k, parts), side, core))
    push(own_ref.at[0], me, beside)
    push(own_ref.at[0], me, twin)
    yield
    arrive(beside)
    push(out_ref.at[beside], beside, twin)
    for k in range(1, parts):
        block = index_of(lax.rem(deep + parts - k, parts), side, core)
        arrive(block)
        push(out_ref.at[block], block, beside)
        push(out_ref.at[block], block, twin)
    for k in range(1, parts):
        block = index_of(lax.rem(deep + parts - k, parts), 1 - side, core)
        arrive(block)
        push(out_ref.at[block], block, twin)
    for k in range(parts):
        for other in range(2):
            arrive(index_of(lax.rem(deep + parts - k, parts), other, 1 - core))
    for copy in started:
        copy.wait_send()
    local.wait()
    yield


def gather_kernel(count, own_ref, out_ref, own_sem, send_sem, recv_sem):
    greet(count)
    for _ in gather_body(count, own_ref, out_ref, own_sem, send_sem, recv_sem):
        pass


def pack_kernel(
    count, q_ref, k_ref, v_ref, c_ref, p_ref, depth_ref, out_w_ref, in_w_ref, outer_w_ref,
    out_ref, second_ref,
    own_ref, tile_depth, own_sem, send_sem, recv_sem,
):
    share, width = q_ref.shape
    share_ffn = outer_w_ref.shape[1]
    own_ref[0, :share, :] = beside_each(q_ref[...], k_ref[...])
    own_ref[0, share : 2 * share, :] = beside_each(v_ref[...], c_ref[...])
    depth = turned(tile_depth, depth_ref[...])
    depth = jnp.concatenate([depth, jnp.zeros((share, width - KERNEL), F32)], 1)
    own_ref[0, 2 * share : 3 * share, :] = beside_each(p_ref[...], depth)
    greet(count)
    moves = gather_body(count, own_ref, out_ref, own_sem, send_sem, recv_sem)
    next(moves)
    second_ref[0, :share, :] = beside_each(out_w_ref[0], out_w_ref[1])
    second_ref[0, share : share + share_ffn, :] = in_w_ref[0]
    second_ref[0, share + share_ffn :, :] = outer_w_ref[0]
    next(moves)


def gather_first(weights, count, ident):
    q, depth, out_w, in_w, outer_w = weights[0], weights[5], weights[6], weights[7], weights[8]
    share, width = q.shape
    share_ffn, group = outer_w.shape[1:]
    parts = count // 4
    vmem = pl.BlockSpec(memory_space=pltpu.VMEM)
    return pl.pallas_call(
        functools.partial(pack_kernel, count),
        out_shape=(
            jax.ShapeDtypeStruct((count, 3 * share, 2 * width), BF16),
            jax.ShapeDtypeStruct((1, share + 2 * share_ffn, group), BF16),
        ),
        in_specs=[vmem] * 9,
        out_specs=(pl.BlockSpec(memory_space=pl.ANY), vmem),
        scratch_shapes=[
            pltpu.VMEM((1, 3 * share, 2 * width), BF16),
            pltpu.VMEM((LANES, LANES), F32),
            pltpu.SemaphoreType.DMA,
            pltpu.SemaphoreType.DMA((4 * parts - 1,)),
            pltpu.SemaphoreType.DMA((count,)),
        ],
        compiler_params=pltpu.CompilerParams(collective_id=ident, has_side_effects=True),
        name="weight_gather",
    )(*weights)


def gather(own, count, ident):
    parts = count // 4
    return pl.pallas_call(
        functools.partial(gather_kernel, count),
        out_shape=jax.ShapeDtypeStruct((count,) + own.shape[1:], own.dtype),
        in_specs=[pl.BlockSpec(memory_space=pl.ANY)],
        out_specs=pl.BlockSpec(memory_space=pl.ANY),
        scratch_shapes=[
            pltpu.SemaphoreType.DMA,
            pltpu.SemaphoreType.DMA((4 * parts - 1,)),
            pltpu.SemaphoreType.DMA((count,)),
        ],
        compiler_params=pltpu.CompilerParams(collective_id=ident, has_side_effects=True),
        name="weight_gather",
    )(own)


class Hops:
    def __init__(self, count, in_ref, twin_in, side_in, deep_in, send_sem, recv_sem):
        self.mp, self.core, self.side, self.deep, self.parts = places(count)
        self.in_ref, self.twin_in, self.side_in, self.deep_in = in_ref, twin_in, side_in, deep_in
        self.send_sem, self.recv_sem = send_sem, recv_sem
        self.beside = index_of(self.deep, 1 - self.side, self.core)
        self.twin = index_of(self.deep, self.side, 1 - self.core)
        self.order = [(k, other) for k in list(range(1, self.parts)) + [0] for other in (1, 0)]
        self.rows = in_ref.shape[1]
        self.step = 48 if self.rows % 48 == 0 else 16

    def depth(self, k):
        return lax.rem(self.deep + k, self.parts)

    def copy(self, source, target_ref, slot, target):
        return pltpu.make_async_remote_copy(
            src_ref=source,
            dst_ref=target_ref,
            send_sem=self.send_sem.at[slot],
            recv_sem=self.recv_sem.at[slot],
            device_id=at(target, self.mp),
            device_id_type=MESH,
        )

    def block(self, slot, core):
        k, other = self.order[slot]
        return index_of(self.depth(k), 1 - self.side if other else self.side, core)

    def first(self, slot):
        return self.copy(self.in_ref.at[self.block(slot, 1 - self.core)], self.twin_in.at[slot], slot, self.twin)

    def second(self, place):
        return self.copy(
            self.twin_in.at[2 * place], self.side_in.at[place], 2 * self.parts + place, self.beside
        )

    def third(self, place):
        k = self.order[2 * place][0]
        target = index_of(self.depth(k), self.side, self.core)
        return self.copy(self.side_in.at[place], self.deep_in.at[place], 3 * self.parts + place, target)

    def add(self, target, term):
        @pl.loop(0, self.rows // self.step)
        def _(i):
            part = pl.ds(pl.multiple_of(i * self.step, 16), self.step)
            total = target[part, :].astype(F32) + term[part, :].astype(F32)
            target[part, :] = total.astype(target.dtype)

    def start_first(self):
        for slot in range(2 * self.parts):
            self.first(slot).start()

    def start_second(self):
        for slot in range(2 * self.parts):
            self.first(slot).wait_recv()
            self.add(self.twin_in.at[slot], self.in_ref.at[self.block(slot, self.core)])
            if self.order[slot][1]:
                self.second(slot // 2).start()

    def start_third(self):
        for place in range(self.parts):
            self.second(place).wait_recv()
            self.add(self.side_in.at[place], self.twin_in.at[2 * place + 1])
            if place < self.parts - 1:
                self.third(place).start()

    def finish(self, out_ref):
        for place in range(self.parts - 1):
            self.third(place).wait_recv()

        @pl.loop(0, self.rows // self.step)
        def _(i):
            part = pl.ds(pl.multiple_of(i * self.step, 16), self.step)
            total = self.side_in[self.parts - 1, part, :].astype(F32)
            for place in range(self.parts - 1):
                total = total + self.deep_in[place, part, :].astype(F32)
            out_ref[part, :] = total

        for slot in range(2 * self.parts):
            self.first(slot).wait_send()
        for place in range(self.parts):
            self.second(place).wait_send()
        for place in range(self.parts - 1):
            self.third(place).wait_send()


def hop_scratch(count, rows, columns):
    parts = count // 4
    return [
        pltpu.VMEM((2 * parts, rows, columns), BF16),
        pltpu.VMEM((parts, rows, columns), BF16),
        pltpu.VMEM((max(parts - 1, 1), rows, columns), BF16),
        pltpu.SemaphoreType.DMA((4 * parts - 1,)),
        pltpu.SemaphoreType.DMA((4 * parts - 1,)),
    ]


def greet_all(count):
    mp, core, side, deep, parts = places(count)
    me = index_of(deep, side, core)
    barrier = pltpu.get_barrier_semaphore()
    pl.semaphore_signal(barrier, inc=1, device_id=at(me, 1 - mp), device_id_type=MESH)
    peers = [index_of(lax.rem(deep + k, parts), side, core) for k in range(1, parts)]
    peers += [index_of(deep, 1 - side, core), index_of(deep, side, 1 - core)]
    for peer in peers:
        pl.semaphore_signal(barrier, inc=1, device_id=at(peer, mp), device_id_type=MESH)
    pl.semaphore_wait(barrier, len(peers) + 1)


PIECES = 4


def tail_kernel(
    count, start,
    in_ref, table_ref, own_ref, other_ref, rest_ref,
    out_ref, total_ref, grad_ref,
    twin_in, side_in, deep_in, send_sem, recv_sem,
    table_in, table_out, table_send, table_recv, piece_in, piece_sum, piece_send, piece_recv, store_sem,
):
    mp, core, side, deep, parts = places(count)
    me = index_of(deep, side, core)
    greet_all(count)
    beside = index_of(deep, 1 - side, core)
    twin = index_of(deep, side, 1 - core)
    hops = Hops(count, in_ref, twin_in, side_in, deep_in, send_sem, recv_sem)
    rows = own_ref.shape[0] // PIECES

    def table_hop(source, slot, target, plane):
        return pltpu.make_async_remote_copy(
            src_ref=source,
            dst_ref=table_in.at[slot],
            send_sem=table_send.at[slot],
            recv_sem=table_recv.at[slot],
            device_id=at(target, plane),
            device_id_type=MESH,
        )

    def piece(i):
        part = pl.ds(i * rows, rows)
        return pltpu.make_async_remote_copy(
            src_ref=other_ref.at[part],
            dst_ref=piece_in.at[part],
            send_sem=piece_send.at[i],
            recv_sem=piece_recv.at[i],
            device_id=at(me, 1 - mp),
            device_id_type=MESH,
        )

    def store(i):
        return pltpu.make_async_copy(
            piece_sum.at[pl.ds(i * rows, rows)], grad_ref.at[pl.ds(start + i * rows, rows)], store_sem.at[i]
        )

    first = table_hop(table_ref, 0, me, 1 - mp)
    first.start()
    hops.start_first()
    for i in range(PIECES):
        piece(i).start()
    first.wait_recv()
    shared = pl.ds(TABLE_OWN, TABLE_ROWS - TABLE_OWN)
    table_out[0, :TABLE_OWN, :] = table_ref[:TABLE_OWN, :]
    table_out[0, shared, :] = table_ref[shared, :] + table_in[0, shared, :]
    second = table_hop(table_out.at[0], 1, twin, mp)
    second.start()
    hops.start_second()
    second.wait_recv()
    table_out[1] = table_out[0] + table_in[1]
    third = table_hop(table_out.at[1], 2, beside, mp)
    third.start()
    hops.start_third()
    third.wait_recv()
    table_out[2] = table_out[1] + table_in[2]
    fourth = [
        table_hop(table_out.at[2], 2 + j, index_of(lax.rem(deep + j, parts), side, core), mp) for j in range(1, parts)
    ]
    for copy in fourth:
        copy.start()
    for i in range(PIECES):
        piece(i).wait_recv()
        part = pl.ds(i * rows, rows)
        piece_sum[part, :] = own_ref[part, :] + piece_in[part, :].astype(F32)
        store(i).start()
    hops.finish(out_ref)
    for copy in fourth:
        copy.wait_recv()
    total = table_out[2]
    for j in range(1, parts):
        total = total + table_in[2 + j]
    total_ref[...] = total
    for copy in [first, second, third] + fourth:
        copy.wait_send()
    for i in range(PIECES):
        piece(i).wait_send()
        store(i).wait()


def tail(blocks, table, own, other, grad_rows, count, ident):
    parts = count // 4
    _, rows, columns = blocks.shape
    start = grad_rows.shape[0] - own.shape[0]
    vmem = pl.BlockSpec(memory_space=pltpu.VMEM)
    place = pl.BlockSpec(memory_space=pl.ANY)
    return pl.pallas_call(
        functools.partial(tail_kernel, count, start),
        out_shape=(
            jax.ShapeDtypeStruct((rows, columns), F32),
            jax.ShapeDtypeStruct(table.shape, F32),
            jax.ShapeDtypeStruct(grad_rows.shape, F32),
        ),
        in_specs=[vmem, vmem, vmem, vmem, place],
        out_specs=(vmem, vmem, place),
        input_output_aliases={4: 2},
        scratch_shapes=hop_scratch(count, rows, columns)
        + [
            pltpu.VMEM((parts + 2,) + table.shape, F32),
            pltpu.VMEM((3,) + table.shape, F32),
            pltpu.SemaphoreType.DMA((parts + 2,)),
            pltpu.SemaphoreType.DMA((parts + 2,)),
            pltpu.VMEM(other.shape, BF16),
            pltpu.VMEM(own.shape, F32),
            pltpu.SemaphoreType.DMA((PIECES,)),
            pltpu.SemaphoreType.DMA((PIECES,)),
            pltpu.SemaphoreType.DMA((PIECES,)),
        ],
        compiler_params=pltpu.CompilerParams(
            collective_id=ident, has_side_effects=True, vmem_limit_bytes=60 << 20
        ),
        name="tail",
    )(blocks, table, own, other, grad_rows)


def wide_row(table, row, count):
    return jnp.concatenate([table[row + k : row + k + 1, :] for k in range(count)], 1)


def final_kernel(
    count, first_ref, second_ref, table_ref,
    q_ref, k_ref, v_ref, qb_ref, vb_ref, depth_ref, p_ref, pb_ref, kw_ref, kb_ref, c_ref, cb_ref, out_ref, ob_ref,
    gain1_ref, bias1_ref, inner_ref, inb_ref, outer_ref, outb_ref, gain2_ref, bias2_ref,
    spread,
):
    share, width = q_ref.shape
    share_ffn, group = outer_ref.shape
    q_ref[...] = second_ref[:share, :width]
    k_ref[...] = second_ref[:share, width : 2 * width]
    v_ref[...] = second_ref[share : 2 * share, :width]
    c_ref[...] = second_ref[share : 2 * share, width : 2 * width]
    p_ref[...] = second_ref[2 * share : 3 * share, :width]
    out_ref[0] = first_ref[:share, :width]
    out_ref[1] = first_ref[:share, width : 2 * width]
    inner_ref[...] = first_ref[share : share + share_ffn, :]
    outer_ref[...] = first_ref[share + share_ffn : share + 2 * share_ffn, :]
    taps = kb_ref.shape[0]
    kw_ref[...] = table_ref[:taps, :width]
    rows = jnp.transpose(jnp.concatenate([table_ref[:64, LANES:], jnp.zeros((64, LANES), F32)], 0))
    kb_ref[...] = rows[width - LANES : width - LANES + 1, :taps].reshape(taps)
    for target, row in ((qb_ref, 54), (vb_ref, 55), (pb_ref, 56), (cb_ref, 57)):
        target[...] = table_ref[row : row + 1, :width].reshape(width)
    for target, row in ((outb_ref, 58), (gain2_ref, 60), (bias2_ref, 62)):
        target[...] = wide_row(table_ref, row, 2)[:, :group].reshape(group)
    inb_ref[...] = wide_row(table_ref, 64, 6)
    for target, row in ((gain1_ref, 99), (bias1_ref, 102), (ob_ref, 105)):
        target[...] = wide_row(table_ref, row, 3).reshape(2 * group)
    spread[...] = jnp.zeros_like(spread)
    for k in range(3):
        spread[:KERNEL, k * WIDE : (k + 1) * WIDE] = table_ref[72 + KERNEL * k : 72 + KERNEL * (k + 1), :]
    model = spread.shape[1]
    dp = lax.axis_index("dp")
    moved = pltpu.roll(spread[...], lax.rem(model - dp * share, model), 1)
    depth_ref[...] = moved[:KERNEL, :share]


def final(first, second, table, share, share_ffn, width, group, taps, count):
    def shape(*sizes):
        return jax.ShapeDtypeStruct(sizes, F32)

    model = 2 * group
    return pl.pallas_call(
        functools.partial(final_kernel, count),
        out_shape=(
            shape(share, width), shape(share, width), shape(share, width), shape(width), shape(width),
            shape(KERNEL, share), shape(share, width), shape(width), shape(taps, width), shape(taps),
            shape(share, width), shape(width), shape(2, share, width), shape(model), shape(model),
            shape(model), shape(share_ffn, group), shape(1, 4 * group), shape(share_ffn, group), shape(group),
            shape(group), shape(group),
        ),
        in_specs=[whole()] * 3,
        out_specs=(whole(),) * 22,
        scratch_shapes=[
            pltpu.VMEM((TAP_ROWS, model), F32),
        ],
        name="final",
    )(first, second, table)


EPSILON = 1e-06
MASK_FILL = -1e30
INV_ROOT2 = 0.7071067811865476
INV_ROOT_TWO_PI = 0.3989422804014327


def nn(left, right):
    return jnp.dot(left, right, preferred_element_type=F32)


def tn(left, right):
    return lax.dot_general(left, right, (((0,), (0,)), ((), ())), preferred_element_type=F32)


def nt(left, right):
    return lax.dot_general(left, right, (((1,), (1,)), ((), ())), preferred_element_type=F32)


def moments(sum_own, square_own, sum_other, square_other, width):
    mean = (sum_own + sum_other) / (2 * width)
    apart = (sum_own - sum_other) / width
    spread = (square_own + square_other + apart * apart * (width / 2)) / (2 * width)
    return mean, lax.rsqrt(spread + EPSILON)


def as_row(value):
    return value.reshape(1, -1)


def spread_marks(marks_ref, columns_ref):
    rows = marks_ref.shape[2]
    columns_ref[...] = jnp.transpose(
        jnp.concatenate([marks_ref[0], jnp.zeros((LANES - TAP_ROWS, rows), F32)], 0)
    )


def write_marks(lengths_ref, s, marks_ref):
    rows = marks_ref.shape[2]
    place = lax.broadcasted_iota(jnp.int32, (1, rows), 1)
    segment = jnp.zeros((1, rows), jnp.int32)
    end = 0
    for document in range(lengths_ref.shape[1]):
        end = end + lengths_ref[s, document]
        segment = segment + (place >= end).astype(jnp.int32)
    segment = segment.astype(F32)
    for tap in range(KERNEL):
        offset = tap - HALF
        there = pltpu.roll(segment, -offset % rows, 1) if offset else segment
        inside = jnp.logical_and(place + offset >= 0, place + offset < rows)
        marks_ref[0, tap : tap + 1, :] = jnp.where(jnp.logical_and(there == segment, inside), 1.0, 0.0)
    marks_ref[0, KERNEL : KERNEL + 1, :] = segment
    marks_ref[0, KERNEL + 1 :, :] = jnp.zeros((TAP_ROWS - KERNEL - 1, rows), F32)


def unpack_wide(target, source_ref, start, low, width):
    cut = target.shape[0] // CUTS
    for k in range(CUTS):
        rows = source_ref[k, pl.ds(start, cut), :].astype(F32)[:, low : low + width]
        rows = jnp.concatenate([rows, jnp.zeros((cut, WIDE - width), F32)], 1)
        target[pl.ds(k * cut, cut), :] = rows.astype(target.dtype)


def tap_places(heads, mp):
    row = lax.broadcasted_iota(jnp.int32, (LANES, LANES), 0)
    column = lax.broadcasted_iota(jnp.int32, (LANES, LANES), 1)
    tap_rows = heads * TAP_ROWS
    far = row >= tap_rows
    inner = jnp.where(far, row - tap_rows, row)
    head, tap = lax.shift_right_logical(inner, 4), jnp.bitwise_and(inner, TAP_ROWS - 1)
    half = jnp.where(far, 1 - mp, mp)
    valid = jnp.logical_and(tap < KERNEL, row < 2 * tap_rows)
    return jnp.logical_and(valid, column == (half * heads + head) * KERNEL + tap)


def write_expansion(target, heads):
    row = lax.broadcasted_iota(jnp.int32, (LANES, WIDE), 0)
    lane = lax.broadcasted_iota(jnp.int32, (LANES, WIDE), 1)
    tap_rows = heads * TAP_ROWS
    inner = jnp.where(row >= tap_rows, row - tap_rows, row)
    inside = jnp.logical_and(lane < heads * HEAD_DIM, row < 2 * tap_rows)
    head = lax.shift_right_logical(lane, 6) * TAP_ROWS
    for tap in range(KERNEL):
        chosen = jnp.logical_and(inside, inner == head + tap)
        target[:, tap * WIDE : (tap + 1) * WIDE] = jnp.where(chosen, 1.0, 0.0).astype(BF16)


def key_window(start, size, rows):
    low = max(0, start - (MOST_DOC - 1)) // size * size
    high = min(rows, -(-(start + size - 1 + MOST_DOC) // size) * size)
    return slice(low, high)


def only_rows(value, head):
    row = lax.broadcasted_iota(jnp.int32, (WIDE, 1), 0)
    return jnp.where(jnp.logical_and(row >= head * HEAD_DIM, row < (head + 1) * HEAD_DIM), value.astype(F32), 0.0)


def head_lanes(head):
    lane = lax.broadcasted_iota(jnp.int32, (1, WIDE), 1)
    return jnp.logical_and(lane >= head * HEAD_DIM, lane < (head + 1) * HEAD_DIM)


def only(value, head):
    return jnp.where(head_lanes(head), value.astype(F32), 0.0)


def high_low(weights, heads):
    high = weights.astype(BF16).astype(F32)
    low = weights - high
    rest = jnp.zeros((LANES - 2 * heads * TAP_ROWS, weights.shape[1]), F32)
    return jnp.transpose(jnp.concatenate([high, low, rest], 0)).astype(BF16)


def front_kernel(
    seqs, count, early,
    hidden_ref, lengths_ref, first_ref, kw_ref, kb_ref, qb_ref, vb_ref, pb_ref, cb_ref, second_ref,
    q_ref, k_ref, v_ref, cv_ref, dl_ref, kc_ref, ca_ref, probs_ref, cc_ref, ctx_ref, lse_ref, second_all_ref,
    marks_ref, taps_ref, depth_ref, expand_ref, inputs_turned_ref, point_turned_ref, early_ref,
    lead_ref, out0_nat, out1_nat, part_out, part_send, part_recv,
    query_ref, key_ref, value_ref, conv_ref, point_ref, vec_ref, bias_ref, depth_wide, tile,
    rows_pad, conv_pad, columns, weights, query_turned, value_turned, context_turned, tap_out, tap_in,
    send_sem, recv_sem, own_sem, gather_send, gather_recv,
):
    s = pl.program_id(0)
    mp, core, side, deep, parts = places(count)
    me = index_of(deep, side, core)
    rows, model = hidden_ref.shape
    chunks = model // LANES
    heads = probs_ref.shape[1] // TAP_ROWS
    tap_rows = heads * TAP_ROWS
    beside = index_of(deep, 1 - side, core)
    twin = index_of(deep, side, 1 - core)

    split = lead_ref.shape[1]
    spans = [pl.ds(0, split), pl.ds(split, second_ref.shape[1] - split)]

    def push(group, source, block, target, slot):
        return pltpu.make_async_remote_copy(
            src_ref=source.at[spans[group]],
            dst_ref=second_all_ref.at[block, spans[group]],
            send_sem=gather_send.at[group, slot],
            recv_sem=gather_recv.at[group, block],
            device_id=at(target, mp),
            device_id_type=MESH,
        )

    def arrive(group, block):
        pltpu.make_async_copy(
            second_ref.at[0, spans[group]], second_all_ref.at[block, spans[group]], gather_recv.at[group, block]
        ).wait()

    own_copy = pltpu.make_async_copy(second_ref.at[0], second_all_ref.at[me], own_sem.at[0])
    lead_copy = pltpu.make_async_copy(second_all_ref.at[:, spans[0]], lead_ref, own_sem.at[1])
    first_hops = [(me, index_of(lax.rem(deep + k, parts), side, core), k - 1) for k in range(1, parts)]
    first_hops += [(me, beside, parts - 1), (me, twin, parts)]
    second_hops = [(beside, [(twin, parts + 1)])]
    for k in range(1, parts):
        block = index_of(lax.rem(deep + parts - k, parts), side, core)
        second_hops.append((block, [(beside, parts + 2 * k), (twin, parts + 2 * k + 1)]))
    third_hops = [
        (index_of(lax.rem(deep + parts - k, parts), 1 - side, core), [(twin, 3 * parts + k - 1)]) for k in range(1, parts)
    ]

    def start_hops(group):
        for block, target, place in first_hops:
            push(group, second_ref.at[0], block, target, place).start()

    def pass_on(group, hops):
        for block, targets in hops:
            arrive(group, block)
            for target, place in targets:
                push(group, second_all_ref.at[block], block, target, place).start()

    def end_hops(group):
        for k in range(parts):
            for other in range(2):
                arrive(group, index_of(lax.rem(deep + parts - k, parts), other, 1 - core))
        for block, target, place in first_hops:
            push(group, second_ref.at[0], block, target, place).wait_send()
        for block, targets in second_hops + third_hops:
            for target, place in targets:
                push(group, second_all_ref.at[block], block, target, place).wait_send()

    def swap_part(which, piece):
        size = rows // PIECES
        return pltpu.make_async_remote_copy(
            src_ref=part_out.at[which, pl.ds(piece * size, size)],
            dst_ref=early_ref.at[pl.ds(which * rows + piece * size, size)],
            send_sem=part_send.at[which, piece],
            recv_sem=part_recv.at[which, piece],
            device_id=at(me, 1 - mp),
            device_id_type=MESH,
        )

    @pl.when(s == 0)
    def _():
        barrier = pltpu.get_barrier_semaphore()
        pl.semaphore_signal(barrier, inc=1, device_id=at(me, 1 - mp), device_id_type=MESH)
        peers = [index_of(lax.rem(deep + k, parts), side, core) for k in range(1, parts)] + [beside, twin]
        for peer in peers:
            pl.semaphore_signal(barrier, inc=1, device_id=at(peer, mp), device_id_type=MESH)
        pl.semaphore_wait(barrier, len(peers) + 1)
        own_copy.start()
        start_hops(0)
        start_hops(1)
        width = heads * HEAD_DIM
        cut = model // CUTS
        for target, place, low in (
            (query_ref, 0, 0), (key_ref, 0, width), (value_ref, 1, 0), (conv_ref, 1, width), (point_ref, 2, 0),
            (depth_wide, 2, width),
        ):
            unpack_wide(target, first_ref, place * cut, low, width)
        depth_ref[...] = jnp.transpose(depth_wide[:, :LANES])[:TAP_ROWS]
        vec_ref[...] = jnp.zeros_like(vec_ref)
        for row, source in enumerate((qb_ref, vb_ref, pb_ref, cb_ref)):
            vec_ref[row : row + 1, :width] = as_row(source[...])
        write_expansion(expand_ref, heads)
        chosen = tap_places(heads, mp)
        tile[...] = jnp.zeros_like(tile)
        tile[:1, : kb_ref.shape[0]] = as_row(kb_ref[...])
        bias = jnp.sum(jnp.where(chosen, tile[:1, :LANES], 0.0), axis=1, keepdims=True)
        bias_ref[...] = jnp.broadcast_to(bias[:tap_rows], bias_ref.shape)
        tile[: kw_ref.shape[0], :width] = kw_ref[...].astype(F32)
        turned_weight = tile[:LANES, :].astype(BF16)
        taps_ref[...] = nn(jnp.where(chosen, 1.0, 0.0).astype(BF16), turned_weight).astype(BF16)
        for place, source in enumerate((query_ref, key_ref, value_ref, conv_ref)):
            inputs_turned_ref[place * WIDE : (place + 1) * WIDE, :] = jnp.transpose(source[...])
        point_turned_ref[...] = jnp.transpose(point_ref[...])
        rows_pad[:, :EDGE, :] = jnp.zeros((chunks, EDGE, LANES), F32)
        rows_pad[:, pl.ds(EDGE + rows, EDGE), :] = jnp.zeros((chunks, EDGE, LANES), F32)
        conv_pad[:, :EDGE, :] = jnp.zeros((2, EDGE, LANES), F32)
        conv_pad[:, pl.ds(EDGE + rows, EDGE), :] = jnp.zeros((2, EDGE, LANES), F32)

    write_marks(lengths_ref, s, marks_ref)
    spread_marks(marks_ref, columns)
    hidden = hidden_ref[...]
    for c in range(chunks):
        rows_pad[c, pl.ds(EDGE, rows), :] = hidden[:, c * LANES : (c + 1) * LANES].astype(F32)

    step = 32

    def depth_step(i, carry):
        base = pl.multiple_of(i * step, step)
        total = [jnp.zeros((step, LANES), F32)] * chunks
        for tap in range(KERNEL):
            mask = jnp.broadcast_to(columns[pl.ds(base, step), tap : tap + 1], (step, LANES))
            for c in range(chunks):
                moved = rows_pad[c, pl.ds(base + EDGE + tap - HALF, step), :]
                total[c] = total[c] + (moved * mask) * depth_ref[tap : tap + 1, c * LANES : (c + 1) * LANES]
        for c in range(chunks):
            dl_ref[pl.ds(base, step), c * LANES : (c + 1) * LANES] = total[c].astype(BF16)
        return carry

    lax.fori_loop(0, rows // step, depth_step, 0)

    @pl.when(s == 0)
    def _():
        pass_on(0, second_hops)

    queries = (nn(hidden, query_ref[...]) + vec_ref[0:1, :]).astype(BF16)
    q_ref[...] = queries
    key_conv = nn(dl_ref[...], point_ref[...]) + vec_ref[2:3, :]
    kc_ref[...] = key_conv
    conv_attn = (key_conv * queries.astype(F32)).astype(BF16)
    ca_ref[...] = conv_attn
    tap_terms = nt(taps_ref[...], conv_attn)
    slot = lax.rem(s, 2)
    tap_out[slot] = tap_terms[tap_rows : 2 * tap_rows]
    swap_taps = pltpu.make_async_remote_copy(
        src_ref=tap_out.at[slot],
        dst_ref=tap_in.at[slot],
        send_sem=send_sem.at[slot],
        recv_sem=recv_sem.at[slot],
        device_id=at(me, 1 - mp),
        device_id_type=MESH,
    )
    swap_taps.start()

    @pl.when(jnp.logical_and(s >= 1, s < early + 1))
    def _():
        for piece in range(PIECES // 2, PIECES):
            swap_part(s - 1, piece).start()

    own_terms = tap_terms[:tap_rows]
    k_ref[...] = nn(hidden, key_ref[...]).astype(BF16)
    v_ref[...] = (nn(hidden, value_ref[...]) + vec_ref[1:2, :]).astype(BF16)
    conv_values = nn(hidden, conv_ref[...]) + vec_ref[3:4, :]
    cv_ref[...] = conv_values
    for c in range(2):
        conv_pad[c, pl.ds(EDGE, rows), :] = conv_values[:, c * LANES : (c + 1) * LANES]

    block = 256
    query_turned[...] = jnp.transpose(q_ref[...])
    value_turned[...] = jnp.transpose(v_ref[...])
    for start in range(0, rows, block):
        part = slice(start, start + block)
        keys = key_window(start, block, rows)
        allowed = columns[keys, KERNEL : KERNEL + 1] == marks_ref[0, KERNEL : KERNEL + 1, part]
        for head in range(heads):
            lanes = slice(head * HEAD_DIM, (head + 1) * HEAD_DIM)
            mine = (only_rows(query_turned[:, part], head) * (HEAD_DIM**-0.5)).astype(BF16)
            scores = jnp.where(allowed, nn(k_ref[keys, :], mine), MASK_FILL)
            top = jnp.max(scores, axis=0, keepdims=True)
            exponent = jnp.exp(scores - top)
            amount = jnp.sum(exponent, axis=0, keepdims=True)
            context_turned[lanes, part] = nn(value_turned[lanes, keys], exponent.astype(BF16)) * (1.0 / amount)
            lse_ref[0, head : head + 1, part] = top + jnp.log(amount)
    lse_ref[0, heads:, :] = jnp.zeros((8 - heads, rows), F32)
    context_turned[heads * HEAD_DIM :, :] = jnp.zeros((WIDE - heads * HEAD_DIM, rows), F32)
    ctx_ref[...] = jnp.transpose(context_turned[...]).astype(BF16)

    @pl.when(s == 0)
    def _():
        pass_on(0, third_hops)


    swap_taps.wait()
    logits = (own_terms + tap_in[slot] + bias_ref[:, :1]).reshape(heads, TAP_ROWS, rows)
    tap = lax.broadcasted_iota(jnp.int32, (heads, TAP_ROWS, rows), 1)
    logits = jnp.where(tap < KERNEL, logits, MASK_FILL)
    exponent = jnp.exp(logits - jnp.max(logits, axis=1, keepdims=True))
    probs = exponent / jnp.sum(exponent, axis=1, keepdims=True)
    probs_ref[0] = probs.reshape(tap_rows, rows)
    tap_mask = jnp.where(tap[0] < KERNEL, marks_ref[0], 0.0)
    weights[...] = high_low((probs * tap_mask[None]).reshape(tap_rows, rows), heads)
    conv_block = 128

    def conv_step(i, carry):
        base = pl.multiple_of(i * conv_block, conv_block)
        part = pl.ds(base, conv_block)
        scale = nn(weights[part, :], expand_ref[...])
        for c in range(2):
            total = jnp.zeros((conv_block, LANES), F32)
            for tap in range(KERNEL):
                low = tap * WIDE + c * LANES
                moved = conv_pad[c, pl.ds(base + EDGE + tap - HALF, conv_block), :]
                total = total + scale[:, low : low + LANES] * moved
            cc_ref[part, c * LANES : (c + 1) * LANES] = total.astype(BF16)
        return carry

    lax.fori_loop(0, rows // conv_block, conv_step, 0)

    @pl.when(s == 0)
    def _():
        own_copy.wait()
        end_hops(0)
        pass_on(1, second_hops)
        if early:
            lead_copy.start()
            lead_copy.wait()
            width = heads * HEAD_DIM
            for target, low in ((out0_nat, 0), (out1_nat, width)):
                unpack_wide(depth_wide, lead_ref, 0, low, width)
                target[...] = jnp.transpose(depth_wide[...].astype(BF16))

    @pl.when(s < early)
    def _():
        half = model // 2
        theirs = pl.ds(pl.multiple_of((1 - mp) * half, half), half)

        def part_step(i, carry):
            part = pl.ds(pl.multiple_of(i * block, block), block)
            other = nn(ctx_ref[part, :], out0_nat[:, theirs]) + nn(cc_ref[part, :], out1_nat[:, theirs])
            part_out[s, part, :] = other.astype(BF16)
            return carry

        lax.fori_loop(0, rows // block, part_step, 0)
        for piece in range(PIECES // 2):
            swap_part(s, piece).start()

    @pl.when(s == min(1, seqs - 1))
    def _():
        pass_on(1, third_hops)

    @pl.when(s == seqs - 1)
    def _():
        end_hops(1)
        for which in range(early):
            for piece in range(PIECES):
                swap_part(which, piece).wait()


def whole():
    return pl.BlockSpec(memory_space=pltpu.VMEM)


def by_seq(rows, columns):
    return pl.BlockSpec((rows, columns), lambda s: (s, 0))


def by_seq_row(rows, columns):
    return pl.BlockSpec((1, rows, columns), lambda s: (s, 0, 0))


def front(hidden, lengths, first, kernel_weight, biases, second, count, early, ident):
    seqs = lengths.shape[0]
    tokens, model = hidden.shape
    rows = tokens // seqs
    tap_rows = kernel_weight.shape[1] // HEAD_DIM * TAP_ROWS
    parts = count // 4
    place = pl.BlockSpec(memory_space=pl.ANY)
    share = model // count
    split = share + -share % TAP_ROWS

    def wide(kind):
        return jax.ShapeDtypeStruct((tokens, WIDE), kind)

    return pl.pallas_call(
        functools.partial(front_kernel, seqs, count, early),
        grid=(seqs,),
        out_shape=(
            wide(BF16), wide(BF16), wide(BF16), wide(F32),
            jax.ShapeDtypeStruct((tokens, model), BF16),
            wide(F32), wide(BF16),
            jax.ShapeDtypeStruct((seqs, tap_rows, rows), F32),
            wide(BF16), wide(BF16),
            jax.ShapeDtypeStruct((seqs, 8, rows), F32),
            jax.ShapeDtypeStruct((count,) + second.shape[1:], BF16),
            jax.ShapeDtypeStruct((seqs, TAP_ROWS, rows), F32),
            jax.ShapeDtypeStruct((LANES, WIDE), BF16),
            jax.ShapeDtypeStruct((TAP_ROWS, model), F32),
            jax.ShapeDtypeStruct((LANES, KERNEL * WIDE), BF16),
            jax.ShapeDtypeStruct((4 * WIDE, model), BF16),
            jax.ShapeDtypeStruct((WIDE, model), BF16),
            jax.ShapeDtypeStruct((tokens, model // 2), BF16),
        ),
        in_specs=[by_seq(rows, model), pl.BlockSpec(memory_space=pltpu.SMEM)] + [whole()] * 7 + [place],
        out_specs=(
            by_seq(rows, WIDE), by_seq(rows, WIDE), by_seq(rows, WIDE), by_seq(rows, WIDE), by_seq(rows, model),
            by_seq(rows, WIDE), by_seq(rows, WIDE), by_seq_row(tap_rows, rows), by_seq(rows, WIDE), by_seq(rows, WIDE),
            by_seq_row(8, rows), place, by_seq_row(TAP_ROWS, rows),
        )
        + (whole(),) * 5
        + (place,),
        scratch_shapes=[
            pltpu.VMEM((count, split, second.shape[2]), BF16),
            pltpu.VMEM((WIDE, model), BF16),
            pltpu.VMEM((WIDE, model), BF16),
            pltpu.VMEM((max(early, 1), rows, model // 2), BF16),
            pltpu.SemaphoreType.DMA((max(early, 1), PIECES)),
            pltpu.SemaphoreType.DMA((max(early, 1), PIECES)),
        ]
        + [pltpu.VMEM((model, WIDE), BF16)] * 5
        + [
            pltpu.VMEM((8, WIDE), F32),
            pltpu.VMEM((tap_rows, LANES), F32),
            pltpu.VMEM((model, WIDE), F32),
            pltpu.VMEM((WIDE, WIDE), F32),
            pltpu.VMEM((model // LANES, rows + 2 * EDGE, LANES), F32),
            pltpu.VMEM((2, rows + 2 * EDGE, LANES), F32),
            pltpu.VMEM((rows, LANES), F32),
            pltpu.VMEM((rows, LANES), BF16),
            pltpu.VMEM((WIDE, rows), BF16),
            pltpu.VMEM((WIDE, rows), BF16),
            pltpu.VMEM((WIDE, rows), F32),
            pltpu.VMEM((2, tap_rows, rows), F32),
            pltpu.VMEM((2, tap_rows, rows), F32),
            pltpu.SemaphoreType.DMA((2,)),
            pltpu.SemaphoreType.DMA((2,)),
            pltpu.SemaphoreType.DMA((2,)),
            pltpu.SemaphoreType.DMA((2, 4 * parts - 1)),
            pltpu.SemaphoreType.DMA((2, count)),
        ],
        compiler_params=pltpu.CompilerParams(
            collective_id=ident, has_side_effects=True, vmem_limit_bytes=62 << 20
        ),
        name="front",
    )(hidden, lengths, first, kernel_weight, *biases, second)


def stat_rows(columns):
    rows = columns[0].shape[0]
    diagonal = lax.broadcasted_iota(jnp.int32, (rows, rows), 0) == lax.broadcasted_iota(jnp.int32, (rows, rows), 1)
    lines = [jnp.sum(jnp.where(diagonal, column, 0.0), axis=0, keepdims=True) for column in columns]
    return jnp.concatenate(lines + [jnp.zeros((8 - len(lines), rows), F32)], 0)


def stat_columns(lines):
    rows = lines[0].shape[1]
    wide = jnp.concatenate(lines + [jnp.zeros((LANES - len(lines), rows), F32)], 0)
    tall = jnp.transpose(wide)
    return [tall[:, k : k + 1] for k in range(len(lines))]


def row_sums(value):
    rows, columns = value.shape
    return jnp.sum(value.reshape(rows // 8, 8, columns), axis=0)


SLOTS = 4
FFN_STEP = 256


def middle_kernel(
    blocks, early,
    early_ref, context_ref, conv_ref, context_late_ref, conv_late_ref, hidden_ref, grad_ref, grad_late_ref, second_ref,
    ob_ref, gain1_ref, bias1_ref, outb_ref, gain2_ref, bias2_ref, inb_ref,
    output_ref, residual_ref, grad_context_ref, grad_conv_ref, pack_ref, small_ref,
    out0_ref, out1_ref, inner_ref, outer_ref, vec_ref, inner_nat, outer_turned, out0_nat, out1_nat, low_units, branch_ref, acc_out0, acc_out1, state, scale_ring, act_ring, slope_ring, low_ring, summed_ring, normed_ring, stat_ring,
    acc_inner, acc_outer, acc_small, acc_bias,
    branch_out, branch_in, stat1_out, stat1_in, stat2_out, stat2_in, stat3_out, stat3_in, back_out, back_in,
    send_sem, recv_sem,
):
    i = pl.program_id(0)
    me = lax.axis_index("mp")
    dp = lax.axis_index("dp")
    width = summed_ring.shape[2]
    hidden_units = inner_ref.shape[0]
    inverse = 1.0 / (2 * width)

    def message(kind, source, target, slot):
        return pltpu.make_async_remote_copy(
            src_ref=source.at[slot],
            dst_ref=target.at[slot],
            send_sem=send_sem.at[kind, slot],
            recv_sem=recv_sem.at[kind, slot],
            device_id=(dp, 1 - me),
            device_id_type=MESH,
        )

    kinds = [
        (branch_out, branch_in), (stat1_out, stat1_in), (stat2_out, stat2_in), (stat3_out, stat3_in), (back_out, back_in),
    ]

    def fresh(kind, b, slot):
        @pl.when(b >= SLOTS)
        def _():
            message(kind, *kinds[kind], slot).wait_send()

    def vec(row):
        return vec_ref[row : row + 1, :width]

    @pl.when(i == 0)
    def _():
        barrier = pltpu.get_barrier_semaphore()
        pl.semaphore_signal(barrier, inc=1, device_id=(dp, 1 - me), device_id_type=MESH)
        pl.semaphore_wait(barrier, 1)
        cut, cut_ffn = 2 * width // CUTS, hidden_units // CUTS
        unpack_wide(out0_ref, second_ref, 0, 0, width // 2)
        unpack_wide(out1_ref, second_ref, 0, width // 2, width // 2)
        for k in range(CUTS):
            inner_ref[pl.ds(k * cut_ffn, cut_ffn), :] = second_ref[k, pl.ds(cut, cut_ffn), :]
            outer_ref[pl.ds(k * cut_ffn, cut_ffn), :] = second_ref[k, pl.ds(cut + cut_ffn, cut_ffn), :]
        for row, source in enumerate((ob_ref, gain1_ref, bias1_ref)):
            value = as_row(source[...])
            vec_ref[row : row + 1, :width] = jnp.where(me == 0, value[:, :width], value[:, width:])
        for row, source in enumerate((outb_ref, gain2_ref, bias2_ref)):
            vec_ref[3 + row : 4 + row, :width] = as_row(source[...])
        vec_ref[7:8, :] = inb_ref[...]
        inner_nat[...] = jnp.transpose(inner_ref[...])
        outer_turned[...] = jnp.transpose(outer_ref[...])
        out0_nat[...] = jnp.transpose(out0_ref[...])
        out1_nat[...] = jnp.transpose(out1_ref[...])
        acc_inner[...] = jnp.zeros_like(acc_inner)
        acc_outer[...] = jnp.zeros_like(acc_outer)
        acc_out0[...] = jnp.zeros_like(acc_out0)
        acc_out1[...] = jnp.zeros_like(acc_out1)
        acc_small[...] = jnp.zeros_like(acc_small)
        acc_bias[...] = jnp.zeros_like(acc_bias)

    @pl.when(i < blocks)
    def _():
        b = i
        slot = lax.rem(b, SLOTS)
        theirs = pl.ds(pl.multiple_of((1 - me) * width, width), width)
        ours = pl.ds(pl.multiple_of(me * width, width), width)

        @pl.when(b >= early)
        def _():
            fresh(0, b - early, slot)
            other = nn(context_ref[...], out0_nat[:, theirs]) + nn(conv_ref[...], out1_nat[:, theirs])
            branch_out[slot] = other.astype(BF16)
            message(0, *kinds[0], slot).start()

        own = nn(context_ref[...], out0_nat[:, ours]) + nn(conv_ref[...], out1_nat[:, ours])
        state[lax.rem(b, 8)] = hidden_ref[:, ours].astype(F32) + (own + vec(0))

        @pl.when(b < early)
        def _():
            state[lax.rem(b, 8)] += early_ref[...].astype(F32)

    @pl.when(jnp.logical_and(i >= 1, i < blocks + 1))
    def _():
        b = i - 1
        slot = lax.rem(b, SLOTS)
        fresh(1, b, slot)

        @pl.when(b >= early)
        def _():
            message(0, *kinds[0], slot).wait_recv()
            state[lax.rem(b, 8)] += branch_in[slot].astype(F32)

        residual = state[lax.rem(b, 8)]
        total = jnp.sum(residual, axis=1, keepdims=True)
        apart = residual - total * (1.0 / width)
        stat1_out[slot] = stat_rows([total, jnp.sum(apart * apart, axis=1, keepdims=True)])
        message(1, *kinds[1], slot).start()

    @pl.when(jnp.logical_and(i >= 2, i < blocks + 2))
    def _():
        b = i - 2
        slot = lax.rem(b, SLOTS)
        two = lax.rem(b, 2)
        message(1, *kinds[1], slot).wait_recv()
        fresh(2, b, slot)
        ours, theirs = stat1_out[slot], stat1_in[slot]
        mean, scale = moments(ours[0:1], ours[1:2], theirs[0:1], theirs[1:2], width)
        mean, scale = stat_columns([mean, scale])
        standard = (state[lax.rem(b, 8)] - mean) * scale
        state[lax.rem(b, 8)] = standard
        scale_ring[lax.rem(b, 4)] = jnp.broadcast_to(scale, scale_ring.shape[1:])
        normed = standard * vec(1) + vec(2)
        low = normed.astype(BF16)
        low_ring[two] = low
        summed = normed + vec(3)
        for start in range(0, hidden_units, FFN_STEP):
            part = pl.ds(start, FFN_STEP)
            inner = nn(low, inner_nat[:, part]) + vec_ref[7:8, start : start + FFN_STEP]
            cdf = 0.5 * (1.0 + lax.erf(inner * INV_ROOT2))
            act = (inner * cdf).astype(BF16)
            act_ring[two, :, part] = act
            slope_ring[two, :, part] = cdf + inner * jnp.exp(-0.5 * inner * inner) * INV_ROOT_TWO_PI
        summed = summed + nn(act_ring[two], outer_ref[...])
        summed_ring[two] = summed
        scaled = grad_ref[...].astype(F32) * vec(4)
        total = jnp.sum(summed, axis=1, keepdims=True)
        apart = summed - total * (1.0 / width)
        stat2_out[slot] = stat_rows(
            [
                total,
                jnp.sum(apart * apart, axis=1, keepdims=True),
                jnp.sum(scaled, axis=1, keepdims=True),
                jnp.sum(scaled * apart, axis=1, keepdims=True),
            ]
        )
        message(2, *kinds[2], slot).start()

    @pl.when(jnp.logical_and(i >= 3, i < blocks + 3))
    def _():
        b = i - 3
        slot = lax.rem(b, SLOTS)
        two = lax.rem(b, 2)
        message(2, *kinds[2], slot).wait_recv()
        fresh(3, b, slot)
        total, square, grads, cross = [stat2_out[slot][k : k + 1] for k in range(4)]
        total_o, square_o, grads_o, cross_o = [stat2_in[slot][k : k + 1] for k in range(4)]
        mean, scale = moments(total, square, total_o, square_o, width)
        mean_grad = (grads + grads_o) * inverse
        product = cross + cross_o + (total * (1.0 / width) - mean) * grads + (total_o * (1.0 / width) - mean) * grads_o
        mean_product = product * scale * inverse
        mean, scale, mean_grad, mean_product = stat_columns([mean, scale, mean_grad, mean_product])
        standard = (summed_ring[two] - mean) * scale
        output_ref[...] = (standard * vec(4) + vec(5)).astype(BF16)
        gradient = grad_late_ref[...].astype(F32)
        grad_summed = scale * (gradient * vec(4) - mean_grad - standard * mean_product)
        low = grad_summed.astype(BF16)
        acc_small[0] += row_sums(low.astype(F32))
        acc_small[1] += row_sums(gradient * standard)
        acc_small[2] += row_sums(gradient)
        normed_low = low_ring[two]
        grad_normed = grad_summed
        for start in range(0, hidden_units, FFN_STEP):
            part = pl.ds(start, FFN_STEP)
            inner_low = (nn(low, outer_turned[:, part]) * slope_ring[two, :, part]).astype(BF16)
            low_units[:, part] = inner_low
            acc_bias[:, part] += row_sums(inner_low.astype(F32))
            acc_outer[:, part] += tn(low, act_ring[two, :, part])
            acc_inner[:, part] += tn(normed_low, inner_low)
        grad_normed = grad_normed + nn(low_units[...], inner_ref[...])
        normed_ring[two] = grad_normed
        standard1 = state[lax.rem(b, 8)]
        scaled = grad_normed * vec(1)
        acc_small[3] += row_sums(grad_normed * standard1)
        acc_small[4] += row_sums(grad_normed)
        sums = stat_rows(
            [jnp.sum(scaled, axis=1, keepdims=True), jnp.sum(scaled * standard1, axis=1, keepdims=True)]
        )
        stat3_out[slot] = sums
        message(3, *kinds[3], slot).start()

    @pl.when(jnp.logical_and(i >= 4, i < blocks + 4))
    def _():
        b = i - 4
        slot = lax.rem(b, SLOTS)
        message(3, *kinds[3], slot).wait_recv()
        fresh(4, b, slot)
        both = stat3_out[slot] + stat3_in[slot]
        first, second = stat_columns([both[0:1], both[1:2]])
        standard = state[lax.rem(b, 8)]
        scaled = normed_ring[lax.rem(b, 2)] * vec(1)
        residual = scale_ring[lax.rem(b, 4)][:, :1] * (scaled - first * inverse - standard * (second * inverse))
        residual_ref[...] = residual
        low = residual.astype(BF16)
        acc_small[5] += row_sums(low.astype(F32))
        back_out[slot] = low
        message(4, *kinds[4], slot).start()

    @pl.when(i >= 5)
    def _():
        b = i - 5
        slot = lax.rem(b, SLOTS)
        message(4, *kinds[4], slot).wait_recv()
        theirs = pl.ds(pl.multiple_of((1 - me) * width, width), width)
        ours = pl.ds(pl.multiple_of(me * width, width), width)
        branch_ref[:, ours] = back_out[slot]
        branch_ref[:, theirs] = back_in[slot]
        branch = branch_ref[...]
        grad_context_ref[...] = nn(branch, out0_ref[...]).astype(BF16)
        grad_conv_ref[...] = nn(branch, out1_ref[...]).astype(BF16)
        acc_out0[...] += tn(context_late_ref[...], branch)
        acc_out1[...] += tn(conv_late_ref[...], branch)

    @pl.when(i == blocks + 4)
    def _():
        for kind in range(5):
            for slot in range(SLOTS):
                message(kind, *kinds[kind], slot).wait_send()
        cut, cut_ffn = 2 * width // CUTS, hidden_units // CUTS
        out_grads = jnp.transpose(jnp.concatenate([acc_out0[: width // 2], acc_out1[: width // 2]], 0)).astype(BF16)
        inner_grads = jnp.transpose(acc_inner[...]).astype(BF16)
        outer_grads = jnp.transpose(acc_outer[...]).astype(BF16)
        for k in range(CUTS):
            part_ffn = slice(k * cut_ffn, (k + 1) * cut_ffn)
            pack_ref[k, pl.ds(0, cut), :] = out_grads[k * cut : (k + 1) * cut]
            pack_ref[k, pl.ds(cut, cut_ffn), :] = inner_grads[part_ffn]
            pack_ref[k, pl.ds(cut + cut_ffn, cut_ffn), :] = outer_grads[part_ffn]
        small_ref[...] = jnp.zeros_like(small_ref)
        for row in range(6):
            small_ref[row : row + 1, :width] = jnp.sum(acc_small[row], axis=0, keepdims=True)
        small_ref[6:7, :] = jnp.sum(acc_bias[...], axis=0, keepdims=True)


def middle(early, early_rows, context, conv_context, hidden, out_grad, second, vectors, ident):
    tokens, model = hidden.shape
    width = model // 2
    local = context.shape[1]
    units = vectors[-1].shape[1]
    rows = 256
    blocks = tokens // rows

    def block(columns, lag):
        return pl.BlockSpec((rows, columns), lambda i: (jnp.clip(i - lag, 0, blocks - 1), 0))

    whole = pl.BlockSpec(memory_space=pltpu.VMEM)
    stat = pltpu.VMEM((SLOTS, 8, rows), F32)
    half = pltpu.VMEM((SLOTS, rows, width), BF16)
    return pl.pallas_call(
        functools.partial(middle_kernel, blocks, early // rows),
        grid=(blocks + 5,),
        out_shape=(
            jax.ShapeDtypeStruct((tokens, width), BF16),
            jax.ShapeDtypeStruct((tokens, width), F32),
            jax.ShapeDtypeStruct((tokens, local), BF16),
            jax.ShapeDtypeStruct((tokens, local), BF16),
            jax.ShapeDtypeStruct((CUTS, (model + 2 * units) // CUTS, width), BF16),
            jax.ShapeDtypeStruct((8, units), F32),
        ),
        in_specs=[
            block(width, 0), block(local, 0), block(local, 0), block(local, 5), block(local, 5), block(model, 0), block(width, 2),
            block(width, 3),
        ]
        + [whole] * 8,
        out_specs=(block(width, 3), block(width, 4), block(local, 5), block(local, 5), whole, whole),
        scratch_shapes=[
            pltpu.VMEM((model, local), BF16),
            pltpu.VMEM((model, local), BF16),
            pltpu.VMEM((units, width), BF16),
            pltpu.VMEM((units, width), BF16),
            pltpu.VMEM((8, units), F32),
            pltpu.VMEM((width, units), BF16),
            pltpu.VMEM((width, units), BF16),
            pltpu.VMEM((local, model), BF16),
            pltpu.VMEM((local, model), BF16),
            pltpu.VMEM((rows, units), BF16),
            pltpu.VMEM((rows, model), BF16),
            pltpu.VMEM((local, model), F32),
            pltpu.VMEM((local, model), F32),
            pltpu.VMEM((8, rows, width), F32),
            pltpu.VMEM((4, rows, 128), F32),
            pltpu.VMEM((2, rows, units), BF16),
            pltpu.VMEM((2, rows, units), F32),
            pltpu.VMEM((2, rows, width), BF16),
            pltpu.VMEM((2, rows, width), F32),
            pltpu.VMEM((2, rows, width), F32),
            pltpu.VMEM((8, 128), F32),
            pltpu.VMEM((width, units), F32),
            pltpu.VMEM((width, units), F32),
            pltpu.VMEM((6, 8, width), F32),
            pltpu.VMEM((8, units), F32),
            half, half, stat, stat, stat, stat, stat, stat, half, half,
            pltpu.SemaphoreType.DMA((5, SLOTS)),
            pltpu.SemaphoreType.DMA((5, SLOTS)),
        ],
        compiler_params=pltpu.CompilerParams(
            collective_id=ident, has_side_effects=True, vmem_limit_bytes=60 << 20
        ),
        name="middle",
    )(early_rows, context, conv_context, context, conv_context, hidden, out_grad, out_grad, second, *vectors)


def back_kernel(
    seqs, count,
    grad_context, grad_conv_ref, marks_ref, q_ref, k_ref, v_ref, cv_ref, ca_ref, probs_ref, lse_ref,
    hidden_any, residual_any, dl_any, kc_any,
    inputs_ref, point_ref, taps_ref, depth_ref, expand_ref, small_ref, pack_in_ref,
    grad_ref, own_ref, other_ref, pack_ref, table_ref, reduced_ref,
    hidden_ref, residual_ref, dl_ref, kc_ref, load_sem,
    other_out, other_in, other_send, other_recv,
    twin_in, side_in, deep_in, hop_send, hop_recv,
    depth_pad, conv_pad, grad_pad, columns, weights, shifted_weights, tap_terms, products,
    grads, grad_q, grad_k, grad_v, key_turned, probs_all, scores_all, turned_query, rows_total, tap_all,
    acc_in, acc_point, acc_bias, acc_tap, acc_tap_bias, acc_depth,
    tap_out, tap_in, send_sem, recv_sem,
):
    s = pl.program_id(0)
    mp = lax.axis_index("mp")
    dp = lax.axis_index("dp")
    rows, model = hidden_ref.shape
    chunks = model // LANES
    heads = probs_ref.shape[1] // TAP_ROWS
    tap_rows = heads * TAP_ROWS
    half = chunks // 2
    slot = lax.rem(s, 2)
    hops = Hops(count, pack_in_ref, twin_in, side_in, deep_in, hop_send, hop_recv)
    here_rows = pl.ds(pl.multiple_of(s * rows, rows), rows)
    loads = [
        pltpu.make_async_copy(source.at[here_rows], target, load_sem.at[k])
        for k, (source, target) in enumerate(
            [(hidden_any, hidden_ref), (residual_any, residual_ref), (dl_any, dl_ref), (kc_any, kc_ref)]
        )
    ]
    for load in loads:
        load.start()

    def swap_rows(which):
        return pltpu.make_async_remote_copy(
            src_ref=other_out.at[which],
            dst_ref=other_in.at[which],
            send_sem=other_send.at[which],
            recv_sem=other_recv.at[which],
            device_id=(dp, 1 - mp),
            device_id_type=MESH,
        )

    @pl.when(s == 0)
    def _():
        greet_all(count)
        hops.start_first()
        for pad in (depth_pad, conv_pad, grad_pad):
            for start in (0, EDGE + rows):
                pad[:, pl.ds(start, EDGE), :] = jnp.zeros((pad.shape[0], EDGE, LANES), F32)
        for acc in (acc_in, acc_point, acc_bias, acc_tap, acc_tap_bias, acc_depth):
            acc[...] = jnp.zeros_like(acc)

    spread_marks(marks_ref, columns)
    block = 256

    for c in range(2):
        lanes = slice(c * LANES, (c + 1) * LANES)
        grad_pad[c, pl.ds(EDGE, rows), :] = grad_conv_ref[:, lanes].astype(F32)
        conv_pad[c, pl.ds(EDGE, rows), :] = cv_ref[:, lanes]

    probs = probs_ref[0].reshape(heads, TAP_ROWS, rows)
    tap = lax.broadcasted_iota(jnp.int32, (heads, TAP_ROWS, rows), 1)
    tap_mask = jnp.where(tap < KERNEL, jnp.broadcast_to(marks_ref[...], (heads, TAP_ROWS, rows)), 0.0)
    masked = (probs * tap_mask).reshape(tap_rows, rows)
    flat_tap = tap.reshape(tap_rows, rows)
    moved = jnp.zeros_like(masked)
    for j in range(KERNEL):
        turn = (j - HALF) % rows
        turned = pltpu.roll(masked, turn, 1) if turn else masked
        moved = jnp.where(flat_tap == j, turned, moved)
    shifted_weights[...] = high_low(moved, heads)
    conv_block = 128

    def conv_step(i, carry):
        base = pl.multiple_of(i * conv_block, conv_block)
        part = pl.ds(base, conv_block)
        scale = nn(shifted_weights[part, :], expand_ref[...])
        for c in range(2):
            here = grad_pad[c, pl.ds(base + EDGE, conv_block), :]
            total = jnp.zeros((conv_block, LANES), F32)
            for j in range(KERNEL):
                low = j * WIDE + c * LANES
                products[:, low : low + LANES] = (
                    here * conv_pad[c, pl.ds(base + EDGE + j - HALF, conv_block), :]
                ).astype(BF16)
                total = total + scale[:, low : low + LANES] * grad_pad[
                    c, pl.ds(base + EDGE + HALF - j, conv_block), :
                ]
            grads[part, 3 * WIDE + c * LANES : 3 * WIDE + (c + 1) * LANES] = total.astype(BF16)
        tap_terms[part, :] = nt(products[...], expand_ref[...])
        return carry

    lax.fori_loop(0, rows // conv_block, conv_step, 0)
    grad_taps = jnp.transpose(tap_terms[...])[:tap_rows].reshape(heads, TAP_ROWS, rows) * tap_mask
    grad_logits = probs * (grad_taps - jnp.sum(probs * grad_taps, axis=1, keepdims=True))
    grad_logits = grad_logits.reshape(tap_rows, rows).astype(BF16)
    tap_out[slot] = grad_logits
    swap_taps = pltpu.make_async_remote_copy(
        src_ref=tap_out.at[slot],
        dst_ref=tap_in.at[slot],
        send_sem=send_sem.at[slot],
        recv_sem=recv_sem.at[slot],
        device_id=(dp, 1 - mp),
        device_id_type=MESH,
    )
    swap_taps.start()

    grad_k[...] = jnp.zeros_like(grad_k)
    grad_v[...] = jnp.zeros_like(grad_v)

    key_turned[...] = jnp.transpose(k_ref[...])
    for start in range(0, rows, block):
        part = slice(start, start + block)
        keys = key_window(start, block, rows)
        allowed = columns[keys, KERNEL : KERNEL + 1] == marks_ref[0, KERNEL : KERNEL + 1, part]
        query, context = q_ref[part, :], grad_context[part, :]
        query_turned, context_turned = jnp.transpose(query), jnp.transpose(context)
        for head in range(heads):
            lanes = slice(head * HEAD_DIM, (head + 1) * HEAD_DIM)
            place = slice(head * block, (head + 1) * block)
            mine = (only_rows(query_turned, head) * (HEAD_DIM**-0.5)).astype(BF16)
            scores = jnp.where(allowed, nn(k_ref[keys, :], mine), MASK_FILL)
            probs = jnp.exp(scores - lse_ref[0, head : head + 1, part])
            probs_all[keys, place] = probs.astype(BF16)
            mixed = probs * nn(v_ref[keys, :], only_rows(context_turned, head).astype(BF16))
            grad_scores = (mixed - probs * jnp.sum(mixed, axis=0, keepdims=True)).astype(BF16)
            scores_all[keys, place] = grad_scores
            turned_query[lanes, :] = nn(key_turned[lanes, keys], grad_scores)
        turned_query[heads * HEAD_DIM :, :] = jnp.zeros((WIDE - heads * HEAD_DIM, block), F32)
        grad_q[part, :] = jnp.transpose(turned_query[...])
        contexts = jnp.concatenate([only(context, head).astype(BF16) for head in range(heads)], 0)
        queries = jnp.concatenate([(only(query, head) * (HEAD_DIM**-0.5)).astype(BF16) for head in range(heads)], 0)
        grad_v[keys, :] += nn(probs_all[keys, :], contexts)
        grad_k[keys, :] += nn(scores_all[keys, :], queries)

    for load in loads:
        load.wait()
    swap_taps.wait()
    tap_all[...] = jnp.zeros_like(tap_all)
    tap_all[:tap_rows, :] = tap_out[slot].astype(F32)
    tap_all[tap_rows : 2 * tap_rows, :] = tap_in[slot].astype(F32)
    every = tap_all[...]
    acc_tap[...] += nn(every.astype(BF16), ca_ref[...])
    acc_tap_bias[...] += sum(every[:, c * LANES : (c + 1) * LANES] for c in range(rows // LANES))
    weights[...] = jnp.transpose(every).astype(BF16)

    def key_step(i, carry):
        base = pl.multiple_of(i * block, block)
        part = pl.ds(base, block)
        grad_attn = nn(weights[part, :], taps_ref[...]).astype(BF16).astype(F32)
        query = q_ref[part, :].astype(F32)
        key_low = (grad_attn * query).astype(BF16)
        grads[part, 4 * WIDE : 5 * WIDE] = key_low
        grad_query = grad_q[part, :] * (HEAD_DIM**-0.5) + grad_attn * kc_ref[part, :]
        grads[part, :WIDE] = grad_query.astype(BF16)
        grads[part, WIDE : 2 * WIDE] = grad_k[part, :].astype(BF16)
        grads[part, 2 * WIDE : 3 * WIDE] = grad_v[part, :].astype(BF16)
        acc_bias[...] += row_sums(grads[part, :].astype(F32))
        grad_depth = nn(key_low, point_ref[...])
        total = nn(grads[part, : 4 * WIDE], inputs_ref[...])
        for c in range(chunks):
            lanes = slice(c * LANES, (c + 1) * LANES)
            depth_pad[c, pl.ds(base + EDGE, block), :] = grad_depth[:, lanes]
            rows_total[c, part, :] = total[:, lanes]
        return carry

    lax.fori_loop(0, rows // block, key_step, 0)
    acc_point[...] += tn(grads[:, 4 * WIDE : 5 * WIDE], dl_ref[...])
    acc_in[...] += tn(hidden_ref[...], grads[:, : 4 * WIDE])
    step = 32

    def depth_step(i, carry):
        base = pl.multiple_of(i * step, step)
        part = pl.ds(base, step)
        total = [rows_total[c, part, :] for c in range(chunks)]
        for j in range(KERNEL):
            mirror = KERNEL - 1 - j
            mask = jnp.broadcast_to(columns[part, j : j + 1], (step, LANES))
            for c in range(chunks):
                lanes = slice(c * LANES, (c + 1) * LANES)
                near = depth_pad[c, pl.ds(base + EDGE + j - HALF, step), :] * mask
                total[c] = total[c] + near * depth_ref[mirror : mirror + 1, lanes]
                acc_depth[mirror, :, lanes] += row_sums(near * hidden_ref[part, lanes].astype(F32))
        for c in range(chunks):
            rows_total[c, part, :] = total[c]
        return carry

    lax.fori_loop(0, rows // step, depth_step, 0)

    @pl.when(s >= 1)
    def _():
        which = s - 1
        swap_rows(which).wait_recv()
        grad_ref[...] = own_ref[...] + other_in[which].astype(F32)

    for c in range(half):
        lanes = slice(c * LANES, (c + 1) * LANES)
        own_ref[:, lanes] = rows_total[mp * half + c] + residual_ref[:, lanes]

    @pl.when(s < seqs - 1)
    def _():
        for c in range(half):
            lanes = slice(c * LANES, (c + 1) * LANES)
            other_out[s, :, lanes] = rows_total[(1 - mp) * half + c].astype(BF16)
        swap_rows(s).start()

    @pl.when(s == 0)
    def _():
        hops.start_second()

    @pl.when(s == min(1, seqs - 1))
    def _():
        hops.start_third()

    @pl.when(s == seqs - 1)
    def _():
        for c in range(half):
            lanes = slice(c * LANES, (c + 1) * LANES)
            other_ref[:, lanes] = rows_total[(1 - mp) * half + c].astype(BF16)
        hops.finish(reduced_ref)
        for which in range(seqs - 1):
            swap_rows(which).wait_send()
        width = heads * HEAD_DIM
        group = model // 2
        cut = model // CUTS
        empty = jnp.zeros((cut, width), F32)
        point_grad = jnp.transpose(acc_point[...])
        for k in range(CUTS):
            part = pl.ds(k * cut, cut)
            for place in range(2):
                first = acc_in[part, 2 * place * WIDE : 2 * place * WIDE + width]
                second = acc_in[part, (2 * place + 1) * WIDE : (2 * place + 1) * WIDE + width]
                pack_ref[k, pl.ds(place * cut, cut), :] = jnp.concatenate([first, second], 1).astype(BF16)
            pack_ref[k, pl.ds(2 * cut, cut), :] = jnp.concatenate([point_grad[k * cut : (k + 1) * cut, :width], empty], 1).astype(BF16)
        table_ref[...] = jnp.zeros_like(table_ref)
        lane = lax.broadcasted_iota(jnp.int32, (LANES, WIDE), 1)
        taps = jnp.where(lane == width, jnp.sum(acc_tap_bias[...], axis=1, keepdims=True), acc_tap[...])
        own_taps = [taps[h * TAP_ROWS : h * TAP_ROWS + KERNEL] for h in range(heads)]
        other_taps = [taps[tap_rows + h * TAP_ROWS : tap_rows + h * TAP_ROWS + KERNEL] for h in range(heads)]
        for h in range(heads):
            table_ref[KERNEL * h : KERNEL * (h + 1), :] = jnp.where(mp == 0, own_taps[h], other_taps[h])
            later = KERNEL * (heads + h)
            table_ref[later : later + KERNEL, :] = jnp.where(mp == 0, other_taps[h], own_taps[h])
        for row, place in ((54, 0), (55, 2), (56, 4), (57, 3)):
            table_ref[row : row + 1, :] = jnp.sum(acc_bias[:, place * WIDE : (place + 1) * WIDE], axis=0, keepdims=True)

        def lay(row, value):
            for k in range(-(-value.shape[1] // WIDE)):
                piece = value[:, k * WIDE : (k + 1) * WIDE]
                table_ref[row + k : row + k + 1, : piece.shape[1]] = piece

        for row, source in ((58, 0), (60, 1), (62, 2)):
            lay(row, small_ref[source : source + 1, :group])
        lay(64, small_ref[6:7, :])
        for row, source in ((99, 3), (102, 4), (105, 5)):
            value = small_ref[source : source + 1, :group]
            blank = jnp.zeros_like(value)
            lay(row, jnp.where(mp == 0, jnp.concatenate([value, blank], 1), jnp.concatenate([blank, value], 1)))
        for j in range(KERNEL):
            total = jnp.sum(acc_depth[j], axis=0, keepdims=True)
            for k in range(model // WIDE):
                row = TABLE_OWN + KERNEL * k + j
                table_ref[row : row + 1, :] = total[:, k * WIDE : (k + 1) * WIDE]


def back(hidden, grad_context, grad_conv, residual, marks, kept, turned_weights, taps, depth, expand, small, pack, count, ident):
    q, k, v, cv, dl, kc, ca, probs, lse = kept
    seqs, _, rows = marks.shape
    tokens, model = hidden.shape
    width = model // 2
    tap_rows = probs.shape[1]
    wide = by_seq(rows, WIDE)
    place = pl.BlockSpec(memory_space=pl.ANY)
    padded_rows = rows + 2 * EDGE
    vmem = pltpu.VMEM
    swaps = max(seqs - 1, 1)
    return pl.pallas_call(
        functools.partial(back_kernel, seqs, count),
        grid=(seqs,),
        out_shape=(
            jax.ShapeDtypeStruct((tokens, width), F32),
            jax.ShapeDtypeStruct((rows, width), F32),
            jax.ShapeDtypeStruct((rows, width), BF16),
            jax.ShapeDtypeStruct((CUTS, 3 * model // CUTS, width), BF16),
            jax.ShapeDtypeStruct((TABLE_ROWS, WIDE), F32),
            jax.ShapeDtypeStruct(pack.shape[1:], F32),
        ),
        in_specs=[wide, wide, by_seq_row(TAP_ROWS, rows), wide, wide, wide, wide, wide]
        + [by_seq_row(tap_rows, rows), by_seq_row(8, rows)]
        + [place] * 4
        + [whole()] * 7,
        out_specs=(pl.BlockSpec((rows, width), lambda s: (jnp.maximum(s - 1, 0), 0)),) + (whole(),) * 5,
        scratch_shapes=[
            vmem((rows, model), BF16),
            vmem((rows, width), F32),
            vmem((rows, model), BF16),
            vmem((rows, WIDE), F32),
            pltpu.SemaphoreType.DMA((4,)),
            vmem((swaps, rows, width), BF16),
            vmem((swaps, rows, width), BF16),
            pltpu.SemaphoreType.DMA((swaps,)),
            pltpu.SemaphoreType.DMA((swaps,)),
        ]
        + hop_scratch(count, pack.shape[1], pack.shape[2])
        + [
            vmem((model // LANES, padded_rows, LANES), F32),
            vmem((2, padded_rows, LANES), F32),
            vmem((2, padded_rows, LANES), F32),
            vmem((rows, LANES), F32),
            vmem((rows, LANES), BF16),
            vmem((rows, LANES), BF16),
            vmem((rows, LANES), F32),
            vmem((128, KERNEL * WIDE), BF16),
            vmem((rows, 5 * WIDE), BF16),
            vmem((rows, WIDE), F32),
            vmem((rows, WIDE), F32),
            vmem((rows, WIDE), F32),
            vmem((WIDE, rows), BF16),
            vmem((rows, tap_rows // TAP_ROWS * 256), BF16),
            vmem((rows, tap_rows // TAP_ROWS * 256), BF16),
            vmem((WIDE, 256), F32),
            vmem((model // LANES, rows, LANES), F32),
            vmem((LANES, rows), F32),
            vmem((model, 4 * WIDE), F32),
            vmem((WIDE, model), F32),
            vmem((8, 5 * WIDE), F32),
            vmem((LANES, WIDE), F32),
            vmem((LANES, LANES), F32),
            vmem((TAP_ROWS, 8, model), F32),
            vmem((2, tap_rows, rows), BF16),
            vmem((2, tap_rows, rows), BF16),
            pltpu.SemaphoreType.DMA((2,)),
            pltpu.SemaphoreType.DMA((2,)),
        ],
        compiler_params=pltpu.CompilerParams(
            collective_id=ident, has_side_effects=True, vmem_limit_bytes=63 << 20
        ),
        name="back",
    )(
        grad_context, grad_conv, marks, q, k, v, cv, ca, probs, lse, hidden, residual, dl, kc,
        *turned_weights, taps, depth, expand, small, pack,
    )


def padded(value, multiple):
    rows = value.shape[-2]
    extra = -rows % multiple
    return jnp.pad(value, [(0, 0)] * (value.ndim - 2) + [(0, extra), (0, 0)])


def recut(pack, sizes, unit, start, count):
    if count == start:
        return pack
    parts, low = [], 0
    for size in sizes:
        rows = pack[:, low : low + size * unit].reshape(-1, pack.shape[2])
        parts.append(rows.reshape(count, -1, pack.shape[2]))
        low += size * unit
    return padded(jnp.concatenate(parts, 1), TAP_ROWS)


def gather_plain(weights, count, ident):
    q, k, v, c, p, depth, out_w, in_w, outer_w = weights
    depth = jnp.pad(depth.T, ((0, 0), (0, q.shape[1] - KERNEL)))
    pairs = [jnp.concatenate(pair, 1) for pair in ((q, k), (v, c), (p, depth), (out_w[0], out_w[1]))]
    first = padded(jnp.concatenate(pairs[:3], 0), TAP_ROWS)[None]
    second = padded(jnp.concatenate([pairs[3], in_w[0], outer_w[0]], 0), TAP_ROWS)[None]
    return recut(gather(first, count, ident), (1, 1, 1), q.shape[0], count, CUTS), second


def final_plain(first, second, table, share, share_ffn, width, group, taps):
    model = 2 * group
    depth = jnp.concatenate([table[72 + KERNEL * k : 72 + KERNEL * (k + 1)] for k in range(model // WIDE)], 1)
    row = lambda at_row, size: table[at_row : at_row + 6].reshape(-1)[:size]
    out = first[:share]
    return (
        second[:share, :width], second[:share, width:], second[share : 2 * share, :width],
        row(54, width), row(55, width),
        lax.dynamic_slice_in_dim(depth, lax.axis_index("dp") * share, share, 1),
        second[2 * share : 3 * share, :width], row(56, width),
        table[:taps, :width], table[:taps, width], second[share : 2 * share, width:], row(57, width),
        jnp.stack([out[:, :width], out[:, width:]]), row(105, model), row(99, model), row(102, model),
        first[share : share + share_ffn], row(64, 4 * group)[None], first[share + share_ffn : share + 2 * share_ffn],
        row(58, group), row(60, group), row(62, group),
    )


def on_device(
    count,
    hidden, doc_lengths, query_weight, key_weight, value_weight, query_bias, value_bias,
    depth_weight, point_weight, point_bias, kernel_weight, kernel_bias, conv_weight, conv_bias,
    out_weight, out_bias, norm1_gain, norm1_bias, ffn_in_weight, ffn_in_bias, ffn_out_weight,
    ffn_out_bias, norm2_gain, norm2_bias, out_grad,
):
    share, width = query_weight.shape
    model = hidden.shape[1]
    group = ffn_out_bias.shape[0]
    share_ffn = ffn_out_weight.shape[1]
    heads = width // HEAD_DIM
    weights = (
        query_weight, key_weight, value_weight, conv_weight, point_weight, depth_weight,
        out_weight.transpose(0, 2, 1), ffn_in_weight.transpose(0, 2, 1), ffn_out_weight,
    )
    first, second = (gather_first if share % TAP_ROWS == 0 else gather_plain)(weights, count, 1)
    seqs = doc_lengths.shape[0]
    early = seqs - 1 if count == CUTS else 0
    biases = [kernel_bias, query_bias, value_bias, point_bias, conv_bias]
    q, k, v, cv, dl, kc, ca, probs, cc, ctx, lse, second_all, marks, taps, depth, expand, *rest = front(
        hidden, doc_lengths, first, kernel_weight.T, biases, second, count, early, 2
    )
    turned_weights, early_rows = rest[:2], rest[2]
    vectors = [out_bias, norm1_gain, norm1_bias, ffn_out_bias, norm2_gain, norm2_bias, ffn_in_bias]
    output, grad_residual, grad_context, grad_conv, pack_mid, sums_mid = middle(
        early * (hidden.shape[0] // seqs), early_rows, ctx, cc, hidden, out_grad, recut(second_all, (1, 2, 2), share, count, CUTS), vectors, 4
    )
    grad_input, own_last, other_last, pack_back, table, first_sum = back(
        hidden, grad_context, grad_conv, grad_residual, marks, (q, k, v, cv, dl, kc, ca, probs, lse),
        turned_weights, taps, depth, expand, sums_mid, recut(pack_mid, (1, 2, 2), model // CUTS, CUTS, count), count, 5,
    )
    second_sum, totals, grad_input = tail(
        recut(pack_back, (1, 1, 1), model // CUTS, CUTS, count), table, own_last, other_last, grad_input, count, 3
    )
    small_cuts = (share, share_ffn, width, group, 2 * heads * KERNEL)
    if share % TAP_ROWS == 0:
        results = final(first_sum, second_sum, totals, *small_cuts, count)
    else:
        results = final_plain(first_sum, second_sum, totals, *small_cuts)
    q_g, k_g, v_g, q_b, v_b, depth_g, p_g, p_b, kw_g, kb_g, c_g, c_b, out_g, out_b, gain1, bias1 = results[:16]
    inner_g, inner_b, outer_g, outer_b, gain2, bias2 = results[16:]
    return (
        output, grad_input, q_g, k_g, v_g, q_b, v_b, depth_g, p_g, p_b, kw_g.T, kb_g, c_g, c_b, out_g.transpose(0, 2, 1),
        out_b, gain1, bias1, inner_g.T[None], inner_b, outer_g[None], outer_b, gain2, bias2,
    )


def solution(mesh):
    in_specs = (
        P("dp", None),
        P("dp", None),
        P("dp", "mp"),
        P("dp", "mp"),
        P("dp", "mp"),
        P("mp"),
        P("mp"),
        P(None, "dp"),
        P("dp", "mp"),
        P("mp"),
        P("mp", None),
        P(),
        P("dp", "mp"),
        P("mp"),
        P(None, "mp", "dp"),
        P(),
        P(),
        P(),
        P("mp", None, "dp"),
        P("mp", None),
        P("mp", "dp", None),
        P("mp"),
        P("mp"),
        P("mp"),
        P("dp", "mp"),
    )
    out_specs = (
        P("dp", "mp"),
        P("dp", "mp"),
        P("dp", "mp"),
        P("dp", "mp"),
        P("dp", "mp"),
        P("mp"),
        P("mp"),
        P(None, "dp"),
        P("dp", "mp"),
        P("mp"),
        P("mp", None),
        P(),
        P("dp", "mp"),
        P("mp"),
        P(None, "mp", "dp"),
        P(),
        P(),
        P(),
        P("mp", None, "dp"),
        P("mp", None),
        P("mp", "dp", None),
        P("mp"),
        P("mp"),
        P("mp"),
    )
    return jax.shard_map(
        functools.partial(on_device, mesh.shape["dp"]), mesh=mesh, in_specs=in_specs, out_specs=out_specs, check_vma=False
    )
```

```python
import functools
import jax
import jax.numpy as jnp
from jax import lax
from jax.experimental import pallas as pl
from jax.experimental.pallas import tpu as pltpu

from jax.sharding import PartitionSpec as P

MESH = pl.DeviceIdType.MESH
BF16 = jnp.bfloat16
F32 = jnp.float32
HEAD_DIM = 64
KERNEL = 9
HALF = KERNEL // 2
CUTS = 16
TABLE_OWN = 72
TABLE_ROWS = 112
TAP_ROWS = 16
WIDE = 256
LANES = 128
EDGE = 8
MOST_DOC = 512


def at(dp, mp):
    return (dp, mp)


def places(count):
    dp = lax.axis_index("dp")
    core = lax.rem(dp, 2)
    side = lax.rem(lax.div(dp, 2), 2)
    deep = lax.div(dp, 4)
    return lax.axis_index("mp"), core, side, deep, count // 4


def index_of(deep, side, core):
    return (deep * 2 + side) * 2 + core


def greet(count):
    mp, core, side, deep, parts = places(count)
    barrier = pltpu.get_barrier_semaphore()
    peers = [index_of(lax.rem(deep + k, parts), side, core) for k in range(1, parts)]
    peers += [index_of(deep, 1 - side, core), index_of(deep, side, 1 - core)]
    for peer in peers:
        pl.semaphore_signal(barrier, inc=1, device_id=at(peer, mp), device_id_type=MESH)
    pl.semaphore_wait(barrier, len(peers))


def turned(tile, value):
    rows, columns = value.shape
    tile[...] = jnp.zeros_like(tile)
    tile[:rows, :columns] = value.astype(F32)
    return jnp.transpose(tile[...])[:columns, :rows]


def beside_each(first, second):
    return jnp.concatenate([first.astype(F32), second.astype(F32)], 1).astype(BF16)


def gather_body(count, own_ref, out_ref, own_sem, send_sem, recv_sem):
    mp, core, side, deep, parts = places(count)
    me = index_of(deep, side, core)
    local = pltpu.make_async_copy(own_ref.at[0], out_ref.at[me], own_sem)
    local.start()
    started = []

    def push(source, block, target):
        copy = pltpu.make_async_remote_copy(
            src_ref=source,
            dst_ref=out_ref.at[block],
            send_sem=send_sem.at[len(started)],
            recv_sem=recv_sem.at[block],
            device_id=at(target, mp),
            device_id_type=MESH,
        )
        copy.start()
        started.append(copy)

    def arrive(block):
        pltpu.make_async_copy(own_ref.at[0], out_ref.at[block], recv_sem.at[block]).wait()

    beside = index_of(deep, 1 - side, core)
    twin = index_of(deep, side, 1 - core)
    for k in range(1, parts):
        push(own_ref.at[0], me, index_of(lax.rem(deep + k, parts), side, core))
    push(own_ref.at[0], me, beside)
    push(own_ref.at[0], me, twin)
    yield
    arrive(beside)
    push(out_ref.at[beside], beside, twin)
    for k in range(1, parts):
        block = index_of(lax.rem(deep + parts - k, parts), side, core)
        arrive(block)
        push(out_ref.at[block], block, beside)
        push(out_ref.at[block], block, twin)
    for k in range(1, parts):
        block = index_of(lax.rem(deep + parts - k, parts), 1 - side, core)
        arrive(block)
        push(out_ref.at[block], block, twin)
    for k in range(parts):
        for other in range(2):
            arrive(index_of(lax.rem(deep + parts - k, parts), other, 1 - core))
    for copy in started:
        copy.wait_send()
    local.wait()
    yield


def gather_kernel(count, own_ref, out_ref, own_sem, send_sem, recv_sem):
    greet(count)
    for _ in gather_body(count, own_ref, out_ref, own_sem, send_sem, recv_sem):
        pass


def pack_kernel(
    count, q_ref, k_ref, v_ref, c_ref, p_ref, depth_ref, out_w_ref, in_w_ref, outer_w_ref,
    out_ref, second_ref,
    own_ref, tile_depth, own_sem, send_sem, recv_sem,
):
    share, width = q_ref.shape
    share_ffn = outer_w_ref.shape[1]
    own_ref[0, :share, :] = beside_each(q_ref[...], k_ref[...])
    own_ref[0, share : 2 * share, :] = beside_each(v_ref[...], c_ref[...])
    depth = turned(tile_depth, depth_ref[...])
    depth = jnp.concatenate([depth, jnp.zeros((share, width - KERNEL), F32)], 1)
    own_ref[0, 2 * share : 3 * share, :] = beside_each(p_ref[...], depth)
    greet(count)
    moves = gather_body(count, own_ref, out_ref, own_sem, send_sem, recv_sem)
    next(moves)
    second_ref[0, :share, :] = beside_each(out_w_ref[0], out_w_ref[1])
    second_ref[0, share : share + share_ffn, :] = in_w_ref[0]
    second_ref[0, share + share_ffn :, :] = outer_w_ref[0]
    next(moves)


def gather_first(weights, count, ident):
    q, depth, out_w, in_w, outer_w = weights[0], weights[5], weights[6], weights[7], weights[8]
    share, width = q.shape
    share_ffn, group = outer_w.shape[1:]
    parts = count // 4
    vmem = pl.BlockSpec(memory_space=pltpu.VMEM)
    return pl.pallas_call(
        functools.partial(pack_kernel, count),
        out_shape=(
            jax.ShapeDtypeStruct((count, 3 * share, 2 * width), BF16),
            jax.ShapeDtypeStruct((1, share + 2 * share_ffn, group), BF16),
        ),
        in_specs=[vmem] * 9,
        out_specs=(pl.BlockSpec(memory_space=pl.ANY), vmem),
        scratch_shapes=[
            pltpu.VMEM((1, 3 * share, 2 * width), BF16),
            pltpu.VMEM((LANES, LANES), F32),
            pltpu.SemaphoreType.DMA,
            pltpu.SemaphoreType.DMA((4 * parts - 1,)),
            pltpu.SemaphoreType.DMA((count,)),
        ],
        compiler_params=pltpu.CompilerParams(collective_id=ident, has_side_effects=True),
        name="weight_gather",
    )(*weights)


def gather(own, count, ident):
    parts = count // 4
    return pl.pallas_call(
        functools.partial(gather_kernel, count),
        out_shape=jax.ShapeDtypeStruct((count,) + own.shape[1:], own.dtype),
        in_specs=[pl.BlockSpec(memory_space=pl.ANY)],
        out_specs=pl.BlockSpec(memory_space=pl.ANY),
        scratch_shapes=[
            pltpu.SemaphoreType.DMA,
            pltpu.SemaphoreType.DMA((4 * parts - 1,)),
            pltpu.SemaphoreType.DMA((count,)),
        ],
        compiler_params=pltpu.CompilerParams(collective_id=ident, has_side_effects=True),
        name="weight_gather",
    )(own)


class Hops:
    def __init__(self, count, in_ref, twin_in, side_in, deep_in, send_sem, recv_sem):
        self.mp, self.core, self.side, self.deep, self.parts = places(count)
        self.in_ref, self.twin_in, self.side_in, self.deep_in = in_ref, twin_in, side_in, deep_in
        self.send_sem, self.recv_sem = send_sem, recv_sem
        self.beside = index_of(self.deep, 1 - self.side, self.core)
        self.twin = index_of(self.deep, self.side, 1 - self.core)
        self.order = [(k, other) for k in list(range(1, self.parts)) + [0] for other in (1, 0)]
        self.rows = in_ref.shape[1]
        self.step = 48 if self.rows % 48 == 0 else 16

    def depth(self, k):
        return lax.rem(self.deep + k, self.parts)

    def copy(self, source, target_ref, slot, target):
        return pltpu.make_async_remote_copy(
            src_ref=source,
            dst_ref=target_ref,
            send_sem=self.send_sem.at[slot],
            recv_sem=self.recv_sem.at[slot],
            device_id=at(target, self.mp),
            device_id_type=MESH,
        )

    def block(self, slot, core):
        k, other = self.order[slot]
        return index_of(self.depth(k), 1 - self.side if other else self.side, core)

    def first(self, slot):
        return self.copy(self.in_ref.at[self.block(slot, 1 - self.core)], self.twin_in.at[slot], slot, self.twin)

    def second(self, place):
        return self.copy(
            self.twin_in.at[2 * place], self.side_in.at[place], 2 * self.parts + place, self.beside
        )

    def third(self, place):
        k = self.order[2 * place][0]
        target = index_of(self.depth(k), self.side, self.core)
        return self.copy(self.side_in.at[place], self.deep_in.at[place], 3 * self.parts + place, target)

    def add(self, target, term):
        @pl.loop(0, self.rows // self.step)
        def _(i):
            part = pl.ds(pl.multiple_of(i * self.step, 16), self.step)
            total = target[part, :].astype(F32) + term[part, :].astype(F32)
            target[part, :] = total.astype(target.dtype)

    def start_first(self):
        for slot in range(2 * self.parts):
            self.first(slot).start()

    def start_second(self):
        for slot in range(2 * self.parts):
            self.first(slot).wait_recv()
            self.add(self.twin_in.at[slot], self.in_ref.at[self.block(slot, self.core)])
            if self.order[slot][1]:
                self.second(slot // 2).start()

    def start_third(self):
        for place in range(self.parts):
            self.second(place).wait_recv()
            self.add(self.side_in.at[place], self.twin_in.at[2 * place + 1])
            if place < self.parts - 1:
                self.third(place).start()

    def finish(self, out_ref):
        for place in range(self.parts - 1):
            self.third(place).wait_recv()

        @pl.loop(0, self.rows // self.step)
        def _(i):
            part = pl.ds(pl.multiple_of(i * self.step, 16), self.step)
            total = self.side_in[self.parts - 1, part, :].astype(F32)
            for place in range(self.parts - 1):
                total = total + self.deep_in[place, part, :].astype(F32)
            out_ref[part, :] = total

        for slot in range(2 * self.parts):
            self.first(slot).wait_send()
        for place in range(self.parts):
            self.second(place).wait_send()
        for place in range(self.parts - 1):
            self.third(place).wait_send()


def hop_scratch(count, rows, columns):
    parts = count // 4
    return [
        pltpu.VMEM((2 * parts, rows, columns), BF16),
        pltpu.VMEM((parts, rows, columns), BF16),
        pltpu.VMEM((max(parts - 1, 1), rows, columns), BF16),
        pltpu.SemaphoreType.DMA((4 * parts - 1,)),
        pltpu.SemaphoreType.DMA((4 * parts - 1,)),
    ]


def greet_all(count):
    mp, core, side, deep, parts = places(count)
    me = index_of(deep, side, core)
    barrier = pltpu.get_barrier_semaphore()
    pl.semaphore_signal(barrier, inc=1, device_id=at(me, 1 - mp), device_id_type=MESH)
    peers = [index_of(lax.rem(deep + k, parts), side, core) for k in range(1, parts)]
    peers += [index_of(deep, 1 - side, core), index_of(deep, side, 1 - core)]
    for peer in peers:
        pl.semaphore_signal(barrier, inc=1, device_id=at(peer, mp), device_id_type=MESH)
    pl.semaphore_wait(barrier, len(peers) + 1)


PIECES = 4


def tail_kernel(
    count, start,
    in_ref, table_ref, own_ref, other_ref, rest_ref,
    out_ref, total_ref, grad_ref,
    twin_in, side_in, deep_in, send_sem, recv_sem,
    table_in, table_out, table_send, table_recv, piece_in, piece_sum, piece_send, piece_recv, store_sem,
):
    mp, core, side, deep, parts = places(count)
    me = index_of(deep, side, core)
    greet_all(count)
    beside = index_of(deep, 1 - side, core)
    twin = index_of(deep, side, 1 - core)
    hops = Hops(count, in_ref, twin_in, side_in, deep_in, send_sem, recv_sem)
    rows = own_ref.shape[0] // PIECES

    def table_hop(source, slot, target, plane):
        return pltpu.make_async_remote_copy(
            src_ref=source,
            dst_ref=table_in.at[slot],
            send_sem=table_send.at[slot],
            recv_sem=table_recv.at[slot],
            device_id=at(target, plane),
            device_id_type=MESH,
        )

    def piece(i):
        part = pl.ds(i * rows, rows)
        return pltpu.make_async_remote_copy(
            src_ref=other_ref.at[part],
            dst_ref=piece_in.at[part],
            send_sem=piece_send.at[i],
            recv_sem=piece_recv.at[i],
            device_id=at(me, 1 - mp),
            device_id_type=MESH,
        )

    def store(i):
        return pltpu.make_async_copy(
            piece_sum.at[pl.ds(i * rows, rows)], grad_ref.at[pl.ds(start + i * rows, rows)], store_sem.at[i]
        )

    first = table_hop(table_ref, 0, me, 1 - mp)
    first.start()
    hops.start_first()
    for i in range(PIECES):
        piece(i).start()
    first.wait_recv()
    shared = pl.ds(TABLE_OWN, TABLE_ROWS - TABLE_OWN)
    table_out[0, :TABLE_OWN, :] = table_ref[:TABLE_OWN, :]
    table_out[0, shared, :] = table_ref[shared, :] + table_in[0, shared, :]
    second = table_hop(table_out.at[0], 1, twin, mp)
    second.start()
    hops.start_second()
    second.wait_recv()
    table_out[1] = table_out[0] + table_in[1]
    third = table_hop(table_out.at[1], 2, beside, mp)
    third.start()
    hops.start_third()
    third.wait_recv()
    table_out[2] = table_out[1] + table_in[2]
    fourth = [
        table_hop(table_out.at[2], 2 + j, index_of(lax.rem(deep + j, parts), side, core), mp) for j in range(1, parts)
    ]
    for copy in fourth:
        copy.start()
    for i in range(PIECES):
        piece(i).wait_recv()
        part = pl.ds(i * rows, rows)
        piece_sum[part, :] = own_ref[part, :] + piece_in[part, :].astype(F32)
        store(i).start()
    hops.finish(out_ref)
    for copy in fourth:
        copy.wait_recv()
    total = table_out[2]
    for j in range(1, parts):
        total = total + table_in[2 + j]
    total_ref[...] = total
    for copy in [first, second, third] + fourth:
        copy.wait_send()
    for i in range(PIECES):
        piece(i).wait_send()
        store(i).wait()


def tail(blocks, table, own, other, grad_rows, count, ident):
    parts = count // 4
    _, rows, columns = blocks.shape
    start = grad_rows.shape[0] - own.shape[0]
    vmem = pl.BlockSpec(memory_space=pltpu.VMEM)
    place = pl.BlockSpec(memory_space=pl.ANY)
    return pl.pallas_call(
        functools.partial(tail_kernel, count, start),
        out_shape=(
            jax.ShapeDtypeStruct((rows, columns), F32),
            jax.ShapeDtypeStruct(table.shape, F32),
            jax.ShapeDtypeStruct(grad_rows.shape, F32),
        ),
        in_specs=[vmem, vmem, vmem, vmem, place],
        out_specs=(vmem, vmem, place),
        input_output_aliases={4: 2},
        scratch_shapes=hop_scratch(count, rows, columns)
        + [
            pltpu.VMEM((parts + 2,) + table.shape, F32),
            pltpu.VMEM((3,) + table.shape, F32),
            pltpu.SemaphoreType.DMA((parts + 2,)),
            pltpu.SemaphoreType.DMA((parts + 2,)),
            pltpu.VMEM(other.shape, BF16),
            pltpu.VMEM(own.shape, F32),
            pltpu.SemaphoreType.DMA((PIECES,)),
            pltpu.SemaphoreType.DMA((PIECES,)),
            pltpu.SemaphoreType.DMA((PIECES,)),
        ],
        compiler_params=pltpu.CompilerParams(
            collective_id=ident, has_side_effects=True, vmem_limit_bytes=60 << 20
        ),
        name="tail",
    )(blocks, table, own, other, grad_rows)


def wide_row(table, row, count):
    return jnp.concatenate([table[row + k : row + k + 1, :] for k in range(count)], 1)


def final_kernel(
    count, first_ref, second_ref, table_ref,
    q_ref, k_ref, v_ref, qb_ref, vb_ref, depth_ref, p_ref, pb_ref, kw_ref, kb_ref, c_ref, cb_ref, out_ref, ob_ref,
    gain1_ref, bias1_ref, inner_ref, inb_ref, outer_ref, outb_ref, gain2_ref, bias2_ref,
    spread,
):
    share, width = q_ref.shape
    share_ffn, group = outer_ref.shape
    q_ref[...] = second_ref[:share, :width]
    k_ref[...] = second_ref[:share, width : 2 * width]
    v_ref[...] = second_ref[share : 2 * share, :width]
    c_ref[...] = second_ref[share : 2 * share, width : 2 * width]
    p_ref[...] = second_ref[2 * share : 3 * share, :width]
    out_ref[0] = first_ref[:share, :width]
    out_ref[1] = first_ref[:share, width : 2 * width]
    inner_ref[...] = first_ref[share : share + share_ffn, :]
    outer_ref[...] = first_ref[share + share_ffn : share + 2 * share_ffn, :]
    taps = kb_ref.shape[0]
    kw_ref[...] = table_ref[:taps, :width]
    rows = jnp.transpose(jnp.concatenate([table_ref[:64, LANES:], jnp.zeros((64, LANES), F32)], 0))
    kb_ref[...] = rows[width - LANES : width - LANES + 1, :taps].reshape(taps)
    for target, row in ((qb_ref, 54), (vb_ref, 55), (pb_ref, 56), (cb_ref, 57)):
        target[...] = table_ref[row : row + 1, :width].reshape(width)
    for target, row in ((outb_ref, 58), (gain2_ref, 60), (bias2_ref, 62)):
        target[...] = wide_row(table_ref, row, 2)[:, :group].reshape(group)
    inb_ref[...] = wide_row(table_ref, 64, 6)
    for target, row in ((gain1_ref, 99), (bias1_ref, 102), (ob_ref, 105)):
        target[...] = wide_row(table_ref, row, 3).reshape(2 * group)
    spread[...] = jnp.zeros_like(spread)
    for k in range(3):
        spread[:KERNEL, k * WIDE : (k + 1) * WIDE] = table_ref[72 + KERNEL * k : 72 + KERNEL * (k + 1), :]
    model = spread.shape[1]
    dp = lax.axis_index("dp")
    moved = pltpu.roll(spread[...], lax.rem(model - dp * share, model), 1)
    depth_ref[...] = moved[:KERNEL, :share]


def final(first, second, table, share, share_ffn, width, group, taps, count):
    def shape(*sizes):
        return jax.ShapeDtypeStruct(sizes, F32)

    model = 2 * group
    return pl.pallas_call(
        functools.partial(final_kernel, count),
        out_shape=(
            shape(share, width), shape(share, width), shape(share, width), shape(width), shape(width),
            shape(KERNEL, share), shape(share, width), shape(width), shape(taps, width), shape(taps),
            shape(share, width), shape(width), shape(2, share, width), shape(model), shape(model),
            shape(model), shape(share_ffn, group), shape(1, 4 * group), shape(share_ffn, group), shape(group),
            shape(group), shape(group),
        ),
        in_specs=[whole()] * 3,
        out_specs=(whole(),) * 22,
        scratch_shapes=[
            pltpu.VMEM((TAP_ROWS, model), F32),
        ],
        name="final",
    )(first, second, table)


EPSILON = 1e-06
MASK_FILL = -1e30
INV_ROOT2 = 0.7071067811865476
INV_ROOT_TWO_PI = 0.3989422804014327


def nn(left, right):
    return jnp.dot(left, right, preferred_element_type=F32)


def tn(left, right):
    return lax.dot_general(left, right, (((0,), (0,)), ((), ())), preferred_element_type=F32)


def nt(left, right):
    return lax.dot_general(left, right, (((1,), (1,)), ((), ())), preferred_element_type=F32)


def moments(sum_own, square_own, sum_other, square_other, width):
    mean = (sum_own + sum_other) / (2 * width)
    apart = (sum_own - sum_other) / width
    spread = (square_own + square_other + apart * apart * (width / 2)) / (2 * width)
    return mean, lax.rsqrt(spread + EPSILON)


def as_row(value):
    return value.reshape(1, -1)


def spread_marks(marks_ref, columns_ref):
    rows = marks_ref.shape[2]
    columns_ref[...] = jnp.transpose(
        jnp.concatenate([marks_ref[0], jnp.zeros((LANES - TAP_ROWS, rows), F32)], 0)
    )


def write_marks(lengths_ref, s, marks_ref):
    rows = marks_ref.shape[2]
    place = lax.broadcasted_iota(jnp.int32, (1, rows), 1)
    segment = jnp.zeros((1, rows), jnp.int32)
    end = 0
    for document in range(lengths_ref.shape[1]):
        end = end + lengths_ref[s, document]
        segment = segment + (place >= end).astype(jnp.int32)
    segment = segment.astype(F32)
    for tap in range(KERNEL):
        offset = tap - HALF
        there = pltpu.roll(segment, -offset % rows, 1) if offset else segment
        inside = jnp.logical_and(place + offset >= 0, place + offset < rows)
        marks_ref[0, tap : tap + 1, :] = jnp.where(jnp.logical_and(there == segment, inside), 1.0, 0.0)
    marks_ref[0, KERNEL : KERNEL + 1, :] = segment
    marks_ref[0, KERNEL + 1 :, :] = jnp.zeros((TAP_ROWS - KERNEL - 1, rows), F32)


def unpack_wide(target, source_ref, start, low, width):
    cut = target.shape[0] // CUTS
    for k in range(CUTS):
        rows = source_ref[k, pl.ds(start, cut), :].astype(F32)[:, low : low + width]
        rows = jnp.concatenate([rows, jnp.zeros((cut, WIDE - width), F32)], 1)
        target[pl.ds(k * cut, cut), :] = rows.astype(target.dtype)


def tap_places(heads, mp):
    row = lax.broadcasted_iota(jnp.int32, (LANES, LANES), 0)
    column = lax.broadcasted_iota(jnp.int32, (LANES, LANES), 1)
    tap_rows = heads * TAP_ROWS
    far = row >= tap_rows
    inner = jnp.where(far, row - tap_rows, row)
    head, tap = lax.shift_right_logical(inner, 4), jnp.bitwise_and(inner, TAP_ROWS - 1)
    half = jnp.where(far, 1 - mp, mp)
    valid = jnp.logical_and(tap < KERNEL, row < 2 * tap_rows)
    return jnp.logical_and(valid, column == (half * heads + head) * KERNEL + tap)


def write_expansion(target, heads):
    row = lax.broadcasted_iota(jnp.int32, (LANES, WIDE), 0)
    lane = lax.broadcasted_iota(jnp.int32, (LANES, WIDE), 1)
    tap_rows = heads * TAP_ROWS
    inner = jnp.where(row >= tap_rows, row - tap_rows, row)
    inside = jnp.logical_and(lane < heads * HEAD_DIM, row < 2 * tap_rows)
    head = lax.shift_right_logical(lane, 6) * TAP_ROWS
    for tap in range(KERNEL):
        chosen = jnp.logical_and(inside, inner == head + tap)
        target[:, tap * WIDE : (tap + 1) * WIDE] = jnp.where(chosen, 1.0, 0.0).astype(BF16)


def key_window(start, size, rows):
    low = max(0, start - (MOST_DOC - 1)) // size * size
    high = min(rows, -(-(start + size - 1 + MOST_DOC) // size) * size)
    return slice(low, high)


def only_rows(value, head):
    row = lax.broadcasted_iota(jnp.int32, (WIDE, 1), 0)
    return jnp.where(jnp.logical_and(row >= head * HEAD_DIM, row < (head + 1) * HEAD_DIM), value.astype(F32), 0.0)


def head_lanes(head):
    lane = lax.broadcasted_iota(jnp.int32, (1, WIDE), 1)
    return jnp.logical_and(lane >= head * HEAD_DIM, lane < (head + 1) * HEAD_DIM)


def only(value, head):
    return jnp.where(head_lanes(head), value.astype(F32), 0.0)


def high_low(weights, heads):
    high = weights.astype(BF16).astype(F32)
    low = weights - high
    rest = jnp.zeros((LANES - 2 * heads * TAP_ROWS, weights.shape[1]), F32)
    return jnp.transpose(jnp.concatenate([high, low, rest], 0)).astype(BF16)


def front_kernel(
    seqs, count, early,
    hidden_ref, lengths_ref, first_ref, kw_ref, kb_ref, qb_ref, vb_ref, pb_ref, cb_ref, second_ref,
    q_ref, k_ref, v_ref, cv_ref, dl_ref, kc_ref, ca_ref, probs_ref, cc_ref, ctx_ref, lse_ref, second_all_ref,
    marks_ref, taps_ref, depth_ref, expand_ref, inputs_turned_ref, point_turned_ref, early_ref,
    lead_ref, out0_nat, out1_nat, part_out, part_send, part_recv,
    query_ref, key_ref, value_ref, conv_ref, point_ref, vec_ref, bias_ref, depth_wide, tile,
    masks, rows_pad, conv_pad, columns, weights, query_turned, value_turned, context_turned, tap_out, tap_in,
    send_sem, recv_sem, own_sem, gather_send, gather_recv,
):
    s = pl.program_id(0)
    mp, core, side, deep, parts = places(count)
    me = index_of(deep, side, core)
    rows, model = hidden_ref.shape
    chunks = model // LANES
    heads = probs_ref.shape[1] // TAP_ROWS
    tap_rows = heads * TAP_ROWS
    beside = index_of(deep, 1 - side, core)
    twin = index_of(deep, side, 1 - core)

    split = lead_ref.shape[1]
    spans = [pl.ds(0, split), pl.ds(split, second_ref.shape[1] - split)]

    def push(group, source, block, target, slot):
        return pltpu.make_async_remote_copy(
            src_ref=source.at[spans[group]],
            dst_ref=second_all_ref.at[block, spans[group]],
            send_sem=gather_send.at[group, slot],
            recv_sem=gather_recv.at[group, block],
            device_id=at(target, mp),
            device_id_type=MESH,
        )

    def arrive(group, block):
        pltpu.make_async_copy(
            second_ref.at[0, spans[group]], second_all_ref.at[block, spans[group]], gather_recv.at[group, block]
        ).wait()

    own_copy = pltpu.make_async_copy(second_ref.at[0], second_all_ref.at[me], own_sem.at[0])
    lead_copy = pltpu.make_async_copy(second_all_ref.at[:, spans[0]], lead_ref, own_sem.at[1])
    first_hops = [(me, index_of(lax.rem(deep + k, parts), side, core), k - 1) for k in range(1, parts)]
    first_hops += [(me, beside, parts - 1), (me, twin, parts)]
    second_hops = [(beside, [(twin, parts + 1)])]
    for k in range(1, parts):
        block = index_of(lax.rem(deep + parts - k, parts), side, core)
        second_hops.append((block, [(beside, parts + 2 * k), (twin, parts + 2 * k + 1)]))
    third_hops = [
        (index_of(lax.rem(deep + parts - k, parts), 1 - side, core), [(twin, 3 * parts + k - 1)]) for k in range(1, parts)
    ]

    def start_hops(group):
        for block, target, place in first_hops:
            push(group, second_ref.at[0], block, target, place).start()

    def pass_on(group, hops):
        for block, targets in hops:
            arrive(group, block)
            for target, place in targets:
                push(group, second_all_ref.at[block], block, target, place).start()

    def end_hops(group):
        for k in range(parts):
            for other in range(2):
                arrive(group, index_of(lax.rem(deep + parts - k, parts), other, 1 - core))
        for block, target, place in first_hops:
            push(group, second_ref.at[0], block, target, place).wait_send()
        for block, targets in second_hops + third_hops:
            for target, place in targets:
                push(group, second_all_ref.at[block], block, target, place).wait_send()

    def swap_part(which, piece):
        size = rows // PIECES
        return pltpu.make_async_remote_copy(
            src_ref=part_out.at[which, pl.ds(piece * size, size)],
            dst_ref=early_ref.at[pl.ds(which * rows + piece * size, size)],
            send_sem=part_send.at[which, piece],
            recv_sem=part_recv.at[which, piece],
            device_id=at(me, 1 - mp),
            device_id_type=MESH,
        )

    @pl.when(s == 0)
    def _():
        barrier = pltpu.get_barrier_semaphore()
        pl.semaphore_signal(barrier, inc=1, device_id=at(me, 1 - mp), device_id_type=MESH)
        peers = [index_of(lax.rem(deep + k, parts), side, core) for k in range(1, parts)] + [beside, twin]
        for peer in peers:
            pl.semaphore_signal(barrier, inc=1, device_id=at(peer, mp), device_id_type=MESH)
        pl.semaphore_wait(barrier, len(peers) + 1)
        own_copy.start()
        start_hops(0)
        start_hops(1)
        width = heads * HEAD_DIM
        cut = model // CUTS
        for target, place, low in (
            (query_ref, 0, 0), (key_ref, 0, width), (value_ref, 1, 0), (conv_ref, 1, width), (point_ref, 2, 0),
            (depth_wide, 2, width),
        ):
            unpack_wide(target, first_ref, place * cut, low, width)
        depth_ref[...] = jnp.transpose(depth_wide[:, :LANES])[:TAP_ROWS]
        vec_ref[...] = jnp.zeros_like(vec_ref)
        for row, source in enumerate((qb_ref, vb_ref, pb_ref, cb_ref)):
            vec_ref[row : row + 1, :width] = as_row(source[...])
        write_expansion(expand_ref, heads)
        chosen = tap_places(heads, mp)
        tile[...] = jnp.zeros_like(tile)
        tile[:1, : kb_ref.shape[0]] = as_row(kb_ref[...])
        bias = jnp.sum(jnp.where(chosen, tile[:1, :LANES], 0.0), axis=1, keepdims=True)
        bias_ref[...] = jnp.broadcast_to(bias[:tap_rows], bias_ref.shape)
        tile[: kw_ref.shape[0], :width] = kw_ref[...].astype(F32)
        turned_weight = tile[:LANES, :].astype(BF16)
        taps_ref[...] = nn(jnp.where(chosen, 1.0, 0.0).astype(BF16), turned_weight).astype(BF16)
        for place, source in enumerate((query_ref, key_ref, value_ref, conv_ref)):
            inputs_turned_ref[place * WIDE : (place + 1) * WIDE, :] = jnp.transpose(source[...])
        point_turned_ref[...] = jnp.transpose(point_ref[...])
        rows_pad[:, :EDGE, :] = jnp.zeros((chunks, EDGE, LANES), F32)
        rows_pad[:, pl.ds(EDGE + rows, EDGE), :] = jnp.zeros((chunks, EDGE, LANES), F32)
        conv_pad[:, :EDGE, :] = jnp.zeros((2, EDGE, LANES), F32)
        conv_pad[:, pl.ds(EDGE + rows, EDGE), :] = jnp.zeros((2, EDGE, LANES), F32)

    write_marks(lengths_ref, s, marks_ref)
    spread_marks(marks_ref, columns)
    hidden = hidden_ref[...]
    for c in range(chunks):
        rows_pad[c, pl.ds(EDGE, rows), :] = hidden[:, c * LANES : (c + 1) * LANES].astype(F32)

    step = masks.shape[1]

    def depth_step(i, carry):
        base = pl.multiple_of(i * step, step)
        part = pl.ds(base, step)
        for tap in range(KERNEL):
            masks[tap] = jnp.broadcast_to(columns[part, tap : tap + 1], (step, LANES))
        for first in range(0, chunks, 2):
            total = [jnp.zeros((step, LANES), F32)] * 2
            for tap in range(KERNEL):
                mask = masks[tap]
                for k in range(2):
                    c = first + k
                    moved = rows_pad[c, pl.ds(base + EDGE + tap - HALF, step), :]
                    total[k] = total[k] + (moved * mask) * depth_ref[tap : tap + 1, c * LANES : (c + 1) * LANES]
            for k in range(2):
                dl_ref[part, (first + k) * LANES : (first + k + 1) * LANES] = total[k].astype(BF16)
        return carry

    lax.fori_loop(0, rows // step, depth_step, 0)

    @pl.when(s == 0)
    def _():
        pass_on(0, second_hops)

    queries = (nn(hidden, query_ref[...]) + vec_ref[0:1, :]).astype(BF16)
    q_ref[...] = queries
    key_conv = nn(dl_ref[...], point_ref[...]) + vec_ref[2:3, :]
    kc_ref[...] = key_conv
    conv_attn = (key_conv * queries.astype(F32)).astype(BF16)
    ca_ref[...] = conv_attn
    tap_terms = nt(taps_ref[...], conv_attn)
    slot = lax.rem(s, 2)
    tap_out[slot] = tap_terms[tap_rows : 2 * tap_rows]
    swap_taps = pltpu.make_async_remote_copy(
        src_ref=tap_out.at[slot],
        dst_ref=tap_in.at[slot],
        send_sem=send_sem.at[slot],
        recv_sem=recv_sem.at[slot],
        device_id=at(me, 1 - mp),
        device_id_type=MESH,
    )
    swap_taps.start()

    @pl.when(jnp.logical_and(s >= 1, s < early))
    def _():
        for piece in range(PIECES // 2, PIECES):
            swap_part(s - 1, piece).start()

    own_terms = tap_terms[:tap_rows]
    k_ref[...] = nn(hidden, key_ref[...]).astype(BF16)
    v_ref[...] = (nn(hidden, value_ref[...]) + vec_ref[1:2, :]).astype(BF16)
    conv_values = nn(hidden, conv_ref[...]) + vec_ref[3:4, :]
    cv_ref[...] = conv_values
    for c in range(2):
        conv_pad[c, pl.ds(EDGE, rows), :] = conv_values[:, c * LANES : (c + 1) * LANES]

    block = 256
    query_turned[...] = jnp.transpose(q_ref[...])
    value_turned[...] = jnp.transpose(v_ref[...])
    for start in range(0, rows, block):
        part = slice(start, start + block)
        keys = key_window(start, block, rows)
        allowed = columns[keys, KERNEL : KERNEL + 1] == marks_ref[0, KERNEL : KERNEL + 1, part]
        for head in range(heads):
            lanes = slice(head * HEAD_DIM, (head + 1) * HEAD_DIM)
            mine = (only_rows(query_turned[:, part], head) * (HEAD_DIM**-0.5)).astype(BF16)
            scores = jnp.where(allowed, nn(k_ref[keys, :], mine), MASK_FILL)
            top = jnp.max(scores, axis=0, keepdims=True)
            exponent = jnp.exp(scores - top)
            amount = jnp.sum(exponent, axis=0, keepdims=True)
            context_turned[lanes, part] = nn(value_turned[lanes, keys], exponent.astype(BF16)) * (1.0 / amount)
            lse_ref[0, head : head + 1, part] = top + jnp.log(amount)
    lse_ref[0, heads:, :] = jnp.zeros((8 - heads, rows), F32)
    context_turned[heads * HEAD_DIM :, :] = jnp.zeros((WIDE - heads * HEAD_DIM, rows), F32)
    ctx_ref[...] = jnp.transpose(context_turned[...]).astype(BF16)

    @pl.when(s == 0)
    def _():
        pass_on(0, third_hops)


    swap_taps.wait()
    logits = (own_terms + tap_in[slot] + bias_ref[:, :1]).reshape(heads, TAP_ROWS, rows)
    tap = lax.broadcasted_iota(jnp.int32, (heads, TAP_ROWS, rows), 1)
    logits = jnp.where(tap < KERNEL, logits, MASK_FILL)
    exponent = jnp.exp(logits - jnp.max(logits, axis=1, keepdims=True))
    probs = exponent / jnp.sum(exponent, axis=1, keepdims=True)
    probs_ref[0] = probs.reshape(tap_rows, rows)
    tap_mask = jnp.where(tap[0] < KERNEL, marks_ref[0], 0.0)
    weights[...] = high_low((probs * tap_mask[None]).reshape(tap_rows, rows), heads)
    conv_block = 128

    def conv_step(i, carry):
        base = pl.multiple_of(i * conv_block, conv_block)
        part = pl.ds(base, conv_block)
        scale = nn(weights[part, :], expand_ref[...])
        for c in range(2):
            total = jnp.zeros((conv_block, LANES), F32)
            for tap in range(KERNEL):
                low = tap * WIDE + c * LANES
                moved = conv_pad[c, pl.ds(base + EDGE + tap - HALF, conv_block), :]
                total = total + scale[:, low : low + LANES] * moved
            cc_ref[part, c * LANES : (c + 1) * LANES] = total.astype(BF16)
        return carry

    lax.fori_loop(0, rows // conv_block, conv_step, 0)

    @pl.when(s == 0)
    def _():
        own_copy.wait()
        end_hops(0)
        pass_on(1, second_hops)
        if early:
            lead_copy.start()
            lead_copy.wait()
            width = heads * HEAD_DIM
            for target, low in ((out0_nat, 0), (out1_nat, width)):
                unpack_wide(depth_wide, lead_ref, 0, low, width)
                target[...] = jnp.transpose(depth_wide[...].astype(BF16))

    @pl.when(s < early)
    def _():
        half = model // 2
        theirs = pl.ds(pl.multiple_of((1 - mp) * half, half), half)

        def part_step(i, carry):
            part = pl.ds(pl.multiple_of(i * block, block), block)
            other = nn(ctx_ref[part, :], out0_nat[:, theirs]) + nn(cc_ref[part, :], out1_nat[:, theirs])
            part_out[s, part, :] = other.astype(BF16)
            return carry

        lax.fori_loop(0, jnp.where(s == early - 1, rows // 2 // block, rows // block), part_step, 0)
        for piece in range(PIECES // 2):
            swap_part(s, piece).start()

    @pl.when(s == min(1, seqs - 1))
    def _():
        pass_on(1, third_hops)

    @pl.when(s == seqs - 1)
    def _():
        end_hops(1)
        for which in range(early):
            for piece in range(PIECES if which < early - 1 else PIECES // 2):
                swap_part(which, piece).wait()


def whole():
    return pl.BlockSpec(memory_space=pltpu.VMEM)


def by_seq(rows, columns):
    return pl.BlockSpec((rows, columns), lambda s: (s, 0))


def by_seq_row(rows, columns):
    return pl.BlockSpec((1, rows, columns), lambda s: (s, 0, 0))


def front(hidden, lengths, first, kernel_weight, biases, second, count, early, ident):
    seqs = lengths.shape[0]
    tokens, model = hidden.shape
    rows = tokens // seqs
    tap_rows = kernel_weight.shape[1] // HEAD_DIM * TAP_ROWS
    parts = count // 4
    place = pl.BlockSpec(memory_space=pl.ANY)
    share = model // count
    split = share + -share % TAP_ROWS

    def wide(kind):
        return jax.ShapeDtypeStruct((tokens, WIDE), kind)

    return pl.pallas_call(
        functools.partial(front_kernel, seqs, count, early),
        grid=(seqs,),
        out_shape=(
            wide(BF16), wide(BF16), wide(BF16), wide(F32),
            jax.ShapeDtypeStruct((tokens, model), BF16),
            wide(F32), wide(BF16),
            jax.ShapeDtypeStruct((seqs, tap_rows, rows), F32),
            wide(BF16), wide(BF16),
            jax.ShapeDtypeStruct((seqs, 8, rows), F32),
            jax.ShapeDtypeStruct((count,) + second.shape[1:], BF16),
            jax.ShapeDtypeStruct((seqs, TAP_ROWS, rows), F32),
            jax.ShapeDtypeStruct((LANES, WIDE), BF16),
            jax.ShapeDtypeStruct((TAP_ROWS, model), F32),
            jax.ShapeDtypeStruct((LANES, KERNEL * WIDE), BF16),
            jax.ShapeDtypeStruct((4 * WIDE, model), BF16),
            jax.ShapeDtypeStruct((WIDE, model), BF16),
            jax.ShapeDtypeStruct((tokens, model // 2), BF16),
        ),
        in_specs=[by_seq(rows, model), pl.BlockSpec(memory_space=pltpu.SMEM)] + [whole()] * 7 + [place],
        out_specs=(
            by_seq(rows, WIDE), by_seq(rows, WIDE), by_seq(rows, WIDE), by_seq(rows, WIDE), by_seq(rows, model),
            by_seq(rows, WIDE), by_seq(rows, WIDE), by_seq_row(tap_rows, rows), by_seq(rows, WIDE), by_seq(rows, WIDE),
            by_seq_row(8, rows), place, by_seq_row(TAP_ROWS, rows),
        )
        + (whole(),) * 5
        + (place,),
        scratch_shapes=[
            pltpu.VMEM((count, split, second.shape[2]), BF16),
            pltpu.VMEM((WIDE, model), BF16),
            pltpu.VMEM((WIDE, model), BF16),
            pltpu.VMEM((max(early, 1), rows, model // 2), BF16),
            pltpu.SemaphoreType.DMA((max(early, 1), PIECES)),
            pltpu.SemaphoreType.DMA((max(early, 1), PIECES)),
        ]
        + [pltpu.VMEM((model, WIDE), BF16)] * 5
        + [
            pltpu.VMEM((8, WIDE), F32),
            pltpu.VMEM((tap_rows, LANES), F32),
            pltpu.VMEM((model, WIDE), F32),
            pltpu.VMEM((WIDE, WIDE), F32),
            pltpu.VMEM((KERNEL, 64, LANES), F32),
            pltpu.VMEM((model // LANES, rows + 2 * EDGE, LANES), F32),
            pltpu.VMEM((2, rows + 2 * EDGE, LANES), F32),
            pltpu.VMEM((rows, LANES), F32),
            pltpu.VMEM((rows, LANES), BF16),
            pltpu.VMEM((WIDE, rows), BF16),
            pltpu.VMEM((WIDE, rows), BF16),
            pltpu.VMEM((WIDE, rows), F32),
            pltpu.VMEM((2, tap_rows, rows), F32),
            pltpu.VMEM((2, tap_rows, rows), F32),
            pltpu.SemaphoreType.DMA((2,)),
            pltpu.SemaphoreType.DMA((2,)),
            pltpu.SemaphoreType.DMA((2,)),
            pltpu.SemaphoreType.DMA((2, 4 * parts - 1)),
            pltpu.SemaphoreType.DMA((2, count)),
        ],
        compiler_params=pltpu.CompilerParams(
            collective_id=ident, has_side_effects=True, vmem_limit_bytes=62 << 20
        ),
        name="front",
    )(hidden, lengths, first, kernel_weight, *biases, second)


def stat_rows(columns):
    rows = columns[0].shape[0]
    diagonal = lax.broadcasted_iota(jnp.int32, (rows, rows), 0) == lax.broadcasted_iota(jnp.int32, (rows, rows), 1)
    lines = [jnp.sum(jnp.where(diagonal, column, 0.0), axis=0, keepdims=True) for column in columns]
    return jnp.concatenate(lines + [jnp.zeros((8 - len(lines), rows), F32)], 0)


def stat_columns(lines):
    rows = lines[0].shape[1]
    wide = jnp.concatenate(lines + [jnp.zeros((LANES - len(lines), rows), F32)], 0)
    tall = jnp.transpose(wide)
    return [tall[:, k : k + 1] for k in range(len(lines))]


def row_sums(value):
    rows, columns = value.shape
    return jnp.sum(value.reshape(rows // 8, 8, columns), axis=0)


SLOTS = 4
LAST_LAG = 6
FFN_STEP = 256


def middle_kernel(
    blocks, early,
    early_ref, context_ahead_ref, conv_ahead_ref, context_ref, conv_ref, context_late_ref, conv_late_ref, hidden_ref, grad_ref, grad_late_ref, second_ref,
    ob_ref, gain1_ref, bias1_ref, outb_ref, gain2_ref, bias2_ref, inb_ref,
    output_ref, residual_ref, grad_context_ref, grad_conv_ref, pack_ref, small_ref,
    out0_ref, out1_ref, inner_ref, outer_ref, vec_ref, inner_nat, outer_turned, out0_nat, out1_nat, low_units, branch_ref, acc_out0, acc_out1, state, scale_ring, act_ring, slope_ring, low_ring, summed_ring, normed_ring, stat_ring,
    acc_inner, acc_outer, acc_small, acc_bias,
    branch_send, branch_recv, branch_out, branch_in, stat1_out, stat1_in, stat2_out, stat2_in, stat3_out, stat3_in, back_out, back_in,
    send_sem, recv_sem,
):
    i = pl.program_id(0)
    me = lax.axis_index("mp")
    dp = lax.axis_index("dp")
    width = summed_ring.shape[2]
    hidden_units = inner_ref.shape[0]
    inverse = 1.0 / (2 * width)

    def message(kind, source, target, slot):
        return pltpu.make_async_remote_copy(
            src_ref=source.at[slot],
            dst_ref=target.at[slot],
            send_sem=send_sem.at[kind, slot],
            recv_sem=recv_sem.at[kind, slot],
            device_id=(dp, 1 - me),
            device_id_type=MESH,
        )

    def ahead(slot):
        return pltpu.make_async_remote_copy(
            src_ref=branch_out.at[slot],
            dst_ref=branch_in.at[slot],
            send_sem=branch_send.at[slot],
            recv_sem=branch_recv.at[slot],
            device_id=(dp, 1 - me),
            device_id_type=MESH,
        )

    kinds = [
        None, (stat1_out, stat1_in), (stat2_out, stat2_in), (stat3_out, stat3_in), (back_out, back_in),
    ]

    def fresh(kind, b, slot):
        @pl.when(b >= SLOTS)
        def _():
            message(kind, *kinds[kind], slot).wait_send()

    def vec(row):
        return vec_ref[row : row + 1, :width]

    @pl.when(i == 0)
    def _():
        barrier = pltpu.get_barrier_semaphore()
        pl.semaphore_signal(barrier, inc=1, device_id=(dp, 1 - me), device_id_type=MESH)
        pl.semaphore_wait(barrier, 1)
        cut, cut_ffn = 2 * width // CUTS, hidden_units // CUTS
        unpack_wide(out0_ref, second_ref, 0, 0, width // 2)
        unpack_wide(out1_ref, second_ref, 0, width // 2, width // 2)
        for k in range(CUTS):
            inner_ref[pl.ds(k * cut_ffn, cut_ffn), :] = second_ref[k, pl.ds(cut, cut_ffn), :]
            outer_ref[pl.ds(k * cut_ffn, cut_ffn), :] = second_ref[k, pl.ds(cut + cut_ffn, cut_ffn), :]
        for row, source in enumerate((ob_ref, gain1_ref, bias1_ref)):
            value = as_row(source[...])
            vec_ref[row : row + 1, :width] = jnp.where(me == 0, value[:, :width], value[:, width:])
        for row, source in enumerate((outb_ref, gain2_ref, bias2_ref)):
            vec_ref[3 + row : 4 + row, :width] = as_row(source[...])
        vec_ref[7:8, :] = inb_ref[...]
        inner_nat[...] = jnp.transpose(inner_ref[...])
        outer_turned[...] = jnp.transpose(outer_ref[...])
        out0_nat[...] = jnp.transpose(out0_ref[...])
        out1_nat[...] = jnp.transpose(out1_ref[...])
        acc_inner[...] = jnp.zeros_like(acc_inner)
        acc_outer[...] = jnp.zeros_like(acc_outer)
        acc_out0[...] = jnp.zeros_like(acc_out0)
        acc_out1[...] = jnp.zeros_like(acc_out1)
        acc_small[...] = jnp.zeros_like(acc_small)
        acc_bias[...] = jnp.zeros_like(acc_bias)

    cuts = branch_in.shape[0] // (blocks - early)

    @pl.when(i < cuts * (blocks - early))
    def _():
        theirs = pl.ds(pl.multiple_of((1 - me) * width, width), width)
        other = nn(context_ahead_ref[...], out0_nat[:, theirs]) + nn(conv_ahead_ref[...], out1_nat[:, theirs])
        branch_out[i] = other.astype(BF16)
        ahead(i).start()

    @pl.when(i < blocks)
    def _():
        b = i
        ours = pl.ds(pl.multiple_of(me * width, width), width)
        own = nn(context_ref[...], out0_nat[:, ours]) + nn(conv_ref[...], out1_nat[:, ours])
        state[lax.rem(b, 8)] = hidden_ref[:, ours].astype(F32) + (own + vec(0))

        @pl.when(b < early)
        def _():
            state[lax.rem(b, 8)] += early_ref[...].astype(F32)

    @pl.when(jnp.logical_and(i >= 1, i < blocks + 1))
    def _():
        b = i - 1
        slot = lax.rem(b, SLOTS)
        fresh(1, b, slot)

        @pl.when(b >= early)
        def _():
            size = branch_in.shape[1]
            for k in range(cuts):
                piece = cuts * (b - early) + k
                ahead(piece).wait_recv()
                state[lax.rem(b, 8), pl.ds(k * size, size), :] += branch_in[piece].astype(F32)

        residual = state[lax.rem(b, 8)]
        total = jnp.sum(residual, axis=1, keepdims=True)
        apart = residual - total * (1.0 / width)
        stat1_out[slot] = stat_rows([total, jnp.sum(apart * apart, axis=1, keepdims=True)])
        message(1, *kinds[1], slot).start()

    @pl.when(jnp.logical_and(i >= 2, i < blocks + 2))
    def _():
        b = i - 2
        slot = lax.rem(b, SLOTS)
        two = lax.rem(b, 2)
        message(1, *kinds[1], slot).wait_recv()
        fresh(2, b, slot)
        ours, theirs = stat1_out[slot], stat1_in[slot]
        mean, scale = moments(ours[0:1], ours[1:2], theirs[0:1], theirs[1:2], width)
        mean, scale = stat_columns([mean, scale])
        standard = (state[lax.rem(b, 8)] - mean) * scale
        state[lax.rem(b, 8)] = standard
        scale_ring[lax.rem(b, 4)] = jnp.broadcast_to(scale, scale_ring.shape[1:])
        normed = standard * vec(1) + vec(2)
        low = normed.astype(BF16)
        low_ring[two] = low
        summed = normed + vec(3)
        for start in range(0, hidden_units, FFN_STEP):
            part = pl.ds(start, FFN_STEP)
            inner = nn(low, inner_nat[:, part]) + vec_ref[7:8, start : start + FFN_STEP]
            cdf = 0.5 * (1.0 + lax.erf(inner * INV_ROOT2))
            act = (inner * cdf).astype(BF16)
            act_ring[two, :, part] = act
            slope_ring[two, :, part] = cdf + inner * jnp.exp(-0.5 * inner * inner) * INV_ROOT_TWO_PI
        summed = summed + nn(act_ring[two], outer_ref[...])
        summed_ring[two] = summed
        scaled = grad_ref[...].astype(F32) * vec(4)
        total = jnp.sum(summed, axis=1, keepdims=True)
        apart = summed - total * (1.0 / width)
        stat2_out[slot] = stat_rows(
            [
                total,
                jnp.sum(apart * apart, axis=1, keepdims=True),
                jnp.sum(scaled, axis=1, keepdims=True),
                jnp.sum(scaled * apart, axis=1, keepdims=True),
            ]
        )
        message(2, *kinds[2], slot).start()

    @pl.when(jnp.logical_and(i >= 3, i < blocks + 3))
    def _():
        b = i - 3
        slot = lax.rem(b, SLOTS)
        two = lax.rem(b, 2)
        message(2, *kinds[2], slot).wait_recv()
        fresh(3, b, slot)
        total, square, grads, cross = [stat2_out[slot][k : k + 1] for k in range(4)]
        total_o, square_o, grads_o, cross_o = [stat2_in[slot][k : k + 1] for k in range(4)]
        mean, scale = moments(total, square, total_o, square_o, width)
        mean_grad = (grads + grads_o) * inverse
        product = cross + cross_o + (total * (1.0 / width) - mean) * grads + (total_o * (1.0 / width) - mean) * grads_o
        mean_product = product * scale * inverse
        mean, scale, mean_grad, mean_product = stat_columns([mean, scale, mean_grad, mean_product])
        standard = (summed_ring[two] - mean) * scale
        output_ref[...] = (standard * vec(4) + vec(5)).astype(BF16)
        gradient = grad_late_ref[...].astype(F32)
        grad_summed = scale * (gradient * vec(4) - mean_grad - standard * mean_product)
        low = grad_summed.astype(BF16)
        acc_small[0] += row_sums(low.astype(F32))
        acc_small[1] += row_sums(gradient * standard)
        acc_small[2] += row_sums(gradient)
        normed_low = low_ring[two]
        grad_normed = grad_summed
        for start in range(0, hidden_units, FFN_STEP):
            part = pl.ds(start, FFN_STEP)
            inner_low = (nn(low, outer_turned[:, part]) * slope_ring[two, :, part]).astype(BF16)
            low_units[:, part] = inner_low
            acc_bias[:, part] += row_sums(inner_low.astype(F32))
            acc_outer[:, part] += tn(low, act_ring[two, :, part])
            acc_inner[:, part] += tn(normed_low, inner_low)
        grad_normed = grad_normed + nn(low_units[...], inner_ref[...])
        normed_ring[two] = grad_normed
        standard1 = state[lax.rem(b, 8)]
        scaled = grad_normed * vec(1)
        acc_small[3] += row_sums(grad_normed * standard1)
        acc_small[4] += row_sums(grad_normed)
        sums = stat_rows(
            [jnp.sum(scaled, axis=1, keepdims=True), jnp.sum(scaled * standard1, axis=1, keepdims=True)]
        )
        stat3_out[slot] = sums
        message(3, *kinds[3], slot).start()

    @pl.when(jnp.logical_and(i >= 4, i < blocks + 4))
    def _():
        b = i - 4
        slot = lax.rem(b, SLOTS)
        message(3, *kinds[3], slot).wait_recv()
        fresh(4, b, slot)
        both = stat3_out[slot] + stat3_in[slot]
        first, second = stat_columns([both[0:1], both[1:2]])
        standard = state[lax.rem(b, 8)]
        scaled = normed_ring[lax.rem(b, 2)] * vec(1)
        residual = scale_ring[lax.rem(b, 4)][:, :1] * (scaled - first * inverse - standard * (second * inverse))
        residual_ref[...] = residual
        low = residual.astype(BF16)
        acc_small[5] += row_sums(low.astype(F32))
        back_out[slot] = low
        message(4, *kinds[4], slot).start()

    @pl.when(i >= LAST_LAG)
    def _():
        b = i - LAST_LAG
        slot = lax.rem(b, SLOTS)
        message(4, *kinds[4], slot).wait_recv()
        theirs = pl.ds(pl.multiple_of((1 - me) * width, width), width)
        ours = pl.ds(pl.multiple_of(me * width, width), width)
        branch_ref[:, ours] = back_out[slot]
        branch_ref[:, theirs] = back_in[slot]
        branch = branch_ref[...]
        grad_context_ref[...] = nn(branch, out0_ref[...]).astype(BF16)
        grad_conv_ref[...] = nn(branch, out1_ref[...]).astype(BF16)
        acc_out0[...] += tn(context_late_ref[...], branch)
        acc_out1[...] += tn(conv_late_ref[...], branch)

    @pl.when(i == blocks + LAST_LAG - 1)
    def _():
        for slot in range(cuts * (blocks - early)):
            ahead(slot).wait_send()
        for kind in range(1, 5):
            for slot in range(SLOTS):
                message(kind, *kinds[kind], slot).wait_send()
        cut, cut_ffn = 2 * width // CUTS, hidden_units // CUTS
        out_grads = jnp.transpose(jnp.concatenate([acc_out0[: width // 2], acc_out1[: width // 2]], 0)).astype(BF16)
        inner_grads = jnp.transpose(acc_inner[...]).astype(BF16)
        outer_grads = jnp.transpose(acc_outer[...]).astype(BF16)
        for k in range(CUTS):
            part_ffn = slice(k * cut_ffn, (k + 1) * cut_ffn)
            pack_ref[k, pl.ds(0, cut), :] = out_grads[k * cut : (k + 1) * cut]
            pack_ref[k, pl.ds(cut, cut_ffn), :] = inner_grads[part_ffn]
            pack_ref[k, pl.ds(cut + cut_ffn, cut_ffn), :] = outer_grads[part_ffn]
        small_ref[...] = jnp.zeros_like(small_ref)
        for row in range(6):
            small_ref[row : row + 1, :width] = jnp.sum(acc_small[row], axis=0, keepdims=True)
        small_ref[6:7, :] = jnp.sum(acc_bias[...], axis=0, keepdims=True)


def middle(early, early_rows, context, conv_context, hidden, out_grad, second, vectors, ident):
    tokens, model = hidden.shape
    width = model // 2
    local = context.shape[1]
    units = vectors[-1].shape[1]
    rows = 256
    blocks = tokens // rows
    early = early // rows

    def block(columns, lag):
        return pl.BlockSpec((rows, columns), lambda i: (jnp.clip(i - lag, 0, blocks - 1), 0))

    cuts = 2 if 2 * early >= blocks else 1
    ahead = pl.BlockSpec((rows // cuts, local), lambda i: (jnp.minimum(cuts * early + i, cuts * blocks - 1), 0))
    whole = pl.BlockSpec(memory_space=pltpu.VMEM)
    stat = pltpu.VMEM((SLOTS, 8, rows), F32)
    half = pltpu.VMEM((SLOTS, rows, width), BF16)
    return pl.pallas_call(
        functools.partial(middle_kernel, blocks, early),
        grid=(blocks + LAST_LAG,),
        out_shape=(
            jax.ShapeDtypeStruct((tokens, width), BF16),
            jax.ShapeDtypeStruct((tokens, width), F32),
            jax.ShapeDtypeStruct((tokens, local), BF16),
            jax.ShapeDtypeStruct((tokens, local), BF16),
            jax.ShapeDtypeStruct((CUTS, (model + 2 * units) // CUTS, width), BF16),
            jax.ShapeDtypeStruct((8, units), F32),
        ),
        in_specs=[
            block(width, 0), ahead, ahead, block(local, 0), block(local, 0), block(local, LAST_LAG), block(local, LAST_LAG), block(model, 0), block(width, 2),
            block(width, 3),
        ]
        + [whole] * 8,
        out_specs=(block(width, 3), block(width, 4), block(local, LAST_LAG), block(local, LAST_LAG), whole, whole),
        scratch_shapes=[
            pltpu.VMEM((model, local), BF16),
            pltpu.VMEM((model, local), BF16),
            pltpu.VMEM((units, width), BF16),
            pltpu.VMEM((units, width), BF16),
            pltpu.VMEM((8, units), F32),
            pltpu.VMEM((width, units), BF16),
            pltpu.VMEM((width, units), BF16),
            pltpu.VMEM((local, model), BF16),
            pltpu.VMEM((local, model), BF16),
            pltpu.VMEM((rows, units), BF16),
            pltpu.VMEM((rows, model), BF16),
            pltpu.VMEM((local, model), F32),
            pltpu.VMEM((local, model), F32),
            pltpu.VMEM((8, rows, width), F32),
            pltpu.VMEM((4, rows, 128), F32),
            pltpu.VMEM((2, rows, units), BF16),
            pltpu.VMEM((2, rows, units), F32),
            pltpu.VMEM((2, rows, width), BF16),
            pltpu.VMEM((2, rows, width), F32),
            pltpu.VMEM((2, rows, width), F32),
            pltpu.VMEM((8, 128), F32),
            pltpu.VMEM((width, units), F32),
            pltpu.VMEM((width, units), F32),
            pltpu.VMEM((6, 8, width), F32),
            pltpu.VMEM((8, units), F32),
            pltpu.SemaphoreType.DMA((cuts * (blocks - early),)),
            pltpu.SemaphoreType.DMA((cuts * (blocks - early),)),
            pltpu.VMEM((cuts * (blocks - early), rows // cuts, width), BF16),
            pltpu.VMEM((cuts * (blocks - early), rows // cuts, width), BF16),
            stat, stat, stat, stat, stat, stat, half, half,
            pltpu.SemaphoreType.DMA((5, SLOTS)),
            pltpu.SemaphoreType.DMA((5, SLOTS)),
        ],
        compiler_params=pltpu.CompilerParams(
            collective_id=ident, has_side_effects=True, vmem_limit_bytes=60 << 20
        ),
        name="middle",
    )(early_rows, context, conv_context, context, conv_context, context, conv_context, hidden, out_grad, out_grad, second, *vectors)


def back_kernel(
    seqs, count,
    grad_context, grad_conv_ref, marks_ref, q_ref, k_ref, v_ref, cv_ref, ca_ref, probs_ref, lse_ref,
    hidden_any, residual_any, dl_any, kc_any,
    inputs_ref, point_ref, taps_ref, depth_ref, expand_ref, small_ref, pack_in_ref,
    grad_ref, own_ref, other_ref, pack_ref, table_ref, reduced_ref,
    hidden_ref, residual_ref, dl_ref, kc_ref, load_sem,
    other_out, other_in, other_send, other_recv,
    twin_in, side_in, deep_in, hop_send, hop_recv,
    masks, depth_pad, conv_pad, grad_pad, columns, weights, shifted_weights, tap_terms, products,
    grads, grad_q, grad_k, grad_v, key_turned, probs_all, scores_all, turned_query, rows_total, tap_all,
    acc_in, acc_point, acc_bias, acc_tap, acc_tap_bias, acc_depth,
    tap_out, tap_in, send_sem, recv_sem,
):
    s = pl.program_id(0)
    mp = lax.axis_index("mp")
    dp = lax.axis_index("dp")
    rows, model = hidden_ref.shape
    chunks = model // LANES
    heads = probs_ref.shape[1] // TAP_ROWS
    tap_rows = heads * TAP_ROWS
    half = chunks // 2
    slot = lax.rem(s, 2)
    hops = Hops(count, pack_in_ref, twin_in, side_in, deep_in, hop_send, hop_recv)
    here_rows = pl.ds(pl.multiple_of(s * rows, rows), rows)
    loads = [
        pltpu.make_async_copy(source.at[here_rows], target, load_sem.at[k])
        for k, (source, target) in enumerate(
            [(hidden_any, hidden_ref), (residual_any, residual_ref), (dl_any, dl_ref), (kc_any, kc_ref)]
        )
    ]
    for load in loads:
        load.start()

    def swap_rows(which):
        return pltpu.make_async_remote_copy(
            src_ref=other_out.at[which],
            dst_ref=other_in.at[which],
            send_sem=other_send.at[which],
            recv_sem=other_recv.at[which],
            device_id=(dp, 1 - mp),
            device_id_type=MESH,
        )

    @pl.when(s == 0)
    def _():
        greet_all(count)
        hops.start_first()
        for pad in (depth_pad, conv_pad, grad_pad):
            for start in (0, EDGE + rows):
                pad[:, pl.ds(start, EDGE), :] = jnp.zeros((pad.shape[0], EDGE, LANES), F32)
        for acc in (acc_in, acc_point, acc_bias, acc_tap, acc_tap_bias, acc_depth):
            acc[...] = jnp.zeros_like(acc)

    spread_marks(marks_ref, columns)
    block = 256

    for c in range(2):
        lanes = slice(c * LANES, (c + 1) * LANES)
        grad_pad[c, pl.ds(EDGE, rows), :] = grad_conv_ref[:, lanes].astype(F32)
        conv_pad[c, pl.ds(EDGE, rows), :] = cv_ref[:, lanes]

    probs = probs_ref[0].reshape(heads, TAP_ROWS, rows)
    tap = lax.broadcasted_iota(jnp.int32, (heads, TAP_ROWS, rows), 1)
    tap_mask = jnp.where(tap < KERNEL, jnp.broadcast_to(marks_ref[...], (heads, TAP_ROWS, rows)), 0.0)
    masked = (probs * tap_mask).reshape(tap_rows, rows)
    flat_tap = tap.reshape(tap_rows, rows)
    moved = jnp.zeros_like(masked)
    for j in range(KERNEL):
        turn = (j - HALF) % rows
        turned = pltpu.roll(masked, turn, 1) if turn else masked
        moved = jnp.where(flat_tap == j, turned, moved)
    shifted_weights[...] = high_low(moved, heads)
    conv_block = 128

    def conv_step(i, carry):
        base = pl.multiple_of(i * conv_block, conv_block)
        part = pl.ds(base, conv_block)
        scale = nn(shifted_weights[part, :], expand_ref[...])
        for c in range(2):
            here = grad_pad[c, pl.ds(base + EDGE, conv_block), :]
            total = jnp.zeros((conv_block, LANES), F32)
            for j in range(KERNEL):
                low = j * WIDE + c * LANES
                products[:, low : low + LANES] = (
                    here * conv_pad[c, pl.ds(base + EDGE + j - HALF, conv_block), :]
                ).astype(BF16)
                total = total + scale[:, low : low + LANES] * grad_pad[
                    c, pl.ds(base + EDGE + HALF - j, conv_block), :
                ]
            grads[part, 3 * WIDE + c * LANES : 3 * WIDE + (c + 1) * LANES] = total.astype(BF16)
        tap_terms[part, :] = nt(products[...], expand_ref[...])
        return carry

    lax.fori_loop(0, rows // conv_block, conv_step, 0)
    grad_taps = jnp.transpose(tap_terms[...])[:tap_rows].reshape(heads, TAP_ROWS, rows) * tap_mask
    grad_logits = probs * (grad_taps - jnp.sum(probs * grad_taps, axis=1, keepdims=True))
    grad_logits = grad_logits.reshape(tap_rows, rows).astype(BF16)
    tap_out[slot] = grad_logits
    swap_taps = pltpu.make_async_remote_copy(
        src_ref=tap_out.at[slot],
        dst_ref=tap_in.at[slot],
        send_sem=send_sem.at[slot],
        recv_sem=recv_sem.at[slot],
        device_id=(dp, 1 - mp),
        device_id_type=MESH,
    )
    swap_taps.start()

    grad_k[...] = jnp.zeros_like(grad_k)
    grad_v[...] = jnp.zeros_like(grad_v)

    key_turned[...] = jnp.transpose(k_ref[...])
    for start in range(0, rows, block):
        part = slice(start, start + block)
        keys = key_window(start, block, rows)
        allowed = columns[keys, KERNEL : KERNEL + 1] == marks_ref[0, KERNEL : KERNEL + 1, part]
        query, context = q_ref[part, :], grad_context[part, :]
        query_turned, context_turned = jnp.transpose(query), jnp.transpose(context)
        for head in range(heads):
            lanes = slice(head * HEAD_DIM, (head + 1) * HEAD_DIM)
            place = slice(head * block, (head + 1) * block)
            mine = (only_rows(query_turned, head) * (HEAD_DIM**-0.5)).astype(BF16)
            scores = jnp.where(allowed, nn(k_ref[keys, :], mine), MASK_FILL)
            probs = jnp.exp(scores - lse_ref[0, head : head + 1, part])
            probs_all[keys, place] = probs.astype(BF16)
            mixed = probs * nn(v_ref[keys, :], only_rows(context_turned, head).astype(BF16))
            grad_scores = (mixed - probs * jnp.sum(mixed, axis=0, keepdims=True)).astype(BF16)
            scores_all[keys, place] = grad_scores
            turned_query[lanes, :] = nn(key_turned[lanes, keys], grad_scores)
        turned_query[heads * HEAD_DIM :, :] = jnp.zeros((WIDE - heads * HEAD_DIM, block), F32)
        grad_q[part, :] = jnp.transpose(turned_query[...])
        contexts = jnp.concatenate([only(context, head).astype(BF16) for head in range(heads)], 0)
        queries = jnp.concatenate([(only(query, head) * (HEAD_DIM**-0.5)).astype(BF16) for head in range(heads)], 0)
        grad_v[keys, :] += nn(probs_all[keys, :], contexts)
        grad_k[keys, :] += nn(scores_all[keys, :], queries)

    for load in loads:
        load.wait()
    swap_taps.wait()
    tap_all[...] = jnp.zeros_like(tap_all)
    tap_all[:tap_rows, :] = tap_out[slot].astype(F32)
    tap_all[tap_rows : 2 * tap_rows, :] = tap_in[slot].astype(F32)
    every = tap_all[...]
    acc_tap[...] += nn(every.astype(BF16), ca_ref[...])
    acc_tap_bias[...] += sum(every[:, c * LANES : (c + 1) * LANES] for c in range(rows // LANES))
    weights[...] = jnp.transpose(every).astype(BF16)

    def key_step(i, carry):
        base = pl.multiple_of(i * block, block)
        part = pl.ds(base, block)
        grad_attn = nn(weights[part, :], taps_ref[...]).astype(BF16).astype(F32)
        query = q_ref[part, :].astype(F32)
        key_low = (grad_attn * query).astype(BF16)
        grads[part, 4 * WIDE : 5 * WIDE] = key_low
        grad_query = grad_q[part, :] * (HEAD_DIM**-0.5) + grad_attn * kc_ref[part, :]
        grads[part, :WIDE] = grad_query.astype(BF16)
        grads[part, WIDE : 2 * WIDE] = grad_k[part, :].astype(BF16)
        grads[part, 2 * WIDE : 3 * WIDE] = grad_v[part, :].astype(BF16)
        acc_bias[...] += row_sums(grads[part, :].astype(F32))
        grad_depth = nn(key_low, point_ref[...])
        total = nn(grads[part, : 4 * WIDE], inputs_ref[...])
        for c in range(chunks):
            lanes = slice(c * LANES, (c + 1) * LANES)
            depth_pad[c, pl.ds(base + EDGE, block), :] = grad_depth[:, lanes]
            rows_total[c, part, :] = total[:, lanes]
        return carry

    lax.fori_loop(0, rows // block, key_step, 0)
    acc_point[...] += tn(grads[:, 4 * WIDE : 5 * WIDE], dl_ref[...])
    acc_in[...] += tn(hidden_ref[...], grads[:, : 4 * WIDE])
    step = masks.shape[1]

    def depth_step(i, carry):
        base = pl.multiple_of(i * step, step)
        part = pl.ds(base, step)
        for j in range(KERNEL):
            masks[j] = jnp.broadcast_to(columns[part, j : j + 1], (step, LANES))
        for first in range(0, chunks, 2):
            total = [rows_total[first + k, part, :] for k in range(2)]
            lanes = [slice((first + k) * LANES, (first + k + 1) * LANES) for k in range(2)]
            here = [hidden_ref[part, lanes[k]].astype(F32) for k in range(2)]
            for j in range(KERNEL):
                mirror = KERNEL - 1 - j
                mask = masks[j]
                for k in range(2):
                    near = depth_pad[first + k, pl.ds(base + EDGE + j - HALF, step), :] * mask
                    total[k] = total[k] + near * depth_ref[mirror : mirror + 1, lanes[k]]
                    acc_depth[mirror, :, lanes[k]] += row_sums(near * here[k])
            for k in range(2):
                rows_total[first + k, part, :] = total[k]
        return carry

    lax.fori_loop(0, rows // step, depth_step, 0)

    @pl.when(s >= 1)
    def _():
        which = s - 1
        swap_rows(which).wait_recv()
        grad_ref[...] = own_ref[...] + other_in[which].astype(F32)

    for c in range(half):
        lanes = slice(c * LANES, (c + 1) * LANES)
        own_ref[:, lanes] = rows_total[mp * half + c] + residual_ref[:, lanes]

    @pl.when(s < seqs - 1)
    def _():
        for c in range(half):
            lanes = slice(c * LANES, (c + 1) * LANES)
            other_out[s, :, lanes] = rows_total[(1 - mp) * half + c].astype(BF16)
        swap_rows(s).start()

    @pl.when(s == 0)
    def _():
        hops.start_second()

    @pl.when(s == min(1, seqs - 1))
    def _():
        hops.start_third()

    @pl.when(s == seqs - 1)
    def _():
        for c in range(half):
            lanes = slice(c * LANES, (c + 1) * LANES)
            other_ref[:, lanes] = rows_total[(1 - mp) * half + c].astype(BF16)
        hops.finish(reduced_ref)
        for which in range(seqs - 1):
            swap_rows(which).wait_send()
        width = heads * HEAD_DIM
        group = model // 2
        cut = model // CUTS
        empty = jnp.zeros((cut, width), F32)
        point_grad = jnp.transpose(acc_point[...])
        for k in range(CUTS):
            part = pl.ds(k * cut, cut)
            for place in range(2):
                first = acc_in[part, 2 * place * WIDE : 2 * place * WIDE + width]
                second = acc_in[part, (2 * place + 1) * WIDE : (2 * place + 1) * WIDE + width]
                pack_ref[k, pl.ds(place * cut, cut), :] = jnp.concatenate([first, second], 1).astype(BF16)
            pack_ref[k, pl.ds(2 * cut, cut), :] = jnp.concatenate([point_grad[k * cut : (k + 1) * cut, :width], empty], 1).astype(BF16)
        table_ref[...] = jnp.zeros_like(table_ref)
        lane = lax.broadcasted_iota(jnp.int32, (LANES, WIDE), 1)
        taps = jnp.where(lane == width, jnp.sum(acc_tap_bias[...], axis=1, keepdims=True), acc_tap[...])
        own_taps = [taps[h * TAP_ROWS : h * TAP_ROWS + KERNEL] for h in range(heads)]
        other_taps = [taps[tap_rows + h * TAP_ROWS : tap_rows + h * TAP_ROWS + KERNEL] for h in range(heads)]
        for h in range(heads):
            table_ref[KERNEL * h : KERNEL * (h + 1), :] = jnp.where(mp == 0, own_taps[h], other_taps[h])
            later = KERNEL * (heads + h)
            table_ref[later : later + KERNEL, :] = jnp.where(mp == 0, other_taps[h], own_taps[h])
        for row, place in ((54, 0), (55, 2), (56, 4), (57, 3)):
            table_ref[row : row + 1, :] = jnp.sum(acc_bias[:, place * WIDE : (place + 1) * WIDE], axis=0, keepdims=True)

        def lay(row, value):
            for k in range(-(-value.shape[1] // WIDE)):
                piece = value[:, k * WIDE : (k + 1) * WIDE]
                table_ref[row + k : row + k + 1, : piece.shape[1]] = piece

        for row, source in ((58, 0), (60, 1), (62, 2)):
            lay(row, small_ref[source : source + 1, :group])
        lay(64, small_ref[6:7, :])
        for row, source in ((99, 3), (102, 4), (105, 5)):
            value = small_ref[source : source + 1, :group]
            blank = jnp.zeros_like(value)
            lay(row, jnp.where(mp == 0, jnp.concatenate([value, blank], 1), jnp.concatenate([blank, value], 1)))
        for j in range(KERNEL):
            total = jnp.sum(acc_depth[j], axis=0, keepdims=True)
            for k in range(model // WIDE):
                row = TABLE_OWN + KERNEL * k + j
                table_ref[row : row + 1, :] = total[:, k * WIDE : (k + 1) * WIDE]


def back(hidden, grad_context, grad_conv, residual, marks, kept, turned_weights, taps, depth, expand, small, pack, count, ident):
    q, k, v, cv, dl, kc, ca, probs, lse = kept
    seqs, _, rows = marks.shape
    tokens, model = hidden.shape
    width = model // 2
    tap_rows = probs.shape[1]
    wide = by_seq(rows, WIDE)
    place = pl.BlockSpec(memory_space=pl.ANY)
    padded_rows = rows + 2 * EDGE
    vmem = pltpu.VMEM
    swaps = max(seqs - 1, 1)
    return pl.pallas_call(
        functools.partial(back_kernel, seqs, count),
        grid=(seqs,),
        out_shape=(
            jax.ShapeDtypeStruct((tokens, width), F32),
            jax.ShapeDtypeStruct((rows, width), F32),
            jax.ShapeDtypeStruct((rows, width), BF16),
            jax.ShapeDtypeStruct((CUTS, 3 * model // CUTS, width), BF16),
            jax.ShapeDtypeStruct((TABLE_ROWS, WIDE), F32),
            jax.ShapeDtypeStruct(pack.shape[1:], F32),
        ),
        in_specs=[wide, wide, by_seq_row(TAP_ROWS, rows), wide, wide, wide, wide, wide]
        + [by_seq_row(tap_rows, rows), by_seq_row(8, rows)]
        + [place] * 4
        + [whole()] * 7,
        out_specs=(pl.BlockSpec((rows, width), lambda s: (jnp.maximum(s - 1, 0), 0)),) + (whole(),) * 5,
        scratch_shapes=[
            vmem((rows, model), BF16),
            vmem((rows, width), F32),
            vmem((rows, model), BF16),
            vmem((rows, WIDE), F32),
            pltpu.SemaphoreType.DMA((4,)),
            vmem((swaps, rows, width), BF16),
            vmem((swaps, rows, width), BF16),
            pltpu.SemaphoreType.DMA((swaps,)),
            pltpu.SemaphoreType.DMA((swaps,)),
        ]
        + hop_scratch(count, pack.shape[1], pack.shape[2])
        + [
            vmem((KERNEL, 64, LANES), F32),
            vmem((model // LANES, padded_rows, LANES), F32),
            vmem((2, padded_rows, LANES), F32),
            vmem((2, padded_rows, LANES), F32),
            vmem((rows, LANES), F32),
            vmem((rows, LANES), BF16),
            vmem((rows, LANES), BF16),
            vmem((rows, LANES), F32),
            vmem((128, KERNEL * WIDE), BF16),
            vmem((rows, 5 * WIDE), BF16),
            vmem((rows, WIDE), F32),
            vmem((rows, WIDE), F32),
            vmem((rows, WIDE), F32),
            vmem((WIDE, rows), BF16),
            vmem((rows, tap_rows // TAP_ROWS * 256), BF16),
            vmem((rows, tap_rows // TAP_ROWS * 256), BF16),
            vmem((WIDE, 256), F32),
            vmem((model // LANES, rows, LANES), F32),
            vmem((LANES, rows), F32),
            vmem((model, 4 * WIDE), F32),
            vmem((WIDE, model), F32),
            vmem((8, 5 * WIDE), F32),
            vmem((LANES, WIDE), F32),
            vmem((LANES, LANES), F32),
            vmem((TAP_ROWS, 8, model), F32),
            vmem((2, tap_rows, rows), BF16),
            vmem((2, tap_rows, rows), BF16),
            pltpu.SemaphoreType.DMA((2,)),
            pltpu.SemaphoreType.DMA((2,)),
        ],
        compiler_params=pltpu.CompilerParams(
            collective_id=ident, has_side_effects=True, vmem_limit_bytes=63 << 20
        ),
        name="back",
    )(
        grad_context, grad_conv, marks, q, k, v, cv, ca, probs, lse, hidden, residual, dl, kc,
        *turned_weights, taps, depth, expand, small, pack,
    )


def padded(value, multiple):
    rows = value.shape[-2]
    extra = -rows % multiple
    return jnp.pad(value, [(0, 0)] * (value.ndim - 2) + [(0, extra), (0, 0)])


def recut(pack, sizes, unit, start, count):
    if count == start:
        return pack
    parts, low = [], 0
    for size in sizes:
        rows = pack[:, low : low + size * unit].reshape(-1, pack.shape[2])
        parts.append(rows.reshape(count, -1, pack.shape[2]))
        low += size * unit
    return padded(jnp.concatenate(parts, 1), TAP_ROWS)


def gather_plain(weights, count, ident):
    q, k, v, c, p, depth, out_w, in_w, outer_w = weights
    depth = jnp.pad(depth.T, ((0, 0), (0, q.shape[1] - KERNEL)))
    pairs = [jnp.concatenate(pair, 1) for pair in ((q, k), (v, c), (p, depth), (out_w[0], out_w[1]))]
    first = padded(jnp.concatenate(pairs[:3], 0), TAP_ROWS)[None]
    second = padded(jnp.concatenate([pairs[3], in_w[0], outer_w[0]], 0), TAP_ROWS)[None]
    return recut(gather(first, count, ident), (1, 1, 1), q.shape[0], count, CUTS), second


def final_plain(first, second, table, share, share_ffn, width, group, taps):
    model = 2 * group
    depth = jnp.concatenate([table[72 + KERNEL * k : 72 + KERNEL * (k + 1)] for k in range(model // WIDE)], 1)
    row = lambda at_row, size: table[at_row : at_row + 6].reshape(-1)[:size]
    out = first[:share]
    return (
        second[:share, :width], second[:share, width:], second[share : 2 * share, :width],
        row(54, width), row(55, width),
        lax.dynamic_slice_in_dim(depth, lax.axis_index("dp") * share, share, 1),
        second[2 * share : 3 * share, :width], row(56, width),
        table[:taps, :width], table[:taps, width], second[share : 2 * share, width:], row(57, width),
        jnp.stack([out[:, :width], out[:, width:]]), row(105, model), row(99, model), row(102, model),
        first[share : share + share_ffn], row(64, 4 * group)[None], first[share + share_ffn : share + 2 * share_ffn],
        row(58, group), row(60, group), row(62, group),
    )


def on_device(
    count,
    hidden, doc_lengths, query_weight, key_weight, value_weight, query_bias, value_bias,
    depth_weight, point_weight, point_bias, kernel_weight, kernel_bias, conv_weight, conv_bias,
    out_weight, out_bias, norm1_gain, norm1_bias, ffn_in_weight, ffn_in_bias, ffn_out_weight,
    ffn_out_bias, norm2_gain, norm2_bias, out_grad,
):
    share, width = query_weight.shape
    model = hidden.shape[1]
    group = ffn_out_bias.shape[0]
    share_ffn = ffn_out_weight.shape[1]
    heads = width // HEAD_DIM
    weights = (
        query_weight, key_weight, value_weight, conv_weight, point_weight, depth_weight,
        out_weight.transpose(0, 2, 1), ffn_in_weight.transpose(0, 2, 1), ffn_out_weight,
    )
    first, second = (gather_first if share % TAP_ROWS == 0 else gather_plain)(weights, count, 1)
    seqs = doc_lengths.shape[0]
    early = seqs - 1 if count == CUTS else 0
    biases = [kernel_bias, query_bias, value_bias, point_bias, conv_bias]
    q, k, v, cv, dl, kc, ca, probs, cc, ctx, lse, second_all, marks, taps, depth, expand, *rest = front(
        hidden, doc_lengths, first, kernel_weight.T, biases, second, count, early, 2
    )
    turned_weights, early_rows = rest[:2], rest[2]
    vectors = [out_bias, norm1_gain, norm1_bias, ffn_out_bias, norm2_gain, norm2_bias, ffn_in_bias]
    output, grad_residual, grad_context, grad_conv, pack_mid, sums_mid = middle(
        max(2 * early - 1, 0) * (hidden.shape[0] // seqs) // 2, early_rows, ctx, cc, hidden, out_grad, recut(second_all, (1, 2, 2), share, count, CUTS), vectors, 4
    )
    grad_input, own_last, other_last, pack_back, table, first_sum = back(
        hidden, grad_context, grad_conv, grad_residual, marks, (q, k, v, cv, dl, kc, ca, probs, lse),
        turned_weights, taps, depth, expand, sums_mid, recut(pack_mid, (1, 2, 2), model // CUTS, CUTS, count), count, 5,
    )
    second_sum, totals, grad_input = tail(
        recut(pack_back, (1, 1, 1), model // CUTS, CUTS, count), table, own_last, other_last, grad_input, count, 3
    )
    small_cuts = (share, share_ffn, width, group, 2 * heads * KERNEL)
    if share % TAP_ROWS == 0:
        results = final(first_sum, second_sum, totals, *small_cuts, count)
    else:
        results = final_plain(first_sum, second_sum, totals, *small_cuts)
    q_g, k_g, v_g, q_b, v_b, depth_g, p_g, p_b, kw_g, kb_g, c_g, c_b, out_g, out_b, gain1, bias1 = results[:16]
    inner_g, inner_b, outer_g, outer_b, gain2, bias2 = results[16:]
    return (
        output, grad_input, q_g, k_g, v_g, q_b, v_b, depth_g, p_g, p_b, kw_g.T, kb_g, c_g, c_b, out_g.transpose(0, 2, 1),
        out_b, gain1, bias1, inner_g.T[None], inner_b, outer_g[None], outer_b, gain2, bias2,
    )


def solution(mesh):
    in_specs = (
        P("dp", None),
        P("dp", None),
        P("dp", "mp"),
        P("dp", "mp"),
        P("dp", "mp"),
        P("mp"),
        P("mp"),
        P(None, "dp"),
        P("dp", "mp"),
        P("mp"),
        P("mp", None),
        P(),
        P("dp", "mp"),
        P("mp"),
        P(None, "mp", "dp"),
        P(),
        P(),
        P(),
        P("mp", None, "dp"),
        P("mp", None),
        P("mp", "dp", None),
        P("mp"),
        P("mp"),
        P("mp"),
        P("dp", "mp"),
    )
    out_specs = (
        P("dp", "mp"),
        P("dp", "mp"),
        P("dp", "mp"),
        P("dp", "mp"),
        P("dp", "mp"),
        P("mp"),
        P("mp"),
        P(None, "dp"),
        P("dp", "mp"),
        P("mp"),
        P("mp", None),
        P(),
        P("dp", "mp"),
        P("mp"),
        P(None, "mp", "dp"),
        P(),
        P(),
        P(),
        P("mp", None, "dp"),
        P("mp", None),
        P("mp", "dp", None),
        P("mp"),
        P("mp"),
        P("mp"),
    )
    return jax.shard_map(
        functools.partial(on_device, mesh.shape["dp"]), mesh=mesh, in_specs=in_specs, out_specs=out_specs, check_vma=False
    )
```

```python
import functools
import jax
import jax.numpy as jnp
from jax import lax
from jax.experimental import pallas as pl
from jax.experimental.pallas import tpu as pltpu

from jax.sharding import PartitionSpec as P

MESH = pl.DeviceIdType.MESH
BF16 = jnp.bfloat16
F32 = jnp.float32
HEAD_DIM = 64
KERNEL = 9
HALF = KERNEL // 2
CUTS = 16
TABLE_OWN = 72
TABLE_ROWS = 112
TAP_ROWS = 16
WIDE = 256
LANES = 128
EDGE = 8
MOST_DOC = 512


def at(dp, mp):
    return (dp, mp)


def places(count):
    dp = lax.axis_index("dp")
    core = lax.rem(dp, 2)
    side = lax.rem(lax.div(dp, 2), 2)
    deep = lax.div(dp, 4)
    return lax.axis_index("mp"), core, side, deep, count // 4


def index_of(deep, side, core):
    return (deep * 2 + side) * 2 + core


def greet(count):
    mp, core, side, deep, parts = places(count)
    barrier = pltpu.get_barrier_semaphore()
    peers = [index_of(lax.rem(deep + k, parts), side, core) for k in range(1, parts)]
    peers += [index_of(deep, 1 - side, core), index_of(deep, side, 1 - core)]
    for peer in peers:
        pl.semaphore_signal(barrier, inc=1, device_id=at(peer, mp), device_id_type=MESH)
    pl.semaphore_wait(barrier, len(peers))


def turned(tile, value):
    rows, columns = value.shape
    tile[...] = jnp.zeros_like(tile)
    tile[:rows, :columns] = value.astype(F32)
    return jnp.transpose(tile[...])[:columns, :rows]


def beside_each(first, second):
    return jnp.concatenate([first.astype(F32), second.astype(F32)], 1).astype(BF16)


def gather_body(count, own_ref, out_ref, own_sem, send_sem, recv_sem):
    mp, core, side, deep, parts = places(count)
    me = index_of(deep, side, core)
    local = pltpu.make_async_copy(own_ref.at[0], out_ref.at[me], own_sem)
    local.start()
    started = []

    def push(source, block, target):
        copy = pltpu.make_async_remote_copy(
            src_ref=source,
            dst_ref=out_ref.at[block],
            send_sem=send_sem.at[len(started)],
            recv_sem=recv_sem.at[block],
            device_id=at(target, mp),
            device_id_type=MESH,
        )
        copy.start()
        started.append(copy)

    def arrive(block):
        pltpu.make_async_copy(own_ref.at[0], out_ref.at[block], recv_sem.at[block]).wait()

    beside = index_of(deep, 1 - side, core)
    twin = index_of(deep, side, 1 - core)
    for k in range(1, parts):
        push(own_ref.at[0], me, index_of(lax.rem(deep + k, parts), side, core))
    push(own_ref.at[0], me, beside)
    push(own_ref.at[0], me, twin)
    yield
    arrive(beside)
    push(out_ref.at[beside], beside, twin)
    for k in range(1, parts):
        block = index_of(lax.rem(deep + parts - k, parts), side, core)
        arrive(block)
        push(out_ref.at[block], block, beside)
        push(out_ref.at[block], block, twin)
    for k in range(1, parts):
        block = index_of(lax.rem(deep + parts - k, parts), 1 - side, core)
        arrive(block)
        push(out_ref.at[block], block, twin)
    for k in range(parts):
        for other in range(2):
            arrive(index_of(lax.rem(deep + parts - k, parts), other, 1 - core))
    for copy in started:
        copy.wait_send()
    local.wait()
    yield


def gather_kernel(count, own_ref, out_ref, own_sem, send_sem, recv_sem):
    greet(count)
    for _ in gather_body(count, own_ref, out_ref, own_sem, send_sem, recv_sem):
        pass


def pack_kernel(
    count, q_ref, k_ref, v_ref, c_ref, p_ref, depth_ref, out_w_ref, in_w_ref, outer_w_ref,
    out_ref, second_ref,
    own_ref, tile_depth, own_sem, send_sem, recv_sem,
):
    share, width = q_ref.shape
    share_ffn = outer_w_ref.shape[1]
    own_ref[0, :share, :] = beside_each(q_ref[...], k_ref[...])
    own_ref[0, share : 2 * share, :] = beside_each(v_ref[...], c_ref[...])
    depth = turned(tile_depth, depth_ref[...])
    depth = jnp.concatenate([depth, jnp.zeros((share, width - KERNEL), F32)], 1)
    own_ref[0, 2 * share : 3 * share, :] = beside_each(p_ref[...], depth)
    greet(count)
    moves = gather_body(count, own_ref, out_ref, own_sem, send_sem, recv_sem)
    next(moves)
    second_ref[0, :share, :] = beside_each(out_w_ref[0], out_w_ref[1])
    second_ref[0, share : share + share_ffn, :] = in_w_ref[0]
    second_ref[0, share + share_ffn :, :] = outer_w_ref[0]
    next(moves)


def gather_first(weights, count, ident):
    q, depth, out_w, in_w, outer_w = weights[0], weights[5], weights[6], weights[7], weights[8]
    share, width = q.shape
    share_ffn, group = outer_w.shape[1:]
    parts = count // 4
    vmem = pl.BlockSpec(memory_space=pltpu.VMEM)
    return pl.pallas_call(
        functools.partial(pack_kernel, count),
        out_shape=(
            jax.ShapeDtypeStruct((count, 3 * share, 2 * width), BF16),
            jax.ShapeDtypeStruct((1, share + 2 * share_ffn, group), BF16),
        ),
        in_specs=[vmem] * 9,
        out_specs=(pl.BlockSpec(memory_space=pl.ANY), vmem),
        scratch_shapes=[
            pltpu.VMEM((1, 3 * share, 2 * width), BF16),
            pltpu.VMEM((LANES, LANES), F32),
            pltpu.SemaphoreType.DMA,
            pltpu.SemaphoreType.DMA((4 * parts - 1,)),
            pltpu.SemaphoreType.DMA((count,)),
        ],
        compiler_params=pltpu.CompilerParams(collective_id=ident, has_side_effects=True),
        name="weight_gather",
    )(*weights)


def gather(own, count, ident):
    parts = count // 4
    return pl.pallas_call(
        functools.partial(gather_kernel, count),
        out_shape=jax.ShapeDtypeStruct((count,) + own.shape[1:], own.dtype),
        in_specs=[pl.BlockSpec(memory_space=pl.ANY)],
        out_specs=pl.BlockSpec(memory_space=pl.ANY),
        scratch_shapes=[
            pltpu.SemaphoreType.DMA,
            pltpu.SemaphoreType.DMA((4 * parts - 1,)),
            pltpu.SemaphoreType.DMA((count,)),
        ],
        compiler_params=pltpu.CompilerParams(collective_id=ident, has_side_effects=True),
        name="weight_gather",
    )(own)


class Hops:
    def __init__(self, count, in_ref, twin_in, side_in, deep_in, send_sem, recv_sem):
        self.mp, self.core, self.side, self.deep, self.parts = places(count)
        self.in_ref, self.twin_in, self.side_in, self.deep_in = in_ref, twin_in, side_in, deep_in
        self.send_sem, self.recv_sem = send_sem, recv_sem
        self.beside = index_of(self.deep, 1 - self.side, self.core)
        self.twin = index_of(self.deep, self.side, 1 - self.core)
        self.order = [(k, other) for k in list(range(1, self.parts)) + [0] for other in (1, 0)]
        self.rows = in_ref.shape[1]
        self.step = 48 if self.rows % 48 == 0 else 16

    def depth(self, k):
        return lax.rem(self.deep + k, self.parts)

    def copy(self, source, target_ref, slot, target):
        return pltpu.make_async_remote_copy(
            src_ref=source,
            dst_ref=target_ref,
            send_sem=self.send_sem.at[slot],
            recv_sem=self.recv_sem.at[slot],
            device_id=at(target, self.mp),
            device_id_type=MESH,
        )

    def block(self, slot, core):
        k, other = self.order[slot]
        return index_of(self.depth(k), 1 - self.side if other else self.side, core)

    def first(self, slot):
        return self.copy(self.in_ref.at[self.block(slot, 1 - self.core)], self.twin_in.at[slot], slot, self.twin)

    def second(self, place):
        return self.copy(
            self.twin_in.at[2 * place], self.side_in.at[place], 2 * self.parts + place, self.beside
        )

    def third(self, place):
        k = self.order[2 * place][0]
        target = index_of(self.depth(k), self.side, self.core)
        return self.copy(self.side_in.at[place], self.deep_in.at[place], 3 * self.parts + place, target)

    def add(self, target, term):
        @pl.loop(0, self.rows // self.step)
        def _(i):
            part = pl.ds(pl.multiple_of(i * self.step, 16), self.step)
            total = target[part, :].astype(F32) + term[part, :].astype(F32)
            target[part, :] = total.astype(target.dtype)

    def start_first(self):
        for slot in range(2 * self.parts):
            self.first(slot).start()

    def start_second(self):
        for slot in range(2 * self.parts):
            self.first(slot).wait_recv()
            self.add(self.twin_in.at[slot], self.in_ref.at[self.block(slot, self.core)])
            if self.order[slot][1]:
                self.second(slot // 2).start()

    def start_third(self):
        for place in range(self.parts):
            self.second(place).wait_recv()
            self.add(self.side_in.at[place], self.twin_in.at[2 * place + 1])
            if place < self.parts - 1:
                self.third(place).start()

    def finish(self, out_ref):
        for place in range(self.parts - 1):
            self.third(place).wait_recv()

        @pl.loop(0, self.rows // self.step)
        def _(i):
            part = pl.ds(pl.multiple_of(i * self.step, 16), self.step)
            total = self.side_in[self.parts - 1, part, :].astype(F32)
            for place in range(self.parts - 1):
                total = total + self.deep_in[place, part, :].astype(F32)
            out_ref[part, :] = total

        for slot in range(2 * self.parts):
            self.first(slot).wait_send()
        for place in range(self.parts):
            self.second(place).wait_send()
        for place in range(self.parts - 1):
            self.third(place).wait_send()


def hop_scratch(count, rows, columns):
    parts = count // 4
    return [
        pltpu.VMEM((2 * parts, rows, columns), BF16),
        pltpu.VMEM((parts, rows, columns), BF16),
        pltpu.VMEM((max(parts - 1, 1), rows, columns), BF16),
        pltpu.SemaphoreType.DMA((4 * parts - 1,)),
        pltpu.SemaphoreType.DMA((4 * parts - 1,)),
    ]


def greet_all(count):
    mp, core, side, deep, parts = places(count)
    me = index_of(deep, side, core)
    barrier = pltpu.get_barrier_semaphore()
    pl.semaphore_signal(barrier, inc=1, device_id=at(me, 1 - mp), device_id_type=MESH)
    peers = [index_of(lax.rem(deep + k, parts), side, core) for k in range(1, parts)]
    peers += [index_of(deep, 1 - side, core), index_of(deep, side, 1 - core)]
    for peer in peers:
        pl.semaphore_signal(barrier, inc=1, device_id=at(peer, mp), device_id_type=MESH)
    pl.semaphore_wait(barrier, len(peers) + 1)


PIECES = 4


def tail_kernel(
    count, start,
    in_ref, table_ref, own_ref, other_ref, rest_ref,
    out_ref, total_ref, grad_ref,
    twin_in, side_in, deep_in, send_sem, recv_sem,
    table_in, table_out, table_send, table_recv, piece_in, piece_sum, piece_send, piece_recv, store_sem,
):
    mp, core, side, deep, parts = places(count)
    me = index_of(deep, side, core)
    greet_all(count)
    beside = index_of(deep, 1 - side, core)
    twin = index_of(deep, side, 1 - core)
    hops = Hops(count, in_ref, twin_in, side_in, deep_in, send_sem, recv_sem)
    rows = own_ref.shape[0] // PIECES

    def table_hop(source, slot, target, plane):
        return pltpu.make_async_remote_copy(
            src_ref=source,
            dst_ref=table_in.at[slot],
            send_sem=table_send.at[slot],
            recv_sem=table_recv.at[slot],
            device_id=at(target, plane),
            device_id_type=MESH,
        )

    def piece(i):
        part = pl.ds(i * rows, rows)
        return pltpu.make_async_remote_copy(
            src_ref=other_ref.at[part],
            dst_ref=piece_in.at[part],
            send_sem=piece_send.at[i],
            recv_sem=piece_recv.at[i],
            device_id=at(me, 1 - mp),
            device_id_type=MESH,
        )

    def store(i):
        return pltpu.make_async_copy(
            piece_sum.at[pl.ds(i * rows, rows)], grad_ref.at[pl.ds(start + i * rows, rows)], store_sem.at[i]
        )

    shared = pl.ds(TABLE_OWN, TABLE_ROWS - TABLE_OWN)
    first = pltpu.make_async_remote_copy(
        src_ref=table_ref.at[shared],
        dst_ref=table_in.at[0, shared],
        send_sem=table_send.at[0],
        recv_sem=table_recv.at[0],
        device_id=at(me, 1 - mp),
        device_id_type=MESH,
    )
    first.start()
    hops.start_first()
    for i in range(PIECES):
        piece(i).start()
    first.wait_recv()
    table_out[0, :TABLE_OWN, :] = table_ref[:TABLE_OWN, :]
    table_out[0, shared, :] = table_ref[shared, :] + table_in[0, shared, :]
    second = table_hop(table_out.at[0], 1, twin, mp)
    second.start()
    second.wait_recv()
    table_out[1] = table_out[0] + table_in[1]
    third = table_hop(table_out.at[1], 2, beside, mp)
    third.start()
    hops.start_second()
    third.wait_recv()
    table_out[2] = table_out[1] + table_in[2]
    fourth = [
        table_hop(table_out.at[2], 2 + j, index_of(lax.rem(deep + j, parts), side, core), mp) for j in range(1, parts)
    ]
    for copy in fourth:
        copy.start()
    hops.start_third()
    for i in range(PIECES):
        piece(i).wait_recv()
        part = pl.ds(i * rows, rows)
        piece_sum[part, :] = own_ref[part, :] + piece_in[part, :].astype(F32)
        store(i).start()
    hops.finish(out_ref)
    for copy in fourth:
        copy.wait_recv()
    total = table_out[2]
    for j in range(1, parts):
        total = total + table_in[2 + j]
    total_ref[...] = total
    for copy in [first, second, third] + fourth:
        copy.wait_send()
    for i in range(PIECES):
        piece(i).wait_send()
        store(i).wait()


def tail(blocks, table, own, other, grad_rows, count, ident):
    parts = count // 4
    _, rows, columns = blocks.shape
    start = grad_rows.shape[0] - own.shape[0]
    vmem = pl.BlockSpec(memory_space=pltpu.VMEM)
    place = pl.BlockSpec(memory_space=pl.ANY)
    return pl.pallas_call(
        functools.partial(tail_kernel, count, start),
        out_shape=(
            jax.ShapeDtypeStruct((rows, columns), F32),
            jax.ShapeDtypeStruct(table.shape, F32),
            jax.ShapeDtypeStruct(grad_rows.shape, F32),
        ),
        in_specs=[vmem, vmem, vmem, vmem, place],
        out_specs=(vmem, vmem, place),
        input_output_aliases={4: 2},
        scratch_shapes=hop_scratch(count, rows, columns)
        + [
            pltpu.VMEM((parts + 2,) + table.shape, F32),
            pltpu.VMEM((3,) + table.shape, F32),
            pltpu.SemaphoreType.DMA((parts + 2,)),
            pltpu.SemaphoreType.DMA((parts + 2,)),
            pltpu.VMEM(other.shape, BF16),
            pltpu.VMEM(own.shape, F32),
            pltpu.SemaphoreType.DMA((PIECES,)),
            pltpu.SemaphoreType.DMA((PIECES,)),
            pltpu.SemaphoreType.DMA((PIECES,)),
        ],
        compiler_params=pltpu.CompilerParams(
            collective_id=ident, has_side_effects=True, vmem_limit_bytes=60 << 20
        ),
        name="tail",
    )(blocks, table, own, other, grad_rows)


def wide_row(table, row, count):
    return jnp.concatenate([table[row + k : row + k + 1, :] for k in range(count)], 1)


def final_kernel(
    count, first_ref, second_ref, table_ref,
    q_ref, k_ref, v_ref, qb_ref, vb_ref, depth_ref, p_ref, pb_ref, kw_ref, kb_ref, c_ref, cb_ref, out_ref, ob_ref,
    gain1_ref, bias1_ref, inner_ref, inb_ref, outer_ref, outb_ref, gain2_ref, bias2_ref,
    spread,
):
    share, width = q_ref.shape
    share_ffn, group = outer_ref.shape
    q_ref[...] = second_ref[:share, :width]
    k_ref[...] = second_ref[:share, width : 2 * width]
    v_ref[...] = second_ref[share : 2 * share, :width]
    c_ref[...] = second_ref[share : 2 * share, width : 2 * width]
    p_ref[...] = second_ref[2 * share : 3 * share, :width]
    out_ref[0] = first_ref[:share, :width]
    out_ref[1] = first_ref[:share, width : 2 * width]
    inner_ref[...] = first_ref[share : share + share_ffn, :]
    outer_ref[...] = first_ref[share + share_ffn : share + 2 * share_ffn, :]
    taps = kb_ref.shape[0]
    kw_ref[...] = table_ref[:taps, :width]
    rows = jnp.transpose(jnp.concatenate([table_ref[:64, LANES:], jnp.zeros((64, LANES), F32)], 0))
    kb_ref[...] = rows[width - LANES : width - LANES + 1, :taps].reshape(taps)
    for target, row in ((qb_ref, 54), (vb_ref, 55), (pb_ref, 56), (cb_ref, 57)):
        target[...] = table_ref[row : row + 1, :width].reshape(width)
    for target, row in ((outb_ref, 58), (gain2_ref, 60), (bias2_ref, 62)):
        target[...] = wide_row(table_ref, row, 2)[:, :group].reshape(group)
    inb_ref[...] = wide_row(table_ref, 64, 6)
    for target, row in ((gain1_ref, 99), (bias1_ref, 102), (ob_ref, 105)):
        target[...] = wide_row(table_ref, row, 3).reshape(2 * group)
    spread[...] = jnp.zeros_like(spread)
    for k in range(3):
        spread[:KERNEL, k * WIDE : (k + 1) * WIDE] = table_ref[72 + KERNEL * k : 72 + KERNEL * (k + 1), :]
    model = spread.shape[1]
    dp = lax.axis_index("dp")
    moved = pltpu.roll(spread[...], lax.rem(model - dp * share, model), 1)
    depth_ref[...] = moved[:KERNEL, :share]


def final(first, second, table, share, share_ffn, width, group, taps, count):
    def shape(*sizes):
        return jax.ShapeDtypeStruct(sizes, F32)

    model = 2 * group
    return pl.pallas_call(
        functools.partial(final_kernel, count),
        out_shape=(
            shape(share, width), shape(share, width), shape(share, width), shape(width), shape(width),
            shape(KERNEL, share), shape(share, width), shape(width), shape(taps, width), shape(taps),
            shape(share, width), shape(width), shape(2, share, width), shape(model), shape(model),
            shape(model), shape(share_ffn, group), shape(1, 4 * group), shape(share_ffn, group), shape(group),
            shape(group), shape(group),
        ),
        in_specs=[whole()] * 3,
        out_specs=(whole(),) * 22,
        scratch_shapes=[
            pltpu.VMEM((TAP_ROWS, model), F32),
        ],
        name="final",
    )(first, second, table)


EPSILON = 1e-06
MASK_FILL = -1e30
INV_ROOT2 = 0.7071067811865476
INV_ROOT_TWO_PI = 0.3989422804014327


def nn(left, right):
    return jnp.dot(left, right, preferred_element_type=F32)


def tn(left, right):
    return lax.dot_general(left, right, (((0,), (0,)), ((), ())), preferred_element_type=F32)


def nt(left, right):
    return lax.dot_general(left, right, (((1,), (1,)), ((), ())), preferred_element_type=F32)


def moments(sum_own, square_own, sum_other, square_other, width):
    mean = (sum_own + sum_other) / (2 * width)
    apart = (sum_own - sum_other) / width
    spread = (square_own + square_other + apart * apart * (width / 2)) / (2 * width)
    return mean, lax.rsqrt(spread + EPSILON)


def as_row(value):
    return value.reshape(1, -1)


def spread_marks(marks_ref, columns_ref):
    rows = marks_ref.shape[2]
    wide = jnp.concatenate([marks_ref[0], jnp.zeros((LANES - TAP_ROWS, rows), F32)], 0)
    columns_ref[...] = jnp.transpose(wide.astype(BF16)).astype(F32)


def write_marks(lengths_ref, s, marks_ref):
    rows = marks_ref.shape[2]
    place = lax.broadcasted_iota(jnp.int32, (1, rows), 1)
    segment = jnp.zeros((1, rows), jnp.int32)
    end = 0
    for document in range(lengths_ref.shape[1]):
        end = end + lengths_ref[s, document]
        segment = segment + (place >= end).astype(jnp.int32)
    segment = segment.astype(F32)
    for tap in range(KERNEL):
        offset = tap - HALF
        there = pltpu.roll(segment, -offset % rows, 1) if offset else segment
        inside = jnp.logical_and(place + offset >= 0, place + offset < rows)
        marks_ref[0, tap : tap + 1, :] = jnp.where(jnp.logical_and(there == segment, inside), 1.0, 0.0)
    marks_ref[0, KERNEL : KERNEL + 1, :] = segment
    marks_ref[0, KERNEL + 1 :, :] = jnp.zeros((TAP_ROWS - KERNEL - 1, rows), F32)


def unpack_wide(target, source_ref, start, low, width):
    cut = target.shape[0] // CUTS
    for k in range(CUTS):
        rows = source_ref[k, pl.ds(start, cut), :].astype(F32)[:, low : low + width]
        rows = jnp.concatenate([rows, jnp.zeros((cut, WIDE - width), F32)], 1)
        target[pl.ds(k * cut, cut), :] = rows.astype(target.dtype)


def tap_places(heads, mp):
    row = lax.broadcasted_iota(jnp.int32, (LANES, LANES), 0)
    column = lax.broadcasted_iota(jnp.int32, (LANES, LANES), 1)
    tap_rows = heads * TAP_ROWS
    far = row >= tap_rows
    inner = jnp.where(far, row - tap_rows, row)
    head, tap = lax.shift_right_logical(inner, 4), jnp.bitwise_and(inner, TAP_ROWS - 1)
    half = jnp.where(far, 1 - mp, mp)
    valid = jnp.logical_and(tap < KERNEL, row < 2 * tap_rows)
    return jnp.logical_and(valid, column == (half * heads + head) * KERNEL + tap)


def write_expansion(target, heads):
    row = lax.broadcasted_iota(jnp.int32, (LANES, WIDE), 0)
    lane = lax.broadcasted_iota(jnp.int32, (LANES, WIDE), 1)
    tap_rows = heads * TAP_ROWS
    inner = jnp.where(row >= tap_rows, row - tap_rows, row)
    inside = jnp.logical_and(lane < heads * HEAD_DIM, row < 2 * tap_rows)
    head = lax.shift_right_logical(lane, 6) * TAP_ROWS
    for tap in range(KERNEL):
        chosen = jnp.logical_and(inside, inner == head + tap)
        target[:, tap * WIDE : (tap + 1) * WIDE] = jnp.where(chosen, 1.0, 0.0).astype(BF16)


def key_window(start, size, rows):
    low = max(0, start - (MOST_DOC - 1)) // size * size
    high = min(rows, -(-(start + size - 1 + MOST_DOC) // size) * size)
    return slice(low, high)


def only_rows(value, head):
    row = lax.broadcasted_iota(jnp.int32, (WIDE, 1), 0)
    return jnp.where(jnp.logical_and(row >= head * HEAD_DIM, row < (head + 1) * HEAD_DIM), value.astype(F32), 0.0)


def head_lanes(head):
    lane = lax.broadcasted_iota(jnp.int32, (1, WIDE), 1)
    return jnp.logical_and(lane >= head * HEAD_DIM, lane < (head + 1) * HEAD_DIM)


def only(value, head):
    return jnp.where(head_lanes(head), value.astype(F32), 0.0)


def high_low(weights, heads):
    high = weights.astype(BF16).astype(F32)
    low = weights - high
    rest = jnp.zeros((LANES - 2 * heads * TAP_ROWS, weights.shape[1]), F32)
    return jnp.transpose(jnp.concatenate([high, low, rest], 0).astype(BF16))


def front_kernel(
    seqs, count, early,
    hidden_ref, lengths_ref, first_ref, kw_ref, kb_ref, qb_ref, vb_ref, pb_ref, cb_ref, second_ref,
    q_ref, k_ref, v_ref, cv_ref, dl_ref, kc_ref, ca_ref, probs_ref, cc_ref, ctx_ref, lse_ref, second_all_ref,
    marks_ref, taps_ref, depth_ref, expand_ref, inputs_turned_ref, point_turned_ref, early_ref,
    lead_ref, out0_nat, out1_nat, part_out, part_send, part_recv,
    query_ref, key_ref, value_ref, conv_ref, point_ref, vec_ref, bias_ref, depth_wide, tile,
    masks, rows_pad, conv_pad, columns, weights, query_turned, value_turned, context_turned, tap_out, tap_in,
    send_sem, recv_sem, own_sem, gather_send, gather_recv,
):
    s = pl.program_id(0)
    mp, core, side, deep, parts = places(count)
    me = index_of(deep, side, core)
    rows, model = hidden_ref.shape
    chunks = model // LANES
    heads = probs_ref.shape[1] // TAP_ROWS
    tap_rows = heads * TAP_ROWS
    beside = index_of(deep, 1 - side, core)
    twin = index_of(deep, side, 1 - core)

    split = lead_ref.shape[1]
    spans = [pl.ds(0, split), pl.ds(split, second_ref.shape[1] - split)]

    def push(group, source, block, target, slot):
        return pltpu.make_async_remote_copy(
            src_ref=source.at[spans[group]],
            dst_ref=second_all_ref.at[block, spans[group]],
            send_sem=gather_send.at[group, slot],
            recv_sem=gather_recv.at[group, block],
            device_id=at(target, mp),
            device_id_type=MESH,
        )

    def arrive(group, block):
        pltpu.make_async_copy(
            second_ref.at[0, spans[group]], second_all_ref.at[block, spans[group]], gather_recv.at[group, block]
        ).wait()

    own_copy = pltpu.make_async_copy(second_ref.at[0], second_all_ref.at[me], own_sem.at[0])
    lead_copy = pltpu.make_async_copy(second_all_ref.at[:, spans[0]], lead_ref, own_sem.at[1])
    first_hops = [(me, index_of(lax.rem(deep + k, parts), side, core), k - 1) for k in range(1, parts)]
    first_hops += [(me, beside, parts - 1), (me, twin, parts)]
    second_hops = [(beside, [(twin, parts + 1)])]
    for k in range(1, parts):
        block = index_of(lax.rem(deep + parts - k, parts), side, core)
        second_hops.append((block, [(beside, parts + 2 * k), (twin, parts + 2 * k + 1)]))
    third_hops = [
        (index_of(lax.rem(deep + parts - k, parts), 1 - side, core), [(twin, 3 * parts + k - 1)]) for k in range(1, parts)
    ]

    def start_hops(group):
        for block, target, place in first_hops:
            push(group, second_ref.at[0], block, target, place).start()

    def pass_on(group, hops):
        for block, targets in hops:
            arrive(group, block)
            for target, place in targets:
                push(group, second_all_ref.at[block], block, target, place).start()

    def end_hops(group):
        for k in range(parts):
            for other in range(2):
                arrive(group, index_of(lax.rem(deep + parts - k, parts), other, 1 - core))
        for block, target, place in first_hops:
            push(group, second_ref.at[0], block, target, place).wait_send()
        for block, targets in second_hops + third_hops:
            for target, place in targets:
                push(group, second_all_ref.at[block], block, target, place).wait_send()

    def swap_part(which, piece):
        size = rows // PIECES
        return pltpu.make_async_remote_copy(
            src_ref=part_out.at[which, pl.ds(piece * size, size)],
            dst_ref=early_ref.at[pl.ds(which * rows + piece * size, size)],
            send_sem=part_send.at[which, piece],
            recv_sem=part_recv.at[which, piece],
            device_id=at(me, 1 - mp),
            device_id_type=MESH,
        )

    @pl.when(s == 0)
    def _():
        barrier = pltpu.get_barrier_semaphore()
        pl.semaphore_signal(barrier, inc=1, device_id=at(me, 1 - mp), device_id_type=MESH)
        peers = [index_of(lax.rem(deep + k, parts), side, core) for k in range(1, parts)] + [beside, twin]
        for peer in peers:
            pl.semaphore_signal(barrier, inc=1, device_id=at(peer, mp), device_id_type=MESH)
        pl.semaphore_wait(barrier, len(peers) + 1)
        own_copy.start()
        start_hops(0)
        start_hops(1)
        width = heads * HEAD_DIM
        cut = model // CUTS
        for target, place, low in (
            (query_ref, 0, 0), (key_ref, 0, width), (value_ref, 1, 0), (conv_ref, 1, width), (point_ref, 2, 0),
            (depth_wide, 2, width),
        ):
            unpack_wide(target, first_ref, place * cut, low, width)
        depth_ref[...] = jnp.transpose(depth_wide[:, :LANES])[:TAP_ROWS]
        vec_ref[...] = jnp.zeros_like(vec_ref)
        for row, source in enumerate((qb_ref, vb_ref, pb_ref, cb_ref)):
            vec_ref[row : row + 1, :width] = as_row(source[...])
        write_expansion(expand_ref, heads)
        chosen = tap_places(heads, mp)
        tile[...] = jnp.zeros_like(tile)
        tile[:1, : kb_ref.shape[0]] = as_row(kb_ref[...])
        bias = jnp.sum(jnp.where(chosen, tile[:1, :LANES], 0.0), axis=1, keepdims=True)
        bias_ref[...] = jnp.broadcast_to(bias[:tap_rows], bias_ref.shape)
        tile[: kw_ref.shape[0], :width] = kw_ref[...].astype(F32)
        turned_weight = tile[:LANES, :].astype(BF16)
        taps_ref[...] = nn(jnp.where(chosen, 1.0, 0.0).astype(BF16), turned_weight).astype(BF16)
        for place, source in enumerate((query_ref, key_ref, value_ref, conv_ref)):
            inputs_turned_ref[place * WIDE : (place + 1) * WIDE, :] = jnp.transpose(source[...])
        point_turned_ref[...] = jnp.transpose(point_ref[...])
        rows_pad[:, :EDGE, :] = jnp.zeros((chunks, EDGE, LANES), F32)
        rows_pad[:, pl.ds(EDGE + rows, EDGE), :] = jnp.zeros((chunks, EDGE, LANES), F32)
        conv_pad[:, :EDGE, :] = jnp.zeros((2, EDGE, LANES), F32)
        conv_pad[:, pl.ds(EDGE + rows, EDGE), :] = jnp.zeros((2, EDGE, LANES), F32)

    write_marks(lengths_ref, s, marks_ref)
    spread_marks(marks_ref, columns)
    hidden = hidden_ref[...]
    for c in range(chunks):
        rows_pad[c, pl.ds(EDGE, rows), :] = hidden[:, c * LANES : (c + 1) * LANES].astype(F32)

    step = masks.shape[1]

    def depth_step(i, carry):
        base = pl.multiple_of(i * step, step)
        part = pl.ds(base, step)
        for tap in range(KERNEL):
            masks[tap] = jnp.broadcast_to(columns[part, tap : tap + 1], (step, LANES))
        for first in range(0, chunks, 2):
            total = [jnp.zeros((step, LANES), F32)] * 2
            for tap in range(KERNEL):
                mask = masks[tap]
                for k in range(2):
                    c = first + k
                    moved = rows_pad[c, pl.ds(base + EDGE + tap - HALF, step), :]
                    total[k] = total[k] + (moved * mask) * depth_ref[tap : tap + 1, c * LANES : (c + 1) * LANES]
            for k in range(2):
                dl_ref[part, (first + k) * LANES : (first + k + 1) * LANES] = total[k].astype(BF16)
        return carry

    lax.fori_loop(0, rows // step, depth_step, 0)

    @pl.when(s == 0)
    def _():
        pass_on(0, second_hops)

    queries = (nn(hidden, query_ref[...]) + vec_ref[0:1, :]).astype(BF16)
    q_ref[...] = queries
    key_conv = nn(dl_ref[...], point_ref[...]) + vec_ref[2:3, :]
    kc_ref[...] = key_conv
    conv_attn = (key_conv * queries.astype(F32)).astype(BF16)
    ca_ref[...] = conv_attn
    tap_terms = nt(taps_ref[...], conv_attn)
    slot = lax.rem(s, 2)
    tap_out[slot] = tap_terms[tap_rows : 2 * tap_rows]
    swap_taps = pltpu.make_async_remote_copy(
        src_ref=tap_out.at[slot],
        dst_ref=tap_in.at[slot],
        send_sem=send_sem.at[slot],
        recv_sem=recv_sem.at[slot],
        device_id=at(me, 1 - mp),
        device_id_type=MESH,
    )
    swap_taps.start()

    @pl.when(jnp.logical_and(s >= 1, s < early))
    def _():
        for piece in range(PIECES // 2, PIECES):
            swap_part(s - 1, piece).start()

    @pl.when(jnp.logical_and(s >= 1, s == early))
    def _():
        swap_part(s - 1, 1).start()

    own_terms = tap_terms[:tap_rows]
    k_ref[...] = nn(hidden, key_ref[...]).astype(BF16)
    v_ref[...] = (nn(hidden, value_ref[...]) + vec_ref[1:2, :]).astype(BF16)
    conv_values = nn(hidden, conv_ref[...]) + vec_ref[3:4, :]
    cv_ref[...] = conv_values
    for c in range(2):
        conv_pad[c, pl.ds(EDGE, rows), :] = conv_values[:, c * LANES : (c + 1) * LANES]

    block = 256
    query_turned[...] = jnp.transpose(q_ref[...])
    value_turned[...] = jnp.transpose(v_ref[...])
    for start in range(0, rows, block):
        part = slice(start, start + block)
        keys = key_window(start, block, rows)
        allowed = columns[keys, KERNEL : KERNEL + 1] == marks_ref[0, KERNEL : KERNEL + 1, part]
        for head in range(heads):
            lanes = slice(head * HEAD_DIM, (head + 1) * HEAD_DIM)
            mine = (only_rows(query_turned[:, part], head) * (HEAD_DIM**-0.5)).astype(BF16)
            scores = jnp.where(allowed, nn(k_ref[keys, :], mine), MASK_FILL)
            top = jnp.max(scores, axis=0, keepdims=True)
            exponent = jnp.exp(scores - top)
            amount = jnp.sum(exponent, axis=0, keepdims=True)
            context_turned[lanes, part] = nn(value_turned[lanes, keys], exponent.astype(BF16)) * (1.0 / amount)
            lse_ref[0, head : head + 1, part] = top + jnp.log(amount)
    lse_ref[0, heads:, :] = jnp.zeros((8 - heads, rows), F32)
    context_turned[heads * HEAD_DIM :, :] = jnp.zeros((WIDE - heads * HEAD_DIM, rows), F32)
    ctx_ref[...] = jnp.transpose(context_turned[...].astype(BF16))

    @pl.when(s == 0)
    def _():
        pass_on(0, third_hops)


    swap_taps.wait()
    logits = (own_terms + tap_in[slot] + bias_ref[:, :1]).reshape(heads, TAP_ROWS, rows)
    tap = lax.broadcasted_iota(jnp.int32, (heads, TAP_ROWS, rows), 1)
    logits = jnp.where(tap < KERNEL, logits, MASK_FILL)
    exponent = jnp.exp(logits - jnp.max(logits, axis=1, keepdims=True))
    probs = exponent / jnp.sum(exponent, axis=1, keepdims=True)
    probs_ref[0] = probs.reshape(tap_rows, rows)
    tap_mask = jnp.where(tap[0] < KERNEL, marks_ref[0], 0.0)
    weights[...] = high_low((probs * tap_mask[None]).reshape(tap_rows, rows), heads)
    conv_block = 128

    def conv_step(i, carry):
        base = pl.multiple_of(i * conv_block, conv_block)
        part = pl.ds(base, conv_block)
        scale = nn(weights[part, :], expand_ref[...])
        for c in range(2):
            total = jnp.zeros((conv_block, LANES), F32)
            for tap in range(KERNEL):
                low = tap * WIDE + c * LANES
                moved = conv_pad[c, pl.ds(base + EDGE + tap - HALF, conv_block), :]
                total = total + scale[:, low : low + LANES] * moved
            cc_ref[part, c * LANES : (c + 1) * LANES] = total.astype(BF16)
        return carry

    lax.fori_loop(0, rows // conv_block, conv_step, 0)

    @pl.when(s == 0)
    def _():
        own_copy.wait()
        end_hops(0)
        pass_on(1, second_hops)
        if early:
            lead_copy.start()
            lead_copy.wait()
            width = heads * HEAD_DIM
            for target, low in ((out0_nat, 0), (out1_nat, width)):
                unpack_wide(depth_wide, lead_ref, 0, low, width)
                target[...] = jnp.transpose(depth_wide[...].astype(BF16))

    @pl.when(s < early)
    def _():
        half = model // 2
        theirs = pl.ds(pl.multiple_of((1 - mp) * half, half), half)

        def part_step(i, carry):
            part = pl.ds(pl.multiple_of(i * block, block), block)
            other = nn(ctx_ref[part, :], out0_nat[:, theirs]) + nn(cc_ref[part, :], out1_nat[:, theirs])
            part_out[s, part, :] = other.astype(BF16)
            return carry

        lax.fori_loop(0, jnp.where(s == early - 1, rows // 2 // block, rows // block), part_step, 0)
        swap_part(s, 0).start()

    @pl.when(s < early - 1)
    def _():
        swap_part(s, 1).start()

    @pl.when(s == min(1, seqs - 1))
    def _():
        pass_on(1, third_hops)

    @pl.when(s == seqs - 1)
    def _():
        end_hops(1)
        for which in range(early):
            for piece in range(PIECES if which < early - 1 else PIECES // 2):
                swap_part(which, piece).wait()


def whole():
    return pl.BlockSpec(memory_space=pltpu.VMEM)


def by_seq(rows, columns):
    return pl.BlockSpec((rows, columns), lambda s: (s, 0))


def by_seq_row(rows, columns):
    return pl.BlockSpec((1, rows, columns), lambda s: (s, 0, 0))


def front(hidden, lengths, first, kernel_weight, biases, second, count, early, ident):
    seqs = lengths.shape[0]
    tokens, model = hidden.shape
    rows = tokens // seqs
    tap_rows = kernel_weight.shape[1] // HEAD_DIM * TAP_ROWS
    parts = count // 4
    place = pl.BlockSpec(memory_space=pl.ANY)
    share = model // count
    split = share + -share % TAP_ROWS

    def wide(kind):
        return jax.ShapeDtypeStruct((tokens, WIDE), kind)

    return pl.pallas_call(
        functools.partial(front_kernel, seqs, count, early),
        grid=(seqs,),
        out_shape=(
            wide(BF16), wide(BF16), wide(BF16), wide(F32),
            jax.ShapeDtypeStruct((tokens, model), BF16),
            wide(F32), wide(BF16),
            jax.ShapeDtypeStruct((seqs, tap_rows, rows), F32),
            wide(BF16), wide(BF16),
            jax.ShapeDtypeStruct((seqs, 8, rows), F32),
            jax.ShapeDtypeStruct((count,) + second.shape[1:], BF16),
            jax.ShapeDtypeStruct((seqs, TAP_ROWS, rows), F32),
            jax.ShapeDtypeStruct((LANES, WIDE), BF16),
            jax.ShapeDtypeStruct((TAP_ROWS, model), F32),
            jax.ShapeDtypeStruct((LANES, KERNEL * WIDE), BF16),
            jax.ShapeDtypeStruct((4 * WIDE, model), BF16),
            jax.ShapeDtypeStruct((WIDE, model), BF16),
            jax.ShapeDtypeStruct((tokens, model // 2), BF16),
        ),
        in_specs=[by_seq(rows, model), pl.BlockSpec(memory_space=pltpu.SMEM)] + [whole()] * 7 + [place],
        out_specs=(
            by_seq(rows, WIDE), by_seq(rows, WIDE), by_seq(rows, WIDE), by_seq(rows, WIDE), by_seq(rows, model),
            by_seq(rows, WIDE), by_seq(rows, WIDE), by_seq_row(tap_rows, rows), by_seq(rows, WIDE), by_seq(rows, WIDE),
            by_seq_row(8, rows), place, by_seq_row(TAP_ROWS, rows),
        )
        + (whole(),) * 5
        + (place,),
        scratch_shapes=[
            pltpu.VMEM((count, split, second.shape[2]), BF16),
            pltpu.VMEM((WIDE, model), BF16),
            pltpu.VMEM((WIDE, model), BF16),
            pltpu.VMEM((max(early, 1), rows, model // 2), BF16),
            pltpu.SemaphoreType.DMA((max(early, 1), PIECES)),
            pltpu.SemaphoreType.DMA((max(early, 1), PIECES)),
        ]
        + [pltpu.VMEM((model, WIDE), BF16)] * 5
        + [
            pltpu.VMEM((8, WIDE), F32),
            pltpu.VMEM((tap_rows, LANES), F32),
            pltpu.VMEM((model, WIDE), F32),
            pltpu.VMEM((WIDE, WIDE), F32),
            pltpu.VMEM((KERNEL, 128, LANES), F32),
            pltpu.VMEM((model // LANES, rows + 2 * EDGE, LANES), F32),
            pltpu.VMEM((2, rows + 2 * EDGE, LANES), F32),
            pltpu.VMEM((rows, LANES), F32),
            pltpu.VMEM((rows, LANES), BF16),
            pltpu.VMEM((WIDE, rows), BF16),
            pltpu.VMEM((WIDE, rows), BF16),
            pltpu.VMEM((WIDE, rows), F32),
            pltpu.VMEM((2, tap_rows, rows), F32),
            pltpu.VMEM((2, tap_rows, rows), F32),
            pltpu.SemaphoreType.DMA((2,)),
            pltpu.SemaphoreType.DMA((2,)),
            pltpu.SemaphoreType.DMA((2,)),
            pltpu.SemaphoreType.DMA((2, 4 * parts - 1)),
            pltpu.SemaphoreType.DMA((2, count)),
        ],
        compiler_params=pltpu.CompilerParams(
            collective_id=ident, has_side_effects=True, vmem_limit_bytes=62 << 20
        ),
        name="front",
    )(hidden, lengths, first, kernel_weight, *biases, second)


def stat_rows(columns):
    rows = columns[0].shape[0]
    diagonal = lax.broadcasted_iota(jnp.int32, (rows, rows), 0) == lax.broadcasted_iota(jnp.int32, (rows, rows), 1)
    lines = [jnp.sum(jnp.where(diagonal, column, 0.0), axis=0, keepdims=True) for column in columns]
    return jnp.concatenate(lines + [jnp.zeros((8 - len(lines), rows), F32)], 0)


def stat_columns(lines):
    rows = lines[0].shape[1]
    wide = jnp.concatenate(lines + [jnp.zeros((8 - len(lines), rows), F32)], 0)
    tall = jnp.transpose(wide)
    return [tall[:, k : k + 1] for k in range(len(lines))]


def row_sums(value):
    rows, columns = value.shape
    return jnp.sum(value.reshape(rows // 8, 8, columns), axis=0)


SLOTS = 4
LAST_LAG = 6
FFN_STEP = 512


def middle_kernel(
    blocks, early,
    early_ref, context_ahead_ref, conv_ahead_ref, context_ref, conv_ref, context_late_ref, conv_late_ref, hidden_ref, grad_ref, grad_late_ref, second_ref,
    ob_ref, gain1_ref, bias1_ref, outb_ref, gain2_ref, bias2_ref, inb_ref,
    output_ref, residual_ref, grad_context_ref, grad_conv_ref, pack_ref, small_ref,
    out0_ref, out1_ref, inner_ref, outer_ref, vec_ref, inner_nat, outer_turned, out0_nat, out1_nat, low_units, branch_ref, acc_out0, acc_out1, state, scale_ring, act_ring, slope_ring, low_ring, summed_ring, normed_ring, stat_ring,
    acc_inner, acc_outer, acc_small, acc_bias,
    branch_send, branch_recv, branch_out, branch_in, stat1_out, stat1_in, stat2_out, stat2_in, stat3_out, stat3_in, back_out, back_in,
    send_sem, recv_sem,
):
    i = pl.program_id(0)
    me = lax.axis_index("mp")
    dp = lax.axis_index("dp")
    width = summed_ring.shape[2]
    hidden_units = inner_ref.shape[0]
    inverse = 1.0 / (2 * width)

    def message(kind, source, target, slot):
        return pltpu.make_async_remote_copy(
            src_ref=source.at[slot],
            dst_ref=target.at[slot],
            send_sem=send_sem.at[kind, slot],
            recv_sem=recv_sem.at[kind, slot],
            device_id=(dp, 1 - me),
            device_id_type=MESH,
        )

    def ahead(slot):
        return pltpu.make_async_remote_copy(
            src_ref=branch_out.at[slot],
            dst_ref=branch_in.at[slot],
            send_sem=branch_send.at[slot],
            recv_sem=branch_recv.at[slot],
            device_id=(dp, 1 - me),
            device_id_type=MESH,
        )

    kinds = [
        None, (stat1_out, stat1_in), (stat2_out, stat2_in), (stat3_out, stat3_in), (back_out, back_in),
    ]

    def fresh(kind, b, slot):
        @pl.when(b >= SLOTS)
        def _():
            message(kind, *kinds[kind], slot).wait_send()

    def vec(row):
        return vec_ref[row : row + 1, :width]

    @pl.when(i == 0)
    def _():
        barrier = pltpu.get_barrier_semaphore()
        pl.semaphore_signal(barrier, inc=1, device_id=(dp, 1 - me), device_id_type=MESH)
        pl.semaphore_wait(barrier, 1)
        cut, cut_ffn = 2 * width // CUTS, hidden_units // CUTS
        unpack_wide(out0_ref, second_ref, 0, 0, width // 2)
        unpack_wide(out1_ref, second_ref, 0, width // 2, width // 2)
        for k in range(CUTS):
            inner_ref[pl.ds(k * cut_ffn, cut_ffn), :] = second_ref[k, pl.ds(cut, cut_ffn), :]
            outer_ref[pl.ds(k * cut_ffn, cut_ffn), :] = second_ref[k, pl.ds(cut + cut_ffn, cut_ffn), :]
        for row, source in enumerate((ob_ref, gain1_ref, bias1_ref)):
            value = as_row(source[...])
            vec_ref[row : row + 1, :width] = jnp.where(me == 0, value[:, :width], value[:, width:])
        for row, source in enumerate((outb_ref, gain2_ref, bias2_ref)):
            vec_ref[3 + row : 4 + row, :width] = as_row(source[...])
        vec_ref[7:8, :] = inb_ref[...]
        inner_nat[...] = jnp.transpose(inner_ref[...])
        outer_turned[...] = jnp.transpose(outer_ref[...])
        out0_nat[...] = jnp.transpose(out0_ref[...])
        out1_nat[...] = jnp.transpose(out1_ref[...])
        acc_inner[...] = jnp.zeros_like(acc_inner)
        acc_outer[...] = jnp.zeros_like(acc_outer)
        acc_out0[...] = jnp.zeros_like(acc_out0)
        acc_out1[...] = jnp.zeros_like(acc_out1)
        acc_small[...] = jnp.zeros_like(acc_small)
        acc_bias[...] = jnp.zeros_like(acc_bias)

    cuts = branch_in.shape[0] // (blocks - early)

    @pl.when(i < cuts * (blocks - early))
    def _():
        theirs = pl.ds(pl.multiple_of((1 - me) * width, width), width)
        other = nn(context_ahead_ref[...], out0_nat[:, theirs]) + nn(conv_ahead_ref[...], out1_nat[:, theirs])
        branch_out[i] = other.astype(BF16)
        ahead(i).start()

    @pl.when(i < blocks)
    def _():
        b = i
        ours = pl.ds(pl.multiple_of(me * width, width), width)
        own = nn(context_ref[...], out0_nat[:, ours]) + nn(conv_ref[...], out1_nat[:, ours])
        state[lax.rem(b, 8)] = hidden_ref[:, ours].astype(F32) + (own + vec(0))

        @pl.when(b < early)
        def _():
            state[lax.rem(b, 8)] += early_ref[...].astype(F32)

    @pl.when(jnp.logical_and(i >= 1, i < blocks + 1))
    def _():
        b = i - 1
        slot = lax.rem(b, SLOTS)
        fresh(1, b, slot)

        @pl.when(b >= early)
        def _():
            size = branch_in.shape[1]
            for k in range(cuts):
                piece = cuts * (b - early) + k
                ahead(piece).wait_recv()
                state[lax.rem(b, 8), pl.ds(k * size, size), :] += branch_in[piece].astype(F32)

        residual = state[lax.rem(b, 8)]
        total = jnp.sum(residual, axis=1, keepdims=True)
        apart = residual - total * (1.0 / width)
        stat1_out[slot] = stat_rows([total, jnp.sum(apart * apart, axis=1, keepdims=True)])
        message(1, *kinds[1], slot).start()

    @pl.when(jnp.logical_and(i >= 2, i < blocks + 2))
    def _():
        b = i - 2
        slot = lax.rem(b, SLOTS)
        two = lax.rem(b, 2)
        message(1, *kinds[1], slot).wait_recv()
        fresh(2, b, slot)
        ours, theirs = stat1_out[slot], stat1_in[slot]
        mean, scale = moments(ours[0:1], ours[1:2], theirs[0:1], theirs[1:2], width)
        mean, scale = stat_columns([mean, scale])
        standard = (state[lax.rem(b, 8)] - mean) * scale
        state[lax.rem(b, 8)] = standard
        scale_ring[lax.rem(b, 4)] = jnp.broadcast_to(scale, scale_ring.shape[1:])
        normed = standard * vec(1) + vec(2)
        low = normed.astype(BF16)
        low_ring[two] = low
        summed = normed + vec(3)
        for start in range(0, hidden_units, FFN_STEP):
            part = pl.ds(start, FFN_STEP)
            inner = nn(low, inner_nat[:, part]) + vec_ref[7:8, start : start + FFN_STEP]
            cdf = 0.5 * (1.0 + lax.erf(inner * INV_ROOT2))
            act = (inner * cdf).astype(BF16)
            act_ring[two, :, part] = act
            slope_ring[two, :, part] = cdf + inner * jnp.exp(-0.5 * inner * inner) * INV_ROOT_TWO_PI
        summed = summed + nn(act_ring[two], outer_ref[...])
        summed_ring[two] = summed
        scaled = grad_ref[...].astype(F32) * vec(4)
        total = jnp.sum(summed, axis=1, keepdims=True)
        apart = summed - total * (1.0 / width)
        stat2_out[slot] = stat_rows(
            [
                total,
                jnp.sum(apart * apart, axis=1, keepdims=True),
                jnp.sum(scaled, axis=1, keepdims=True),
                jnp.sum(scaled * apart, axis=1, keepdims=True),
            ]
        )
        message(2, *kinds[2], slot).start()

    @pl.when(jnp.logical_and(i >= 3, i < blocks + 3))
    def _():
        b = i - 3
        slot = lax.rem(b, SLOTS)
        two = lax.rem(b, 2)
        message(2, *kinds[2], slot).wait_recv()
        fresh(3, b, slot)
        total, square, grads, cross = [stat2_out[slot][k : k + 1] for k in range(4)]
        total_o, square_o, grads_o, cross_o = [stat2_in[slot][k : k + 1] for k in range(4)]
        mean, scale = moments(total, square, total_o, square_o, width)
        mean_grad = (grads + grads_o) * inverse
        product = cross + cross_o + (total * (1.0 / width) - mean) * grads + (total_o * (1.0 / width) - mean) * grads_o
        mean_product = product * scale * inverse
        mean, scale, mean_grad, mean_product = stat_columns([mean, scale, mean_grad, mean_product])
        standard = (summed_ring[two] - mean) * scale
        output_ref[...] = (standard * vec(4) + vec(5)).astype(BF16)
        gradient = grad_late_ref[...].astype(F32)
        grad_summed = scale * (gradient * vec(4) - mean_grad - standard * mean_product)
        low = grad_summed.astype(BF16)
        acc_small[0] += row_sums(low.astype(F32))
        acc_small[1] += row_sums(gradient * standard)
        acc_small[2] += row_sums(gradient)
        normed_low = low_ring[two]
        grad_normed = grad_summed
        for start in range(0, hidden_units, FFN_STEP):
            part = pl.ds(start, FFN_STEP)
            inner_low = (nn(low, outer_turned[:, part]) * slope_ring[two, :, part]).astype(BF16)
            low_units[:, part] = inner_low
            acc_bias[:, part] += row_sums(inner_low.astype(F32))
            acc_outer[:, part] += tn(low, act_ring[two, :, part])
            acc_inner[:, part] += tn(normed_low, inner_low)
        grad_normed = grad_normed + nn(low_units[...], inner_ref[...])
        normed_ring[two] = grad_normed
        standard1 = state[lax.rem(b, 8)]
        scaled = grad_normed * vec(1)
        acc_small[3] += row_sums(grad_normed * standard1)
        acc_small[4] += row_sums(grad_normed)
        sums = stat_rows(
            [jnp.sum(scaled, axis=1, keepdims=True), jnp.sum(scaled * standard1, axis=1, keepdims=True)]
        )
        stat3_out[slot] = sums
        message(3, *kinds[3], slot).start()

    @pl.when(jnp.logical_and(i >= 4, i < blocks + 4))
    def _():
        b = i - 4
        slot = lax.rem(b, SLOTS)
        message(3, *kinds[3], slot).wait_recv()
        fresh(4, b, slot)
        both = stat3_out[slot] + stat3_in[slot]
        first, second = stat_columns([both[0:1], both[1:2]])
        standard = state[lax.rem(b, 8)]
        scaled = normed_ring[lax.rem(b, 2)] * vec(1)
        residual = scale_ring[lax.rem(b, 4)][:, :1] * (scaled - first * inverse - standard * (second * inverse))
        residual_ref[...] = residual
        low = residual.astype(BF16)
        acc_small[5] += row_sums(low.astype(F32))
        back_out[slot] = low
        message(4, *kinds[4], slot).start()

    @pl.when(i >= LAST_LAG)
    def _():
        b = i - LAST_LAG
        slot = lax.rem(b, SLOTS)
        message(4, *kinds[4], slot).wait_recv()
        theirs = pl.ds(pl.multiple_of((1 - me) * width, width), width)
        ours = pl.ds(pl.multiple_of(me * width, width), width)
        branch_ref[:, ours] = back_out[slot]
        branch_ref[:, theirs] = back_in[slot]
        branch = branch_ref[...]
        grad_context_ref[...] = nn(branch, out0_ref[...]).astype(BF16)
        grad_conv_ref[...] = nn(branch, out1_ref[...]).astype(BF16)
        acc_out0[...] += tn(context_late_ref[...], branch)
        acc_out1[...] += tn(conv_late_ref[...], branch)

    @pl.when(i == blocks + LAST_LAG - 1)
    def _():
        for slot in range(cuts * (blocks - early)):
            ahead(slot).wait_send()
        for kind in range(1, 5):
            for slot in range(SLOTS):
                message(kind, *kinds[kind], slot).wait_send()
        cut, cut_ffn = 2 * width // CUTS, hidden_units // CUTS
        both = jnp.concatenate([acc_out0[: width // 2], acc_out1[: width // 2]], 0)
        out_grads = jnp.transpose(both.astype(BF16))
        inner_grads = jnp.transpose(acc_inner[...].astype(BF16))
        outer_grads = jnp.transpose(acc_outer[...].astype(BF16))
        for k in range(CUTS):
            part_ffn = slice(k * cut_ffn, (k + 1) * cut_ffn)
            pack_ref[k, pl.ds(0, cut), :] = out_grads[k * cut : (k + 1) * cut]
            pack_ref[k, pl.ds(cut, cut_ffn), :] = inner_grads[part_ffn]
            pack_ref[k, pl.ds(cut + cut_ffn, cut_ffn), :] = outer_grads[part_ffn]
        small_ref[...] = jnp.zeros_like(small_ref)
        for row in range(6):
            small_ref[row : row + 1, :width] = jnp.sum(acc_small[row], axis=0, keepdims=True)
        small_ref[6:7, :] = jnp.sum(acc_bias[...], axis=0, keepdims=True)


def middle(early, early_rows, context, conv_context, hidden, out_grad, second, vectors, ident):
    tokens, model = hidden.shape
    width = model // 2
    local = context.shape[1]
    units = vectors[-1].shape[1]
    rows = 256
    blocks = tokens // rows
    early = early // rows

    def block(columns, lag):
        return pl.BlockSpec((rows, columns), lambda i: (jnp.clip(i - lag, 0, blocks - 1), 0))

    cuts = 2 if 2 * early >= blocks else 1
    ahead = pl.BlockSpec((rows // cuts, local), lambda i: (jnp.minimum(cuts * early + i, cuts * blocks - 1), 0))
    whole = pl.BlockSpec(memory_space=pltpu.VMEM)
    stat = pltpu.VMEM((SLOTS, 8, rows), F32)
    half = pltpu.VMEM((SLOTS, rows, width), BF16)
    return pl.pallas_call(
        functools.partial(middle_kernel, blocks, early),
        grid=(blocks + LAST_LAG,),
        out_shape=(
            jax.ShapeDtypeStruct((tokens, width), BF16),
            jax.ShapeDtypeStruct((tokens, width), F32),
            jax.ShapeDtypeStruct((tokens, local), BF16),
            jax.ShapeDtypeStruct((tokens, local), BF16),
            jax.ShapeDtypeStruct((CUTS, (model + 2 * units) // CUTS, width), BF16),
            jax.ShapeDtypeStruct((8, units), F32),
        ),
        in_specs=[
            block(width, 0), ahead, ahead, block(local, 0), block(local, 0), block(local, LAST_LAG), block(local, LAST_LAG), block(model, 0), block(width, 2),
            block(width, 3),
        ]
        + [whole] * 8,
        out_specs=(block(width, 3), block(width, 4), block(local, LAST_LAG), block(local, LAST_LAG), whole, whole),
        scratch_shapes=[
            pltpu.VMEM((model, local), BF16),
            pltpu.VMEM((model, local), BF16),
            pltpu.VMEM((units, width), BF16),
            pltpu.VMEM((units, width), BF16),
            pltpu.VMEM((8, units), F32),
            pltpu.VMEM((width, units), BF16),
            pltpu.VMEM((width, units), BF16),
            pltpu.VMEM((local, model), BF16),
            pltpu.VMEM((local, model), BF16),
            pltpu.VMEM((rows, units), BF16),
            pltpu.VMEM((rows, model), BF16),
            pltpu.VMEM((local, model), F32),
            pltpu.VMEM((local, model), F32),
            pltpu.VMEM((8, rows, width), F32),
            pltpu.VMEM((4, rows, 128), F32),
            pltpu.VMEM((2, rows, units), BF16),
            pltpu.VMEM((2, rows, units), F32),
            pltpu.VMEM((2, rows, width), BF16),
            pltpu.VMEM((2, rows, width), F32),
            pltpu.VMEM((2, rows, width), F32),
            pltpu.VMEM((8, 128), F32),
            pltpu.VMEM((width, units), F32),
            pltpu.VMEM((width, units), F32),
            pltpu.VMEM((6, 8, width), F32),
            pltpu.VMEM((8, units), F32),
            pltpu.SemaphoreType.DMA((cuts * (blocks - early),)),
            pltpu.SemaphoreType.DMA((cuts * (blocks - early),)),
            pltpu.VMEM((cuts * (blocks - early), rows // cuts, width), BF16),
            pltpu.VMEM((cuts * (blocks - early), rows // cuts, width), BF16),
            stat, stat, stat, stat, stat, stat, half, half,
            pltpu.SemaphoreType.DMA((5, SLOTS)),
            pltpu.SemaphoreType.DMA((5, SLOTS)),
        ],
        compiler_params=pltpu.CompilerParams(
            collective_id=ident, has_side_effects=True, vmem_limit_bytes=60 << 20
        ),
        name="middle",
    )(early_rows, context, conv_context, context, conv_context, context, conv_context, hidden, out_grad, out_grad, second, *vectors)


def back_kernel(
    seqs, count,
    grad_context, grad_conv_ref, marks_ref, q_ref, k_ref, v_ref, cv_ref, ca_ref, probs_ref, lse_ref,
    hidden_any, residual_any, dl_any, kc_any,
    inputs_ref, point_ref, taps_ref, depth_ref, expand_ref, small_ref, pack_in_ref,
    grad_ref, own_ref, other_ref, pack_ref, table_ref, reduced_ref,
    hidden_ref, residual_ref, dl_ref, kc_ref, load_sem,
    other_out, other_in, other_send, other_recv,
    twin_in, side_in, deep_in, hop_send, hop_recv,
    masks, depth_pad, conv_pad, grad_pad, columns, weights, shifted_weights, tap_terms, products,
    grads, grad_q, grad_k, grad_v, key_turned, probs_all, scores_all, turned_query, rows_total, tap_all,
    acc_in, acc_point, acc_bias, acc_tap, acc_tap_bias, acc_depth,
    tap_out, tap_in, send_sem, recv_sem,
):
    s = pl.program_id(0)
    mp = lax.axis_index("mp")
    dp = lax.axis_index("dp")
    rows, model = hidden_ref.shape
    chunks = model // LANES
    heads = probs_ref.shape[1] // TAP_ROWS
    tap_rows = heads * TAP_ROWS
    half = chunks // 2
    slot = lax.rem(s, 2)
    hops = Hops(count, pack_in_ref, twin_in, side_in, deep_in, hop_send, hop_recv)
    here_rows = pl.ds(pl.multiple_of(s * rows, rows), rows)
    loads = [
        pltpu.make_async_copy(source.at[here_rows], target, load_sem.at[k])
        for k, (source, target) in enumerate(
            [(hidden_any, hidden_ref), (residual_any, residual_ref), (dl_any, dl_ref), (kc_any, kc_ref)]
        )
    ]
    for load in loads:
        load.start()

    def swap_rows(which):
        return pltpu.make_async_remote_copy(
            src_ref=other_out.at[which],
            dst_ref=other_in.at[which],
            send_sem=other_send.at[which],
            recv_sem=other_recv.at[which],
            device_id=(dp, 1 - mp),
            device_id_type=MESH,
        )

    @pl.when(s == 0)
    def _():
        greet_all(count)
        hops.start_first()
        for pad in (depth_pad, conv_pad, grad_pad):
            for start in (0, EDGE + rows):
                pad[:, pl.ds(start, EDGE), :] = jnp.zeros((pad.shape[0], EDGE, LANES), F32)
        for acc in (acc_in, acc_point, acc_bias, acc_tap, acc_tap_bias, acc_depth):
            acc[...] = jnp.zeros_like(acc)

    spread_marks(marks_ref, columns)
    block = 256

    for c in range(2):
        lanes = slice(c * LANES, (c + 1) * LANES)
        grad_pad[c, pl.ds(EDGE, rows), :] = grad_conv_ref[:, lanes].astype(F32)
        conv_pad[c, pl.ds(EDGE, rows), :] = cv_ref[:, lanes]

    probs = probs_ref[0].reshape(heads, TAP_ROWS, rows)
    tap = lax.broadcasted_iota(jnp.int32, (heads, TAP_ROWS, rows), 1)
    tap_mask = jnp.where(tap < KERNEL, jnp.broadcast_to(marks_ref[...], (heads, TAP_ROWS, rows)), 0.0)
    masked = (probs * tap_mask).reshape(tap_rows, rows)
    flat_tap = tap.reshape(tap_rows, rows)
    moved = jnp.zeros_like(masked)
    for j in range(KERNEL):
        turn = (j - HALF) % rows
        turned = pltpu.roll(masked, turn, 1) if turn else masked
        moved = jnp.where(flat_tap == j, turned, moved)
    shifted_weights[...] = high_low(moved, heads)
    conv_block = 128

    def conv_step(i, carry):
        base = pl.multiple_of(i * conv_block, conv_block)
        part = pl.ds(base, conv_block)
        scale = nn(shifted_weights[part, :], expand_ref[...])
        for c in range(2):
            here = grad_pad[c, pl.ds(base + EDGE, conv_block), :]
            total = jnp.zeros((conv_block, LANES), F32)
            for j in range(KERNEL):
                low = j * WIDE + c * LANES
                products[:, low : low + LANES] = (
                    here * conv_pad[c, pl.ds(base + EDGE + j - HALF, conv_block), :]
                ).astype(BF16)
                total = total + scale[:, low : low + LANES] * grad_pad[
                    c, pl.ds(base + EDGE + HALF - j, conv_block), :
                ]
            grads[part, 3 * WIDE + c * LANES : 3 * WIDE + (c + 1) * LANES] = total.astype(BF16)
        tap_terms[part, :] = nt(products[...], expand_ref[...])
        return carry

    lax.fori_loop(0, rows // conv_block, conv_step, 0)
    grad_taps = jnp.transpose(tap_terms[...])[:tap_rows].reshape(heads, TAP_ROWS, rows) * tap_mask
    grad_logits = probs * (grad_taps - jnp.sum(probs * grad_taps, axis=1, keepdims=True))
    grad_logits = grad_logits.reshape(tap_rows, rows).astype(BF16)
    tap_out[slot] = grad_logits
    swap_taps = pltpu.make_async_remote_copy(
        src_ref=tap_out.at[slot],
        dst_ref=tap_in.at[slot],
        send_sem=send_sem.at[slot],
        recv_sem=recv_sem.at[slot],
        device_id=(dp, 1 - mp),
        device_id_type=MESH,
    )
    swap_taps.start()

    grad_k[...] = jnp.zeros_like(grad_k)
    grad_v[...] = jnp.zeros_like(grad_v)

    key_turned[...] = jnp.transpose(k_ref[...])
    for start in range(0, rows, block):
        part = slice(start, start + block)
        keys = key_window(start, block, rows)
        allowed = columns[keys, KERNEL : KERNEL + 1] == marks_ref[0, KERNEL : KERNEL + 1, part]
        query, context = q_ref[part, :], grad_context[part, :]
        query_turned, context_turned = jnp.transpose(query), jnp.transpose(context)
        for head in range(heads):
            lanes = slice(head * HEAD_DIM, (head + 1) * HEAD_DIM)
            place = slice(head * block, (head + 1) * block)
            mine = (only_rows(query_turned, head) * (HEAD_DIM**-0.5)).astype(BF16)
            scores = jnp.where(allowed, nn(k_ref[keys, :], mine), MASK_FILL)
            probs = jnp.exp(scores - lse_ref[0, head : head + 1, part])
            probs_all[keys, place] = probs.astype(BF16)
            mixed = probs * nn(v_ref[keys, :], only_rows(context_turned, head).astype(BF16))
            grad_scores = (mixed - probs * jnp.sum(mixed, axis=0, keepdims=True)).astype(BF16)
            scores_all[keys, place] = grad_scores
            turned_query[lanes, :] = nn(key_turned[lanes, keys], grad_scores)
        turned_query[heads * HEAD_DIM :, :] = jnp.zeros((WIDE - heads * HEAD_DIM, block), F32)
        grad_q[part, :] = jnp.transpose(turned_query[...])
        contexts = jnp.concatenate([only(context, head).astype(BF16) for head in range(heads)], 0)
        queries = jnp.concatenate([(only(query, head) * (HEAD_DIM**-0.5)).astype(BF16) for head in range(heads)], 0)
        grad_v[keys, :] += nn(probs_all[keys, :], contexts)
        grad_k[keys, :] += nn(scores_all[keys, :], queries)

    for load in loads:
        load.wait()
    swap_taps.wait()
    tap_all[...] = jnp.zeros_like(tap_all)
    tap_all[:tap_rows, :] = tap_out[slot].astype(F32)
    tap_all[tap_rows : 2 * tap_rows, :] = tap_in[slot].astype(F32)
    every = tap_all[...]
    acc_tap[...] += nn(every.astype(BF16), ca_ref[...])
    acc_tap_bias[...] += sum(every[:, c * LANES : (c + 1) * LANES] for c in range(rows // LANES))
    weights[...] = jnp.transpose(every.astype(BF16))

    def key_step(i, carry, block=512):
        base = pl.multiple_of(i * block, block)
        part = pl.ds(base, block)
        grad_attn = nn(weights[part, :], taps_ref[...]).astype(BF16).astype(F32)
        query = q_ref[part, :].astype(F32)
        key_low = (grad_attn * query).astype(BF16)
        grads[part, 4 * WIDE : 5 * WIDE] = key_low
        grad_query = grad_q[part, :] * (HEAD_DIM**-0.5) + grad_attn * kc_ref[part, :]
        grads[part, :WIDE] = grad_query.astype(BF16)
        grads[part, WIDE : 2 * WIDE] = grad_k[part, :].astype(BF16)
        grads[part, 2 * WIDE : 3 * WIDE] = grad_v[part, :].astype(BF16)
        acc_bias[...] += row_sums(grads[part, :].astype(F32))
        grad_depth = nn(key_low, point_ref[...])
        total = nn(grads[part, : 4 * WIDE], inputs_ref[...])
        for c in range(chunks):
            lanes = slice(c * LANES, (c + 1) * LANES)
            depth_pad[c, pl.ds(base + EDGE, block), :] = grad_depth[:, lanes]
            rows_total[c, part, :] = total[:, lanes]
        return carry

    lax.fori_loop(0, rows // 512, key_step, 0)
    acc_point[...] += tn(grads[:, 4 * WIDE : 5 * WIDE], dl_ref[...])
    acc_in[...] += tn(hidden_ref[...], grads[:, : 4 * WIDE])
    step = masks.shape[1]

    def depth_step(i, carry):
        base = pl.multiple_of(i * step, step)
        part = pl.ds(base, step)
        for j in range(KERNEL):
            masks[j] = jnp.broadcast_to(columns[part, j : j + 1], (step, LANES))
        for first in range(0, chunks, 2):
            total = [rows_total[first + k, part, :] for k in range(2)]
            lanes = [slice((first + k) * LANES, (first + k + 1) * LANES) for k in range(2)]
            here = [hidden_ref[part, lanes[k]].astype(F32) for k in range(2)]
            for j in range(KERNEL):
                mirror = KERNEL - 1 - j
                mask = masks[j]
                for k in range(2):
                    near = depth_pad[first + k, pl.ds(base + EDGE + j - HALF, step), :] * mask
                    total[k] = total[k] + near * depth_ref[mirror : mirror + 1, lanes[k]]
                    acc_depth[mirror, :, lanes[k]] += row_sums(near * here[k])
            for k in range(2):
                rows_total[first + k, part, :] = total[k]
        return carry

    lax.fori_loop(0, rows // step, depth_step, 0)

    @pl.when(s >= 1)
    def _():
        which = s - 1
        swap_rows(which).wait_recv()
        grad_ref[...] = own_ref[...] + other_in[which].astype(F32)

    for c in range(half):
        lanes = slice(c * LANES, (c + 1) * LANES)
        own_ref[:, lanes] = rows_total[mp * half + c] + residual_ref[:, lanes]

    @pl.when(s < seqs - 1)
    def _():
        for c in range(half):
            lanes = slice(c * LANES, (c + 1) * LANES)
            other_out[s, :, lanes] = rows_total[(1 - mp) * half + c].astype(BF16)
        swap_rows(s).start()

    @pl.when(s == 0)
    def _():
        hops.start_second()

    @pl.when(s == min(1, seqs - 1))
    def _():
        hops.start_third()

    @pl.when(s == seqs - 1)
    def _():
        for c in range(half):
            lanes = slice(c * LANES, (c + 1) * LANES)
            other_ref[:, lanes] = rows_total[(1 - mp) * half + c].astype(BF16)
        hops.finish(reduced_ref)
        for which in range(seqs - 1):
            swap_rows(which).wait_send()
        width = heads * HEAD_DIM
        group = model // 2
        cut = model // CUTS
        empty = jnp.zeros((cut, width), F32)
        point_grad = jnp.transpose(acc_point[...].astype(BF16)).astype(F32)
        for k in range(CUTS):
            part = pl.ds(k * cut, cut)
            for place in range(2):
                first = acc_in[part, 2 * place * WIDE : 2 * place * WIDE + width]
                second = acc_in[part, (2 * place + 1) * WIDE : (2 * place + 1) * WIDE + width]
                pack_ref[k, pl.ds(place * cut, cut), :] = jnp.concatenate([first, second], 1).astype(BF16)
            pack_ref[k, pl.ds(2 * cut, cut), :] = jnp.concatenate([point_grad[k * cut : (k + 1) * cut, :width], empty], 1).astype(BF16)
        table_ref[...] = jnp.zeros_like(table_ref)
        lane = lax.broadcasted_iota(jnp.int32, (LANES, WIDE), 1)
        taps = jnp.where(lane == width, jnp.sum(acc_tap_bias[...], axis=1, keepdims=True), acc_tap[...])
        own_taps = [taps[h * TAP_ROWS : h * TAP_ROWS + KERNEL] for h in range(heads)]
        other_taps = [taps[tap_rows + h * TAP_ROWS : tap_rows + h * TAP_ROWS + KERNEL] for h in range(heads)]
        for h in range(heads):
            table_ref[KERNEL * h : KERNEL * (h + 1), :] = jnp.where(mp == 0, own_taps[h], other_taps[h])
            later = KERNEL * (heads + h)
            table_ref[later : later + KERNEL, :] = jnp.where(mp == 0, other_taps[h], own_taps[h])
        for row, place in ((54, 0), (55, 2), (56, 4), (57, 3)):
            table_ref[row : row + 1, :] = jnp.sum(acc_bias[:, place * WIDE : (place + 1) * WIDE], axis=0, keepdims=True)

        def lay(row, value):
            for k in range(-(-value.shape[1] // WIDE)):
                piece = value[:, k * WIDE : (k + 1) * WIDE]
                table_ref[row + k : row + k + 1, : piece.shape[1]] = piece

        for row, source in ((58, 0), (60, 1), (62, 2)):
            lay(row, small_ref[source : source + 1, :group])
        lay(64, small_ref[6:7, :])
        for row, source in ((99, 3), (102, 4), (105, 5)):
            value = small_ref[source : source + 1, :group]
            blank = jnp.zeros_like(value)
            lay(row, jnp.where(mp == 0, jnp.concatenate([value, blank], 1), jnp.concatenate([blank, value], 1)))
        for j in range(KERNEL):
            total = jnp.sum(acc_depth[j], axis=0, keepdims=True)
            for k in range(model // WIDE):
                row = TABLE_OWN + KERNEL * k + j
                table_ref[row : row + 1, :] = total[:, k * WIDE : (k + 1) * WIDE]


def back(hidden, grad_context, grad_conv, residual, marks, kept, turned_weights, taps, depth, expand, small, pack, count, ident):
    q, k, v, cv, dl, kc, ca, probs, lse = kept
    seqs, _, rows = marks.shape
    tokens, model = hidden.shape
    width = model // 2
    tap_rows = probs.shape[1]
    wide = by_seq(rows, WIDE)
    place = pl.BlockSpec(memory_space=pl.ANY)
    padded_rows = rows + 2 * EDGE
    vmem = pltpu.VMEM
    swaps = max(seqs - 1, 1)
    return pl.pallas_call(
        functools.partial(back_kernel, seqs, count),
        grid=(seqs,),
        out_shape=(
            jax.ShapeDtypeStruct((tokens, width), F32),
            jax.ShapeDtypeStruct((rows, width), F32),
            jax.ShapeDtypeStruct((rows, width), BF16),
            jax.ShapeDtypeStruct((CUTS, 3 * model // CUTS, width), BF16),
            jax.ShapeDtypeStruct((TABLE_ROWS, WIDE), F32),
            jax.ShapeDtypeStruct(pack.shape[1:], F32),
        ),
        in_specs=[wide, wide, by_seq_row(TAP_ROWS, rows), wide, wide, wide, wide, wide]
        + [by_seq_row(tap_rows, rows), by_seq_row(8, rows)]
        + [place] * 4
        + [whole()] * 7,
        out_specs=(pl.BlockSpec((rows, width), lambda s: (jnp.maximum(s - 1, 0), 0)),) + (whole(),) * 5,
        scratch_shapes=[
            vmem((rows, model), BF16),
            vmem((rows, width), F32),
            vmem((rows, model), BF16),
            vmem((rows, WIDE), F32),
            pltpu.SemaphoreType.DMA((4,)),
            vmem((swaps, rows, width), BF16),
            vmem((swaps, rows, width), BF16),
            pltpu.SemaphoreType.DMA((swaps,)),
            pltpu.SemaphoreType.DMA((swaps,)),
        ]
        + hop_scratch(count, pack.shape[1], pack.shape[2])
        + [
            vmem((KERNEL, 128, LANES), F32),
            vmem((model // LANES, padded_rows, LANES), F32),
            vmem((2, padded_rows, LANES), F32),
            vmem((2, padded_rows, LANES), F32),
            vmem((rows, LANES), F32),
            vmem((rows, LANES), BF16),
            vmem((rows, LANES), BF16),
            vmem((rows, LANES), F32),
            vmem((128, KERNEL * WIDE), BF16),
            vmem((rows, 5 * WIDE), BF16),
            vmem((rows, WIDE), F32),
            vmem((rows, WIDE), F32),
            vmem((rows, WIDE), F32),
            vmem((WIDE, rows), BF16),
            vmem((rows, tap_rows // TAP_ROWS * 256), BF16),
            vmem((rows, tap_rows // TAP_ROWS * 256), BF16),
            vmem((WIDE, 256), F32),
            vmem((model // LANES, rows, LANES), F32),
            vmem((LANES, rows), F32),
            vmem((model, 4 * WIDE), F32),
            vmem((WIDE, model), F32),
            vmem((8, 5 * WIDE), F32),
            vmem((LANES, WIDE), F32),
            vmem((LANES, LANES), F32),
            vmem((TAP_ROWS, 8, model), F32),
            vmem((2, tap_rows, rows), BF16),
            vmem((2, tap_rows, rows), BF16),
            pltpu.SemaphoreType.DMA((2,)),
            pltpu.SemaphoreType.DMA((2,)),
        ],
        compiler_params=pltpu.CompilerParams(
            collective_id=ident, has_side_effects=True, vmem_limit_bytes=63 << 20
        ),
        name="back",
    )(
        grad_context, grad_conv, marks, q, k, v, cv, ca, probs, lse, hidden, residual, dl, kc,
        *turned_weights, taps, depth, expand, small, pack,
    )


def padded(value, multiple):
    rows = value.shape[-2]
    extra = -rows % multiple
    return jnp.pad(value, [(0, 0)] * (value.ndim - 2) + [(0, extra), (0, 0)])


def recut(pack, sizes, unit, start, count):
    if count == start:
        return pack
    parts, low = [], 0
    for size in sizes:
        rows = pack[:, low : low + size * unit].reshape(-1, pack.shape[2])
        parts.append(rows.reshape(count, -1, pack.shape[2]))
        low += size * unit
    return padded(jnp.concatenate(parts, 1), TAP_ROWS)


def gather_plain(weights, count, ident):
    q, k, v, c, p, depth, out_w, in_w, outer_w = weights
    depth = jnp.pad(depth.T, ((0, 0), (0, q.shape[1] - KERNEL)))
    pairs = [jnp.concatenate(pair, 1) for pair in ((q, k), (v, c), (p, depth), (out_w[0], out_w[1]))]
    first = padded(jnp.concatenate(pairs[:3], 0), TAP_ROWS)[None]
    second = padded(jnp.concatenate([pairs[3], in_w[0], outer_w[0]], 0), TAP_ROWS)[None]
    return recut(gather(first, count, ident), (1, 1, 1), q.shape[0], count, CUTS), second


def final_plain(first, second, table, share, share_ffn, width, group, taps):
    model = 2 * group
    depth = jnp.concatenate([table[72 + KERNEL * k : 72 + KERNEL * (k + 1)] for k in range(model // WIDE)], 1)
    row = lambda at_row, size: table[at_row : at_row + 6].reshape(-1)[:size]
    out = first[:share]
    return (
        second[:share, :width], second[:share, width:], second[share : 2 * share, :width],
        row(54, width), row(55, width),
        lax.dynamic_slice_in_dim(depth, lax.axis_index("dp") * share, share, 1),
        second[2 * share : 3 * share, :width], row(56, width),
        table[:taps, :width], table[:taps, width], second[share : 2 * share, width:], row(57, width),
        jnp.stack([out[:, :width], out[:, width:]]), row(105, model), row(99, model), row(102, model),
        first[share : share + share_ffn], row(64, 4 * group)[None], first[share + share_ffn : share + 2 * share_ffn],
        row(58, group), row(60, group), row(62, group),
    )


def on_device(
    count,
    hidden, doc_lengths, query_weight, key_weight, value_weight, query_bias, value_bias,
    depth_weight, point_weight, point_bias, kernel_weight, kernel_bias, conv_weight, conv_bias,
    out_weight, out_bias, norm1_gain, norm1_bias, ffn_in_weight, ffn_in_bias, ffn_out_weight,
    ffn_out_bias, norm2_gain, norm2_bias, out_grad,
):
    share, width = query_weight.shape
    model = hidden.shape[1]
    group = ffn_out_bias.shape[0]
    share_ffn = ffn_out_weight.shape[1]
    heads = width // HEAD_DIM
    weights = (
        query_weight, key_weight, value_weight, conv_weight, point_weight, depth_weight,
        out_weight.transpose(0, 2, 1), ffn_in_weight.transpose(0, 2, 1), ffn_out_weight,
    )
    first, second = (gather_first if share % TAP_ROWS == 0 else gather_plain)(weights, count, 1)
    seqs = doc_lengths.shape[0]
    early = seqs - 1 if count == CUTS else 0
    biases = [kernel_bias, query_bias, value_bias, point_bias, conv_bias]
    q, k, v, cv, dl, kc, ca, probs, cc, ctx, lse, second_all, marks, taps, depth, expand, *rest = front(
        hidden, doc_lengths, first, kernel_weight.T, biases, second, count, early, 2
    )
    turned_weights, early_rows = rest[:2], rest[2]
    vectors = [out_bias, norm1_gain, norm1_bias, ffn_out_bias, norm2_gain, norm2_bias, ffn_in_bias]
    output, grad_residual, grad_context, grad_conv, pack_mid, sums_mid = middle(
        max(2 * early - 1, 0) * (hidden.shape[0] // seqs) // 2, early_rows, ctx, cc, hidden, out_grad, recut(second_all, (1, 2, 2), share, count, CUTS), vectors, 4
    )
    grad_input, own_last, other_last, pack_back, table, first_sum = back(
        hidden, grad_context, grad_conv, grad_residual, marks, (q, k, v, cv, dl, kc, ca, probs, lse),
        turned_weights, taps, depth, expand, sums_mid, recut(pack_mid, (1, 2, 2), model // CUTS, CUTS, count), count, 5,
    )
    second_sum, totals, grad_input = tail(
        recut(pack_back, (1, 1, 1), model // CUTS, CUTS, count), table, own_last, other_last, grad_input, count, 3
    )
    small_cuts = (share, share_ffn, width, group, 2 * heads * KERNEL)
    if share % TAP_ROWS == 0:
        results = final(first_sum, second_sum, totals, *small_cuts, count)
    else:
        results = final_plain(first_sum, second_sum, totals, *small_cuts)
    q_g, k_g, v_g, q_b, v_b, depth_g, p_g, p_b, kw_g, kb_g, c_g, c_b, out_g, out_b, gain1, bias1 = results[:16]
    inner_g, inner_b, outer_g, outer_b, gain2, bias2 = results[16:]
    return (
        output, grad_input, q_g, k_g, v_g, q_b, v_b, depth_g, p_g, p_b, kw_g.T, kb_g, c_g, c_b, out_g.transpose(0, 2, 1),
        out_b, gain1, bias1, inner_g.T[None], inner_b, outer_g[None], outer_b, gain2, bias2,
    )


def solution(mesh):
    in_specs = (
        P("dp", None),
        P("dp", None),
        P("dp", "mp"),
        P("dp", "mp"),
        P("dp", "mp"),
        P("mp"),
        P("mp"),
        P(None, "dp"),
        P("dp", "mp"),
        P("mp"),
        P("mp", None),
        P(),
        P("dp", "mp"),
        P("mp"),
        P(None, "mp", "dp"),
        P(),
        P(),
        P(),
        P("mp", None, "dp"),
        P("mp", None),
        P("mp", "dp", None),
        P("mp"),
        P("mp"),
        P("mp"),
        P("dp", "mp"),
    )
    out_specs = (
        P("dp", "mp"),
        P("dp", "mp"),
        P("dp", "mp"),
        P("dp", "mp"),
        P("dp", "mp"),
        P("mp"),
        P("mp"),
        P(None, "dp"),
        P("dp", "mp"),
        P("mp"),
        P("mp", None),
        P(),
        P("dp", "mp"),
        P("mp"),
        P(None, "mp", "dp"),
        P(),
        P(),
        P(),
        P("mp", None, "dp"),
        P("mp", None),
        P("mp", "dp", None),
        P("mp"),
        P("mp"),
        P("mp"),
    )
    return jax.shard_map(
        functools.partial(on_device, mesh.shape["dp"]), mesh=mesh, in_specs=in_specs, out_specs=out_specs, check_vma=False
    )
```

```python
import functools
import jax
import jax.numpy as jnp
from jax import lax
from jax.experimental import pallas as pl
from jax.experimental.pallas import tpu as pltpu

from jax.sharding import PartitionSpec as P

MESH = pl.DeviceIdType.MESH
BF16 = jnp.bfloat16
F32 = jnp.float32
HEAD_DIM = 64
KERNEL = 9
HALF = KERNEL // 2
CUTS = 16
TABLE_OWN = 72
TABLE_ROWS = 112
TAP_ROWS = 16
WIDE = 256
LANES = 128
EDGE = 8
MOST_DOC = 512


def at(dp, mp):
    return (dp, mp)


def places(count):
    dp = lax.axis_index("dp")
    core = lax.rem(dp, 2)
    side = lax.rem(lax.div(dp, 2), 2)
    deep = lax.div(dp, 4)
    return lax.axis_index("mp"), core, side, deep, count // 4


def index_of(deep, side, core):
    return (deep * 2 + side) * 2 + core


def greet(count):
    mp, core, side, deep, parts = places(count)
    barrier = pltpu.get_barrier_semaphore()
    peers = [index_of(lax.rem(deep + k, parts), side, core) for k in range(1, parts)]
    peers += [index_of(deep, 1 - side, core), index_of(deep, side, 1 - core)]
    for peer in peers:
        pl.semaphore_signal(barrier, inc=1, device_id=at(peer, mp), device_id_type=MESH)
    pl.semaphore_wait(barrier, len(peers))


def turned(tile, value):
    rows, columns = value.shape
    tile[...] = jnp.zeros_like(tile)
    tile[:rows, :columns] = value.astype(F32)
    return jnp.transpose(tile[...])[:columns, :rows]


def beside_each(first, second):
    return jnp.concatenate([first.astype(F32), second.astype(F32)], 1).astype(BF16)


def gather_body(count, own_ref, out_ref, own_sem, send_sem, recv_sem):
    mp, core, side, deep, parts = places(count)
    me = index_of(deep, side, core)
    local = pltpu.make_async_copy(own_ref.at[0], out_ref.at[me], own_sem)
    local.start()
    started = []

    def push(source, block, target):
        copy = pltpu.make_async_remote_copy(
            src_ref=source,
            dst_ref=out_ref.at[block],
            send_sem=send_sem.at[len(started)],
            recv_sem=recv_sem.at[block],
            device_id=at(target, mp),
            device_id_type=MESH,
        )
        copy.start()
        started.append(copy)

    def arrive(block):
        pltpu.make_async_copy(own_ref.at[0], out_ref.at[block], recv_sem.at[block]).wait()

    beside = index_of(deep, 1 - side, core)
    twin = index_of(deep, side, 1 - core)
    for k in range(1, parts):
        push(own_ref.at[0], me, index_of(lax.rem(deep + k, parts), side, core))
    push(own_ref.at[0], me, beside)
    push(own_ref.at[0], me, twin)
    yield
    arrive(beside)
    push(out_ref.at[beside], beside, twin)
    for k in range(1, parts):
        block = index_of(lax.rem(deep + parts - k, parts), side, core)
        arrive(block)
        push(out_ref.at[block], block, beside)
        push(out_ref.at[block], block, twin)
    for k in range(1, parts):
        block = index_of(lax.rem(deep + parts - k, parts), 1 - side, core)
        arrive(block)
        push(out_ref.at[block], block, twin)
    for k in range(parts):
        for other in range(2):
            arrive(index_of(lax.rem(deep + parts - k, parts), other, 1 - core))
    for copy in started:
        copy.wait_send()
    local.wait()
    yield


def gather_kernel(count, own_ref, out_ref, own_sem, send_sem, recv_sem):
    greet(count)
    for _ in gather_body(count, own_ref, out_ref, own_sem, send_sem, recv_sem):
        pass


def pack_kernel(
    count, q_ref, k_ref, v_ref, c_ref, p_ref, depth_ref, out_w_ref, in_w_ref, outer_w_ref,
    out_ref, second_ref,
    own_ref, tile_depth, own_sem, send_sem, recv_sem,
):
    share, width = q_ref.shape
    share_ffn = outer_w_ref.shape[1]
    own_ref[0, :share, :] = beside_each(q_ref[...], k_ref[...])
    own_ref[0, share : 2 * share, :] = beside_each(v_ref[...], c_ref[...])
    depth = turned(tile_depth, depth_ref[...])
    depth = jnp.concatenate([depth, jnp.zeros((share, width - KERNEL), F32)], 1)
    own_ref[0, 2 * share : 3 * share, :] = beside_each(p_ref[...], depth)
    greet(count)
    moves = gather_body(count, own_ref, out_ref, own_sem, send_sem, recv_sem)
    next(moves)
    second_ref[0, :share, :] = beside_each(out_w_ref[0], out_w_ref[1])
    second_ref[0, share : share + share_ffn, :] = in_w_ref[0]
    second_ref[0, share + share_ffn :, :] = outer_w_ref[0]
    next(moves)


def gather_first(weights, count, ident):
    q, depth, out_w, in_w, outer_w = weights[0], weights[5], weights[6], weights[7], weights[8]
    share, width = q.shape
    share_ffn, group = outer_w.shape[1:]
    parts = count // 4
    vmem = pl.BlockSpec(memory_space=pltpu.VMEM)
    return pl.pallas_call(
        functools.partial(pack_kernel, count),
        out_shape=(
            jax.ShapeDtypeStruct((count, 3 * share, 2 * width), BF16),
            jax.ShapeDtypeStruct((1, share + 2 * share_ffn, group), BF16),
        ),
        in_specs=[vmem] * 9,
        out_specs=(pl.BlockSpec(memory_space=pl.ANY), vmem),
        scratch_shapes=[
            pltpu.VMEM((1, 3 * share, 2 * width), BF16),
            pltpu.VMEM((LANES, LANES), F32),
            pltpu.SemaphoreType.DMA,
            pltpu.SemaphoreType.DMA((4 * parts - 1,)),
            pltpu.SemaphoreType.DMA((count,)),
        ],
        compiler_params=pltpu.CompilerParams(collective_id=ident, has_side_effects=True),
        name="weight_gather",
    )(*weights)


def gather(own, count, ident):
    parts = count // 4
    return pl.pallas_call(
        functools.partial(gather_kernel, count),
        out_shape=jax.ShapeDtypeStruct((count,) + own.shape[1:], own.dtype),
        in_specs=[pl.BlockSpec(memory_space=pl.ANY)],
        out_specs=pl.BlockSpec(memory_space=pl.ANY),
        scratch_shapes=[
            pltpu.SemaphoreType.DMA,
            pltpu.SemaphoreType.DMA((4 * parts - 1,)),
            pltpu.SemaphoreType.DMA((count,)),
        ],
        compiler_params=pltpu.CompilerParams(collective_id=ident, has_side_effects=True),
        name="weight_gather",
    )(own)


class Hops:
    def __init__(self, count, in_ref, twin_in, side_in, deep_in, send_sem, recv_sem):
        self.mp, self.core, self.side, self.deep, self.parts = places(count)
        self.in_ref, self.twin_in, self.side_in, self.deep_in = in_ref, twin_in, side_in, deep_in
        self.send_sem, self.recv_sem = send_sem, recv_sem
        self.beside = index_of(self.deep, 1 - self.side, self.core)
        self.twin = index_of(self.deep, self.side, 1 - self.core)
        self.order = [(k, other) for k in list(range(1, self.parts)) + [0] for other in (1, 0)]
        self.rows = in_ref.shape[1]
        self.step = 48 if self.rows % 48 == 0 else 16

    def depth(self, k):
        return lax.rem(self.deep + k, self.parts)

    def copy(self, source, target_ref, slot, target):
        return pltpu.make_async_remote_copy(
            src_ref=source,
            dst_ref=target_ref,
            send_sem=self.send_sem.at[slot],
            recv_sem=self.recv_sem.at[slot],
            device_id=at(target, self.mp),
            device_id_type=MESH,
        )

    def block(self, slot, core):
        k, other = self.order[slot]
        return index_of(self.depth(k), 1 - self.side if other else self.side, core)

    def first(self, slot):
        return self.copy(self.in_ref.at[self.block(slot, 1 - self.core)], self.twin_in.at[slot], slot, self.twin)

    def second(self, place):
        return self.copy(
            self.twin_in.at[2 * place], self.side_in.at[place], 2 * self.parts + place, self.beside
        )

    def third(self, place):
        k = self.order[2 * place][0]
        target = index_of(self.depth(k), self.side, self.core)
        return self.copy(self.side_in.at[place], self.deep_in.at[place], 3 * self.parts + place, target)

    def add(self, target, term):
        @pl.loop(0, self.rows // self.step)
        def _(i):
            part = pl.ds(pl.multiple_of(i * self.step, 16), self.step)
            total = target[part, :].astype(F32) + term[part, :].astype(F32)
            target[part, :] = total.astype(target.dtype)

    def start_first(self):
        for slot in range(2 * self.parts):
            self.first(slot).start()

    def start_second(self):
        for slot in range(2 * self.parts):
            self.first(slot).wait_recv()
            self.add(self.twin_in.at[slot], self.in_ref.at[self.block(slot, self.core)])
            if self.order[slot][1]:
                self.second(slot // 2).start()

    def start_third(self):
        for place in range(self.parts):
            self.second(place).wait_recv()
            self.add(self.side_in.at[place], self.twin_in.at[2 * place + 1])
            if place < self.parts - 1:
                self.third(place).start()

    def finish(self, out_ref):
        for place in range(self.parts - 1):
            self.third(place).wait_recv()

        @pl.loop(0, self.rows // self.step)
        def _(i):
            part = pl.ds(pl.multiple_of(i * self.step, 16), self.step)
            total = self.side_in[self.parts - 1, part, :].astype(F32)
            for place in range(self.parts - 1):
                total = total + self.deep_in[place, part, :].astype(F32)
            out_ref[part, :] = total

        for slot in range(2 * self.parts):
            self.first(slot).wait_send()
        for place in range(self.parts):
            self.second(place).wait_send()
        for place in range(self.parts - 1):
            self.third(place).wait_send()


def hop_scratch(count, rows, columns):
    parts = count // 4
    return [
        pltpu.VMEM((2 * parts, rows, columns), BF16),
        pltpu.VMEM((parts, rows, columns), BF16),
        pltpu.VMEM((max(parts - 1, 1), rows, columns), BF16),
        pltpu.SemaphoreType.DMA((4 * parts - 1,)),
        pltpu.SemaphoreType.DMA((4 * parts - 1,)),
    ]


def greet_all(count):
    mp, core, side, deep, parts = places(count)
    me = index_of(deep, side, core)
    barrier = pltpu.get_barrier_semaphore()
    pl.semaphore_signal(barrier, inc=1, device_id=at(me, 1 - mp), device_id_type=MESH)
    peers = [index_of(lax.rem(deep + k, parts), side, core) for k in range(1, parts)]
    peers += [index_of(deep, 1 - side, core), index_of(deep, side, 1 - core)]
    for peer in peers:
        pl.semaphore_signal(barrier, inc=1, device_id=at(peer, mp), device_id_type=MESH)
    pl.semaphore_wait(barrier, len(peers) + 1)


PIECES = 4


def tail_kernel(
    count, start,
    in_ref, table_ref, own_ref, other_ref, rest_ref,
    out_ref, total_ref, grad_ref,
    twin_in, side_in, deep_in, send_sem, recv_sem,
    table_in, table_out, table_send, table_recv, piece_in, piece_sum, piece_send, piece_recv, store_sem,
):
    mp, core, side, deep, parts = places(count)
    me = index_of(deep, side, core)
    greet_all(count)
    beside = index_of(deep, 1 - side, core)
    twin = index_of(deep, side, 1 - core)
    hops = Hops(count, in_ref, twin_in, side_in, deep_in, send_sem, recv_sem)
    rows = own_ref.shape[0] // PIECES

    def table_hop(source, slot, target, plane):
        return pltpu.make_async_remote_copy(
            src_ref=source,
            dst_ref=table_in.at[slot],
            send_sem=table_send.at[slot],
            recv_sem=table_recv.at[slot],
            device_id=at(target, plane),
            device_id_type=MESH,
        )

    def piece(i):
        part = pl.ds(i * rows, rows)
        return pltpu.make_async_remote_copy(
            src_ref=other_ref.at[part],
            dst_ref=piece_in.at[part],
            send_sem=piece_send.at[i],
            recv_sem=piece_recv.at[i],
            device_id=at(me, 1 - mp),
            device_id_type=MESH,
        )

    def store(i):
        return pltpu.make_async_copy(
            piece_sum.at[pl.ds(i * rows, rows)], grad_ref.at[pl.ds(start + i * rows, rows)], store_sem.at[i]
        )

    shared = pl.ds(TABLE_OWN, TABLE_ROWS - TABLE_OWN)
    first = pltpu.make_async_remote_copy(
        src_ref=table_ref.at[shared],
        dst_ref=table_in.at[0, shared],
        send_sem=table_send.at[0],
        recv_sem=table_recv.at[0],
        device_id=at(me, 1 - mp),
        device_id_type=MESH,
    )
    first.start()
    hops.start_first()
    for i in range(PIECES):
        piece(i).start()
    first.wait_recv()
    table_out[0, :TABLE_OWN, :] = table_ref[:TABLE_OWN, :]
    table_out[0, shared, :] = table_ref[shared, :] + table_in[0, shared, :]
    second = table_hop(table_out.at[0], 1, twin, mp)
    second.start()
    second.wait_recv()
    table_out[1] = table_out[0] + table_in[1]
    third = table_hop(table_out.at[1], 2, beside, mp)
    third.start()
    hops.start_second()
    third.wait_recv()
    table_out[2] = table_out[1] + table_in[2]
    fourth = [
        table_hop(table_out.at[2], 2 + j, index_of(lax.rem(deep + j, parts), side, core), mp) for j in range(1, parts)
    ]
    for copy in fourth:
        copy.start()
    hops.start_third()
    for i in range(PIECES):
        piece(i).wait_recv()
        part = pl.ds(i * rows, rows)
        piece_sum[part, :] = own_ref[part, :] + piece_in[part, :].astype(F32)
        store(i).start()
    hops.finish(out_ref)
    for copy in fourth:
        copy.wait_recv()
    total = table_out[2]
    for j in range(1, parts):
        total = total + table_in[2 + j]
    total_ref[...] = total
    for copy in [first, second, third] + fourth:
        copy.wait_send()
    for i in range(PIECES):
        piece(i).wait_send()
        store(i).wait()


def tail(blocks, table, own, other, grad_rows, count, ident):
    parts = count // 4
    _, rows, columns = blocks.shape
    start = grad_rows.shape[0] - own.shape[0]
    vmem = pl.BlockSpec(memory_space=pltpu.VMEM)
    place = pl.BlockSpec(memory_space=pl.ANY)
    return pl.pallas_call(
        functools.partial(tail_kernel, count, start),
        out_shape=(
            jax.ShapeDtypeStruct((rows, columns), F32),
            jax.ShapeDtypeStruct(table.shape, F32),
            jax.ShapeDtypeStruct(grad_rows.shape, F32),
        ),
        in_specs=[vmem, vmem, vmem, vmem, place],
        out_specs=(vmem, vmem, place),
        input_output_aliases={4: 2},
        scratch_shapes=hop_scratch(count, rows, columns)
        + [
            pltpu.VMEM((parts + 2,) + table.shape, F32),
            pltpu.VMEM((3,) + table.shape, F32),
            pltpu.SemaphoreType.DMA((parts + 2,)),
            pltpu.SemaphoreType.DMA((parts + 2,)),
            pltpu.VMEM(other.shape, BF16),
            pltpu.VMEM(own.shape, F32),
            pltpu.SemaphoreType.DMA((PIECES,)),
            pltpu.SemaphoreType.DMA((PIECES,)),
            pltpu.SemaphoreType.DMA((PIECES,)),
        ],
        compiler_params=pltpu.CompilerParams(
            collective_id=ident, has_side_effects=True, vmem_limit_bytes=60 << 20
        ),
        name="tail",
    )(blocks, table, own, other, grad_rows)


def wide_row(table, row, count):
    return jnp.concatenate([table[row + k : row + k + 1, :] for k in range(count)], 1)


def final_kernel(
    count, first_ref, second_ref, table_ref,
    q_ref, k_ref, v_ref, qb_ref, vb_ref, depth_ref, p_ref, pb_ref, kw_ref, kb_ref, c_ref, cb_ref, out_ref, ob_ref,
    gain1_ref, bias1_ref, inner_ref, inb_ref, outer_ref, outb_ref, gain2_ref, bias2_ref,
    spread,
):
    share, width = q_ref.shape
    share_ffn, group = outer_ref.shape
    q_ref[...] = second_ref[:share, :width]
    k_ref[...] = second_ref[:share, width : 2 * width]
    v_ref[...] = second_ref[share : 2 * share, :width]
    c_ref[...] = second_ref[share : 2 * share, width : 2 * width]
    p_ref[...] = second_ref[2 * share : 3 * share, :width]
    out_ref[0] = first_ref[:share, :width]
    out_ref[1] = first_ref[:share, width : 2 * width]
    inner_ref[...] = first_ref[share : share + share_ffn, :]
    outer_ref[...] = first_ref[share + share_ffn : share + 2 * share_ffn, :]
    taps = kb_ref.shape[0]
    kw_ref[...] = table_ref[:taps, :width]
    rows = jnp.transpose(jnp.concatenate([table_ref[:64, LANES:], jnp.zeros((64, LANES), F32)], 0))
    kb_ref[...] = rows[width - LANES : width - LANES + 1, :taps].reshape(taps)
    for target, row in ((qb_ref, 54), (vb_ref, 55), (pb_ref, 56), (cb_ref, 57)):
        target[...] = table_ref[row : row + 1, :width].reshape(width)
    for target, row in ((outb_ref, 58), (gain2_ref, 60), (bias2_ref, 62)):
        target[...] = wide_row(table_ref, row, 2)[:, :group].reshape(group)
    inb_ref[...] = wide_row(table_ref, 64, 6)
    for target, row in ((gain1_ref, 99), (bias1_ref, 102), (ob_ref, 105)):
        target[...] = wide_row(table_ref, row, 3).reshape(2 * group)
    spread[...] = jnp.zeros_like(spread)
    for k in range(3):
        spread[:KERNEL, k * WIDE : (k + 1) * WIDE] = table_ref[72 + KERNEL * k : 72 + KERNEL * (k + 1), :]
    model = spread.shape[1]
    dp = lax.axis_index("dp")
    moved = pltpu.roll(spread[...], lax.rem(model - dp * share, model), 1)
    depth_ref[...] = moved[:KERNEL, :share]


def final(first, second, table, share, share_ffn, width, group, taps, count):
    def shape(*sizes):
        return jax.ShapeDtypeStruct(sizes, F32)

    model = 2 * group
    return pl.pallas_call(
        functools.partial(final_kernel, count),
        out_shape=(
            shape(share, width), shape(share, width), shape(share, width), shape(width), shape(width),
            shape(KERNEL, share), shape(share, width), shape(width), shape(taps, width), shape(taps),
            shape(share, width), shape(width), shape(2, share, width), shape(model), shape(model),
            shape(model), shape(share_ffn, group), shape(1, 4 * group), shape(share_ffn, group), shape(group),
            shape(group), shape(group),
        ),
        in_specs=[whole()] * 3,
        out_specs=(whole(),) * 22,
        scratch_shapes=[
            pltpu.VMEM((TAP_ROWS, model), F32),
        ],
        name="final",
    )(first, second, table)


EPSILON = 1e-06
MASK_FILL = -1e30
INV_ROOT2 = 0.7071067811865476
INV_ROOT_TWO_PI = 0.3989422804014327


def nn(left, right):
    return jnp.dot(left, right, preferred_element_type=F32)


def tn(left, right):
    return lax.dot_general(left, right, (((0,), (0,)), ((), ())), preferred_element_type=F32)


def nt(left, right):
    return lax.dot_general(left, right, (((1,), (1,)), ((), ())), preferred_element_type=F32)


def moments(sum_own, square_own, sum_other, square_other, width):
    mean = (sum_own + sum_other) / (2 * width)
    apart = (sum_own - sum_other) / width
    spread = (square_own + square_other + apart * apart * (width / 2)) / (2 * width)
    return mean, lax.rsqrt(spread + EPSILON)


def as_row(value):
    return value.reshape(1, -1)


def spread_marks(marks_ref, columns_ref):
    rows = marks_ref.shape[2]
    wide = jnp.concatenate([marks_ref[0], jnp.zeros((LANES - TAP_ROWS, rows), F32)], 0)
    columns_ref[...] = jnp.transpose(wide.astype(BF16)).astype(F32)


def write_marks(lengths_ref, s, marks_ref):
    rows = marks_ref.shape[2]
    place = lax.broadcasted_iota(jnp.int32, (1, rows), 1)
    segment = jnp.zeros((1, rows), jnp.int32)
    end = 0
    for document in range(lengths_ref.shape[1]):
        end = end + lengths_ref[s, document]
        segment = segment + (place >= end).astype(jnp.int32)
    segment = segment.astype(F32)
    for tap in range(KERNEL):
        offset = tap - HALF
        there = pltpu.roll(segment, -offset % rows, 1) if offset else segment
        inside = jnp.logical_and(place + offset >= 0, place + offset < rows)
        marks_ref[0, tap : tap + 1, :] = jnp.where(jnp.logical_and(there == segment, inside), 1.0, 0.0)
    marks_ref[0, KERNEL : KERNEL + 1, :] = segment
    marks_ref[0, KERNEL + 1 :, :] = jnp.zeros((TAP_ROWS - KERNEL - 1, rows), F32)


def unpack_wide(target, source_ref, start, low, width):
    cut = target.shape[0] // CUTS
    for k in range(CUTS):
        rows = source_ref[k, pl.ds(start, cut), :].astype(F32)[:, low : low + width]
        rows = jnp.concatenate([rows, jnp.zeros((cut, WIDE - width), F32)], 1)
        target[pl.ds(k * cut, cut), :] = rows.astype(target.dtype)


def tap_places(heads, mp):
    row = lax.broadcasted_iota(jnp.int32, (LANES, LANES), 0)
    column = lax.broadcasted_iota(jnp.int32, (LANES, LANES), 1)
    tap_rows = heads * TAP_ROWS
    far = row >= tap_rows
    inner = jnp.where(far, row - tap_rows, row)
    head, tap = lax.shift_right_logical(inner, 4), jnp.bitwise_and(inner, TAP_ROWS - 1)
    half = jnp.where(far, 1 - mp, mp)
    valid = jnp.logical_and(tap < KERNEL, row < 2 * tap_rows)
    return jnp.logical_and(valid, column == (half * heads + head) * KERNEL + tap)


def write_expansion(target, heads):
    row = lax.broadcasted_iota(jnp.int32, (LANES, WIDE), 0)
    lane = lax.broadcasted_iota(jnp.int32, (LANES, WIDE), 1)
    tap_rows = heads * TAP_ROWS
    inner = jnp.where(row >= tap_rows, row - tap_rows, row)
    inside = jnp.logical_and(lane < heads * HEAD_DIM, row < 2 * tap_rows)
    head = lax.shift_right_logical(lane, 6) * TAP_ROWS
    for tap in range(KERNEL):
        chosen = jnp.logical_and(inside, inner == head + tap)
        target[:, tap * WIDE : (tap + 1) * WIDE] = jnp.where(chosen, 1.0, 0.0).astype(BF16)


def key_window(start, size, rows):
    low = max(0, start - (MOST_DOC - 1)) // size * size
    high = min(rows, -(-(start + size - 1 + MOST_DOC) // size) * size)
    return slice(low, high)


def only_rows(value, head):
    row = lax.broadcasted_iota(jnp.int32, (WIDE, 1), 0)
    return jnp.where(jnp.logical_and(row >= head * HEAD_DIM, row < (head + 1) * HEAD_DIM), value.astype(F32), 0.0)


def head_lanes(head):
    lane = lax.broadcasted_iota(jnp.int32, (1, WIDE), 1)
    return jnp.logical_and(lane >= head * HEAD_DIM, lane < (head + 1) * HEAD_DIM)


def only(value, head):
    return jnp.where(head_lanes(head), value.astype(F32), 0.0)


def high_low(weights, heads):
    high = weights.astype(BF16).astype(F32)
    low = weights - high
    rest = jnp.zeros((LANES - 2 * heads * TAP_ROWS, weights.shape[1]), F32)
    return jnp.transpose(jnp.concatenate([high, low, rest], 0).astype(BF16))


def front_kernel(
    seqs, count, early,
    hidden_ref, lengths_ref, first_ref, kw_ref, kb_ref, qb_ref, vb_ref, pb_ref, cb_ref, second_ref,
    q_ref, k_ref, v_ref, cv_ref, dl_ref, kc_ref, ca_ref, probs_ref, cc_ref, ctx_ref, lse_ref, second_all_ref,
    marks_ref, taps_ref, depth_ref, expand_ref, inputs_turned_ref, point_turned_ref, early_ref,
    lead_ref, out0_nat, out1_nat, part_out, part_send, part_recv,
    query_ref, key_ref, value_ref, conv_ref, point_ref, vec_ref, bias_ref, depth_wide, tile,
    masks, rows_pad, conv_pad, columns, weights, query_turned, value_turned, context_turned, tap_out, tap_in,
    send_sem, recv_sem, own_sem, gather_send, gather_recv,
):
    s = pl.program_id(0)
    mp, core, side, deep, parts = places(count)
    me = index_of(deep, side, core)
    rows, model = hidden_ref.shape
    chunks = model // LANES
    heads = probs_ref.shape[1] // TAP_ROWS
    tap_rows = heads * TAP_ROWS
    beside = index_of(deep, 1 - side, core)
    twin = index_of(deep, side, 1 - core)

    split = lead_ref.shape[1]
    spans = [pl.ds(0, split), pl.ds(split, second_ref.shape[1] - split)]

    def push(group, source, block, target, slot):
        return pltpu.make_async_remote_copy(
            src_ref=source.at[spans[group]],
            dst_ref=second_all_ref.at[block, spans[group]],
            send_sem=gather_send.at[group, slot],
            recv_sem=gather_recv.at[group, block],
            device_id=at(target, mp),
            device_id_type=MESH,
        )

    def arrive(group, block):
        pltpu.make_async_copy(
            second_ref.at[0, spans[group]], second_all_ref.at[block, spans[group]], gather_recv.at[group, block]
        ).wait()

    own_copy = pltpu.make_async_copy(second_ref.at[0], second_all_ref.at[me], own_sem.at[0])
    lead_copy = pltpu.make_async_copy(second_all_ref.at[:, spans[0]], lead_ref, own_sem.at[1])
    first_hops = [(me, index_of(lax.rem(deep + k, parts), side, core), k - 1) for k in range(1, parts)]
    first_hops += [(me, beside, parts - 1), (me, twin, parts)]
    second_hops = [(beside, [(twin, parts + 1)])]
    for k in range(1, parts):
        block = index_of(lax.rem(deep + parts - k, parts), side, core)
        second_hops.append((block, [(beside, parts + 2 * k), (twin, parts + 2 * k + 1)]))
    third_hops = [
        (index_of(lax.rem(deep + parts - k, parts), 1 - side, core), [(twin, 3 * parts + k - 1)]) for k in range(1, parts)
    ]

    def start_hops(group):
        for block, target, place in first_hops:
            push(group, second_ref.at[0], block, target, place).start()

    def pass_on(group, hops):
        for block, targets in hops:
            arrive(group, block)
            for target, place in targets:
                push(group, second_all_ref.at[block], block, target, place).start()

    def end_hops(group):
        for k in range(parts):
            for other in range(2):
                arrive(group, index_of(lax.rem(deep + parts - k, parts), other, 1 - core))
        for block, target, place in first_hops:
            push(group, second_ref.at[0], block, target, place).wait_send()
        for block, targets in second_hops + third_hops:
            for target, place in targets:
                push(group, second_all_ref.at[block], block, target, place).wait_send()

    def swap_part(which, piece):
        size = rows // PIECES
        return pltpu.make_async_remote_copy(
            src_ref=part_out.at[which, pl.ds(piece * size, size)],
            dst_ref=early_ref.at[pl.ds(which * rows + piece * size, size)],
            send_sem=part_send.at[which, piece],
            recv_sem=part_recv.at[which, piece],
            device_id=at(me, 1 - mp),
            device_id_type=MESH,
        )

    @pl.when(s == 0)
    def _():
        barrier = pltpu.get_barrier_semaphore()
        pl.semaphore_signal(barrier, inc=1, device_id=at(me, 1 - mp), device_id_type=MESH)
        peers = [index_of(lax.rem(deep + k, parts), side, core) for k in range(1, parts)] + [beside, twin]
        for peer in peers:
            pl.semaphore_signal(barrier, inc=1, device_id=at(peer, mp), device_id_type=MESH)
        pl.semaphore_wait(barrier, len(peers) + 1)
        own_copy.start()
        start_hops(0)
        start_hops(1)
        width = heads * HEAD_DIM
        cut = model // CUTS
        for target, place, low in (
            (query_ref, 0, 0), (key_ref, 0, width), (value_ref, 1, 0), (conv_ref, 1, width), (point_ref, 2, 0),
            (depth_wide, 2, width),
        ):
            unpack_wide(target, first_ref, place * cut, low, width)
        depth_ref[...] = jnp.transpose(depth_wide[:, :LANES])[:TAP_ROWS]
        vec_ref[...] = jnp.zeros_like(vec_ref)
        for row, source in enumerate((qb_ref, vb_ref, pb_ref, cb_ref)):
            vec_ref[row : row + 1, :width] = as_row(source[...])
        write_expansion(expand_ref, heads)
        chosen = tap_places(heads, mp)
        tile[...] = jnp.zeros_like(tile)
        tile[:1, : kb_ref.shape[0]] = as_row(kb_ref[...])
        bias = jnp.sum(jnp.where(chosen, tile[:1, :LANES], 0.0), axis=1, keepdims=True)
        bias_ref[...] = jnp.broadcast_to(bias[:tap_rows], bias_ref.shape)
        tile[: kw_ref.shape[0], :width] = kw_ref[...].astype(F32)
        turned_weight = tile[:LANES, :].astype(BF16)
        taps_ref[...] = nn(jnp.where(chosen, 1.0, 0.0).astype(BF16), turned_weight).astype(BF16)
        for place, source in enumerate((query_ref, key_ref, value_ref, conv_ref)):
            inputs_turned_ref[place * WIDE : (place + 1) * WIDE, :] = jnp.transpose(source[...])
        point_turned_ref[...] = jnp.transpose(point_ref[...])
        rows_pad[:, :EDGE, :] = jnp.zeros((chunks, EDGE, LANES), F32)
        rows_pad[:, pl.ds(EDGE + rows, EDGE), :] = jnp.zeros((chunks, EDGE, LANES), F32)
        conv_pad[:, :EDGE, :] = jnp.zeros((2, EDGE, LANES), F32)
        conv_pad[:, pl.ds(EDGE + rows, EDGE), :] = jnp.zeros((2, EDGE, LANES), F32)

    write_marks(lengths_ref, s, marks_ref)
    spread_marks(marks_ref, columns)
    hidden = hidden_ref[...]
    for c in range(chunks):
        rows_pad[c, pl.ds(EDGE, rows), :] = hidden[:, c * LANES : (c + 1) * LANES].astype(F32)

    step = masks.shape[1]

    def depth_step(i, carry):
        base = pl.multiple_of(i * step, step)
        part = pl.ds(base, step)
        for tap in range(KERNEL):
            masks[tap] = jnp.broadcast_to(columns[part, tap : tap + 1], (step, LANES))
        for first in range(0, chunks, 2):
            total = [jnp.zeros((step, LANES), F32)] * 2
            for tap in range(KERNEL):
                mask = masks[tap]
                for k in range(2):
                    c = first + k
                    moved = rows_pad[c, pl.ds(base + EDGE + tap - HALF, step), :]
                    total[k] = total[k] + (moved * mask) * depth_ref[tap : tap + 1, c * LANES : (c + 1) * LANES]
            for k in range(2):
                dl_ref[part, (first + k) * LANES : (first + k + 1) * LANES] = total[k].astype(BF16)
        return carry

    lax.fori_loop(0, rows // step, depth_step, 0)

    @pl.when(s == 0)
    def _():
        pass_on(0, second_hops)

    queries = (nn(hidden, query_ref[...]) + vec_ref[0:1, :]).astype(BF16)
    q_ref[...] = queries
    key_conv = nn(dl_ref[...], point_ref[...]) + vec_ref[2:3, :]
    kc_ref[...] = key_conv
    conv_attn = (key_conv * queries.astype(F32)).astype(BF16)
    ca_ref[...] = conv_attn
    tap_terms = nt(taps_ref[...], conv_attn)
    slot = lax.rem(s, 2)
    tap_out[slot] = tap_terms[tap_rows : 2 * tap_rows]
    swap_taps = pltpu.make_async_remote_copy(
        src_ref=tap_out.at[slot],
        dst_ref=tap_in.at[slot],
        send_sem=send_sem.at[slot],
        recv_sem=recv_sem.at[slot],
        device_id=at(me, 1 - mp),
        device_id_type=MESH,
    )
    swap_taps.start()

    @pl.when(jnp.logical_and(s >= 1, s < early))
    def _():
        for piece in range(PIECES // 2, PIECES):
            swap_part(s - 1, piece).start()

    @pl.when(jnp.logical_and(s >= 1, s == early))
    def _():
        swap_part(s - 1, 1).start()

    own_terms = tap_terms[:tap_rows]
    k_ref[...] = nn(hidden, key_ref[...]).astype(BF16)
    v_ref[...] = (nn(hidden, value_ref[...]) + vec_ref[1:2, :]).astype(BF16)
    conv_values = nn(hidden, conv_ref[...]) + vec_ref[3:4, :]
    cv_ref[...] = conv_values
    for c in range(2):
        conv_pad[c, pl.ds(EDGE, rows), :] = conv_values[:, c * LANES : (c + 1) * LANES]

    block = 256
    query_turned[...] = jnp.transpose(q_ref[...])
    value_turned[...] = jnp.transpose(v_ref[...])
    for start in range(0, rows, block):
        part = slice(start, start + block)
        keys = key_window(start, block, rows)
        allowed = columns[keys, KERNEL : KERNEL + 1] == marks_ref[0, KERNEL : KERNEL + 1, part]
        for head in range(heads):
            lanes = slice(head * HEAD_DIM, (head + 1) * HEAD_DIM)
            mine = (only_rows(query_turned[:, part], head) * (HEAD_DIM**-0.5)).astype(BF16)
            scores = jnp.where(allowed, nn(k_ref[keys, :], mine), MASK_FILL)
            top = jnp.max(scores, axis=0, keepdims=True)
            exponent = jnp.exp(scores - top)
            amount = jnp.sum(exponent, axis=0, keepdims=True)
            context_turned[lanes, part] = nn(value_turned[lanes, keys], exponent.astype(BF16)) * (1.0 / amount)
            lse_ref[0, head : head + 1, part] = top + jnp.log(amount)
    lse_ref[0, heads:, :] = jnp.zeros((8 - heads, rows), F32)
    context_turned[heads * HEAD_DIM :, :] = jnp.zeros((WIDE - heads * HEAD_DIM, rows), F32)
    ctx_ref[...] = jnp.transpose(context_turned[...].astype(BF16))

    @pl.when(s == 0)
    def _():
        pass_on(0, third_hops)


    swap_taps.wait()
    logits = (own_terms + tap_in[slot] + bias_ref[:, :1]).reshape(heads, TAP_ROWS, rows)
    tap = lax.broadcasted_iota(jnp.int32, (heads, TAP_ROWS, rows), 1)
    logits = jnp.where(tap < KERNEL, logits, MASK_FILL)
    exponent = jnp.exp(logits - jnp.max(logits, axis=1, keepdims=True))
    probs = exponent / jnp.sum(exponent, axis=1, keepdims=True)
    probs_ref[0] = probs.reshape(tap_rows, rows)
    tap_mask = jnp.where(tap[0] < KERNEL, marks_ref[0], 0.0)
    weights[...] = high_low((probs * tap_mask[None]).reshape(tap_rows, rows), heads)
    conv_block = 128

    def conv_step(i, carry):
        base = pl.multiple_of(i * conv_block, conv_block)
        part = pl.ds(base, conv_block)
        scale = nn(weights[part, :], expand_ref[...])
        for c in range(2):
            total = jnp.zeros((conv_block, LANES), F32)
            for tap in range(KERNEL):
                low = tap * WIDE + c * LANES
                moved = conv_pad[c, pl.ds(base + EDGE + tap - HALF, conv_block), :]
                total = total + scale[:, low : low + LANES] * moved
            cc_ref[part, c * LANES : (c + 1) * LANES] = total.astype(BF16)
        return carry

    lax.fori_loop(0, rows // conv_block, conv_step, 0)

    @pl.when(s == 0)
    def _():
        own_copy.wait()
        end_hops(0)
        pass_on(1, second_hops)
        if early:
            lead_copy.start()
            lead_copy.wait()
            width = heads * HEAD_DIM
            for target, low in ((out0_nat, 0), (out1_nat, width)):
                unpack_wide(depth_wide, lead_ref, 0, low, width)
                target[...] = jnp.transpose(depth_wide[...].astype(BF16))

    @pl.when(s < early)
    def _():
        half = model // 2
        theirs = pl.ds(pl.multiple_of((1 - mp) * half, half), half)

        def part_step(i, carry):
            part = pl.ds(pl.multiple_of(i * block, block), block)
            other = nn(ctx_ref[part, :], out0_nat[:, theirs]) + nn(cc_ref[part, :], out1_nat[:, theirs])
            part_out[s, part, :] = other.astype(BF16)
            return carry

        lax.fori_loop(0, jnp.where(s == early - 1, rows // 2 // block, rows // block), part_step, 0)
        swap_part(s, 0).start()

    @pl.when(s < early - 1)
    def _():
        swap_part(s, 1).start()

    @pl.when(s == min(1, seqs - 1))
    def _():
        pass_on(1, third_hops)

    @pl.when(s == seqs - 1)
    def _():
        end_hops(1)
        for which in range(early):
            for piece in range(PIECES if which < early - 1 else PIECES // 2):
                swap_part(which, piece).wait()


def whole():
    return pl.BlockSpec(memory_space=pltpu.VMEM)


def by_seq(rows, columns):
    return pl.BlockSpec((rows, columns), lambda s: (s, 0))


def by_seq_row(rows, columns):
    return pl.BlockSpec((1, rows, columns), lambda s: (s, 0, 0))


def front(hidden, lengths, first, kernel_weight, biases, second, count, early, ident):
    seqs = lengths.shape[0]
    tokens, model = hidden.shape
    rows = tokens // seqs
    tap_rows = kernel_weight.shape[1] // HEAD_DIM * TAP_ROWS
    parts = count // 4
    place = pl.BlockSpec(memory_space=pl.ANY)
    share = model // count
    split = share + -share % TAP_ROWS

    def wide(kind):
        return jax.ShapeDtypeStruct((tokens, WIDE), kind)

    return pl.pallas_call(
        functools.partial(front_kernel, seqs, count, early),
        grid=(seqs,),
        out_shape=(
            wide(BF16), wide(BF16), wide(BF16), wide(F32),
            jax.ShapeDtypeStruct((tokens, model), BF16),
            wide(F32), wide(BF16),
            jax.ShapeDtypeStruct((seqs, tap_rows, rows), F32),
            wide(BF16), wide(BF16),
            jax.ShapeDtypeStruct((seqs, 8, rows), F32),
            jax.ShapeDtypeStruct((count,) + second.shape[1:], BF16),
            jax.ShapeDtypeStruct((seqs, TAP_ROWS, rows), F32),
            jax.ShapeDtypeStruct((LANES, WIDE), BF16),
            jax.ShapeDtypeStruct((TAP_ROWS, model), F32),
            jax.ShapeDtypeStruct((LANES, KERNEL * WIDE), BF16),
            jax.ShapeDtypeStruct((4 * WIDE, model), BF16),
            jax.ShapeDtypeStruct((WIDE, model), BF16),
            jax.ShapeDtypeStruct((tokens, model // 2), BF16),
        ),
        in_specs=[by_seq(rows, model), pl.BlockSpec(memory_space=pltpu.SMEM)] + [whole()] * 7 + [place],
        out_specs=(
            by_seq(rows, WIDE), by_seq(rows, WIDE), by_seq(rows, WIDE), by_seq(rows, WIDE), by_seq(rows, model),
            by_seq(rows, WIDE), by_seq(rows, WIDE), by_seq_row(tap_rows, rows), by_seq(rows, WIDE), by_seq(rows, WIDE),
            by_seq_row(8, rows), place, by_seq_row(TAP_ROWS, rows),
        )
        + (whole(),) * 5
        + (place,),
        scratch_shapes=[
            pltpu.VMEM((count, split, second.shape[2]), BF16),
            pltpu.VMEM((WIDE, model), BF16),
            pltpu.VMEM((WIDE, model), BF16),
            pltpu.VMEM((max(early, 1), rows, model // 2), BF16),
            pltpu.SemaphoreType.DMA((max(early, 1), PIECES)),
            pltpu.SemaphoreType.DMA((max(early, 1), PIECES)),
        ]
        + [pltpu.VMEM((model, WIDE), BF16)] * 5
        + [
            pltpu.VMEM((8, WIDE), F32),
            pltpu.VMEM((tap_rows, LANES), F32),
            pltpu.VMEM((model, WIDE), F32),
            pltpu.VMEM((WIDE, WIDE), F32),
            pltpu.VMEM((KERNEL, 64, LANES), F32),
            pltpu.VMEM((model // LANES, rows + 2 * EDGE, LANES), F32),
            pltpu.VMEM((2, rows + 2 * EDGE, LANES), F32),
            pltpu.VMEM((rows, LANES), F32),
            pltpu.VMEM((rows, LANES), BF16),
            pltpu.VMEM((WIDE, rows), BF16),
            pltpu.VMEM((WIDE, rows), BF16),
            pltpu.VMEM((WIDE, rows), F32),
            pltpu.VMEM((2, tap_rows, rows), F32),
            pltpu.VMEM((2, tap_rows, rows), F32),
            pltpu.SemaphoreType.DMA((2,)),
            pltpu.SemaphoreType.DMA((2,)),
            pltpu.SemaphoreType.DMA((2,)),
            pltpu.SemaphoreType.DMA((2, 4 * parts - 1)),
            pltpu.SemaphoreType.DMA((2, count)),
        ],
        compiler_params=pltpu.CompilerParams(
            collective_id=ident, has_side_effects=True, vmem_limit_bytes=62 << 20
        ),
        name="front",
    )(hidden, lengths, first, kernel_weight, *biases, second)


def stat_rows(columns):
    rows = columns[0].shape[0]
    diagonal = lax.broadcasted_iota(jnp.int32, (rows, rows), 0) == lax.broadcasted_iota(jnp.int32, (rows, rows), 1)
    lines = [jnp.sum(jnp.where(diagonal, column, 0.0), axis=0, keepdims=True) for column in columns]
    return jnp.concatenate(lines + [jnp.zeros((8 - len(lines), rows), F32)], 0)


def stat_columns(lines):
    rows = lines[0].shape[1]
    wide = jnp.concatenate(lines + [jnp.zeros((8 - len(lines), rows), F32)], 0)
    tall = jnp.transpose(wide)
    return [tall[:, k : k + 1] for k in range(len(lines))]


def row_sums(value):
    rows, columns = value.shape
    return jnp.sum(value.reshape(rows // 8, 8, columns), axis=0)


SLOTS = 4
LAST_LAG = 6
FFN_STEP = 512


def middle_kernel(
    blocks, early,
    early_ref, context_ahead_ref, conv_ahead_ref, context_ref, conv_ref, context_late_ref, conv_late_ref, hidden_ref, grad_ref, grad_late_ref, second_ref,
    ob_ref, gain1_ref, bias1_ref, outb_ref, gain2_ref, bias2_ref, inb_ref,
    output_ref, residual_ref, grad_context_ref, grad_conv_ref, pack_ref, small_ref,
    out0_ref, out1_ref, inner_ref, outer_ref, vec_ref, inner_nat, outer_turned, out0_nat, out1_nat, low_units, branch_ref, acc_out0, acc_out1, state, scale_ring, act_ring, slope_ring, low_ring, summed_ring, normed_ring, stat_ring,
    acc_inner, acc_outer, acc_small, acc_bias,
    branch_send, branch_recv, branch_out, branch_in, stat1_out, stat1_in, stat2_out, stat2_in, stat3_out, stat3_in, back_out, back_in,
    send_sem, recv_sem,
):
    i = pl.program_id(0)
    me = lax.axis_index("mp")
    dp = lax.axis_index("dp")
    width = summed_ring.shape[2]
    hidden_units = inner_ref.shape[0]
    inverse = 1.0 / (2 * width)

    def message(kind, source, target, slot):
        return pltpu.make_async_remote_copy(
            src_ref=source.at[slot],
            dst_ref=target.at[slot],
            send_sem=send_sem.at[kind, slot],
            recv_sem=recv_sem.at[kind, slot],
            device_id=(dp, 1 - me),
            device_id_type=MESH,
        )

    def ahead(slot):
        return pltpu.make_async_remote_copy(
            src_ref=branch_out.at[slot],
            dst_ref=branch_in.at[slot],
            send_sem=branch_send.at[slot],
            recv_sem=branch_recv.at[slot],
            device_id=(dp, 1 - me),
            device_id_type=MESH,
        )

    kinds = [
        None, (stat1_out, stat1_in), (stat2_out, stat2_in), (stat3_out, stat3_in), (back_out, back_in),
    ]

    def fresh(kind, b, slot):
        @pl.when(b >= SLOTS)
        def _():
            message(kind, *kinds[kind], slot).wait_send()

    def vec(row):
        return vec_ref[row : row + 1, :width]

    @pl.when(i == 0)
    def _():
        barrier = pltpu.get_barrier_semaphore()
        pl.semaphore_signal(barrier, inc=1, device_id=(dp, 1 - me), device_id_type=MESH)
        pl.semaphore_wait(barrier, 1)
        cut, cut_ffn = 2 * width // CUTS, hidden_units // CUTS
        unpack_wide(out0_ref, second_ref, 0, 0, width // 2)
        unpack_wide(out1_ref, second_ref, 0, width // 2, width // 2)
        for k in range(CUTS):
            inner_ref[pl.ds(k * cut_ffn, cut_ffn), :] = second_ref[k, pl.ds(cut, cut_ffn), :]
            outer_ref[pl.ds(k * cut_ffn, cut_ffn), :] = second_ref[k, pl.ds(cut + cut_ffn, cut_ffn), :]
        for row, source in enumerate((ob_ref, gain1_ref, bias1_ref)):
            value = as_row(source[...])
            vec_ref[row : row + 1, :width] = jnp.where(me == 0, value[:, :width], value[:, width:])
        for row, source in enumerate((outb_ref, gain2_ref, bias2_ref)):
            vec_ref[3 + row : 4 + row, :width] = as_row(source[...])
        vec_ref[7:8, :] = inb_ref[...]
        inner_nat[...] = jnp.transpose(inner_ref[...])
        outer_turned[...] = jnp.transpose(outer_ref[...])
        out0_nat[...] = jnp.transpose(out0_ref[...])
        out1_nat[...] = jnp.transpose(out1_ref[...])
        acc_inner[...] = jnp.zeros_like(acc_inner)
        acc_outer[...] = jnp.zeros_like(acc_outer)
        acc_out0[...] = jnp.zeros_like(acc_out0)
        acc_out1[...] = jnp.zeros_like(acc_out1)
        acc_small[...] = jnp.zeros_like(acc_small)
        acc_bias[...] = jnp.zeros_like(acc_bias)

    cuts = branch_in.shape[0] // (blocks - early)

    @pl.when(i < cuts * (blocks - early))
    def _():
        theirs = pl.ds(pl.multiple_of((1 - me) * width, width), width)
        other = nn(context_ahead_ref[...], out0_nat[:, theirs]) + nn(conv_ahead_ref[...], out1_nat[:, theirs])
        branch_out[i] = other.astype(BF16)
        ahead(i).start()

    @pl.when(i < blocks)
    def _():
        b = i
        ours = pl.ds(pl.multiple_of(me * width, width), width)
        own = nn(context_ref[...], out0_nat[:, ours]) + nn(conv_ref[...], out1_nat[:, ours])
        state[lax.rem(b, 8)] = hidden_ref[:, ours].astype(F32) + (own + vec(0))

        @pl.when(b < early)
        def _():
            state[lax.rem(b, 8)] += early_ref[...].astype(F32)

    @pl.when(jnp.logical_and(i >= 1, i < blocks + 1))
    def _():
        b = i - 1
        slot = lax.rem(b, SLOTS)
        fresh(1, b, slot)

        @pl.when(b >= early)
        def _():
            size = branch_in.shape[1]
            for k in range(cuts):
                piece = cuts * (b - early) + k
                ahead(piece).wait_recv()
                state[lax.rem(b, 8), pl.ds(k * size, size), :] += branch_in[piece].astype(F32)

        residual = state[lax.rem(b, 8)]
        total = jnp.sum(residual, axis=1, keepdims=True)
        apart = residual - total * (1.0 / width)
        stat1_out[slot] = stat_rows([total, jnp.sum(apart * apart, axis=1, keepdims=True)])
        message(1, *kinds[1], slot).start()

    @pl.when(jnp.logical_and(i >= 2, i < blocks + 2))
    def _():
        b = i - 2
        slot = lax.rem(b, SLOTS)
        two = lax.rem(b, 2)
        message(1, *kinds[1], slot).wait_recv()
        fresh(2, b, slot)
        ours, theirs = stat1_out[slot], stat1_in[slot]
        mean, scale = moments(ours[0:1], ours[1:2], theirs[0:1], theirs[1:2], width)
        mean, scale = stat_columns([mean, scale])
        standard = (state[lax.rem(b, 8)] - mean) * scale
        state[lax.rem(b, 8)] = standard
        scale_ring[lax.rem(b, 4)] = jnp.broadcast_to(scale, scale_ring.shape[1:])
        normed = standard * vec(1) + vec(2)
        low = normed.astype(BF16)
        low_ring[two] = low
        summed = normed + vec(3)
        for start in range(0, hidden_units, FFN_STEP):
            part = pl.ds(start, FFN_STEP)
            inner = nn(low, inner_nat[:, part]) + vec_ref[7:8, start : start + FFN_STEP]
            cdf = 0.5 * (1.0 + lax.erf(inner * INV_ROOT2))
            act = (inner * cdf).astype(BF16)
            act_ring[two, :, part] = act
            slope_ring[two, :, part] = cdf + inner * jnp.exp(-0.5 * inner * inner) * INV_ROOT_TWO_PI
        summed = summed + nn(act_ring[two], outer_ref[...])
        summed_ring[two] = summed
        scaled = grad_ref[...].astype(F32) * vec(4)
        total = jnp.sum(summed, axis=1, keepdims=True)
        apart = summed - total * (1.0 / width)
        stat2_out[slot] = stat_rows(
            [
                total,
                jnp.sum(apart * apart, axis=1, keepdims=True),
                jnp.sum(scaled, axis=1, keepdims=True),
                jnp.sum(scaled * apart, axis=1, keepdims=True),
            ]
        )
        message(2, *kinds[2], slot).start()

    @pl.when(jnp.logical_and(i >= 3, i < blocks + 3))
    def _():
        b = i - 3
        slot = lax.rem(b, SLOTS)
        two = lax.rem(b, 2)
        message(2, *kinds[2], slot).wait_recv()
        fresh(3, b, slot)
        total, square, grads, cross = [stat2_out[slot][k : k + 1] for k in range(4)]
        total_o, square_o, grads_o, cross_o = [stat2_in[slot][k : k + 1] for k in range(4)]
        mean, scale = moments(total, square, total_o, square_o, width)
        mean_grad = (grads + grads_o) * inverse
        product = cross + cross_o + (total * (1.0 / width) - mean) * grads + (total_o * (1.0 / width) - mean) * grads_o
        mean_product = product * scale * inverse
        mean, scale, mean_grad, mean_product = stat_columns([mean, scale, mean_grad, mean_product])
        standard = (summed_ring[two] - mean) * scale
        output_ref[...] = (standard * vec(4) + vec(5)).astype(BF16)
        gradient = grad_late_ref[...].astype(F32)
        grad_summed = scale * (gradient * vec(4) - mean_grad - standard * mean_product)
        low = grad_summed.astype(BF16)
        acc_small[0] += row_sums(low.astype(F32))
        acc_small[1] += row_sums(gradient * standard)
        acc_small[2] += row_sums(gradient)
        normed_low = low_ring[two]
        grad_normed = grad_summed
        for start in range(0, hidden_units, FFN_STEP):
            part = pl.ds(start, FFN_STEP)
            inner_low = (nn(low, outer_turned[:, part]) * slope_ring[two, :, part]).astype(BF16)
            low_units[:, part] = inner_low
            acc_bias[:, part] += row_sums(inner_low.astype(F32))
            acc_outer[:, part] += tn(low, act_ring[two, :, part])
            acc_inner[:, part] += tn(normed_low, inner_low)
        grad_normed = grad_normed + nn(low_units[...], inner_ref[...])
        normed_ring[two] = grad_normed
        standard1 = state[lax.rem(b, 8)]
        scaled = grad_normed * vec(1)
        acc_small[3] += row_sums(grad_normed * standard1)
        acc_small[4] += row_sums(grad_normed)
        sums = stat_rows(
            [jnp.sum(scaled, axis=1, keepdims=True), jnp.sum(scaled * standard1, axis=1, keepdims=True)]
        )
        stat3_out[slot] = sums
        message(3, *kinds[3], slot).start()

    @pl.when(jnp.logical_and(i >= 4, i < blocks + 4))
    def _():
        b = i - 4
        slot = lax.rem(b, SLOTS)
        message(3, *kinds[3], slot).wait_recv()
        fresh(4, b, slot)
        both = stat3_out[slot] + stat3_in[slot]
        first, second = stat_columns([both[0:1], both[1:2]])
        standard = state[lax.rem(b, 8)]
        scaled = normed_ring[lax.rem(b, 2)] * vec(1)
        residual = scale_ring[lax.rem(b, 4)][:, :1] * (scaled - first * inverse - standard * (second * inverse))
        residual_ref[...] = residual
        low = residual.astype(BF16)
        acc_small[5] += row_sums(low.astype(F32))
        back_out[slot] = low
        message(4, *kinds[4], slot).start()

    @pl.when(i >= LAST_LAG)
    def _():
        b = i - LAST_LAG
        slot = lax.rem(b, SLOTS)
        message(4, *kinds[4], slot).wait_recv()
        theirs = pl.ds(pl.multiple_of((1 - me) * width, width), width)
        ours = pl.ds(pl.multiple_of(me * width, width), width)
        branch_ref[:, ours] = back_out[slot]
        branch_ref[:, theirs] = back_in[slot]
        branch = branch_ref[...]
        grad_context_ref[...] = nn(branch, out0_ref[...]).astype(BF16)
        grad_conv_ref[...] = nn(branch, out1_ref[...]).astype(BF16)
        acc_out0[...] += tn(context_late_ref[...], branch)
        acc_out1[...] += tn(conv_late_ref[...], branch)

    @pl.when(i == blocks + LAST_LAG - 1)
    def _():
        for slot in range(cuts * (blocks - early)):
            ahead(slot).wait_send()
        for kind in range(1, 5):
            for slot in range(SLOTS):
                message(kind, *kinds[kind], slot).wait_send()
        cut, cut_ffn = 2 * width // CUTS, hidden_units // CUTS
        both = jnp.concatenate([acc_out0[: width // 2], acc_out1[: width // 2]], 0)
        out_grads = jnp.transpose(both.astype(BF16))
        inner_grads = jnp.transpose(acc_inner[...].astype(BF16))
        outer_grads = jnp.transpose(acc_outer[...].astype(BF16))
        for k in range(CUTS):
            part_ffn = slice(k * cut_ffn, (k + 1) * cut_ffn)
            pack_ref[k, pl.ds(0, cut), :] = out_grads[k * cut : (k + 1) * cut]
            pack_ref[k, pl.ds(cut, cut_ffn), :] = inner_grads[part_ffn]
            pack_ref[k, pl.ds(cut + cut_ffn, cut_ffn), :] = outer_grads[part_ffn]
        small_ref[...] = jnp.zeros_like(small_ref)
        for row in range(6):
            small_ref[row : row + 1, :width] = jnp.sum(acc_small[row], axis=0, keepdims=True)
        small_ref[6:7, :] = jnp.sum(acc_bias[...], axis=0, keepdims=True)


def middle(early, early_rows, context, conv_context, hidden, out_grad, second, vectors, ident):
    tokens, model = hidden.shape
    width = model // 2
    local = context.shape[1]
    units = vectors[-1].shape[1]
    rows = 256
    blocks = tokens // rows
    early = early // rows

    def block(columns, lag):
        return pl.BlockSpec((rows, columns), lambda i: (jnp.clip(i - lag, 0, blocks - 1), 0))

    cuts = 2 if 2 * early >= blocks else 1
    ahead = pl.BlockSpec((rows // cuts, local), lambda i: (jnp.minimum(cuts * early + i, cuts * blocks - 1), 0))
    whole = pl.BlockSpec(memory_space=pltpu.VMEM)
    stat = pltpu.VMEM((SLOTS, 8, rows), F32)
    half = pltpu.VMEM((SLOTS, rows, width), BF16)
    return pl.pallas_call(
        functools.partial(middle_kernel, blocks, early),
        grid=(blocks + LAST_LAG,),
        out_shape=(
            jax.ShapeDtypeStruct((tokens, width), BF16),
            jax.ShapeDtypeStruct((tokens, width), F32),
            jax.ShapeDtypeStruct((tokens, local), BF16),
            jax.ShapeDtypeStruct((tokens, local), BF16),
            jax.ShapeDtypeStruct((CUTS, (model + 2 * units) // CUTS, width), BF16),
            jax.ShapeDtypeStruct((8, units), F32),
        ),
        in_specs=[
            block(width, 0), ahead, ahead, block(local, 0), block(local, 0), block(local, LAST_LAG), block(local, LAST_LAG), block(model, 0), block(width, 2),
            block(width, 3),
        ]
        + [whole] * 8,
        out_specs=(block(width, 3), block(width, 4), block(local, LAST_LAG), block(local, LAST_LAG), whole, whole),
        scratch_shapes=[
            pltpu.VMEM((model, local), BF16),
            pltpu.VMEM((model, local), BF16),
            pltpu.VMEM((units, width), BF16),
            pltpu.VMEM((units, width), BF16),
            pltpu.VMEM((8, units), F32),
            pltpu.VMEM((width, units), BF16),
            pltpu.VMEM((width, units), BF16),
            pltpu.VMEM((local, model), BF16),
            pltpu.VMEM((local, model), BF16),
            pltpu.VMEM((rows, units), BF16),
            pltpu.VMEM((rows, model), BF16),
            pltpu.VMEM((local, model), F32),
            pltpu.VMEM((local, model), F32),
            pltpu.VMEM((8, rows, width), F32),
            pltpu.VMEM((4, rows, 128), F32),
            pltpu.VMEM((2, rows, units), BF16),
            pltpu.VMEM((2, rows, units), F32),
            pltpu.VMEM((2, rows, width), BF16),
            pltpu.VMEM((2, rows, width), F32),
            pltpu.VMEM((2, rows, width), F32),
            pltpu.VMEM((8, 128), F32),
            pltpu.VMEM((width, units), F32),
            pltpu.VMEM((width, units), F32),
            pltpu.VMEM((6, 8, width), F32),
            pltpu.VMEM((8, units), F32),
            pltpu.SemaphoreType.DMA((cuts * (blocks - early),)),
            pltpu.SemaphoreType.DMA((cuts * (blocks - early),)),
            pltpu.VMEM((cuts * (blocks - early), rows // cuts, width), BF16),
            pltpu.VMEM((cuts * (blocks - early), rows // cuts, width), BF16),
            stat, stat, stat, stat, stat, stat, half, half,
            pltpu.SemaphoreType.DMA((5, SLOTS)),
            pltpu.SemaphoreType.DMA((5, SLOTS)),
        ],
        compiler_params=pltpu.CompilerParams(
            collective_id=ident, has_side_effects=True, vmem_limit_bytes=60 << 20
        ),
        name="middle",
    )(early_rows, context, conv_context, context, conv_context, context, conv_context, hidden, out_grad, out_grad, second, *vectors)


def back_kernel(
    seqs, count,
    grad_context, grad_conv_ref, marks_ref, q_ref, k_ref, v_ref, cv_ref, ca_ref, probs_ref, lse_ref,
    hidden_any, residual_any, dl_any, kc_any,
    inputs_ref, point_ref, taps_ref, depth_ref, expand_ref, small_ref, pack_in_ref,
    grad_ref, own_ref, other_ref, pack_ref, table_ref, reduced_ref,
    hidden_ref, residual_ref, dl_ref, kc_ref, load_sem,
    other_out, other_in, other_send, other_recv,
    twin_in, side_in, deep_in, hop_send, hop_recv,
    masks, depth_pad, conv_pad, grad_pad, columns, weights, shifted_weights, tap_terms, products,
    grads, grad_q, grad_k, grad_v, key_turned, probs_all, scores_all, turned_query, rows_total, tap_all,
    acc_in, acc_point, acc_bias, acc_tap, acc_tap_bias, acc_depth,
    tap_out, tap_in, send_sem, recv_sem,
):
    s = pl.program_id(0)
    mp = lax.axis_index("mp")
    dp = lax.axis_index("dp")
    rows, model = hidden_ref.shape
    chunks = model // LANES
    heads = probs_ref.shape[1] // TAP_ROWS
    tap_rows = heads * TAP_ROWS
    half = chunks // 2
    slot = lax.rem(s, 2)
    hops = Hops(count, pack_in_ref, twin_in, side_in, deep_in, hop_send, hop_recv)
    here_rows = pl.ds(pl.multiple_of(s * rows, rows), rows)
    loads = [
        pltpu.make_async_copy(source.at[here_rows], target, load_sem.at[k])
        for k, (source, target) in enumerate(
            [(hidden_any, hidden_ref), (residual_any, residual_ref), (dl_any, dl_ref), (kc_any, kc_ref)]
        )
    ]
    for load in loads:
        load.start()

    def swap_rows(which):
        return pltpu.make_async_remote_copy(
            src_ref=other_out.at[which],
            dst_ref=other_in.at[which],
            send_sem=other_send.at[which],
            recv_sem=other_recv.at[which],
            device_id=(dp, 1 - mp),
            device_id_type=MESH,
        )

    @pl.when(s == 0)
    def _():
        greet_all(count)
        hops.start_first()
        for pad in (depth_pad, conv_pad, grad_pad):
            for start in (0, EDGE + rows):
                pad[:, pl.ds(start, EDGE), :] = jnp.zeros((pad.shape[0], EDGE, LANES), F32)
        for acc in (acc_in, acc_point, acc_bias, acc_tap, acc_tap_bias, acc_depth):
            acc[...] = jnp.zeros_like(acc)

    spread_marks(marks_ref, columns)
    block = 256

    for c in range(2):
        lanes = slice(c * LANES, (c + 1) * LANES)
        grad_pad[c, pl.ds(EDGE, rows), :] = grad_conv_ref[:, lanes].astype(F32)
        conv_pad[c, pl.ds(EDGE, rows), :] = cv_ref[:, lanes]

    probs = probs_ref[0].reshape(heads, TAP_ROWS, rows)
    tap = lax.broadcasted_iota(jnp.int32, (heads, TAP_ROWS, rows), 1)
    tap_mask = jnp.where(tap < KERNEL, jnp.broadcast_to(marks_ref[...], (heads, TAP_ROWS, rows)), 0.0)
    masked = (probs * tap_mask).reshape(tap_rows, rows)
    flat_tap = tap.reshape(tap_rows, rows)
    moved = jnp.zeros_like(masked)
    for j in range(KERNEL):
        turn = (j - HALF) % rows
        turned = pltpu.roll(masked, turn, 1) if turn else masked
        moved = jnp.where(flat_tap == j, turned, moved)
    shifted_weights[...] = high_low(moved, heads)
    conv_block = 128

    def conv_step(i, carry):
        base = pl.multiple_of(i * conv_block, conv_block)
        part = pl.ds(base, conv_block)
        scale = nn(shifted_weights[part, :], expand_ref[...])
        for c in range(2):
            here = grad_pad[c, pl.ds(base + EDGE, conv_block), :]
            total = jnp.zeros((conv_block, LANES), F32)
            for j in range(KERNEL):
                low = j * WIDE + c * LANES
                products[:, low : low + LANES] = (
                    here * conv_pad[c, pl.ds(base + EDGE + j - HALF, conv_block), :]
                ).astype(BF16)
                total = total + scale[:, low : low + LANES] * grad_pad[
                    c, pl.ds(base + EDGE + HALF - j, conv_block), :
                ]
            grads[part, 3 * WIDE + c * LANES : 3 * WIDE + (c + 1) * LANES] = total.astype(BF16)
        tap_terms[part, :] = nt(products[...], expand_ref[...])
        return carry

    lax.fori_loop(0, rows // conv_block, conv_step, 0)
    grad_taps = jnp.transpose(tap_terms[...])[:tap_rows].reshape(heads, TAP_ROWS, rows) * tap_mask
    grad_logits = probs * (grad_taps - jnp.sum(probs * grad_taps, axis=1, keepdims=True))
    grad_logits = grad_logits.reshape(tap_rows, rows).astype(BF16)
    tap_out[slot] = grad_logits
    swap_taps = pltpu.make_async_remote_copy(
        src_ref=tap_out.at[slot],
        dst_ref=tap_in.at[slot],
        send_sem=send_sem.at[slot],
        recv_sem=recv_sem.at[slot],
        device_id=(dp, 1 - mp),
        device_id_type=MESH,
    )
    swap_taps.start()

    grad_k[...] = jnp.zeros_like(grad_k)
    grad_v[...] = jnp.zeros_like(grad_v)

    key_turned[...] = jnp.transpose(k_ref[...])
    for start in range(0, rows, block):
        part = slice(start, start + block)
        keys = key_window(start, block, rows)
        allowed = columns[keys, KERNEL : KERNEL + 1] == marks_ref[0, KERNEL : KERNEL + 1, part]
        query, context = q_ref[part, :], grad_context[part, :]
        query_turned, context_turned = jnp.transpose(query), jnp.transpose(context)
        for head in range(heads):
            lanes = slice(head * HEAD_DIM, (head + 1) * HEAD_DIM)
            place = slice(head * block, (head + 1) * block)
            mine = (only_rows(query_turned, head) * (HEAD_DIM**-0.5)).astype(BF16)
            scores = jnp.where(allowed, nn(k_ref[keys, :], mine), MASK_FILL)
            probs = jnp.exp(scores - lse_ref[0, head : head + 1, part])
            probs_all[keys, place] = probs.astype(BF16)
            mixed = probs * nn(v_ref[keys, :], only_rows(context_turned, head).astype(BF16))
            grad_scores = (mixed - probs * jnp.sum(mixed, axis=0, keepdims=True)).astype(BF16)
            scores_all[keys, place] = grad_scores
            turned_query[lanes, :] = nn(key_turned[lanes, keys], grad_scores)
        turned_query[heads * HEAD_DIM :, :] = jnp.zeros((WIDE - heads * HEAD_DIM, block), F32)
        grad_q[part, :] = jnp.transpose(turned_query[...])
        contexts = jnp.concatenate([only(context, head).astype(BF16) for head in range(heads)], 0)
        queries = jnp.concatenate([(only(query, head) * (HEAD_DIM**-0.5)).astype(BF16) for head in range(heads)], 0)
        grad_v[keys, :] += nn(probs_all[keys, :], contexts)
        grad_k[keys, :] += nn(scores_all[keys, :], queries)

    for load in loads:
        load.wait()
    swap_taps.wait()
    tap_all[...] = jnp.zeros_like(tap_all)
    tap_all[:tap_rows, :] = tap_out[slot].astype(F32)
    tap_all[tap_rows : 2 * tap_rows, :] = tap_in[slot].astype(F32)
    every = tap_all[...]
    acc_tap[...] += nn(every.astype(BF16), ca_ref[...])
    acc_tap_bias[...] += sum(every[:, c * LANES : (c + 1) * LANES] for c in range(rows // LANES))
    weights[...] = jnp.transpose(every.astype(BF16))

    def key_step(i, carry):
        base = pl.multiple_of(i * block, block)
        part = pl.ds(base, block)
        grad_attn = nn(weights[part, :], taps_ref[...]).astype(BF16).astype(F32)
        query = q_ref[part, :].astype(F32)
        key_low = (grad_attn * query).astype(BF16)
        grads[part, 4 * WIDE : 5 * WIDE] = key_low
        grad_query = grad_q[part, :] * (HEAD_DIM**-0.5) + grad_attn * kc_ref[part, :]
        grads[part, :WIDE] = grad_query.astype(BF16)
        grads[part, WIDE : 2 * WIDE] = grad_k[part, :].astype(BF16)
        grads[part, 2 * WIDE : 3 * WIDE] = grad_v[part, :].astype(BF16)
        acc_bias[...] += row_sums(grads[part, :].astype(F32))
        grad_depth = nn(key_low, point_ref[...])
        total = nn(grads[part, : 4 * WIDE], inputs_ref[...])
        for c in range(chunks):
            lanes = slice(c * LANES, (c + 1) * LANES)
            depth_pad[c, pl.ds(base + EDGE, block), :] = grad_depth[:, lanes]
            rows_total[c, part, :] = total[:, lanes]
        return carry

    lax.fori_loop(0, rows // block, key_step, 0)
    acc_point[...] += tn(grads[:, 4 * WIDE : 5 * WIDE], dl_ref[...])
    acc_in[...] += tn(hidden_ref[...], grads[:, : 4 * WIDE])
    step = masks.shape[1]

    def depth_step(i, carry):
        base = pl.multiple_of(i * step, step)
        part = pl.ds(base, step)
        for j in range(KERNEL):
            masks[j] = jnp.broadcast_to(columns[part, j : j + 1], (step, LANES))
        for first in range(0, chunks, 2):
            total = [rows_total[first + k, part, :] for k in range(2)]
            lanes = [slice((first + k) * LANES, (first + k + 1) * LANES) for k in range(2)]
            here = [hidden_ref[part, lanes[k]].astype(F32) for k in range(2)]
            for j in range(KERNEL):
                mirror = KERNEL - 1 - j
                mask = masks[j]
                for k in range(2):
                    near = depth_pad[first + k, pl.ds(base + EDGE + j - HALF, step), :] * mask
                    total[k] = total[k] + near * depth_ref[mirror : mirror + 1, lanes[k]]
                    acc_depth[mirror, :, lanes[k]] += row_sums(near * here[k])
            for k in range(2):
                rows_total[first + k, part, :] = total[k]
        return carry

    lax.fori_loop(0, rows // step, depth_step, 0)

    @pl.when(s >= 1)
    def _():
        which = s - 1
        swap_rows(which).wait_recv()
        grad_ref[...] = own_ref[...] + other_in[which].astype(F32)

    for c in range(half):
        lanes = slice(c * LANES, (c + 1) * LANES)
        own_ref[:, lanes] = rows_total[mp * half + c] + residual_ref[:, lanes]

    @pl.when(s < seqs - 1)
    def _():
        for c in range(half):
            lanes = slice(c * LANES, (c + 1) * LANES)
            other_out[s, :, lanes] = rows_total[(1 - mp) * half + c].astype(BF16)
        swap_rows(s).start()

    @pl.when(s == 0)
    def _():
        hops.start_second()

    @pl.when(s == min(1, seqs - 1))
    def _():
        hops.start_third()

    @pl.when(s == seqs - 1)
    def _():
        for c in range(half):
            lanes = slice(c * LANES, (c + 1) * LANES)
            other_ref[:, lanes] = rows_total[(1 - mp) * half + c].astype(BF16)
        hops.finish(reduced_ref)
        for which in range(seqs - 1):
            swap_rows(which).wait_send()
        width = heads * HEAD_DIM
        group = model // 2
        cut = model // CUTS
        empty = jnp.zeros((cut, width), F32)
        point_grad = jnp.transpose(acc_point[...].astype(BF16)).astype(F32)
        for k in range(CUTS):
            part = pl.ds(k * cut, cut)
            for place in range(2):
                first = acc_in[part, 2 * place * WIDE : 2 * place * WIDE + width]
                second = acc_in[part, (2 * place + 1) * WIDE : (2 * place + 1) * WIDE + width]
                pack_ref[k, pl.ds(place * cut, cut), :] = jnp.concatenate([first, second], 1).astype(BF16)
            pack_ref[k, pl.ds(2 * cut, cut), :] = jnp.concatenate([point_grad[k * cut : (k + 1) * cut, :width], empty], 1).astype(BF16)
        table_ref[...] = jnp.zeros_like(table_ref)
        lane = lax.broadcasted_iota(jnp.int32, (LANES, WIDE), 1)
        taps = jnp.where(lane == width, jnp.sum(acc_tap_bias[...], axis=1, keepdims=True), acc_tap[...])
        own_taps = [taps[h * TAP_ROWS : h * TAP_ROWS + KERNEL] for h in range(heads)]
        other_taps = [taps[tap_rows + h * TAP_ROWS : tap_rows + h * TAP_ROWS + KERNEL] for h in range(heads)]
        for h in range(heads):
            table_ref[KERNEL * h : KERNEL * (h + 1), :] = jnp.where(mp == 0, own_taps[h], other_taps[h])
            later = KERNEL * (heads + h)
            table_ref[later : later + KERNEL, :] = jnp.where(mp == 0, other_taps[h], own_taps[h])
        for row, place in ((54, 0), (55, 2), (56, 4), (57, 3)):
            table_ref[row : row + 1, :] = jnp.sum(acc_bias[:, place * WIDE : (place + 1) * WIDE], axis=0, keepdims=True)

        def lay(row, value):
            for k in range(-(-value.shape[1] // WIDE)):
                piece = value[:, k * WIDE : (k + 1) * WIDE]
                table_ref[row + k : row + k + 1, : piece.shape[1]] = piece

        for row, source in ((58, 0), (60, 1), (62, 2)):
            lay(row, small_ref[source : source + 1, :group])
        lay(64, small_ref[6:7, :])
        for row, source in ((99, 3), (102, 4), (105, 5)):
            value = small_ref[source : source + 1, :group]
            blank = jnp.zeros_like(value)
            lay(row, jnp.where(mp == 0, jnp.concatenate([value, blank], 1), jnp.concatenate([blank, value], 1)))
        for j in range(KERNEL):
            total = jnp.sum(acc_depth[j], axis=0, keepdims=True)
            for k in range(model // WIDE):
                row = TABLE_OWN + KERNEL * k + j
                table_ref[row : row + 1, :] = total[:, k * WIDE : (k + 1) * WIDE]


def back(hidden, grad_context, grad_conv, residual, marks, kept, turned_weights, taps, depth, expand, small, pack, count, ident):
    q, k, v, cv, dl, kc, ca, probs, lse = kept
    seqs, _, rows = marks.shape
    tokens, model = hidden.shape
    width = model // 2
    tap_rows = probs.shape[1]
    wide = by_seq(rows, WIDE)
    place = pl.BlockSpec(memory_space=pl.ANY)
    padded_rows = rows + 2 * EDGE
    vmem = pltpu.VMEM
    swaps = max(seqs - 1, 1)
    return pl.pallas_call(
        functools.partial(back_kernel, seqs, count),
        grid=(seqs,),
        out_shape=(
            jax.ShapeDtypeStruct((tokens, width), F32),
            jax.ShapeDtypeStruct((rows, width), F32),
            jax.ShapeDtypeStruct((rows, width), BF16),
            jax.ShapeDtypeStruct((CUTS, 3 * model // CUTS, width), BF16),
            jax.ShapeDtypeStruct((TABLE_ROWS, WIDE), F32),
            jax.ShapeDtypeStruct(pack.shape[1:], F32),
        ),
        in_specs=[wide, wide, by_seq_row(TAP_ROWS, rows), wide, wide, wide, wide, wide]
        + [by_seq_row(tap_rows, rows), by_seq_row(8, rows)]
        + [place] * 4
        + [whole()] * 7,
        out_specs=(pl.BlockSpec((rows, width), lambda s: (jnp.maximum(s - 1, 0), 0)),) + (whole(),) * 5,
        scratch_shapes=[
            vmem((rows, model), BF16),
            vmem((rows, width), F32),
            vmem((rows, model), BF16),
            vmem((rows, WIDE), F32),
            pltpu.SemaphoreType.DMA((4,)),
            vmem((swaps, rows, width), BF16),
            vmem((swaps, rows, width), BF16),
            pltpu.SemaphoreType.DMA((swaps,)),
            pltpu.SemaphoreType.DMA((swaps,)),
        ]
        + hop_scratch(count, pack.shape[1], pack.shape[2])
        + [
            vmem((KERNEL, 64, LANES), F32),
            vmem((model // LANES, padded_rows, LANES), F32),
            vmem((2, padded_rows, LANES), F32),
            vmem((2, padded_rows, LANES), F32),
            vmem((rows, LANES), F32),
            vmem((rows, LANES), BF16),
            vmem((rows, LANES), BF16),
            vmem((rows, LANES), F32),
            vmem((128, KERNEL * WIDE), BF16),
            vmem((rows, 5 * WIDE), BF16),
            vmem((rows, WIDE), F32),
            vmem((rows, WIDE), F32),
            vmem((rows, WIDE), F32),
            vmem((WIDE, rows), BF16),
            vmem((rows, tap_rows // TAP_ROWS * 256), BF16),
            vmem((rows, tap_rows // TAP_ROWS * 256), BF16),
            vmem((WIDE, 256), F32),
            vmem((model // LANES, rows, LANES), F32),
            vmem((LANES, rows), F32),
            vmem((model, 4 * WIDE), F32),
            vmem((WIDE, model), F32),
            vmem((8, 5 * WIDE), F32),
            vmem((LANES, WIDE), F32),
            vmem((LANES, LANES), F32),
            vmem((TAP_ROWS, 8, model), F32),
            vmem((2, tap_rows, rows), BF16),
            vmem((2, tap_rows, rows), BF16),
            pltpu.SemaphoreType.DMA((2,)),
            pltpu.SemaphoreType.DMA((2,)),
        ],
        compiler_params=pltpu.CompilerParams(
            collective_id=ident, has_side_effects=True, vmem_limit_bytes=63 << 20
        ),
        name="back",
    )(
        grad_context, grad_conv, marks, q, k, v, cv, ca, probs, lse, hidden, residual, dl, kc,
        *turned_weights, taps, depth, expand, small, pack,
    )


def padded(value, multiple):
    rows = value.shape[-2]
    extra = -rows % multiple
    return jnp.pad(value, [(0, 0)] * (value.ndim - 2) + [(0, extra), (0, 0)])


def recut(pack, sizes, unit, start, count):
    if count == start:
        return pack
    parts, low = [], 0
    for size in sizes:
        rows = pack[:, low : low + size * unit].reshape(-1, pack.shape[2])
        parts.append(rows.reshape(count, -1, pack.shape[2]))
        low += size * unit
    return padded(jnp.concatenate(parts, 1), TAP_ROWS)


def gather_plain(weights, count, ident):
    q, k, v, c, p, depth, out_w, in_w, outer_w = weights
    depth = jnp.pad(depth.T, ((0, 0), (0, q.shape[1] - KERNEL)))
    pairs = [jnp.concatenate(pair, 1) for pair in ((q, k), (v, c), (p, depth), (out_w[0], out_w[1]))]
    first = padded(jnp.concatenate(pairs[:3], 0), TAP_ROWS)[None]
    second = padded(jnp.concatenate([pairs[3], in_w[0], outer_w[0]], 0), TAP_ROWS)[None]
    return recut(gather(first, count, ident), (1, 1, 1), q.shape[0], count, CUTS), second


def final_plain(first, second, table, share, share_ffn, width, group, taps):
    model = 2 * group
    depth = jnp.concatenate([table[72 + KERNEL * k : 72 + KERNEL * (k + 1)] for k in range(model // WIDE)], 1)
    row = lambda at_row, size: table[at_row : at_row + 6].reshape(-1)[:size]
    out = first[:share]
    return (
        second[:share, :width], second[:share, width:], second[share : 2 * share, :width],
        row(54, width), row(55, width),
        lax.dynamic_slice_in_dim(depth, lax.axis_index("dp") * share, share, 1),
        second[2 * share : 3 * share, :width], row(56, width),
        table[:taps, :width], table[:taps, width], second[share : 2 * share, width:], row(57, width),
        jnp.stack([out[:, :width], out[:, width:]]), row(105, model), row(99, model), row(102, model),
        first[share : share + share_ffn], row(64, 4 * group)[None], first[share + share_ffn : share + 2 * share_ffn],
        row(58, group), row(60, group), row(62, group),
    )


def on_device(
    count,
    hidden, doc_lengths, query_weight, key_weight, value_weight, query_bias, value_bias,
    depth_weight, point_weight, point_bias, kernel_weight, kernel_bias, conv_weight, conv_bias,
    out_weight, out_bias, norm1_gain, norm1_bias, ffn_in_weight, ffn_in_bias, ffn_out_weight,
    ffn_out_bias, norm2_gain, norm2_bias, out_grad,
):
    share, width = query_weight.shape
    model = hidden.shape[1]
    group = ffn_out_bias.shape[0]
    share_ffn = ffn_out_weight.shape[1]
    heads = width // HEAD_DIM
    weights = (
        query_weight, key_weight, value_weight, conv_weight, point_weight, depth_weight,
        out_weight.transpose(0, 2, 1), ffn_in_weight.transpose(0, 2, 1), ffn_out_weight,
    )
    first, second = (gather_first if share % TAP_ROWS == 0 else gather_plain)(weights, count, 1)
    seqs = doc_lengths.shape[0]
    early = seqs - 1 if count == CUTS else 0
    biases = [kernel_bias, query_bias, value_bias, point_bias, conv_bias]
    q, k, v, cv, dl, kc, ca, probs, cc, ctx, lse, second_all, marks, taps, depth, expand, *rest = front(
        hidden, doc_lengths, first, kernel_weight.T, biases, second, count, early, 2
    )
    turned_weights, early_rows = rest[:2], rest[2]
    vectors = [out_bias, norm1_gain, norm1_bias, ffn_out_bias, norm2_gain, norm2_bias, ffn_in_bias]
    output, grad_residual, grad_context, grad_conv, pack_mid, sums_mid = middle(
        max(2 * early - 1, 0) * (hidden.shape[0] // seqs) // 2, early_rows, ctx, cc, hidden, out_grad, recut(second_all, (1, 2, 2), share, count, CUTS), vectors, 4
    )
    grad_input, own_last, other_last, pack_back, table, first_sum = back(
        hidden, grad_context, grad_conv, grad_residual, marks, (q, k, v, cv, dl, kc, ca, probs, lse),
        turned_weights, taps, depth, expand, sums_mid, recut(pack_mid, (1, 2, 2), model // CUTS, CUTS, count), count, 5,
    )
    second_sum, totals, grad_input = tail(
        recut(pack_back, (1, 1, 1), model // CUTS, CUTS, count), table, own_last, other_last, grad_input, count, 3
    )
    small_cuts = (share, share_ffn, width, group, 2 * heads * KERNEL)
    if share % TAP_ROWS == 0:
        results = final(first_sum, second_sum, totals, *small_cuts, count)
    else:
        results = final_plain(first_sum, second_sum, totals, *small_cuts)
    q_g, k_g, v_g, q_b, v_b, depth_g, p_g, p_b, kw_g, kb_g, c_g, c_b, out_g, out_b, gain1, bias1 = results[:16]
    inner_g, inner_b, outer_g, outer_b, gain2, bias2 = results[16:]
    return (
        output, grad_input, q_g, k_g, v_g, q_b, v_b, depth_g, p_g, p_b, kw_g.T, kb_g, c_g, c_b, out_g.transpose(0, 2, 1),
        out_b, gain1, bias1, inner_g.T[None], inner_b, outer_g[None], outer_b, gain2, bias2,
    )


def solution(mesh):
    in_specs = (
        P("dp", None),
        P("dp", None),
        P("dp", "mp"),
        P("dp", "mp"),
        P("dp", "mp"),
        P("mp"),
        P("mp"),
        P(None, "dp"),
        P("dp", "mp"),
        P("mp"),
        P("mp", None),
        P(),
        P("dp", "mp"),
        P("mp"),
        P(None, "mp", "dp"),
        P(),
        P(),
        P(),
        P("mp", None, "dp"),
        P("mp", None),
        P("mp", "dp", None),
        P("mp"),
        P("mp"),
        P("mp"),
        P("dp", "mp"),
    )
    out_specs = (
        P("dp", "mp"),
        P("dp", "mp"),
        P("dp", "mp"),
        P("dp", "mp"),
        P("dp", "mp"),
        P("mp"),
        P("mp"),
        P(None, "dp"),
        P("dp", "mp"),
        P("mp"),
        P("mp", None),
        P(),
        P("dp", "mp"),
        P("mp"),
        P(None, "mp", "dp"),
        P(),
        P(),
        P(),
        P("mp", None, "dp"),
        P("mp", None),
        P("mp", "dp", None),
        P("mp"),
        P("mp"),
        P("mp"),
    )
    return jax.shard_map(
        functools.partial(on_device, mesh.shape["dp"]), mesh=mesh, in_specs=in_specs, out_specs=out_specs, check_vma=False
    )
```
